32 devices in a mesh: dp: 4 (over y, core), rep: 2 (over x), tensor: 4 (over z).
Axes of the slice: x: 2, y: 2, z: 4, core: 2. Of those that a mesh axis runs over, the one named last changes fastest.
Arguments:
- query_tokens: bfloat16 [2, 8, 256, 768], P(None, ('dp', 'rep')), may hold values from -6 to 6
- query_drop: int32 [2, 8, 256], P(None, ('dp', 'rep')), may hold values 0 or 1
- query_length: int32 [2, 8], P(None, ('dp', 'rep')), may hold values from 1 to 256, 1280 in all within a row
- key_tokens: bfloat16 [2, 8, 256, 768], P(None, ('dp', 'rep')), may hold values from -6 to 6
- key_drop: int32 [2, 8, 256], P(None, ('dp', 'rep')), may hold values 0 or 1
- key_length: int32 [2, 8], P(None, ('dp', 'rep')), may hold values from 1 to 256, 1280 in all within a row
- negatives: bfloat16 [8192, 768], P(('rep', 'tensor')), may hold values from -0.59765625 to 0.59765625
- attend_weight: bfloat16 [2, 2, 768, 3, 768], P(None, None, None, None, 'tensor'), may hold values from -0.21875 to 0.21875
- attend_bias: bfloat16 [2, 2, 2, 768], P(None, None, None, 'tensor'), may hold values from -1.5 to 1.5
- merge_weight: bfloat16 [2, 2, 768, 768], P(None, None, 'tensor'), may hold values from -0.875 to 0.875
- merge_bias: bfloat16 [2, 2, 768], replicated, may hold values from -1.5 to 1.5
- expand_weight: bfloat16 [2, 2, 768, 3072], P(None, None, None, 'tensor'), may hold values from -0.21875 to 0.21875
- expand_bias: bfloat16 [2, 2, 3072], P(None, None, 'tensor'), may hold values from -1.5 to 1.5
- shrink_weight: bfloat16 [2, 2, 3072, 768], P(None, None, 'tensor'), may hold values from -0.109375 to 0.109375
- shrink_bias: bfloat16 [2, 2, 768], replicated, may hold values from -1.5 to 1.5
- norm_gain: bfloat16 [2, 2, 2, 768], replicated, may hold values from 0.5 to 1.5
- norm_shift: bfloat16 [2, 2, 2, 768], replicated, may hold values from -1.5 to 1.5
Outputs:
- activations: bfloat16 [2, 8, 256, 768], P(None, ('dp', 'rep'), 'tensor')
- input_grad: bfloat16 [2, 8, 256, 768], P(None, ('dp', 'rep'), 'tensor')
- attend_weight_grad: float32 [2, 768, 3, 768], P(None, ('dp', 'rep'), None, 'tensor')
- attend_bias_grad: float32 [2, 2, 768], P(None, None, 'tensor')
- merge_weight_grad: float32 [2, 768, 768], P(None, 'tensor', ('dp', 'rep'))
- merge_bias_grad: float32 [2, 768], P(None, ('dp', 'rep'))
- expand_weight_grad: float32 [2, 768, 3072], P(None, ('dp', 'rep'), 'tensor')
- expand_bias_grad: float32 [2, 3072], P(None, 'tensor')
- shrink_weight_grad: float32 [2, 3072, 768], P(None, 'tensor', ('dp', 'rep'))
- shrink_bias_grad: float32 [2, 768], P(None, ('dp', 'rep'))
- norm_gain_grad: float32 [2, 2, 768], P(None, None, ('dp', 'rep'))
- norm_shift_grad: float32 [2, 2, 768], P(None, None, ('dp', 'rep'))
- loss: float32 [], replicated
The draws below stay inside these ranges and needn't reach their ends.
Inputs may be any that keep to these rules, and one draw needn't show every extreme that they name: `query_length`: in each micro-batch the lengths of the 8 query crops sum to 1280 and the longest is exactly 256. `key_length`: in each micro-batch the lengths of the 8 key crops sum to 1280 and the longest is exactly 256.
All inputs are finite; a program needn't handle non-finite values. No bound on the sum of `query_drop` or of `query_length` or of `key_drop` or of `key_length` on one device may be relied on, other than what follows from the above.
Results may differ from the reference program's by a relative error of at most 0.018.
Values may be sent and summed in bfloat16 or wider, within the bound.
A program may use at most 192 MiB of HBM per device.

```python
import math
import jax
import jax.numpy as jnp
import numpy as np
from jax import lax

D = 768
FF = 3072
HEAD_DIM = 64
LAYERS = 2
ENCODERS = 2
CROP_SLOTS = 256
MICRO = 2
CROPS = 8
QUEUE = 8192


def plant(drawn, key, low, top_value):
    longest = drawn.shape.index(max(drawn.shape))
    spots = []
    for shift in (0, 1):
        where = [jax.random.randint(jax.random.fold_in(key, axis), (), 0, length) for axis, length in enumerate(drawn.shape)]
        where[longest] = (where[longest] + shift) % drawn.shape[longest]
        spots.append(tuple(where))
    return drawn.at[spots[0]].set(low).at[spots[1]].set(top_value)


def spiked(array, rng, source, target, parts, factor):
    def block_of(dim):
        return (jnp.arange(array.shape[dim]) // (array.shape[dim] // parts)).reshape((-1,) + (1,) * (array.ndim - 1 - dim))

    near = jax.random.permutation(rng, parts)[block_of(target)]
    second = (block_of(target) + parts // 2) % parts
    return jnp.where((block_of(source) == near) | (block_of(source) == second), factor * array, array)


def block_scale(key, shape, shards, least, high):
    gain = 1.0
    for dim, shards_of in shards:
        draws = jax.random.uniform(jax.random.fold_in(jax.random.fold_in(key, 6), dim), (shards_of,), jnp.float32, least / len(shards), high / len(shards))
        gain = gain * jnp.repeat(jnp.exp(draws), shape[dim] // shards_of).reshape((-1,) + (1,) * (len(shape) - 1 - dim))
    return gain


def split_up(count, total, most, lean):
    portions = [(1 << 20) // math.isqrt(standing ** lean) + 1 for standing in range(2, count + 1)]
    surplus, holding = total - most - (count - 1), [1] * (count - 1)
    while surplus > 0:
        free = [i for i in range(count - 1) if holding[i] < most]
        mass, remaining = sum([portions[i] for i in free]), surplus
        for i in free:
            more = min(most - holding[i], max(1, remaining * portions[i] // mass), surplus)
            holding[i] = holding[i] + more
            surplus = surplus - more
    return np.array([most] + holding)


def uneven(rng, count, total, bound, skew):
    if count == 2:
        one = jax.random.randint(rng, (), max(1, total - bound), min(bound, total - 1) + 1)
        return jnp.stack([one, total - one])
    tallies = jnp.asarray(split_up(count, total, bound, skew), jnp.int32)
    twos = (count - 1) // 2
    giver, sink = tallies[1:1 + 2 * twos:2], tallies[2:2 + 2 * twos:2]
    room = jnp.minimum(giver - 1, bound - sink)
    moved = jax.random.randint(jax.random.fold_in(rng, 1), (twos,), 0, 1 << 20) % (room + 1)
    tallies = tallies.at[1:1 + 2 * twos:2].set(giver - moved).at[2:2 + 2 * twos:2].set(sink + moved)
    return tallies[jax.random.permutation(jax.random.fold_in(rng, 2), count)]


def gaussian(key, shape, spread, reach, shards=(), dtype=jnp.bfloat16):
    array = jax.random.normal(key, shape, jnp.float32) * spread
    if len(shards) > 0:
        array = block_scale(key, shape, shards, -0.22, 0.18) * array
    return jnp.clip(array, min=-reach, max=reach).astype(dtype)


def noise_with(rng, shape, spread, limit, cuts, heavy, dtype=jnp.bfloat16):
    values = spread * jax.random.normal(rng, shape, jnp.float32)
    if cuts:
        values = values * block_scale(rng, shape, cuts, -0.22, 0.18)
    return jnp.clip(spiked(values, jax.random.fold_in(rng, 3), *heavy), -limit, limit).astype(dtype)


def setup_inputs(seed: int = 0) -> dict:
    arg_keys = jax.random.split(jax.random.key(seed), 18)
    query_tokens = noise_with(arg_keys[0], (MICRO, CROPS, CROP_SLOTS, D), 1.0, 6.0, ((1, 8),), (1, 3, 8, 2.0))
    query_drop = plant((jax.random.randint(arg_keys[1], (MICRO, CROPS, CROP_SLOTS), 0, 10) < 1).astype(jnp.int32), jax.random.fold_in(arg_keys[1], 1), 0, 1)
    query_length = jax.vmap(lambda own: uneven(own, CROPS, CROPS * CROP_SLOTS * 5 // 8, CROP_SLOTS, 2))(jax.random.split(arg_keys[2], MICRO)).reshape((MICRO, CROPS)).astype(jnp.int32)
    key_tokens = noise_with(arg_keys[3], (MICRO, CROPS, CROP_SLOTS, D), 1.0, 6.0, ((1, 8),), (1, 3, 8, 2.0))
    key_drop = plant((jax.random.randint(arg_keys[4], (MICRO, CROPS, CROP_SLOTS), 0, 10) < 1).astype(jnp.int32), jax.random.fold_in(arg_keys[4], 1), 0, 1)
    key_length = jax.vmap(lambda own: uneven(own, CROPS, CROPS * CROP_SLOTS * 5 // 8, CROP_SLOTS, 2))(jax.random.split(arg_keys[5], MICRO)).reshape((MICRO, CROPS)).astype(jnp.int32)
    negatives = gaussian(arg_keys[6], (QUEUE, D), 0.1, 0.59765625, ((0, 8),))
    attend_weight = gaussian(arg_keys[7], (ENCODERS, LAYERS, D, 3, D), D ** -0.5, 0.21875, ((4, 4),))
    attend_bias = gaussian(arg_keys[8], (ENCODERS, LAYERS, 2, D), 0.3, 1.5, ((3, 4),))
    merge_weight = gaussian(arg_keys[9], (ENCODERS, LAYERS, D, D), (D // 16) ** -0.5, 0.875, ((2, 4),))
    merge_bias = gaussian(arg_keys[10], (ENCODERS, LAYERS, D), 0.3, 1.5)
    expand_weight = gaussian(arg_keys[11], (ENCODERS, LAYERS, D, FF), D ** -0.5, 0.21875, ((3, 4),))
    expand_bias = gaussian(arg_keys[12], (ENCODERS, LAYERS, FF), 0.3, 1.5, ((2, 4),))
    shrink_weight = gaussian(arg_keys[13], (ENCODERS, LAYERS, FF, D), FF ** -0.5, 0.109375, ((2, 4),))
    shrink_bias = gaussian(arg_keys[14], (ENCODERS, LAYERS, D), 0.3, 1.5)
    norm_gain = jnp.clip(1.0 + 0.1 * jax.random.normal(arg_keys[15], (ENCODERS, LAYERS, 2, D), jnp.float32), 0.5, 1.5).astype(jnp.bfloat16)
    norm_shift = gaussian(arg_keys[16], (ENCODERS, LAYERS, 2, D), 0.3, 1.5)
    return {"query_tokens": query_tokens, "query_drop": query_drop, "query_length": query_length, "key_tokens": key_tokens, "key_drop": key_drop, "key_length": key_length, "negatives": negatives, "attend_weight": attend_weight, "attend_bias": attend_bias, "merge_weight": merge_weight, "merge_bias": merge_bias, "expand_weight": expand_weight, "expand_bias": expand_bias, "shrink_weight": shrink_weight, "shrink_bias": shrink_bias, "norm_gain": norm_gain, "norm_shift": norm_shift}


@jax.custom_vjp
def low(v):
    return lax.optimization_barrier(v.astype(jnp.bfloat16)).astype(jnp.float32)

@jax.custom_vjp
def low_back(v):
    return v

def low_keep(v):
    return (low(v), None)

def low_pass(kept, grad):
    return (grad,)

def back_keep(v):
    return (v, None)

def back_low(kept, grad):
    return (low(grad),)
low.defvjp(low_keep, low_pass)
low_back.defvjp(back_keep, back_low)
SOFTMAX_WARMTH = 0.05
NORM_EPS = 1e-12
UNIT_EPS = 1e-06
MASKED = -1e+30
TOP_PRECISION = lax.Precision.HIGHEST

def packing_plan(dropped_flags, crop_lengths):
    position = lax.broadcasted_iota(jnp.int32, dropped_flags.shape, dropped_flags.ndim - 1)
    retained_flag = ((position < crop_lengths[..., None]) & ((dropped_flags == 0) | (position == 0))).astype(jnp.int32)
    slot_lookup = (jnp.cumsum(retained_flag, axis=-1) - 1).astype(jnp.int32)
    token_counts = lax.optimization_barrier(jnp.sum(retained_flag, axis=-1)).astype(jnp.int32)
    matches = (slot_lookup[..., None, :] == position[..., :, None]) & (retained_flag[..., None, :] == 1)
    source_index = lax.optimization_barrier(jnp.sum(jnp.where(matches, position[..., None, :], 0), axis=-1)).astype(jnp.int32)
    return (retained_flag, slot_lookup, source_index, token_counts)

def layer_norm(total_rows, gain_row, shift_row):
    mean_row = lax.optimization_barrier(jnp.mean(total_rows, axis=-1, keepdims=True))
    centered = total_rows - mean_row
    variance = lax.optimization_barrier(jnp.mean(centered * centered, axis=-1, keepdims=True))
    return centered * lax.rsqrt(variance + NORM_EPS) * gain_row + shift_row

def encoder_layer(hidden, valid_keys, params):
    heads_matrix, heads_offset, merge_matrix, merge_offset, expand_matrix, expand_offset, shrink_matrix, shrink_offset, gain_rows, shift_rows = params
    row_count, model_width = hidden.shape
    head_count = model_width // HEAD_DIM
    hidden_low = low(hidden)
    project = low_back(jnp.einsum('sd,dtf->stf', hidden_low, heads_matrix, precision=TOP_PRECISION))
    queries = low(project[:, 0] + heads_offset[0]).reshape(row_count, head_count, HEAD_DIM)
    key_rows = low(project[:, 1]).reshape(row_count, head_count, HEAD_DIM)
    values = low(project[:, 2] + heads_offset[1]).reshape(row_count, head_count, HEAD_DIM)
    raw_scores = low_back(jnp.einsum('qhe,khe->hqk', queries, key_rows, precision=TOP_PRECISION))
    scores = jnp.where(valid_keys[None, None, :], raw_scores * HEAD_DIM ** (-0.5), MASKED)
    row_top = lax.optimization_barrier(jnp.max(scores, axis=-1, keepdims=True))
    exponent = jnp.exp(scores - row_top)
    chances = low(exponent / lax.optimization_barrier(jnp.sum(exponent, axis=-1, keepdims=True)))
    mixed_heads = low(low_back(jnp.einsum('hqk,khe->qhe', chances, values, precision=TOP_PRECISION))).reshape(row_count, model_width)
    branch = low_back(jnp.dot(mixed_heads, merge_matrix, precision=TOP_PRECISION)) + merge_offset
    first_norm = layer_norm(hidden + branch, gain_rows[0], shift_rows[0])
    inner_pre = low_back(jnp.dot(low(first_norm), expand_matrix, precision=TOP_PRECISION)) + expand_offset
    active = low(jax.nn.gelu(inner_pre, approximate=False))
    second = low_back(jnp.dot(active, shrink_matrix, precision=TOP_PRECISION)) + shrink_offset
    return layer_norm(first_norm + second, gain_rows[1], shift_rows[1])

def encode(tokens, dropped_flags, crop_lengths, params):
    retained_flag, slot_lookup, source_index, token_counts = packing_plan(dropped_flags, crop_lengths)
    position = lax.broadcasted_iota(jnp.int32, dropped_flags.shape, 2)
    valid_keys = position < token_counts[..., None]
    picked = jnp.take_along_axis(tokens, source_index[..., None], axis=2)
    compact = jnp.where(valid_keys[..., None], picked, 0.0)
    flat_rows = compact.reshape(-1, CROP_SLOTS, D)
    flat_valid = valid_keys.reshape(-1, CROP_SLOTS)

    def one_crop(pair):
        rows_now, mask_now = pair
        for layer_at in range(LAYERS):
            rows_now = encoder_layer(rows_now, mask_now, tuple((item[layer_at] for item in params)))
        return rows_now
    outputs = lax.map(jax.checkpoint(one_crop), (flat_rows, flat_valid)).reshape(compact.shape)
    pooled = lax.optimization_barrier(jnp.sum(jnp.where(valid_keys[..., None], outputs, 0.0), axis=2)) / token_counts[..., None].astype(jnp.float32)
    return (outputs, pooled)

def unit_rows(vectors):
    return vectors * lax.rsqrt(lax.optimization_barrier(jnp.sum(vectors * vectors, axis=-1, keepdims=True)) + UNIT_EPS)

def contrast(query_direction, key_direction, queued_negative_keys):
    positive_score = lax.optimization_barrier(jnp.sum(query_direction * key_direction, axis=-1)) / SOFTMAX_WARMTH
    query_flattened = low(query_direction).reshape(-1, D)
    negative_score = jnp.dot(query_flattened, queued_negative_keys.T, precision=TOP_PRECISION) / SOFTMAX_WARMTH
    negative_score = negative_score.reshape(positive_score.shape + (queued_negative_keys.shape[0],))
    row_top = jnp.maximum(lax.optimization_barrier(jnp.max(negative_score, axis=-1)), positive_score)
    exponent_sum = jnp.exp(positive_score - row_top) + lax.optimization_barrier(jnp.sum(jnp.exp(negative_score - row_top[..., None]), axis=-1))
    return row_top + jnp.log(exponent_sum) - positive_score

def reference(query_tokens, query_drop, query_length, key_tokens, key_drop, key_length, negatives, attend_weight, attend_bias, merge_weight, merge_bias, expand_weight, expand_bias, shrink_weight, shrink_bias, norm_gain, norm_shift):
    stacked = (attend_weight, attend_bias, merge_weight, merge_bias, expand_weight, expand_bias, shrink_weight, shrink_bias, norm_gain, norm_shift)
    params_all = tuple((item.astype(jnp.float32) for item in stacked))
    query_params = tuple((item[0] for item in params_all))
    moving_params = tuple((item[1] for item in params_all))
    queued_negative_keys = negatives.astype(jnp.float32)
    unused_out, key_pooled = encode(key_tokens.astype(jnp.float32), key_drop, key_length, moving_params)
    key_direction = unit_rows(key_pooled)

    def objective(tokens, params):
        outputs, pooled = encode(tokens, query_drop, query_length, params)
        per_query = contrast(unit_rows(pooled), key_direction, queued_negative_keys)
        return (CROP_SLOTS * jnp.sum(per_query), (outputs, per_query))
    scaled, pullback, aux_out = jax.vjp(objective, query_tokens.astype(jnp.float32), query_params, has_aux=True)
    token_grad, param_grads = pullback(jnp.ones_like(scaled))
    outputs, per_query = aux_out
    return (outputs.astype(jnp.bfloat16), token_grad.astype(jnp.bfloat16), param_grads[0], param_grads[1], param_grads[2], param_grads[3], param_grads[4], param_grads[5], param_grads[6], param_grads[7], param_grads[8], param_grads[9], jnp.mean(per_query))
```

```python
import jax
import jax.numpy as jnp
from jax import lax
from jax.experimental import pallas as pl
from jax.experimental.pallas import tpu as pltpu
from jax.sharding import PartitionSpec as P

HEAD_DIM = 64
CROP_SLOTS = 256
SOFTMAX_WARMTH = 0.05
NORM_EPS = 1e-12
UNIT_EPS = 1e-06
MASKED = -1e30
TOP_PRECISION = lax.Precision.HIGHEST
ROOT_HALF = 0.7071067811865476
INV_ROOT_TAU = 0.3989422804014327

MESH = pl.DeviceIdType.MESH
BF = jnp.bfloat16
F32 = jnp.float32
CHUNKS = 4
TILE = 64
VMEM_LIMIT = 62 * 1024 * 1024


def nn(a, b):
    return jnp.dot(a, b, preferred_element_type=F32)


def nt(a, b):
    return lax.dot_general(a, b, (((1,), (1,)), ((), ())), preferred_element_type=F32)


def tn(a, b):
    return lax.dot_general(a, b, (((0,), (0,)), ((), ())), preferred_element_type=F32)


def greet_line():
    z = lax.axis_index("tensor")
    sem = pltpu.get_barrier_semaphore()
    for d in (1, 2, 3):
        pl.semaphore_signal(sem, inc=1, device_id={"tensor": (z + d) % 4}, device_id_type=MESH)
    pl.semaphore_wait(sem, 3)


class Line:
    def __init__(self, part, sbuf, tbuf, x1, x2, s_sem, t_sem, r1, r2):
        z = lax.axis_index("tensor")
        self.mid = (z + 1) // 2 == 1
        self.end = (z + 1) // 2 != 1
        self.inner = 1 + z // 2
        self.outer = 3 * (z // 2)
        self.cross = 3 - z
        self.part, self.sbuf, self.tbuf, self.x1, self.x2 = part, sbuf, tbuf, x1, x2
        self.s_sem, self.t_sem, self.r1, self.r2 = s_sem, t_sem, r1, r2
        self.size = part.shape[1] // CHUNKS

    def rows(self, c):
        return pl.ds(c * self.size, self.size)

    def to_inner(self, s, c):
        return pltpu.make_async_remote_copy(
            src_ref=self.sbuf.at[s, self.rows(c)], dst_ref=self.x2.at[s, self.rows(c)],
            send_sem=self.s_sem.at[s, c], recv_sem=self.r2.at[s, c],
            device_id={"tensor": self.inner}, device_id_type=MESH)

    def to_cross(self, s, c, slot):
        return pltpu.make_async_remote_copy(
            src_ref=self.sbuf.at[s, self.rows(c)], dst_ref=self.x1.at[slot, s, self.rows(c)],
            send_sem=self.s_sem.at[s, c], recv_sem=self.r1.at[slot, s, c],
            device_id={"tensor": self.cross}, device_id_type=MESH)

    def to_outer(self, s, c, slot):
        return pltpu.make_async_remote_copy(
            src_ref=self.tbuf.at[s, self.rows(c)], dst_ref=self.x1.at[slot, s, self.rows(c)],
            send_sem=self.t_sem.at[s, c], recv_sem=self.r1.at[slot, s, c],
            device_id={"tensor": self.outer}, device_id_type=MESH)

    def begin(self, s):
        @pl.when(self.end)
        def _():
            for c in range(CHUNKS):
                rows = self.rows(c)
                self.sbuf[s, rows] = self.part[s, rows].astype(BF)
                self.to_inner(s, c).start()

    def inward(self, s, c, slot, live):
        @pl.when(self.mid & live)
        def _():
            rows = self.rows(c)
            self.to_inner(s, c).wait_recv()
            self.sbuf[s, rows] = (self.part[s, rows] + self.x2[s, rows].astype(F32)).astype(BF)
            self.to_cross(s, c, slot).start()

    def outward(self, s, c, slot, live):
        @pl.when(self.mid & live)
        def _():
            rows = self.rows(c)
            self.to_cross(s, c, slot).wait_recv()
            joint = self.part[s, rows] + self.x1[slot, s, rows].astype(F32)
            self.part[s, rows] = joint + self.x2[s, rows].astype(F32)
            self.tbuf[s, rows] = joint.astype(BF)
            self.to_outer(s, c, slot).start()

    def finish(self, s, slot):
        @pl.when(self.end)
        def _():
            for c in range(CHUNKS):
                rows = self.rows(c)
                self.to_outer(s, c, slot).wait_recv()
                self.part[s, rows] = self.part[s, rows] + self.x1[slot, s, rows].astype(F32)
            for c in range(CHUNKS):
                self.to_inner(s, c).wait_send()

        @pl.when(self.mid)
        def _():
            for c in range(CHUNKS):
                self.to_cross(s, c, slot).wait_send()
                self.to_outer(s, c, slot).wait_send()


def line_scratch(streams, rows, width):
    return [
        pltpu.VMEM((streams, rows, width), F32),
        pltpu.VMEM((streams, rows, width), BF),
        pltpu.VMEM((streams, rows, width), BF),
        pltpu.VMEM((2, streams, rows, width), BF),
        pltpu.VMEM((streams, rows, width), BF),
        pltpu.SemaphoreType.DMA((streams, CHUNKS)),
        pltpu.SemaphoreType.DMA((streams, CHUNKS)),
        pltpu.SemaphoreType.DMA((2, streams, CHUNKS)),
        pltpu.SemaphoreType.DMA((streams, CHUNKS)),
    ]


def tiles(rows, body):
    def step(c, carry):
        body(pl.ds(pl.multiple_of(c * TILE, TILE), TILE))
        return carry

    lax.fori_loop(0, rows // TILE, step, 0)


def normalize(total, gain, shift):
    mean = jnp.mean(total, axis=-1, keepdims=True)
    centered = total - mean
    inverse = lax.rsqrt(jnp.mean(centered * centered, axis=-1, keepdims=True) + NORM_EPS)
    normed = centered * inverse
    return normed * gain + shift, normed, inverse


def head_masks(width, scale):
    lane = lax.broadcasted_iota(jnp.int32, (1, width), 1)
    return [
        jnp.where((lane >= h * HEAD_DIM) & (lane < (h + 1) * HEAD_DIM), scale, 0.0).astype(BF)
        for h in range(width // HEAD_DIM)
    ]


def forward_kernel(
    q_tok, q_drop, q_len, k_tok, k_drop, k_len,
    wqkv, abias, wm, mbias, we, ebias, ws, sbias, gains, shifts,
    acts, pooled, slots, xin, proj, probs, mixed, n1, i1, first, slope, active, n2, i2,
    h, hb, qkv, pb, mx, inner, act, vbias, valid, part, sbuf, tbuf, x1, x2, s_sem, t_sem, r1, r2,
):
    micro = q_tok.shape[0]
    rows, width = q_tok.shape[2:]
    layers = we.shape[1]
    local = wm.shape[2]
    heads = local // HEAD_DIM
    streams = 2 * micro
    last = 2 * layers * streams
    greet_line()
    line = Line(part, sbuf, tbuf, x1, x2, s_sem, t_sem, r1, r2)

    def compact(tok, drop, length, slots_out, s, m):
        pos = lax.broadcasted_iota(jnp.int32, (1, rows), 1)
        kept = (pos < length) & ((drop[m] == 0) | (pos == 0))
        kept_f = jnp.broadcast_to(jnp.where(kept, 1.0, 0.0), (16, rows))
        down = lax.broadcasted_iota(jnp.int32, (rows, rows), 0)
        along = lax.broadcasted_iota(jnp.int32, (rows, rows), 1)
        tri = jnp.where(down <= along, 1.0, 0.0).astype(BF)
        order = nn(kept_f.astype(BF), tri)[0:1] - 1.0
        order = jnp.where(kept, order, -1.0)
        count = jnp.sum(kept_f[0:1], axis=-1, keepdims=True)
        pick = jnp.where(order == down.astype(F32), 1.0, 0.0).astype(BF)
        rows_now = nn(pick, tok[m, 0])
        h[s] = rows_now
        hb[...] = rows_now.astype(BF)
        fits = pos.astype(F32) < count
        vbias[s] = jnp.broadcast_to(jnp.where(fits, 0.0, MASKED), (8, rows))
        valid[s] = jnp.broadcast_to(jnp.where(fits, 1.0, 0.0), (8, rows))
        pooled[s, 1:2] = jnp.broadcast_to(count, (1, width))
        if slots_out:
            slots[m] = jnp.broadcast_to(order, (8, rows))

    def at(i):
        j = jnp.maximum(i, 0)
        return j % streams, (j // streams) % 2, (i >= 0) & (i < last)

    def serve(i, *which):
        s1, slot1, live1 = at(i - 1)
        s2, slot2, live2 = at(i - 2)
        for kind, c in which:
            if kind == 1:
                line.inward(s1, c, slot1, live1)
            else:
                line.outward(s2, c, slot2, live2)

    def attention_pass(layer, s):
        i = layer * 2 * streams + s
        e, m = 1 - s // micro, s % micro
        is_q = s >= micro
        serve(i, (1, 0))

        @pl.when(layer == 0)
        def _():
            @pl.when(s < micro)
            def _():
                compact(k_tok, k_drop, k_len[m, 0], False, s, m)

            @pl.when(is_q)
            def _():
                compact(q_tok, q_drop, q_len[m, 0], True, s, m)

        @pl.when(layer > 0)
        def _():
            line.finish(s, 1)
            lp = layer - 1
            bias = sbias[e, lp].astype(F32)
            gain = gains[e, lp, 1:2].astype(F32)
            shift = shifts[e, lp, 1:2].astype(F32)

            def norm(r):
                out, normed, inverse = normalize(h[s, r] + part[s, r] + bias, gain, shift)
                h[s, r] = out
                hb[r] = out.astype(BF)

                @pl.when(is_q)
                def _():
                    n2[lp, m, r] = normed
                    i2[lp, m, r] = jnp.broadcast_to(inverse, (TILE, 128))

            tiles(rows, norm)

        serve(i, (1, 1))

        @pl.when(layer < layers)
        def _():
            @pl.when(is_q)
            def _():
                xin[layer, m] = hb[...]

            rows_now = hb[...]
            for j in range(3):
                bias = 0.0 if j == 1 else abias[e, layer, j // 2 : j // 2 + 1].astype(F32)
                qkv[j] = (nn(rows_now, wqkv[e, layer, j]) + bias).astype(BF)

            @pl.when(is_q)
            def _():
                for j in range(3):
                    proj[layer, m, j] = qkv[j]

        serve(i, (1, 2), (2, 0))
        q_masks = head_masks(local, HEAD_DIM**-0.5)
        v_masks = head_masks(local, 1.0)

        def one_head(hd):
            @pl.when(layer < layers)
            def _():
                scores = nt(qkv[0] * q_masks[hd], qkv[1]) + vbias[s, 0:1]
                expo = jnp.exp(scores - jnp.max(scores, axis=-1, keepdims=True))
                chance = (expo / jnp.sum(expo, axis=-1, keepdims=True)).astype(BF)
                pb[hd] = chance

                @pl.when(is_q)
                def _():
                    probs[layer, m, hd] = chance

                out = nn(chance, qkv[2] * v_masks[hd])
                if hd == 0:
                    mx[...] = out
                else:
                    mx[...] += out

        for hd in range(heads):
            one_head(hd)
            if hd == 0:
                serve(i, (1, 3), (2, 1))
            elif hd == 1:
                serve(i, (2, 2))

        @pl.when(layer < layers)
        def _():
            mixed_now = mx[...].astype(BF)

            @pl.when(is_q)
            def _():
                mixed[layer, m] = mixed_now

            part[s] = nn(mixed_now, wm[e, layer])
            line.begin(s)

        serve(i, (2, 3))

        @pl.when(layer == layers)
        def _():
            pooled[s, 0:1] = jnp.dot(valid[s], h[s], precision=TOP_PRECISION, preferred_element_type=F32)[0:1]

            @pl.when(is_q)
            def _():
                acts[m] = hb[...]

    def forward_pass(layer, s):
        i = (layer * 2 + 1) * streams + s
        e, m = 1 - s // micro, s % micro
        is_q = s >= micro
        serve(i, (1, 0))
        line.finish(s, 0)
        bias = mbias[e, layer].astype(F32)
        gain = gains[e, layer, 0:1].astype(F32)
        shift = shifts[e, layer, 0:1].astype(F32)

        def norm(r):
            out, normed, inverse = normalize(h[s, r] + part[s, r] + bias, gain, shift)
            h[s, r] = out
            hb[r] = out.astype(BF)

            @pl.when(is_q)
            def _():
                n1[layer, m, r] = normed
                i1[layer, m, r] = jnp.broadcast_to(inverse, (TILE, 128))
                first[layer, m, r] = out.astype(BF)

        tiles(rows, norm)
        serve(i, (1, 1), (2, 0))
        inner[...] = nn(hb[...], we[e, layer])
        serve(i, (1, 2), (2, 1))
        bias_e = ebias[e, layer].astype(F32)

        def gelu(r):
            u = inner[r] + bias_e
            phi = 0.5 * (1.0 + lax.erf(u * ROOT_HALF))
            out = (u * phi).astype(BF)
            act[r] = out

            @pl.when(is_q)
            def _():
                active[layer, m, r] = out
                slope[layer, m, r] = phi + u * jnp.exp(-0.5 * u * u) * INV_ROOT_TAU

        tiles(rows, gelu)
        serve(i, (1, 3), (2, 2))
        part[s] = nn(act[...], ws[e, layer])
        line.begin(s)
        serve(i, (2, 3))

    def layer_step(layer, carry):
        def a_step(s, c):
            attention_pass(layer, s)
            return c

        lax.fori_loop(0, streams, a_step, 0)

        @pl.when(layer < layers)
        def _():
            def f_step(s, c):
                forward_pass(layer, s)
                return c

            lax.fori_loop(0, streams, f_step, 0)

        return carry

    lax.fori_loop(0, layers + 1, layer_step, 0)


def run_forward(q_tok, q_drop, q_len, k_tok, k_drop, k_len, weights):
    micro, _, rows, width = q_tok.shape
    wqkv, abias, wm, mbias, we, ebias, ws, sbias, gains, shifts = weights
    layers, local, units = we.shape[1], wm.shape[2], we.shape[3]
    heads = local // HEAD_DIM
    streams = 2 * micro
    lm = (layers, micro)
    shapes = [
        ((micro, rows, width), BF),
        ((streams, 8, width), F32),
        ((micro, 8, rows), F32),
        (lm + (rows, width), BF),
        (lm + (3, rows, local), BF),
        (lm + (heads, rows, rows), BF),
        (lm + (rows, local), BF),
        (lm + (rows, width), F32),
        (lm + (rows, 128), F32),
        (lm + (rows, width), BF),
        (lm + (rows, units), F32),
        (lm + (rows, units), BF),
        (lm + (rows, width), F32),
        (lm + (rows, 128), F32),
    ]
    vm = pl.BlockSpec(memory_space=pltpu.VMEM)
    sm = pl.BlockSpec(memory_space=pltpu.SMEM)
    return pl.pallas_call(
        forward_kernel,
        out_shape=[jax.ShapeDtypeStruct(*s) for s in shapes],
        in_specs=[vm, vm, sm, vm, vm, sm] + [vm] * 10,
        out_specs=[vm] * len(shapes),
        scratch_shapes=[
            pltpu.VMEM((streams, rows, width), F32),
            pltpu.VMEM((rows, width), BF),
            pltpu.VMEM((3, rows, local), BF),
            pltpu.VMEM((heads, rows, rows), BF),
            pltpu.VMEM((rows, local), F32),
            pltpu.VMEM((rows, units), F32),
            pltpu.VMEM((rows, units), BF),
            pltpu.VMEM((streams, 8, rows), F32),
            pltpu.VMEM((streams, 8, rows), F32),
        ]
        + line_scratch(streams, rows, width),
        compiler_params=pltpu.CompilerParams(
            collective_id=0, has_side_effects=True, vmem_limit_bytes=VMEM_LIMIT
        ),
        name="encoders_forward",
    )(q_tok, q_drop, q_len, k_tok, k_drop, k_len, *weights)


def norm_back(g, normed, inverse, gain):
    scaled = g * gain
    return inverse * (
        scaled
        - jnp.mean(scaled, axis=-1, keepdims=True)
        - normed * jnp.mean(scaled * normed, axis=-1, keepdims=True)
    )


def fold(x):
    return jnp.sum(x.reshape(x.shape[0] // 8, 8, x.shape[1]), axis=0)


def backward_kernel(
    pgrad, slots, xin, proj, probs, mixed, n1, i1, first, slope, active, n2, i2,
    wqkv, wm, we, ws, gains,
    g_in, g_attend, g_merge, g_expand, g_shrink, g_vec, g_abias,
    dr, low, dinner, tmp, dqkv, dsc, dpart, part, sbuf, tbuf, x1, x2, s_sem, t_sem, r1, r2,
):
    layers, micro, rows, width = xin.shape
    local = wm.shape[1]
    heads = local // HEAD_DIM
    streams = micro
    last = 2 * layers * streams
    greet_line()
    line = Line(part, sbuf, tbuf, x1, x2, s_sem, t_sem, r1, r2)
    g_vec[...] = jnp.zeros_like(g_vec)
    g_abias[...] = jnp.zeros_like(g_abias)

    def serve(i, *which):
        j = jnp.maximum(i - 1, 0)
        s, slot, live = j % streams, (j // streams) % 2, (i >= 1) & (i <= last)
        for kind, c in which:
            if kind == 1:
                line.inward(s, c, slot, live)
            else:
                line.outward(s, c, slot, live)

    def add_to(ref, s, value):
        @pl.when(s == 0)
        def _():
            ref[...] = value

        @pl.when(s > 0)
        def _():
            ref[...] += value

    def mlp_back(step, s):
        layer = layers - 1 - step
        i = step * 2 * streams + s

        @pl.when(step == 0)
        def _():
            def seed(c, carry):
                r = pl.ds(pl.multiple_of(c * TILE, TILE), TILE)
                pos = (lax.broadcasted_iota(jnp.int32, (TILE, 1), 0) + c * TILE).astype(F32)
                part[s, r] = jnp.where(pos < pgrad[s, 1:2, 0:1], pgrad[s, 0:1], 0.0)
                dr[s, r] = jnp.zeros((TILE, width), F32)
                return carry

            lax.fori_loop(0, rows // TILE, seed, 0)

        @pl.when(step > 0)
        def _():
            line.finish(s, 1)

        gain = gains[layer, 1:2].astype(F32)

        def back(r):
            g = part[s, r] + dr[s, r]
            normed = n2[layer, s, r]
            out = norm_back(g, normed, i2[layer, s, r][:, 0:1], gain)
            dr[s, r] = out
            low[s, r] = out.astype(BF)
            g_vec[layer, 1] += fold(g * normed)
            g_vec[layer, 3] += fold(g)
            g_vec[layer, 4] += fold(out)

        tiles(rows, back)
        serve(i, (1, 0))
        tmp[...] = nt(low[s], ws[layer])
        serve(i, (1, 1))

        def slopes(r):
            out = tmp[r] * slope[layer, s, r]
            dinner[r] = out.astype(BF)
            g_vec[layer, 6] += fold(out)

        tiles(rows, slopes)
        part[s] = nt(dinner[...], we[layer])
        line.begin(s)
        serve(i, (1, 2), (2, 0))
        add_to(g_shrink.at[layer], s, tn(active[layer, s], low[s]))
        serve(i, (1, 3), (2, 1))
        add_to(g_expand.at[layer], s, tn(first[layer, s], dinner[...]))
        serve(i, (2, 2), (2, 3))

    def attention_back(step, s):
        layer = layers - 1 - step
        i = (step * 2 + 1) * streams + s
        line.finish(s, 0)
        gain = gains[layer, 0:1].astype(F32)

        def back(r):
            g = part[s, r] + dr[s, r]
            normed = n1[layer, s, r]
            out = norm_back(g, normed, i1[layer, s, r][:, 0:1], gain)
            dr[s, r] = out
            low[s, r] = out.astype(BF)
            g_vec[layer, 0] += fold(g * normed)
            g_vec[layer, 2] += fold(g)
            g_vec[layer, 5] += fold(out)

        tiles(rows, back)
        serve(i, (1, 0))
        dmix = nt(low[s], wm[layer]).astype(BF)
        serve(i, (1, 1))
        masks = head_masks(local, 1.0)
        for hd in range(heads):
            chance_b = probs[layer, s, hd]
            chance = chance_b.astype(F32)
            dm = dmix * masks[hd]
            dch = nt(dm, proj[layer, s, 2])
            ds = chance * (dch - jnp.sum(chance * dch, axis=-1, keepdims=True))
            draw = (ds * HEAD_DIM**-0.5).astype(BF)
            dq = nn(draw, proj[layer, s, 1] * masks[hd])
            dk = tn(draw, proj[layer, s, 0] * masks[hd])
            dv = tn(chance_b, dm)
            if hd == 0:
                dqkv[0] = dq
                dqkv[1] = dk
                dqkv[2] = dv
            else:
                dqkv[0] += dq
                dqkv[1] += dk
                dqkv[2] += dv
            if hd == 0:
                serve(i, (1, 2), (2, 0))
            elif hd == 1:
                serve(i, (1, 3), (2, 1))
        g_abias[layer, 0] += fold(dqkv[0])
        g_abias[layer, 1] += fold(dqkv[2])
        for j in range(3):
            dsc[j] = dqkv[j].astype(BF)
        part[s] = nt(dsc[0], wqkv[layer, 0]) + nt(dsc[1], wqkv[layer, 1]) + nt(dsc[2], wqkv[layer, 2])
        line.begin(s)
        serve(i, (2, 2), (2, 3))
        add_to(g_merge.at[layer], s, tn(mixed[layer, s], low[s]))
        for j in range(3):
            add_to(g_attend.at[layer, j], s, tn(xin[layer, s], dsc[j]))

    def layer_step(step, carry):
        def m_step(s, c):
            mlp_back(step, s)
            return c

        def a_step(s, c):
            attention_back(step, s)
            return c

        lax.fori_loop(0, streams, m_step, 0)
        lax.fori_loop(0, streams, a_step, 0)
        return carry

    lax.fori_loop(0, layers, layer_step, 0)

    def tail(s, carry):
        @pl.when(s == 0)
        def _():
            for c in range(CHUNKS):
                serve(last, (1, c), (2, c))

        line.finish(s, 1)

        def back(r):
            low[s, r] = (part[s, r] + dr[s, r]).astype(BF)

        tiles(rows, back)
        down = lax.broadcasted_iota(jnp.int32, (rows, rows), 0).astype(F32)
        pick = jnp.where(slots[s, 0:1] == down, 1.0, 0.0).astype(BF)
        g_in[s] = tn(pick, low[s]).astype(BF)
        return carry

    lax.fori_loop(0, streams, tail, 0)


def run_backward(pgrad, slots, saved, weights):
    wqkv, abias, wm, mbias, we, ebias, ws, sbias, gains, shifts = weights
    layers, micro, rows, width = saved[0].shape
    local, units = wm.shape[2], we.shape[3]
    heads = local // HEAD_DIM
    shapes = [
        ((micro, rows, width), BF),
        ((layers, 3, width, local), F32),
        ((layers, local, width), F32),
        ((layers, width, units), F32),
        ((layers, units, width), F32),
        ((layers, 7, 8, width), F32),
        ((layers, 2, 8, local), F32),
    ]
    vm = pl.BlockSpec(memory_space=pltpu.VMEM)
    return pl.pallas_call(
        backward_kernel,
        out_shape=[jax.ShapeDtypeStruct(*s) for s in shapes],
        in_specs=[vm] * 18,
        out_specs=[vm] * len(shapes),
        scratch_shapes=[
            pltpu.VMEM((micro, rows, width), F32),
            pltpu.VMEM((micro, rows, width), BF),
            pltpu.VMEM((rows, units), BF),
            pltpu.VMEM((rows, units), F32),
            pltpu.VMEM((3, rows, local), F32),
            pltpu.VMEM((3, rows, local), BF),
            pltpu.VMEM((8, 128), F32),
        ]
        + line_scratch(micro, rows, width),
        compiler_params=pltpu.CompilerParams(
            collective_id=1, has_side_effects=True, vmem_limit_bytes=VMEM_LIMIT
        ),
        name="encoder_backward",
    )(pgrad, slots, *saved, wqkv[0], wm[0], we[0], ws[0], gains[0])


def contrast(mean_q, mean_k, negatives):
    key_dir = mean_k * lax.rsqrt(jnp.sum(mean_k * mean_k, axis=-1, keepdims=True) + UNIT_EPS)
    scale = lax.rsqrt(jnp.sum(mean_q * mean_q, axis=-1, keepdims=True) + UNIT_EPS)
    direction = mean_q * scale
    positive = jnp.sum(direction * key_dir, axis=-1) / SOFTMAX_WARMTH
    micro, width = mean_q.shape
    asked = lax.all_gather(direction.astype(BF), "rep", axis=0, tiled=True)
    logits = nt(asked, negatives) / SOFTMAX_WARMTH
    top = jnp.max(logits, axis=-1, keepdims=True)
    expo = jnp.exp(logits - top)
    total = jnp.sum(expo, axis=-1, keepdims=True)
    keys = jnp.dot(expo, negatives.astype(F32), precision=TOP_PRECISION)
    packed = jnp.concatenate([keys, jnp.broadcast_to(top, (top.shape[0], 128)), jnp.broadcast_to(total, (top.shape[0], 128))], axis=1)
    pieces = lax.all_gather(packed, ("rep", "tensor"), axis=0, tiled=False)
    mine = lax.dynamic_slice_in_dim(pieces, lax.axis_index("rep") * micro, micro, 1)
    keys, top, total = mine[..., :width], mine[..., width], mine[..., width + 128]
    best = jnp.maximum(jnp.max(top, axis=0), positive)
    weight = jnp.exp(top - best)
    own = jnp.exp(positive - best)
    total = jnp.sum(total * weight, axis=0) + own
    keys = jnp.sum(keys * weight[..., None], axis=0) + own[:, None] * key_dir
    per_query = best + jnp.log(total) - positive
    dqn = (keys / total[:, None] - key_dir) * (CROP_SLOTS / SOFTMAX_WARMTH)
    mean_grad = scale * (dqn - direction * jnp.sum(direction * dqn, axis=-1, keepdims=True))
    return per_query, mean_grad


def per_device(
    query_tokens, query_drop, query_length, key_tokens, key_drop, key_length, negatives,
    attend_weight, attend_bias, merge_weight, merge_bias, expand_weight, expand_bias,
    shrink_weight, shrink_bias, norm_gain, norm_shift,
):
    micro, _, rows, width = query_tokens.shape
    weights = (
        jnp.transpose(attend_weight, (0, 1, 3, 2, 4)),
        attend_bias,
        merge_weight,
        merge_bias[:, :, None],
        expand_weight,
        expand_bias[:, :, None],
        shrink_weight,
        shrink_bias[:, :, None],
        norm_gain,
        norm_shift,
    )
    acts, pooled, slots, *saved = run_forward(
        query_tokens, query_drop, query_length, key_tokens, key_drop, key_length, weights
    )
    counts = pooled[:, 1]
    means = pooled[:, 0] / counts
    per_query, mean_grad = contrast(means[micro:], means[:micro], negatives)
    pgrad = jnp.concatenate(
        [(mean_grad / counts[micro:])[:, None], counts[micro:, None], jnp.zeros((micro, 6, width), F32)], axis=1
    )
    g_in, g_attend, g_merge, g_expand, g_shrink, g_vec, g_abias = run_backward(pgrad, slots, saved, weights)
    share = rows // lax.axis_size("tensor")
    start = lax.axis_index("tensor") * share
    activations = lax.dynamic_slice_in_dim(acts, start, share, 1)[:, None]
    input_grad = lax.dynamic_slice_in_dim(g_in, start, share, 1)[:, None]
    groups = ("dp", "rep")
    attend = jnp.transpose(lax.psum_scatter(g_attend, groups, scatter_dimension=2, tiled=True), (0, 2, 1, 3))
    merge = lax.psum_scatter(g_merge, groups, scatter_dimension=2, tiled=True)
    expand = lax.psum_scatter(g_expand, groups, scatter_dimension=1, tiled=True)
    shrink = lax.psum_scatter(g_shrink, groups, scatter_dimension=2, tiled=True)
    vec = jnp.sum(g_vec, axis=2)
    shared, expand_bias_grad, attend_bias_grad, loss = lax.psum(
        (vec[:, :6], vec[:, 6], jnp.sum(g_abias, axis=2), jnp.sum(per_query)), groups
    )
    size = width // (lax.axis_size("dp") * lax.axis_size("rep"))
    own = lax.dynamic_slice_in_dim(shared, lax.axis_index(groups) * size, size, 2)
    loss = loss / (micro * lax.axis_size("dp") * lax.axis_size("rep"))
    return (
        activations, input_grad, attend, attend_bias_grad, merge, own[:, 5], expand,
        expand_bias_grad, shrink, own[:, 4], own[:, 0:2], own[:, 2:4], loss,
    )


def solution(mesh):
    return jax.shard_map(
        per_device,
        mesh=mesh,
        in_specs=(
            P(None, ("dp", "rep"), None, None),
            P(None, ("dp", "rep"), None),
            P(None, ("dp", "rep")),
            P(None, ("dp", "rep"), None, None),
            P(None, ("dp", "rep"), None),
            P(None, ("dp", "rep")),
            P(("rep", "tensor"), None),
            P(None, None, None, None, "tensor"),
            P(None, None, None, "tensor"),
            P(None, None, "tensor", None),
            P(),
            P(None, None, None, "tensor"),
            P(None, None, "tensor"),
            P(None, None, "tensor", None),
            P(),
            P(),
            P(),
        ),
        out_specs=(
            P(None, ("dp", "rep"), "tensor", None),
            P(None, ("dp", "rep"), "tensor", None),
            P(None, ("dp", "rep"), None, "tensor"),
            P(None, None, "tensor"),
            P(None, "tensor", ("dp", "rep")),
            P(None, ("dp", "rep")),
            P(None, ("dp", "rep"), "tensor"),
            P(None, "tensor"),
            P(None, "tensor", ("dp", "rep")),
            P(None, ("dp", "rep")),
            P(None, None, ("dp", "rep")),
            P(None, None, ("dp", "rep")),
            P(),
        ),
        check_vma=False,
    )
```

```python
import functools

import jax
import jax.numpy as jnp
from jax import lax
from jax.experimental import pallas as pl
from jax.experimental.pallas import tpu as pltpu
from jax.sharding import PartitionSpec as P

HEAD_DIM = 64
CROP_SLOTS = 256
SOFTMAX_WARMTH = 0.05
NORM_EPS = 1e-12
UNIT_EPS = 1e-06
MASKED = -1e30
TOP_PRECISION = lax.Precision.HIGHEST
ROOT_HALF = 0.7071067811865476
INV_ROOT_TAU = 0.3989422804014327

MESH = pl.DeviceIdType.MESH
BF = jnp.bfloat16
F32 = jnp.float32
CHUNKS = 4
TILE = 64
VMEM_LIMIT = 62 * 1024 * 1024


def nn(a, b):
    return jnp.dot(a, b, preferred_element_type=F32)


def nt(a, b):
    return lax.dot_general(a, b, (((1,), (1,)), ((), ())), preferred_element_type=F32)


def tn(a, b):
    return lax.dot_general(a, b, (((0,), (0,)), ((), ())), preferred_element_type=F32)


def greet_line():
    z = lax.axis_index("tensor")
    sem = pltpu.get_barrier_semaphore()
    for d in (1, 2, 3):
        pl.semaphore_signal(sem, inc=1, device_id={"tensor": (z + d) % 4}, device_id_type=MESH)
    pl.semaphore_wait(sem, 3)


class Line:
    def __init__(self, part, sbuf, tbuf, x1, x2, s_sem, t_sem, r1, r2):
        z = lax.axis_index("tensor")
        self.mid = (z + 1) // 2 == 1
        self.end = (z + 1) // 2 != 1
        self.inner = 1 + z // 2
        self.outer = 3 * (z // 2)
        self.cross = 3 - z
        self.part, self.sbuf, self.tbuf, self.x1, self.x2 = part, sbuf, tbuf, x1, x2
        self.s_sem, self.t_sem, self.r1, self.r2 = s_sem, t_sem, r1, r2
        self.size = part.shape[1] // CHUNKS

    def rows(self, c):
        return pl.ds(c * self.size, self.size)

    def to_inner(self, s, c):
        return pltpu.make_async_remote_copy(
            src_ref=self.sbuf.at[s, self.rows(c)], dst_ref=self.x2.at[s, self.rows(c)],
            send_sem=self.s_sem.at[s, c], recv_sem=self.r2.at[s, c],
            device_id={"tensor": self.inner}, device_id_type=MESH)

    def to_cross(self, s, c, slot):
        return pltpu.make_async_remote_copy(
            src_ref=self.sbuf.at[s, self.rows(c)], dst_ref=self.x1.at[slot, s, self.rows(c)],
            send_sem=self.s_sem.at[s, c], recv_sem=self.r1.at[slot, s, c],
            device_id={"tensor": self.cross}, device_id_type=MESH)

    def to_outer(self, s, c, slot):
        return pltpu.make_async_remote_copy(
            src_ref=self.tbuf.at[s, self.rows(c)], dst_ref=self.x1.at[slot, s, self.rows(c)],
            send_sem=self.t_sem.at[s, c], recv_sem=self.r1.at[slot, s, c],
            device_id={"tensor": self.outer}, device_id_type=MESH)

    def begin(self, s):
        @pl.when(self.end)
        def _():
            for c in range(CHUNKS):
                rows = self.rows(c)
                self.sbuf[s, rows] = self.part[s, rows].astype(BF)
                self.to_inner(s, c).start()

    def inward(self, s, c, slot, live):
        @pl.when(self.mid & live)
        def _():
            rows = self.rows(c)
            self.to_inner(s, c).wait_recv()
            self.sbuf[s, rows] = (self.part[s, rows] + self.x2[s, rows].astype(F32)).astype(BF)
            self.to_cross(s, c, slot).start()

    def outward(self, s, c, slot, live):
        @pl.when(self.mid & live)
        def _():
            rows = self.rows(c)
            self.to_cross(s, c, slot).wait_recv()
            joint = self.part[s, rows] + self.x1[slot, s, rows].astype(F32)
            self.part[s, rows] = joint + self.x2[s, rows].astype(F32)
            self.tbuf[s, rows] = joint.astype(BF)
            self.to_outer(s, c, slot).start()

    def finish(self, s, slot):
        @pl.when(self.end)
        def _():
            for c in range(CHUNKS):
                rows = self.rows(c)
                self.to_outer(s, c, slot).wait_recv()
                self.part[s, rows] = self.part[s, rows] + self.x1[slot, s, rows].astype(F32)
            for c in range(CHUNKS):
                self.to_inner(s, c).wait_send()

        @pl.when(self.mid)
        def _():
            for c in range(CHUNKS):
                self.to_cross(s, c, slot).wait_send()
                self.to_outer(s, c, slot).wait_send()


def line_scratch(streams, rows, width):
    return [
        pltpu.VMEM((streams, rows, width), F32),
        pltpu.VMEM((streams, rows, width), BF),
        pltpu.VMEM((streams, rows, width), BF),
        pltpu.VMEM((2, streams, rows, width), BF),
        pltpu.VMEM((streams, rows, width), BF),
        pltpu.SemaphoreType.DMA((streams, CHUNKS)),
        pltpu.SemaphoreType.DMA((streams, CHUNKS)),
        pltpu.SemaphoreType.DMA((2, streams, CHUNKS)),
        pltpu.SemaphoreType.DMA((streams, CHUNKS)),
    ]


def tiles(rows, body):
    def step(c, carry):
        body(pl.ds(pl.multiple_of(c * TILE, TILE), TILE))
        return carry

    lax.fori_loop(0, rows // TILE, step, 0)


def normalize(total, gain, shift):
    mean = jnp.mean(total, axis=-1, keepdims=True)
    centered = total - mean
    inverse = lax.rsqrt(jnp.mean(centered * centered, axis=-1, keepdims=True) + NORM_EPS)
    normed = centered * inverse
    return normed * gain + shift, normed, inverse


def head_masks(width, scale):
    lane = lax.broadcasted_iota(jnp.int32, (1, width), 1)
    return [
        jnp.where((lane >= h * HEAD_DIM) & (lane < (h + 1) * HEAD_DIM), scale, 0.0).astype(BF)
        for h in range(width // HEAD_DIM)
    ]


def forward_kernel(
    q_tok, q_drop, q_len, k_tok, k_drop, k_len,
    wqkv, abias, wm, mbias, we, ebias, ws, sbias, gains, shifts,
    acts, pooled, slots, *rest,
):
    kept, rest = rest[:11], rest[11:]
    saved, rest = rest[:11], rest[11:]
    loaded, rest = rest[:4], rest[4:]
    h, hb, qkv, pb, mx, inner, act, vbias, valid, save_sem, load_sem, *line_refs = rest
    xin, proj, probs, mixed, n1, i1, first, slope, active, n2, i2 = saved
    part = line_refs[0]
    stored = (wqkv, wm, we, ws)
    wqkv, wm, we, ws = loaded
    micro = q_tok.shape[0]
    rows, width = q_tok.shape[2:]
    layers = we.shape[1]
    local = wm.shape[2]
    heads = local // HEAD_DIM
    streams = 2 * micro
    last = 2 * layers * streams

    def load(k, e, layer):
        return pltpu.make_async_copy(stored[k].at[e, layer], loaded[k].at[e, layer], load_sem.at[k, e, layer])

    for layer in range(layers):
        for e in (1, 0):
            for k in range(4):
                load(k, e, layer).start()

    def save(k, layer, m):
        return pltpu.make_async_copy(saved[k].at[layer, m], kept[k].at[layer, m], save_sem.at[k, layer, m])

    greet_line()
    line = Line(*line_refs)

    def compact(tok, drop, length, slots_out, s, m):
        pos = lax.broadcasted_iota(jnp.int32, (1, rows), 1)
        kept = (pos < length) & ((drop[m] == 0) | (pos == 0))
        kept_f = jnp.broadcast_to(jnp.where(kept, 1.0, 0.0), (16, rows))
        down = lax.broadcasted_iota(jnp.int32, (rows, rows), 0)
        along = lax.broadcasted_iota(jnp.int32, (rows, rows), 1)
        tri = jnp.where(down <= along, 1.0, 0.0).astype(BF)
        order = nn(kept_f.astype(BF), tri)[0:1] - 1.0
        order = jnp.where(kept, order, -1.0)
        count = jnp.sum(kept_f[0:1], axis=-1, keepdims=True)
        pick = jnp.where(order == down.astype(F32), 1.0, 0.0).astype(BF)
        rows_now = nn(pick, tok[m, 0])
        h[s] = rows_now
        hb[...] = rows_now.astype(BF)
        fits = pos.astype(F32) < count
        vbias[s] = jnp.broadcast_to(jnp.where(fits, 0.0, MASKED), (8, rows))
        valid[s] = jnp.broadcast_to(jnp.where(fits, 1.0, 0.0), (8, rows))
        pooled[s, 1:2] = jnp.broadcast_to(count, (1, width))
        if slots_out:
            slots[m] = jnp.broadcast_to(order, (8, rows))

    def at(i):
        j = jnp.maximum(i, 0)
        return j % streams, (j // streams) % 2, (i >= 0) & (i < last)

    def serve(i, *which):
        s1, slot1, live1 = at(i - 1)
        s2, slot2, live2 = at(i - 2)
        for kind, c in which:
            if kind == 1:
                line.inward(s1, c, slot1, live1)
            else:
                line.outward(s2, c, slot2, live2)

    def attention_pass(layer, s):
        i = layer * 2 * streams + s
        e, m = 1 - s // micro, s % micro
        is_q = s >= micro
        serve(i, (1, 0))

        @pl.when(layer == 0)
        def _():
            @pl.when(s < micro)
            def _():
                compact(k_tok, k_drop, k_len[m, 0], False, s, m)

            @pl.when(is_q)
            def _():
                compact(q_tok, q_drop, q_len[m, 0], True, s, m)

        @pl.when(layer > 0)
        def _():
            line.finish(s, 1)
            lp = layer - 1
            bias = sbias[e, lp].astype(F32)
            gain = gains[e, lp, 1:2].astype(F32)
            shift = shifts[e, lp, 1:2].astype(F32)

            def norm(r):
                out, normed, inverse = normalize(h[s, r] + part[s, r] + bias, gain, shift)
                h[s, r] = out
                hb[r] = out.astype(BF)

                @pl.when(is_q)
                def _():
                    n2[lp, m, r] = normed
                    i2[lp, m, r] = jnp.broadcast_to(inverse, (TILE, 128))

            tiles(rows, norm)

            @pl.when(is_q)
            def _():
                for k in (9, 10):
                    save(k, lp, m).start()

        serve(i, (1, 1))

        @pl.when((layer < layers) & (m == 0))
        def _():
            for k in (0, 1):
                load(k, e, layer).wait()

        @pl.when(layer < layers)
        def _():
            @pl.when(is_q)
            def _():
                xin[layer, m] = hb[...]
                save(0, layer, m).start()

            rows_now = hb[...]
            for j in range(3):
                bias = 0.0 if j == 1 else abias[e, layer, j // 2 : j // 2 + 1].astype(F32)
                qkv[j] = (nn(rows_now, wqkv[e, layer, j]) + bias).astype(BF)

            @pl.when(is_q)
            def _():
                for j in range(3):
                    proj[layer, m, j] = qkv[j]
                save(1, layer, m).start()

        serve(i, (1, 2), (2, 0))
        q_masks = head_masks(local, HEAD_DIM**-0.5)
        v_masks = head_masks(local, 1.0)

        def one_head(hd):
            @pl.when(layer < layers)
            def _():
                scores = nt(qkv[0] * q_masks[hd], qkv[1]) + vbias[s, 0:1]
                expo = jnp.exp(scores - jnp.max(scores, axis=-1, keepdims=True))
                chance = (expo / jnp.sum(expo, axis=-1, keepdims=True)).astype(BF)
                pb[hd] = chance

                @pl.when(is_q)
                def _():
                    probs[layer, m, hd] = chance

                out = nn(chance, qkv[2] * v_masks[hd])
                if hd == 0:
                    mx[...] = out
                else:
                    mx[...] += out

        for hd in range(heads):
            one_head(hd)
            if hd == 0:
                serve(i, (1, 3), (2, 1))
            elif hd == 1:
                serve(i, (2, 2))

        @pl.when(layer < layers)
        def _():
            mixed_now = mx[...].astype(BF)

            @pl.when(is_q)
            def _():
                mixed[layer, m] = mixed_now
                for k in (2, 3):
                    save(k, layer, m).start()

            part[s] = nn(mixed_now, wm[e, layer])
            line.begin(s)

        serve(i, (2, 3))

        @pl.when(layer == layers)
        def _():
            pooled[s, 0:1] = jnp.dot(valid[s], h[s], precision=TOP_PRECISION, preferred_element_type=F32)[0:1]

            @pl.when(is_q)
            def _():
                acts[m] = hb[...]

    def forward_pass(layer, s):
        i = (layer * 2 + 1) * streams + s
        e, m = 1 - s // micro, s % micro
        is_q = s >= micro
        serve(i, (1, 0))
        line.finish(s, 0)
        bias = mbias[e, layer].astype(F32)
        gain = gains[e, layer, 0:1].astype(F32)
        shift = shifts[e, layer, 0:1].astype(F32)

        def norm(r):
            out, normed, inverse = normalize(h[s, r] + part[s, r] + bias, gain, shift)
            h[s, r] = out
            hb[r] = out.astype(BF)

            @pl.when(is_q)
            def _():
                n1[layer, m, r] = normed
                i1[layer, m, r] = jnp.broadcast_to(inverse, (TILE, 128))
                first[layer, m, r] = out.astype(BF)

        tiles(rows, norm)

        @pl.when(m == 0)
        def _():
            for k in (2, 3):
                load(k, e, layer).wait()

        @pl.when(is_q)
        def _():
            for k in (4, 5, 6):
                save(k, layer, m).start()

        serve(i, (1, 1), (2, 0))
        inner[...] = nn(hb[...], we[e, layer])
        serve(i, (1, 2), (2, 1))
        bias_e = ebias[e, layer].astype(F32)

        def gelu(r):
            u = inner[r] + bias_e
            phi = 0.5 * (1.0 + lax.erf(u * ROOT_HALF))
            out = (u * phi).astype(BF)
            act[r] = out

            @pl.when(is_q)
            def _():
                active[layer, m, r] = out
                slope[layer, m, r] = phi + u * jnp.exp(-0.5 * u * u) * INV_ROOT_TAU

        tiles(rows, gelu)

        @pl.when(is_q)
        def _():
            for k in (7, 8):
                save(k, layer, m).start()

        serve(i, (1, 3), (2, 2))
        part[s] = nn(act[...], ws[e, layer])
        line.begin(s)
        serve(i, (2, 3))

    def layer_step(layer, carry):
        def a_step(s, c):
            attention_pass(layer, s)
            return c

        lax.fori_loop(0, streams, a_step, 0)

        @pl.when(layer < layers)
        def _():
            def f_step(s, c):
                forward_pass(layer, s)
                return c

            lax.fori_loop(0, streams, f_step, 0)

        return carry

    lax.fori_loop(0, layers + 1, layer_step, 0)

    def drain(j, carry):
        for k in range(len(saved)):
            save(k, j // micro, j % micro).wait()
        return carry

    lax.fori_loop(0, layers * micro, drain, 0)


def run_forward(q_tok, q_drop, q_len, k_tok, k_drop, k_len, weights):
    micro, _, rows, width = q_tok.shape
    wqkv, abias, wm, mbias, we, ebias, ws, sbias, gains, shifts = weights
    layers, local, units = we.shape[1], wm.shape[2], we.shape[3]
    heads = local // HEAD_DIM
    streams = 2 * micro
    lm = (layers, micro)
    shapes = [
        ((micro, rows, width), BF),
        ((streams, 8, width), F32),
        ((micro, 8, rows), F32),
        (lm + (rows, width), BF),
        (lm + (3, rows, local), BF),
        (lm + (heads, rows, rows), BF),
        (lm + (rows, local), BF),
        (lm + (rows, width), F32),
        (lm + (rows, 128), F32),
        (lm + (rows, width), BF),
        (lm + (rows, units), F32),
        (lm + (rows, units), BF),
        (lm + (rows, width), F32),
        (lm + (rows, 128), F32),
    ]
    vm = pl.BlockSpec(memory_space=pltpu.VMEM)
    hb = pl.BlockSpec(memory_space=pl.ANY)
    sm = pl.BlockSpec(memory_space=pltpu.SMEM)
    return pl.pallas_call(
        forward_kernel,
        out_shape=[jax.ShapeDtypeStruct(*s) for s in shapes],
        in_specs=[vm, vm, sm, vm, vm, sm] + [hb, vm, hb, vm, hb, vm, hb, vm, vm, vm],
        out_specs=[vm] * 3 + [hb] * 11,
        scratch_shapes=[pltpu.VMEM(*s) for s in shapes[3:]]
        + [pltpu.VMEM(w.shape, BF) for w in (wqkv, wm, we, ws)]
        + [
            pltpu.VMEM((streams, rows, width), F32),
            pltpu.VMEM((rows, width), BF),
            pltpu.VMEM((3, rows, local), BF),
            pltpu.VMEM((heads, rows, rows), BF),
            pltpu.VMEM((rows, local), F32),
            pltpu.VMEM((rows, units), F32),
            pltpu.VMEM((rows, units), BF),
            pltpu.VMEM((streams, 8, rows), F32),
            pltpu.VMEM((streams, 8, rows), F32),
            pltpu.SemaphoreType.DMA((11,) + lm),
            pltpu.SemaphoreType.DMA((4, 2, layers)),
        ]
        + line_scratch(streams, rows, width),
        compiler_params=pltpu.CompilerParams(
            collective_id=0, has_side_effects=True, vmem_limit_bytes=VMEM_LIMIT
        ),
        name="encoders_forward",
    )(q_tok, q_drop, q_len, k_tok, k_drop, k_len, *weights)


def norm_back(g, normed, inverse, gain):
    scaled = g * gain
    return inverse * (
        scaled
        - jnp.mean(scaled, axis=-1, keepdims=True)
        - normed * jnp.mean(scaled * normed, axis=-1, keepdims=True)
    )


def fold(x):
    return jnp.sum(x.reshape(x.shape[0] // 8, 8, x.shape[1]), axis=0)


class Plane:
    def __init__(self, grads, sends, recvs, out, send_sem, recv_sem, credit):
        dp, self.x = lax.axis_index("dp"), lax.axis_index("rep")
        self.y, self.c = dp // 2, dp % 2
        self.partner = {
            "c": {"dp": dp + 1 - 2 * self.c},
            "x": {"rep": 1 - self.x},
            "y": {"dp": (dp + 2) % 4},
        }
        self.grads, self.sends, self.recvs, self.out = grads, sends, recvs, out
        self.send_sem, self.recv_sem, self.credit = send_sem, recv_sem, credit
        self.block = grads.shape[2] // 8

    def copy(self, u, stage, half):
        way = ("c", "xy"[half], "yx"[half])[stage]
        return pltpu.make_async_remote_copy(
            src_ref=self.sends[stage].at[u, half], dst_ref=self.recvs[stage].at[u, half],
            send_sem=self.send_sem.at[u, stage, half], recv_sem=self.recv_sem.at[u, stage, half],
            device_id=self.partner[way], device_id_type=MESH)

    def spots(self, stage, half, own):
        pick = (lambda v: v) if own else (lambda v: 1 - v)
        if stage == 0:
            return [(4 * y + 2 * pick(self.c), 2 * y, 2) for y in (0, 1)]
        if stage == 1 and half == 0:
            return [(4 * y + 2 * self.c + pick(self.x), y, 1) for y in (0, 1)]
        if stage == 1:
            return [(4 * pick(self.y) + 2 * self.c, 0, 2)]
        if half == 0:
            return [(4 * pick(self.y) + 2 * self.c + self.x, 0, 1)]
        return [(4 * self.y + 2 * self.c + pick(self.x), 0, 1)]

    def parts(self, stage, half, own):
        for here, there, blocks in self.spots(stage, half, own):
            for b in range(blocks):
                start = (here + b) * self.block
                yield pl.ds(pl.multiple_of(start, 8), self.block), pl.ds((there + b) * self.block, self.block)

    def send(self, u, stage, live, spend):
        @pl.when(live)
        def _():
            for half in (0, 1):
                for here, there in self.parts(stage, half, False):
                    self.sends[stage][u, half, there] = self.grads[u, half, here].astype(BF)

            @pl.when(spend)
            def _():
                pl.semaphore_wait(self.credit.at[u, stage], 2)

            for half in (0, 1):
                self.copy(u, stage, half).start()

    def take(self, u, stage, live, give, layer):
        @pl.when(live)
        def _():
            for half in (0, 1):
                self.copy(u, stage, half).wait()
                for here, there in self.parts(stage, half, True):
                    total = self.grads[u, half, here] + self.recvs[stage][u, half, there].astype(F32)
                    if stage == 2:
                        self.out[layer, u, half] = total
                    else:
                        self.grads[u, half, here] = total

            @pl.when(give)
            def _():
                for half in (0, 1):
                    way = ("c", "xy"[half], "yx"[half])[stage]
                    pl.semaphore_signal(
                        self.credit.at[u, stage], inc=1, device_id=self.partner[way], device_id_type=MESH
                    )


def greet_all():
    z, dp, rep = lax.axis_index("tensor"), lax.axis_index("dp"), lax.axis_index("rep")
    sem = pltpu.get_barrier_semaphore()
    others = [{"tensor": (z + d) % 4} for d in (1, 2, 3)]
    others += [{"rep": 1 - rep, "tensor": (z + d) % 4} for d in (0, 1, 2, 3)]
    others += [{"dp": dp + 1 - 2 * (dp % 2)}, {"dp": (dp + 2) % 4}]
    for other in others:
        pl.semaphore_signal(sem, inc=1, device_id=other, device_id_type=MESH)
    pl.semaphore_wait(sem, len(others))


def backward_kernel(inside, *refs):
    seed, slots, negs, gains, *rest = refs
    kept, rest = rest[:11], rest[11:]
    stored, rest = rest[:4], rest[4:]
    g_in, vec, out_big, out_small, *rest = rest
    saved, rest = rest[:11], rest[11:]
    loaded, rest = rest[:4], rest[4:]
    g_vec, g_abias, dr, low, dinner, tmp, dqkv, dsc, pgrad, load_sem, *rest = rest
    line_refs, rest = rest[:9], rest[9:]
    xin, proj, probs, mixed, n1, i1, first, slope, active, n2, i2 = saved
    wqkv, wm, we, ws = loaded
    part = line_refs[0]
    layers, micro, rows, width = xin.shape
    local = wm.shape[1]
    half_units = we.shape[2] // 2
    heads = local // HEAD_DIM
    streams = micro
    last = 2 * layers * streams
    order = (9, 10, 7, 8, 6, 4, 5, 3, 2, 1, 0)

    def load_saved(k, layer):
        return pltpu.make_async_copy(kept[k].at[layer], saved[k].at[layer], load_sem.at[k, layer])

    def load_weight(k, layer):
        return pltpu.make_async_copy(stored[k].at[0, layer], loaded[k].at[layer], load_sem.at[11 + k, layer])

    for layer in reversed(range(layers)):
        for k in order[:2]:
            load_saved(k, layer).start()
        for k in (3, 2):
            load_weight(k, layer).start()
        for k in order[2:]:
            load_saved(k, layer).start()
        for k in (1, 0):
            load_weight(k, layer).start()
    g_vec[...] = jnp.zeros_like(g_vec)
    g_abias[...] = jnp.zeros_like(g_abias)
    vec[...] = jnp.zeros_like(vec)
    if inside:
        (g_big, g_small, b1, b2, b3, e1, e2, e3, s1, s2, s3, t1, t2, t3, big_s, big_r, small_s, small_r,
         big_c, small_c, v_rcv, v_send, v_recv, ask, asked, reply, heard, ask_sem, reply_sem, heard_sem) = rest
        greet_all()
        big = Plane(g_big, (b1, b2, b3), (e1, e2, e3), out_big, big_s, big_r, big_c)
        small = Plane(g_small, (s1, s2, s3), (t1, t2, t3), out_small, small_s, small_r, small_c)
        contrast_inside(seed, negs, pgrad, vec, ask, asked, reply, heard, ask_sem, reply_sem, heard_sem)
    else:
        greet_line()
        pgrad[...] = seed[...]
    line = Line(*line_refs)

    def serve(i, *which):
        j = jnp.maximum(i - 1, 0)
        s, slot, live = j % streams, (j // streams) % 2, (i >= 1) & (i <= last)
        for kind, c in which:
            if kind == 1:
                line.inward(s, c, slot, live)
            else:
                line.outward(s, c, slot, live)

    def add_to(large, u, half, layer, s, value):
        if inside:
            ref = (g_big if large else g_small).at[u, half]
        else:
            ref = (out_big if large else out_small).at[layer, u, half]

        @pl.when(s == 0)
        def _():
            ref[...] = value

        @pl.when(s > 0)
        def _():
            ref[...] += value

    def plane(what, large, stage, live, step):
        if inside:
            group = big if large else small
            for u in (0, 1):
                if what == "send":
                    group.send(u, stage, live, step > 0)
                else:
                    group.take(u, stage, live, step < layers - 1, layers - 1 - step)

    def mlp_back(step, s):
        layer = layers - 1 - step
        i = step * 2 * streams + s

        @pl.when(s == 0)
        def _():
            for k in (4, 6, 7, 8, 9, 10):
                load_saved(k, layer).wait()
            for k in (2, 3):
                load_weight(k, layer).wait()

        @pl.when(step == 0)
        def _():
            def begin(c, carry):
                r = pl.ds(pl.multiple_of(c * TILE, TILE), TILE)
                pos = (lax.broadcasted_iota(jnp.int32, (TILE, 1), 0) + c * TILE).astype(F32)
                part[s, r] = jnp.where(pos < pgrad[s, 1:2, 0:1], pgrad[s, 0:1], 0.0)
                dr[s, r] = jnp.zeros((TILE, width), F32)
                return carry

            lax.fori_loop(0, rows // TILE, begin, 0)

        @pl.when(step > 0)
        def _():
            line.finish(s, 1)

        gain = gains[layer, 1:2].astype(F32)

        def back(r):
            g = part[s, r] + dr[s, r]
            normed = n2[layer, s, r]
            out = norm_back(g, normed, i2[layer, s, r][:, 0:1], gain)
            dr[s, r] = out
            low[s, r] = out.astype(BF)
            g_vec[layer, 1] += fold(g * normed)
            g_vec[layer, 3] += fold(g)
            g_vec[layer, 4] += fold(out)

        tiles(rows, back)
        serve(i, (1, 0))
        tmp[...] = nt(low[s], ws[layer])
        serve(i, (1, 1))

        def slopes(r):
            out = tmp[r] * slope[layer, s, r]
            dinner[r] = out.astype(BF)
            g_vec[layer, 6] += fold(out)

        tiles(rows, slopes)
        part[s] = nt(dinner[...], we[layer])
        line.begin(s)
        serve(i, (1, 2), (2, 0))
        plane("take", True, 2, (step > 0) & (s == 0), step - 1)
        plane("take", False, 0, (step > 0) & (s == 0), step - 1)
        plane("send", False, 1, (step > 0) & (s == 0), step - 1)
        for half in (0, 1):
            cols = pl.ds(half * half_units, half_units)
            add_to(True, 0, half, layer, s, tn(low[s], active[layer, s, :, cols]))
        serve(i, (1, 3), (2, 1))
        for half in (0, 1):
            cols = pl.ds(half * half_units, half_units)
            add_to(True, 1, half, layer, s, tn(first[layer, s], dinner[:, cols]))
        plane("send", True, 0, s == streams - 1, step)
        plane("take", False, 1, (step > 0) & (s == streams - 1), step - 1)
        plane("send", False, 2, (step > 0) & (s == streams - 1), step - 1)
        serve(i, (2, 2), (2, 3))

    def attention_back(step, s):
        layer = layers - 1 - step
        i = (step * 2 + 1) * streams + s

        @pl.when(s == 0)
        def _():
            for k in (0, 1, 2, 3, 5):
                load_saved(k, layer).wait()
            for k in (0, 1):
                load_weight(k, layer).wait()

        line.finish(s, 0)
        gain = gains[layer, 0:1].astype(F32)

        def back(r):
            g = part[s, r] + dr[s, r]
            normed = n1[layer, s, r]
            out = norm_back(g, normed, i1[layer, s, r][:, 0:1], gain)
            dr[s, r] = out
            low[s, r] = out.astype(BF)
            g_vec[layer, 0] += fold(g * normed)
            g_vec[layer, 2] += fold(g)
            g_vec[layer, 5] += fold(out)

        tiles(rows, back)
        serve(i, (1, 0))
        dmix = nt(low[s], wm[layer]).astype(BF)
        serve(i, (1, 1))
        masks = head_masks(local, 1.0)
        for hd in range(heads):
            chance_b = probs[layer, s, hd]
            chance = chance_b.astype(F32)
            dm = dmix * masks[hd]
            dch = nt(dm, proj[layer, s, 2])
            ds = chance * (dch - jnp.sum(chance * dch, axis=-1, keepdims=True))
            draw = (ds * HEAD_DIM**-0.5).astype(BF)
            dq = nn(draw, proj[layer, s, 1] * masks[hd])
            dk = tn(draw, proj[layer, s, 0] * masks[hd])
            dv = tn(chance_b, dm)
            if hd == 0:
                dqkv[0] = dq
                dqkv[1] = dk
                dqkv[2] = dv
            else:
                dqkv[0] += dq
                dqkv[1] += dk
                dqkv[2] += dv
            if hd == 0:
                serve(i, (1, 2), (2, 0))
            elif hd == 1:
                serve(i, (1, 3), (2, 1))
        g_abias[layer, 0] += fold(dqkv[0])
        g_abias[layer, 1] += fold(dqkv[2])
        for j in range(3):
            dsc[j] = dqkv[j].astype(BF)
        part[s] = nt(dsc[0], wqkv[layer, 0]) + nt(dsc[1], wqkv[layer, 1]) + nt(dsc[2], wqkv[layer, 2])
        line.begin(s)
        serve(i, (2, 2), (2, 3))
        plane("take", True, 0, s == 0, step)
        plane("send", True, 1, s == 0, step)
        plane("take", True, 1, s == streams - 1, step)
        plane("send", True, 2, s == streams - 1, step)
        plane("take", False, 2, (step > 0) & (s == 0), step - 1)
        for j in range(3):
            add_to(False, j // 2, j % 2, layer, s, tn(xin[layer, s], dsc[j]))
        add_to(False, 1, 1, layer, s, tn(low[s], mixed[layer, s]))
        plane("send", False, 0, s == streams - 1, step)

    def layer_step(step, carry):
        def m_step(s, c):
            mlp_back(step, s)
            return c

        def a_step(s, c):
            attention_back(step, s)
            return c

        lax.fori_loop(0, streams, m_step, 0)
        lax.fori_loop(0, streams, a_step, 0)
        return carry

    lax.fori_loop(0, layers, layer_step, 0)

    for layer in range(layers):
        for k in range(7):
            vec[layer * 7 + k : layer * 7 + k + 1] = jnp.sum(g_vec[layer, k], axis=0, keepdims=True)
        for k in range(2):
            row = layers * 7 + layer * 2 + k
            vec[row : row + 1, 0:local] = jnp.sum(g_abias[layer, k], axis=0, keepdims=True)

    def vec_copy(stage):
        return pltpu.make_async_remote_copy(
            src_ref=vec, dst_ref=v_rcv.at[stage], send_sem=v_send.at[stage], recv_sem=v_recv.at[stage],
            device_id=big.partner["cxy"[stage]], device_id_type=MESH)

    def vec_take(stage):
        if inside:
            vec_copy(stage).wait()
            vec[...] += v_rcv[stage]

    def vec_send(stage):
        if inside:
            vec_copy(stage).start()

    end = layers - 1
    vec_send(0)
    serve(last, (1, 0))
    plane("take", False, 0, True, end)
    plane("send", False, 1, True, end)
    vec_take(0)
    vec_send(1)
    serve(last, (1, 1))
    plane("take", True, 2, True, end)
    serve(last, (1, 2), (2, 0))
    plane("take", False, 1, True, end)
    plane("send", False, 2, True, end)
    vec_take(1)
    vec_send(2)
    serve(last, (1, 3), (2, 1), (2, 2), (2, 3))

    def tail(s, carry):
        line.finish(s, 1)

        def back(r):
            low[s, r] = (part[s, r] + dr[s, r]).astype(BF)

        tiles(rows, back)
        down = lax.broadcasted_iota(jnp.int32, (rows, rows), 0).astype(F32)
        pick = jnp.where(slots[s, 0:1] == down, 1.0, 0.0).astype(BF)
        g_in[s] = tn(pick, low[s]).astype(BF)
        return carry

    lax.fori_loop(0, streams, tail, 0)
    plane("take", False, 2, True, end)
    vec_take(2)


def run_backward(inside, seed, slots, negatives, saved, weights):
    wqkv, abias, wm, mbias, we, ebias, ws, sbias, gains, shifts = weights
    layers, micro, rows, width = saved[0].shape
    local, units = wm.shape[2], we.shape[3]
    tall = 8 * ((9 * layers + 2 + 7) // 8)
    kinds = ((units // 2, "big"), (local, "small"))
    high = width // 8 if inside else width
    shapes = [((micro, rows, width), BF), ((tall, width), F32)]
    shapes += [((layers, 2, 2, high, w), F32) for w, _ in kinds]
    vm = pl.BlockSpec(memory_space=pltpu.VMEM)
    hb = pl.BlockSpec(memory_space=pl.ANY)
    dma = pltpu.SemaphoreType.DMA
    scratch = [pltpu.VMEM(v.shape, v.dtype) for v in saved]
    scratch += [pltpu.VMEM(w.shape[1:], BF) for w in (wqkv, wm, we, ws)]
    scratch += [
        pltpu.VMEM((layers, 7, 8, width), F32),
        pltpu.VMEM((layers, 2, 8, local), F32),
        pltpu.VMEM((micro, rows, width), F32),
        pltpu.VMEM((micro, rows, width), BF),
        pltpu.VMEM((rows, units), BF),
        pltpu.VMEM((rows, units), F32),
        pltpu.VMEM((3, rows, local), F32),
        pltpu.VMEM((3, rows, local), BF),
        pltpu.VMEM((micro, 8, width), F32),
        dma((15, layers)),
    ]
    scratch += line_scratch(micro, rows, width)
    if inside:
        scratch += [pltpu.VMEM((2, 2, width, w), F32) for w, _ in kinds]
        for w, _ in kinds:
            for _ in range(2):
                scratch += [pltpu.VMEM((2, 2, width // n, w), BF) for n in (2, 4, 8)]
        scratch += [dma((2, 3, 2))] * 4
        scratch += [pltpu.SemaphoreType.REGULAR((2, 3))] * 2
        scratch += [pltpu.VMEM((3, tall, width), F32), dma((3,)), dma((3,))]
        scratch += [
            pltpu.VMEM((16, width), BF),
            pltpu.VMEM((16, width), BF),
            pltpu.VMEM((2, 8, width), F32),
            pltpu.VMEM((8, 8, width), F32),
            dma((2,)),
            dma((8,)),
            dma((8,)),
        ]
    return pl.pallas_call(
        functools.partial(backward_kernel, inside),
        out_shape=[jax.ShapeDtypeStruct(*s) for s in shapes],
        in_specs=[vm] * 4 + [hb] * 15,
        out_specs=[vm] * len(shapes),
        scratch_shapes=scratch,
        compiler_params=pltpu.CompilerParams(
            collective_id=1, has_side_effects=True, vmem_limit_bytes=VMEM_LIMIT
        ),
        name="encoder_backward",
    )(seed, slots, negatives, gains[0], *saved, wqkv, wm, we, ws)


def contrast_inside(pooled, negs, pgrad, vec, ask, asked, reply, heard, ask_sem, reply_sem, heard_sem):
    z, rep = lax.axis_index("tensor"), lax.axis_index("rep")
    micro = pgrad.shape[0]
    width = negs.shape[1]
    scales, counts, dirs, key_dirs, positives = [], [], [], [], []
    ask[...] = jnp.zeros_like(ask)
    for m in range(micro):
        count = pooled[micro + m, 1:2]
        mean_q = pooled[micro + m, 0:1] / count
        mean_k = pooled[m, 0:1] / pooled[m, 1:2]
        scale = lax.rsqrt(jnp.sum(mean_q * mean_q, axis=-1, keepdims=True) + UNIT_EPS)
        key_dir = mean_k * lax.rsqrt(jnp.sum(mean_k * mean_k, axis=-1, keepdims=True) + UNIT_EPS)
        direction = mean_q * scale
        ask[m : m + 1] = direction.astype(BF)
        positives.append(jnp.sum(direction * key_dir, axis=-1, keepdims=True) / SOFTMAX_WARMTH)
        scales.append(scale)
        counts.append(count)
        dirs.append(direction)
        key_dirs.append(key_dir)
    question = pltpu.make_async_remote_copy(
        src_ref=ask, dst_ref=asked, send_sem=ask_sem.at[0], recv_sem=ask_sem.at[1],
        device_id={"rep": 1 - rep}, device_id_type=MESH)
    question.start()

    def answer(which, rows_now):
        logits = nt(rows_now, negs[...]) / SOFTMAX_WARMTH
        top = jnp.max(logits, axis=-1, keepdims=True)
        expo = jnp.exp(logits - top)
        total = jnp.sum(expo, axis=-1, keepdims=True)
        high = expo.astype(BF)
        rest = expo - high.astype(F32)
        mid = rest.astype(BF)
        tiny = (rest - mid.astype(F32)).astype(BF)
        keys = nn(high, negs[...]) + nn(mid, negs[...]) + nn(tiny, negs[...])
        reply[which, 0:micro] = keys[0:micro]
        reply[which, micro : 2 * micro] = jnp.broadcast_to(top[0:micro], (micro, width))
        reply[which, 2 * micro : 3 * micro] = jnp.broadcast_to(total[0:micro], (micro, width))

    def tell(which, d):
        other = {"tensor": (z + d) % 4} if which == 0 else {"rep": 1 - rep, "tensor": (z + d) % 4}
        k = which * 4 + d
        return pltpu.make_async_remote_copy(
            src_ref=reply.at[which], dst_ref=heard.at[k], send_sem=reply_sem.at[k], recv_sem=heard_sem.at[k],
            device_id=other, device_id_type=MESH)

    answer(0, ask[...])
    for d in (1, 2, 3):
        tell(0, d).start()
    question.wait()
    answer(1, asked[...])
    for d in (0, 1, 2, 3):
        tell(1, d).start()
    for k in range(1, 8):
        tell(k // 4, k % 4).wait()
    everyone = [reply[0]] + [heard[k] for k in range(1, 8)]
    loss = 0.0
    for m in range(micro):
        positive = positives[m]
        best = positive
        for one in everyone:
            best = jnp.maximum(best, one[micro + m : micro + m + 1, 0:1])
        own = jnp.exp(positive - best)
        total, keys = own, own * key_dirs[m]
        for one in everyone:
            weight = jnp.exp(one[micro + m : micro + m + 1, 0:1] - best)
            total = total + weight * one[2 * micro + m : 2 * micro + m + 1, 0:1]
            keys = keys + weight * one[m : m + 1]
        loss = loss + best + jnp.log(total) - positive
        dqn = (keys / total - key_dirs[m]) * (CROP_SLOTS / SOFTMAX_WARMTH)
        mean_grad = scales[m] * (dqn - dirs[m] * jnp.sum(dirs[m] * dqn, axis=-1, keepdims=True))
        pgrad[m, 0:1] = mean_grad / counts[m]
        pgrad[m, 1:2] = counts[m]
    vec[vec.shape[0] - 1 : vec.shape[0]] = jnp.broadcast_to(loss, (1, width))


def contrast(mean_q, mean_k, negatives):
    key_dir = mean_k * lax.rsqrt(jnp.sum(mean_k * mean_k, axis=-1, keepdims=True) + UNIT_EPS)
    scale = lax.rsqrt(jnp.sum(mean_q * mean_q, axis=-1, keepdims=True) + UNIT_EPS)
    direction = mean_q * scale
    positive = jnp.sum(direction * key_dir, axis=-1) / SOFTMAX_WARMTH
    micro, width = mean_q.shape
    asked = lax.all_gather(direction.astype(BF), "rep", axis=0, tiled=True)
    logits = nt(asked, negatives) / SOFTMAX_WARMTH
    top = jnp.max(logits, axis=-1, keepdims=True)
    expo = jnp.exp(logits - top)
    total = jnp.sum(expo, axis=-1, keepdims=True)
    keys = jnp.dot(expo, negatives.astype(F32), precision=TOP_PRECISION)
    packed = jnp.concatenate([keys, jnp.broadcast_to(top, (top.shape[0], 128)), jnp.broadcast_to(total, (top.shape[0], 128))], axis=1)
    pieces = lax.all_gather(packed, ("rep", "tensor"), axis=0, tiled=False)
    mine = lax.dynamic_slice_in_dim(pieces, lax.axis_index("rep") * micro, micro, 1)
    keys, top, total = mine[..., :width], mine[..., width], mine[..., width + 128]
    best = jnp.maximum(jnp.max(top, axis=0), positive)
    weight = jnp.exp(top - best)
    own = jnp.exp(positive - best)
    total = jnp.sum(total * weight, axis=0) + own
    keys = jnp.sum(keys * weight[..., None], axis=0) + own[:, None] * key_dir
    per_query = best + jnp.log(total) - positive
    dqn = (keys / total[:, None] - key_dir) * (CROP_SLOTS / SOFTMAX_WARMTH)
    mean_grad = scale * (dqn - direction * jnp.sum(direction * dqn, axis=-1, keepdims=True))
    return per_query, mean_grad


def per_device(
    query_tokens, query_drop, query_length, key_tokens, key_drop, key_length, negatives,
    attend_weight, attend_bias, merge_weight, merge_bias, expand_weight, expand_bias,
    shrink_weight, shrink_bias, norm_gain, norm_shift,
):
    micro, _, rows, width = query_tokens.shape
    weights = (
        jnp.transpose(attend_weight, (0, 1, 3, 2, 4)),
        attend_bias,
        merge_weight,
        merge_bias[:, :, None],
        expand_weight,
        expand_bias[:, :, None],
        shrink_weight,
        shrink_bias[:, :, None],
        norm_gain,
        norm_shift,
    )
    acts, pooled, slots, *saved = run_forward(
        query_tokens, query_drop, query_length, key_tokens, key_drop, key_length, weights
    )
    layers = expand_weight.shape[1]
    groups = ("dp", "rep")
    inside = lax.axis_size("dp") == 4 and lax.axis_size("rep") == 2
    if inside:
        g_in, vec, g_big, g_small = run_backward(inside, pooled, slots, negatives, saved, weights)
        loss = vec[-1, 0]
    else:
        counts = pooled[:, 1]
        means = pooled[:, 0] / counts
        per_query, mean_grad = contrast(means[micro:], means[:micro], negatives)
        pgrad = jnp.concatenate(
            [(mean_grad / counts[micro:])[:, None], counts[micro:, None], jnp.zeros((micro, 6, width), F32)], axis=1
        )
        g_in, vec, g_big, g_small = run_backward(inside, pgrad, slots, negatives, saved, weights)
        g_big = lax.psum_scatter(g_big, groups, scatter_dimension=3, tiled=True)
        g_small = lax.psum_scatter(g_small, groups, scatter_dimension=3, tiled=True)
        vec, loss = lax.psum((vec, jnp.sum(per_query)), groups)
    share = rows // lax.axis_size("tensor")
    start = lax.axis_index("tensor") * share
    activations = lax.dynamic_slice_in_dim(acts, start, share, 1)[:, None]
    input_grad = lax.dynamic_slice_in_dim(g_in, start, share, 1)[:, None]
    shrink = jnp.concatenate([g_big[:, 0, 0], g_big[:, 0, 1]], axis=2).transpose(0, 2, 1)
    expand = jnp.concatenate([g_big[:, 1, 0], g_big[:, 1, 1]], axis=2)
    attend = jnp.stack([g_small[:, 0, 0], g_small[:, 0, 1], g_small[:, 1, 0]], axis=2)
    merge = g_small[:, 1, 1].transpose(0, 2, 1)
    local = attend_weight.shape[4]
    rows7 = vec[: 7 * layers].reshape(layers, 7, width)
    attend_bias_grad = vec[7 * layers : 9 * layers, :local].reshape(layers, 2, local)
    size = width // (lax.axis_size("dp") * lax.axis_size("rep"))
    own = lax.dynamic_slice_in_dim(rows7, lax.axis_index(groups) * size, size, 2)
    loss = loss / (micro * lax.axis_size("dp") * lax.axis_size("rep"))
    return (
        activations, input_grad, attend, attend_bias_grad, merge, own[:, 5], expand,
        rows7[:, 6], shrink, own[:, 4], own[:, 0:2], own[:, 2:4], loss,
    )


def solution(mesh):
    return jax.shard_map(
        per_device,
        mesh=mesh,
        in_specs=(
            P(None, ("dp", "rep"), None, None),
            P(None, ("dp", "rep"), None),
            P(None, ("dp", "rep")),
            P(None, ("dp", "rep"), None, None),
            P(None, ("dp", "rep"), None),
            P(None, ("dp", "rep")),
            P(("rep", "tensor"), None),
            P(None, None, None, None, "tensor"),
            P(None, None, None, "tensor"),
            P(None, None, "tensor", None),
            P(),
            P(None, None, None, "tensor"),
            P(None, None, "tensor"),
            P(None, None, "tensor", None),
            P(),
            P(),
            P(),
        ),
        out_specs=(
            P(None, ("dp", "rep"), "tensor", None),
            P(None, ("dp", "rep"), "tensor", None),
            P(None, ("dp", "rep"), None, "tensor"),
            P(None, None, "tensor"),
            P(None, "tensor", ("dp", "rep")),
            P(None, ("dp", "rep")),
            P(None, ("dp", "rep"), "tensor"),
            P(None, "tensor"),
            P(None, "tensor", ("dp", "rep")),
            P(None, ("dp", "rep")),
            P(None, None, ("dp", "rep")),
            P(None, None, ("dp", "rep")),
            P(),
        ),
        check_vma=False,
    )
```

```python
import functools

import jax
import jax.numpy as jnp
from jax import lax
from jax.experimental import pallas as pl
from jax.experimental.pallas import tpu as pltpu
from jax.sharding import PartitionSpec as P

HEAD_DIM = 64
CROP_SLOTS = 256
SOFTMAX_WARMTH = 0.05
NORM_EPS = 1e-12
UNIT_EPS = 1e-06
MASKED = -1e30
TOP_PRECISION = lax.Precision.HIGHEST
ROOT_HALF = 0.7071067811865476
INV_ROOT_TAU = 0.3989422804014327

MESH = pl.DeviceIdType.MESH
BF = jnp.bfloat16
F32 = jnp.float32
CHUNKS = 8
LAG = 3
TILE = 64
VMEM_LIMIT = 62 * 1024 * 1024


def nn(a, b):
    return jnp.dot(a, b, preferred_element_type=F32)


def nt(a, b):
    return lax.dot_general(a, b, (((1,), (1,)), ((), ())), preferred_element_type=F32)


def tn(a, b):
    return lax.dot_general(a, b, (((0,), (0,)), ((), ())), preferred_element_type=F32)


def greet_line():
    z = lax.axis_index("tensor")
    sem = pltpu.get_barrier_semaphore()
    for d in (1, 2, 3):
        pl.semaphore_signal(sem, inc=1, device_id={"tensor": (z + d) % 4}, device_id_type=MESH)
    pl.semaphore_wait(sem, 3)


class Line:
    def __init__(self, part, sbuf, tbuf, x1, x2, s_sem, t_sem, r1, r2):
        z = lax.axis_index("tensor")
        self.mid = (z + 1) // 2 == 1
        self.end = (z + 1) // 2 != 1
        self.inner = 1 + z // 2
        self.outer = 3 * (z // 2)
        self.cross = 3 - z
        self.part, self.sbuf, self.tbuf, self.x1, self.x2 = part, sbuf, tbuf, x1, x2
        self.s_sem, self.t_sem, self.r1, self.r2 = s_sem, t_sem, r1, r2
        self.size = part.shape[1] // CHUNKS

    def rows(self, c):
        return pl.ds(c * self.size, self.size)

    def to_inner(self, s, c):
        return pltpu.make_async_remote_copy(
            src_ref=self.sbuf.at[s, self.rows(c)], dst_ref=self.x2.at[s, self.rows(c)],
            send_sem=self.s_sem.at[s, c], recv_sem=self.r2.at[s, c],
            device_id={"tensor": self.inner}, device_id_type=MESH)

    def to_cross(self, s, c, slot):
        return pltpu.make_async_remote_copy(
            src_ref=self.sbuf.at[s, self.rows(c)], dst_ref=self.x1.at[slot, s, self.rows(c)],
            send_sem=self.s_sem.at[s, c], recv_sem=self.r1.at[slot, s, c],
            device_id={"tensor": self.cross}, device_id_type=MESH)

    def to_outer(self, s, c, slot):
        return pltpu.make_async_remote_copy(
            src_ref=self.tbuf.at[s, self.rows(c)], dst_ref=self.x1.at[slot, s, self.rows(c)],
            send_sem=self.t_sem.at[s, c], recv_sem=self.r1.at[slot, s, c],
            device_id={"tensor": self.outer}, device_id_type=MESH)

    def begin(self, s):
        @pl.when(self.end)
        def _():
            for c in range(CHUNKS):
                rows = self.rows(c)
                self.sbuf[s, rows] = self.part[s, rows].astype(BF)
                self.to_inner(s, c).start()

    def inward(self, s, c, slot, live):
        @pl.when(self.mid & live)
        def _():
            rows = self.rows(c)
            self.to_inner(s, c).wait_recv()
            self.sbuf[s, rows] = (self.part[s, rows] + self.x2[s, rows].astype(F32)).astype(BF)
            self.to_cross(s, c, slot).start()

    def outward(self, s, c, slot, live):
        @pl.when(self.mid & live)
        def _():
            rows = self.rows(c)
            self.to_cross(s, c, slot).wait_recv()
            joint = self.part[s, rows] + self.x1[slot, s, rows].astype(F32)
            self.part[s, rows] = joint + self.x2[s, rows].astype(F32)
            self.tbuf[s, rows] = joint.astype(BF)
            self.to_outer(s, c, slot).start()

    def finish(self, s, slot):
        @pl.when(self.end)
        def _():
            for c in range(CHUNKS):
                rows = self.rows(c)
                self.to_outer(s, c, slot).wait_recv()
                self.part[s, rows] = self.part[s, rows] + self.x1[slot, s, rows].astype(F32)
            for c in range(CHUNKS):
                self.to_inner(s, c).wait_send()

        @pl.when(self.mid)
        def _():
            for c in range(CHUNKS):
                self.to_cross(s, c, slot).wait_send()
                self.to_outer(s, c, slot).wait_send()


def line_scratch(streams, rows, width):
    return [
        pltpu.VMEM((streams, rows, width), F32),
        pltpu.VMEM((streams, rows, width), BF),
        pltpu.VMEM((streams, rows, width), BF),
        pltpu.VMEM((2, streams, rows, width), BF),
        pltpu.VMEM((streams, rows, width), BF),
        pltpu.SemaphoreType.DMA((streams, CHUNKS)),
        pltpu.SemaphoreType.DMA((streams, CHUNKS)),
        pltpu.SemaphoreType.DMA((2, streams, CHUNKS)),
        pltpu.SemaphoreType.DMA((streams, CHUNKS)),
    ]


def tiles(rows, body):
    def step(c, carry):
        body(pl.ds(pl.multiple_of(c * TILE, TILE), TILE))
        return carry

    lax.fori_loop(0, rows // TILE, step, 0)


def normalize(total, gain, shift):
    mean = jnp.mean(total, axis=-1, keepdims=True)
    centered = total - mean
    inverse = lax.rsqrt(jnp.mean(centered * centered, axis=-1, keepdims=True) + NORM_EPS)
    normed = centered * inverse
    return normed * gain + shift, normed, inverse


def head_masks(width, scale):
    lane = lax.broadcasted_iota(jnp.int32, (1, width), 1)
    return [
        jnp.where((lane >= h * HEAD_DIM) & (lane < (h + 1) * HEAD_DIM), scale, 0.0).astype(BF)
        for h in range(width // HEAD_DIM)
    ]


def forward_kernel(
    q_tok, q_drop, q_len, k_tok, k_drop, k_len,
    wqkv, abias, wm, mbias, we, ebias, ws, sbias, gains, shifts,
    acts, pooled, slots, *rest,
):
    kept, rest = rest[:11], rest[11:]
    saved, rest = rest[:11], rest[11:]
    loaded, rest = rest[:4], rest[4:]
    h, hb, qkv, pb, mx, inner, act, vbias, valid, vecs, save_sem, load_sem, *line_refs = rest
    xin, proj, probs, mixed, n1, i1, first, slope, active, n2, i2 = saved
    part = line_refs[0]
    stored = (wqkv, wm, we, ws)
    wqkv, wm, we, ws = loaded
    micro = q_tok.shape[0]
    rows, width = q_tok.shape[2:]
    layers = we.shape[1]
    local = wm.shape[2]
    heads = local // HEAD_DIM
    streams = 2 * micro
    last = 2 * layers * streams

    def load(k, e, layer):
        return pltpu.make_async_copy(stored[k].at[e, layer], loaded[k].at[e, layer], load_sem.at[k, e, layer])

    for layer in range(layers):
        for e in (1, 0):
            for k in range(4):
                load(k, e, layer).start()

    def save(k, layer, m):
        return pltpu.make_async_copy(saved[k].at[layer, m], kept[k].at[layer, m], save_sem.at[k, layer, m])

    for e in range(2):
        for layer in range(layers):
            for row, ref in enumerate((mbias, ebias, sbias)):
                vecs[e, layer, row : row + 1] = ref[e, layer : layer + 1].astype(F32)
            vecs[e, layer, 3:5] = gains[e, layer].astype(F32)
            vecs[e, layer, 5:7] = shifts[e, layer].astype(F32)
    greet_line()
    line = Line(*line_refs)

    def compact(tok, drop, length, slots_out, s, m):
        pos = lax.broadcasted_iota(jnp.int32, (1, rows), 1)
        kept = (pos < length) & ((drop[m] == 0) | (pos == 0))
        kept_f = jnp.broadcast_to(jnp.where(kept, 1.0, 0.0), (16, rows))
        down = lax.broadcasted_iota(jnp.int32, (rows, rows), 0)
        along = lax.broadcasted_iota(jnp.int32, (rows, rows), 1)
        tri = jnp.where(down <= along, 1.0, 0.0).astype(BF)
        order = nn(kept_f.astype(BF), tri)[0:1] - 1.0
        order = jnp.where(kept, order, -1.0)
        count = jnp.sum(kept_f[0:1], axis=-1, keepdims=True)
        pick = jnp.where(order == down.astype(F32), 1.0, 0.0).astype(BF)
        rows_now = nn(pick, tok[m, 0])
        h[s] = rows_now
        hb[...] = rows_now.astype(BF)
        fits = pos.astype(F32) < count
        vbias[s] = jnp.broadcast_to(jnp.where(fits, 0.0, MASKED), (8, rows))
        valid[s] = jnp.broadcast_to(jnp.where(fits, 1.0, 0.0), (8, rows))
        pooled[s, 1:2] = jnp.broadcast_to(count, (1, width))
        if slots_out:
            slots[m] = jnp.broadcast_to(order, (8, rows))

    def at(i):
        j = jnp.maximum(i, 0)
        return j % streams, (j // streams) % 2, (i >= 0) & (i < last)

    def tick(i, *which):
        for c in which:
            s, slot, live = at(i - 1)
            line.inward(s, c, slot, live)
            if c < LAG:
                s, slot, live = at(i - 2)
            line.outward(s, (c - LAG) % CHUNKS, slot, live)

    def attention_pass(layer, s):
        i = layer * 2 * streams + s
        e, m = 1 - s // micro, s % micro
        is_q = s >= micro
        tick(i, 0)

        @pl.when(layer == 0)
        def _():
            @pl.when(s < micro)
            def _():
                compact(k_tok, k_drop, k_len[m], False, s, m)

            @pl.when(is_q)
            def _():
                compact(q_tok, q_drop, q_len[m], True, s, m)

        @pl.when(layer > 0)
        def _():
            line.finish(s, 1)
            lp = layer - 1
            bias, gain, shift = vecs[e, lp, 2:3], vecs[e, lp, 4:5], vecs[e, lp, 6:7]

            def norm(r):
                out, normed, inverse = normalize(h[s, r] + part[s, r] + bias, gain, shift)
                h[s, r] = out
                hb[r] = out.astype(BF)

                @pl.when(is_q)
                def _():
                    n2[lp, m, r] = normed
                    i2[lp, m, r] = jnp.broadcast_to(inverse, (TILE, 128))

            tiles(rows, norm)

            @pl.when(is_q)
            def _():
                for k in (9, 10):
                    save(k, lp, m).start()

        tick(i, 1, 2)

        @pl.when((layer < layers) & (m == 0))
        def _():
            for k in (0, 1):
                load(k, e, layer).wait()

        @pl.when(layer < layers)
        def _():
            @pl.when(is_q)
            def _():
                xin[layer, m] = hb[...]
                save(0, layer, m).start()

            rows_now = hb[...]
            for j in range(3):
                bias = 0.0 if j == 1 else abias[e, layer, j // 2 : j // 2 + 1].astype(F32)
                qkv[j] = (nt(rows_now, wqkv[e, layer, j]) + bias).astype(BF)

            @pl.when(is_q)
            def _():
                for j in range(3):
                    proj[layer, m, j] = qkv[j]
                save(1, layer, m).start()

        tick(i, 3)
        q_masks = head_masks(local, HEAD_DIM**-0.5)
        v_masks = head_masks(local, 1.0)

        def one_head(hd):
            @pl.when(layer < layers)
            def _():
                scores = nt(qkv[0] * q_masks[hd], qkv[1]) + vbias[s, 0:1]
                expo = jnp.exp(scores - jnp.max(scores, axis=-1, keepdims=True))
                chance = (expo / jnp.sum(expo, axis=-1, keepdims=True)).astype(BF)
                pb[hd] = chance

                @pl.when(is_q)
                def _():
                    probs[layer, m, hd] = chance

                out = nn(chance, qkv[2] * v_masks[hd])
                if hd == 0:
                    mx[...] = out
                else:
                    mx[...] += out

        for hd in range(heads):
            one_head(hd)
            tick(i, 4 + hd)

        @pl.when(layer < layers)
        def _():
            mixed_now = mx[...].astype(BF)

            @pl.when(is_q)
            def _():
                mixed[layer, m] = mixed_now
                for k in (2, 3):
                    save(k, layer, m).start()

            part[s] = nn(mixed_now, wm[e, layer])
            line.begin(s)

        tick(i, *range(4 + heads, CHUNKS))

        @pl.when(layer == layers)
        def _():
            pooled[s, 0:1] = jnp.dot(valid[s], h[s], precision=TOP_PRECISION, preferred_element_type=F32)[0:1]

            @pl.when(is_q)
            def _():
                share = rows // lax.axis_size("tensor")
                start = pl.multiple_of(lax.axis_index("tensor") * share, 16)
                acts[m] = hb[pl.ds(start, share)]

    def forward_pass(layer, s):
        i = (layer * 2 + 1) * streams + s
        e, m = 1 - s // micro, s % micro
        is_q = s >= micro
        tick(i, 0, 1)
        line.finish(s, 0)
        bias, gain, shift = vecs[e, layer, 0:1], vecs[e, layer, 3:4], vecs[e, layer, 5:6]

        def norm(r):
            out, normed, inverse = normalize(h[s, r] + part[s, r] + bias, gain, shift)
            h[s, r] = out
            hb[r] = out.astype(BF)

            @pl.when(is_q)
            def _():
                n1[layer, m, r] = normed
                i1[layer, m, r] = jnp.broadcast_to(inverse, (TILE, 128))
                first[layer, m, r] = out.astype(BF)

        tiles(rows, norm)

        @pl.when(m == 0)
        def _():
            for k in (2, 3):
                load(k, e, layer).wait()

        @pl.when(is_q)
        def _():
            for k in (4, 5, 6):
                save(k, layer, m).start()

        tick(i, 2, 3)
        inner[...] = nn(hb[...], we[e, layer])
        tick(i, 4)
        bias_e = vecs[e, layer, 1:2]

        def gelu(r):
            u = inner[r] + bias_e
            phi = 0.5 * (1.0 + lax.erf(u * ROOT_HALF))
            out = (u * phi).astype(BF)
            act[r] = out

            @pl.when(is_q)
            def _():
                active[layer, m, r] = out
                slope[layer, m, r] = phi + u * jnp.exp(-0.5 * u * u) * INV_ROOT_TAU

        tiles(rows, gelu)

        @pl.when(is_q)
        def _():
            for k in (7, 8):
                save(k, layer, m).start()

        tick(i, 5, 6)
        part[s] = nn(act[...], ws[e, layer])
        line.begin(s)
        tick(i, 7)

    def layer_step(layer, carry):
        def a_step(s, c):
            attention_pass(layer, s)
            return c

        lax.fori_loop(0, streams, a_step, 0)

        @pl.when(layer < layers)
        def _():
            def f_step(s, c):
                forward_pass(layer, s)
                return c

            lax.fori_loop(0, streams, f_step, 0)

        return carry

    lax.fori_loop(0, layers + 1, layer_step, 0)

    def drain(j, carry):
        for k in range(len(saved)):
            save(k, j // micro, j % micro).wait()
        return carry

    lax.fori_loop(0, layers * micro, drain, 0)


def run_forward(q_tok, q_drop, q_len, k_tok, k_drop, k_len, weights):
    micro, _, rows, width = q_tok.shape
    wqkv, abias, wm, mbias, we, ebias, ws, sbias, gains, shifts = weights
    layers, local, units = we.shape[1], wm.shape[2], we.shape[3]
    heads = local // HEAD_DIM
    streams = 2 * micro
    lm = (layers, micro)
    shapes = [
        ((micro, rows // lax.axis_size("tensor"), width), BF),
        ((streams, 8, width), F32),
        ((micro, 8, rows), F32),
        (lm + (rows, width), BF),
        (lm + (3, rows, local), BF),
        (lm + (heads, rows, rows), BF),
        (lm + (rows, local), BF),
        (lm + (rows, width), F32),
        (lm + (rows, 128), F32),
        (lm + (rows, width), BF),
        (lm + (rows, units), F32),
        (lm + (rows, units), BF),
        (lm + (rows, width), F32),
        (lm + (rows, 128), F32),
    ]
    vm = pl.BlockSpec(memory_space=pltpu.VMEM)
    hb = pl.BlockSpec(memory_space=pl.ANY)
    sm = pl.BlockSpec(memory_space=pltpu.SMEM)
    return pl.pallas_call(
        forward_kernel,
        out_shape=[jax.ShapeDtypeStruct(*s) for s in shapes],
        in_specs=[vm, vm, sm, vm, vm, sm] + [hb, vm, hb, vm, hb, vm, hb, vm, vm, vm],
        out_specs=[vm] * 3 + [hb] * 11,
        scratch_shapes=[pltpu.VMEM(*s) for s in shapes[3:]]
        + [pltpu.VMEM(w.shape, BF) for w in (wqkv, wm, we, ws)]
        + [
            pltpu.VMEM((streams, rows, width), F32),
            pltpu.VMEM((rows, width), BF),
            pltpu.VMEM((3, rows, local), BF),
            pltpu.VMEM((heads, rows, rows), BF),
            pltpu.VMEM((rows, local), F32),
            pltpu.VMEM((rows, units), F32),
            pltpu.VMEM((rows, units), BF),
            pltpu.VMEM((streams, 8, rows), F32),
            pltpu.VMEM((streams, 8, rows), F32),
            pltpu.VMEM((2, layers, 8, width), F32),
            pltpu.SemaphoreType.DMA((11,) + lm),
            pltpu.SemaphoreType.DMA((4, 2, layers)),
        ]
        + line_scratch(streams, rows, width),
        compiler_params=pltpu.CompilerParams(
            collective_id=0, has_side_effects=True, vmem_limit_bytes=VMEM_LIMIT
        ),
        name="encoders_forward",
    )(q_tok, q_drop, q_len, k_tok, k_drop, k_len, *weights)


def norm_back(g, normed, inverse, gain):
    scaled = g * gain
    return inverse * (
        scaled
        - jnp.mean(scaled, axis=-1, keepdims=True)
        - normed * jnp.mean(scaled * normed, axis=-1, keepdims=True)
    )


def fold(x):
    return jnp.sum(x.reshape(x.shape[0] // 8, 8, x.shape[1]), axis=0)


class Plane:
    def __init__(self, grads, sends, recvs, out, send_sem, recv_sem, credit):
        dp, self.x = lax.axis_index("dp"), lax.axis_index("rep")
        self.y, self.c = dp // 2, dp % 2
        self.partner = {
            "c": {"dp": dp + 1 - 2 * self.c},
            "x": {"rep": 1 - self.x},
            "y": {"dp": (dp + 2) % 4},
        }
        self.grads, self.sends, self.recvs, self.out = grads, sends, recvs, out
        self.send_sem, self.recv_sem, self.credit = send_sem, recv_sem, credit
        self.block = grads.shape[2] // 8

    def copy(self, u, stage, half):
        way = ("c", "xy"[half], "yx"[half])[stage]
        return pltpu.make_async_remote_copy(
            src_ref=self.sends[stage].at[u, half], dst_ref=self.recvs[stage].at[u, half],
            send_sem=self.send_sem.at[u, stage, half], recv_sem=self.recv_sem.at[u, stage, half],
            device_id=self.partner[way], device_id_type=MESH)

    def spots(self, stage, half, own):
        pick = (lambda v: v) if own else (lambda v: 1 - v)
        if stage == 0:
            return [(4 * y + 2 * pick(self.c), 2 * y, 2) for y in (0, 1)]
        if stage == 1 and half == 0:
            return [(4 * y + 2 * self.c + pick(self.x), y, 1) for y in (0, 1)]
        if stage == 1:
            return [(4 * pick(self.y) + 2 * self.c, 0, 2)]
        if half == 0:
            return [(4 * pick(self.y) + 2 * self.c + self.x, 0, 1)]
        return [(4 * self.y + 2 * self.c + pick(self.x), 0, 1)]

    def parts(self, stage, half, own):
        for here, there, blocks in self.spots(stage, half, own):
            for b in range(blocks):
                start = (here + b) * self.block
                yield pl.ds(pl.multiple_of(start, 8), self.block), pl.ds((there + b) * self.block, self.block)

    def send(self, u, stage, live, spend):
        @pl.when(live)
        def _():
            for half in (0, 1):
                for here, there in self.parts(stage, half, False):
                    self.sends[stage][u, half, there] = self.grads[u, half, here].astype(BF)

            @pl.when(spend)
            def _():
                pl.semaphore_wait(self.credit.at[u, stage], 2)

            for half in (0, 1):
                self.copy(u, stage, half).start()

    def take(self, u, stage, live, give, layer):
        @pl.when(live)
        def _():
            for half in (0, 1):
                self.copy(u, stage, half).wait()
                for here, there in self.parts(stage, half, True):
                    total = self.grads[u, half, here] + self.recvs[stage][u, half, there].astype(F32)
                    if stage == 2:
                        self.out[layer, u, half] = total
                    else:
                        self.grads[u, half, here] = total

            @pl.when(give)
            def _():
                for half in (0, 1):
                    way = ("c", "xy"[half], "yx"[half])[stage]
                    pl.semaphore_signal(
                        self.credit.at[u, stage], inc=1, device_id=self.partner[way], device_id_type=MESH
                    )


def greet_all():
    z, dp, rep = lax.axis_index("tensor"), lax.axis_index("dp"), lax.axis_index("rep")
    sem = pltpu.get_barrier_semaphore()
    others = [{"tensor": (z + d) % 4} for d in (1, 2, 3)]
    others += [{"rep": 1 - rep, "tensor": (z + d) % 4} for d in (0, 1, 2, 3)]
    others += [{"dp": dp + 1 - 2 * (dp % 2)}, {"dp": (dp + 2) % 4}]
    for other in others:
        pl.semaphore_signal(sem, inc=1, device_id=other, device_id_type=MESH)
    pl.semaphore_wait(sem, len(others))


def backward_kernel(inside, *refs):
    seed, slots, negs, gains, *rest = refs
    kept, rest = rest[:11], rest[11:]
    stored, rest = rest[:4], rest[4:]
    g_in, vec, out_big, out_small, *rest = rest
    saved, rest = rest[:11], rest[11:]
    loaded, rest = rest[:4], rest[4:]
    g_vec, g_abias, dr, low, dinner, tmp, dqkv, dsc, pgrad, load_sem, *rest = rest
    line_refs, rest = rest[:9], rest[9:]
    xin, proj, probs, mixed, n1, i1, first, slope, active, n2, i2 = saved
    wqkv, wm, we, ws = loaded
    part = line_refs[0]
    layers, micro, rows, width = xin.shape
    local = wm.shape[1]
    half_units = we.shape[2] // 2
    heads = local // HEAD_DIM
    streams = micro
    last = 2 * layers * streams
    order = (9, 10, 7, 8, 6, 4, 5, 3, 2, 1, 0)

    def load_saved(k, layer):
        return pltpu.make_async_copy(kept[k].at[layer], saved[k].at[layer], load_sem.at[k, layer])

    def load_weight(k, layer):
        return pltpu.make_async_copy(stored[k].at[0, layer], loaded[k].at[layer], load_sem.at[11 + k, layer])

    for layer in reversed(range(layers)):
        for k in order[:2]:
            load_saved(k, layer).start()
        for k in (3, 2):
            load_weight(k, layer).start()
        for k in order[2:]:
            load_saved(k, layer).start()
        for k in (1, 0):
            load_weight(k, layer).start()
    g_vec[...] = jnp.zeros_like(g_vec)
    g_abias[...] = jnp.zeros_like(g_abias)
    vec[...] = jnp.zeros_like(vec)
    if inside:
        (g_big, g_small, b1, b2, b3, e1, e2, e3, s1, s2, s3, t1, t2, t3, big_s, big_r, small_s, small_r,
         big_c, small_c, v_rcv, v_send, v_recv, ask, asked, reply, heard, ask_sem, reply_sem, heard_sem) = rest
        greet_all()
        big = Plane(g_big, (b1, b2, b3), (e1, e2, e3), out_big, big_s, big_r, big_c)
        small = Plane(g_small, (s1, s2, s3), (t1, t2, t3), out_small, small_s, small_r, small_c)
        contrast_inside(seed, negs, pgrad, vec, ask, asked, reply, heard, ask_sem, reply_sem, heard_sem)
    else:
        greet_line()
        pgrad[...] = seed[...]
    line = Line(*line_refs)

    def tick(i, *which):
        j = jnp.maximum(i - 1, 0)
        s, slot, live = j % streams, (j // streams) % 2, (i >= 1) & (i <= last)
        for c in which:
            if c < CHUNKS:
                line.inward(s, c, slot, live)
            if c >= LAG:
                line.outward(s, c - LAG, slot, live)

    def add_to(large, u, half, layer, s, value):
        if inside:
            ref = (g_big if large else g_small).at[u, half]
        else:
            ref = (out_big if large else out_small).at[layer, u, half]

        @pl.when(s == 0)
        def _():
            ref[...] = value

        @pl.when(s > 0)
        def _():
            ref[...] += value

    def plane(what, large, stage, live, step):
        if inside:
            group = big if large else small
            for u in (0, 1):
                if what == "send":
                    group.send(u, stage, live, step > 0)
                else:
                    group.take(u, stage, live, step < layers - 1, layers - 1 - step)

    def mlp_back(step, s):
        layer = layers - 1 - step
        i = step * 2 * streams + s

        @pl.when(s == 0)
        def _():
            for k in (4, 6, 7, 8, 9, 10):
                load_saved(k, layer).wait()
            for k in (2, 3):
                load_weight(k, layer).wait()

        @pl.when(step == 0)
        def _():
            def begin(c, carry):
                r = pl.ds(pl.multiple_of(c * TILE, TILE), TILE)
                pos = (lax.broadcasted_iota(jnp.int32, (TILE, 1), 0) + c * TILE).astype(F32)
                part[s, r] = jnp.where(pos < pgrad[s, 1:2, 0:1], pgrad[s, 0:1], 0.0)
                dr[s, r] = jnp.zeros((TILE, width), F32)
                return carry

            lax.fori_loop(0, rows // TILE, begin, 0)

        @pl.when(step > 0)
        def _():
            line.finish(s, 1)

        gain = gains[0, layer, 1:2].astype(F32)

        def back(r):
            g = part[s, r] + dr[s, r]
            normed = n2[layer, s, r]
            out = norm_back(g, normed, i2[layer, s, r][:, 0:1], gain)
            dr[s, r] = out
            low[s, r] = out.astype(BF)
            g_vec[layer, 1] += fold(g * normed)
            g_vec[layer, 3] += fold(g)
            g_vec[layer, 4] += fold(out)

        tiles(rows, back)
        tick(i, 0)
        tmp[...] = nt(low[s], ws[layer])
        tick(i, 1)

        def slopes(r):
            out = tmp[r] * slope[layer, s, r]
            dinner[r] = out.astype(BF)
            g_vec[layer, 6] += fold(out)

        tiles(rows, slopes)
        tick(i, 2)
        part[s] = nt(dinner[...], we[layer])
        line.begin(s)
        tick(i, 3)
        plane("take", True, 2, (step > 0) & (s == 0), step - 1)
        plane("take", False, 0, (step > 0) & (s == 0), step - 1)
        plane("send", False, 1, (step > 0) & (s == 0), step - 1)
        for half in (0, 1):
            cols = pl.ds(half * half_units, half_units)
            add_to(True, 0, half, layer, s, tn(low[s], active[layer, s, :, cols]))
            tick(i, 4 + half)
        for half in (0, 1):
            cols = pl.ds(half * half_units, half_units)
            add_to(True, 1, half, layer, s, tn(first[layer, s], dinner[:, cols]))
            tick(i, 6 + half)
        plane("send", True, 0, s == streams - 1, step)
        plane("take", False, 1, (step > 0) & (s == streams - 1), step - 1)
        plane("send", False, 2, (step > 0) & (s == streams - 1), step - 1)
        tick(i, *range(CHUNKS, CHUNKS + LAG))

    def attention_back(step, s):
        layer = layers - 1 - step
        i = (step * 2 + 1) * streams + s

        @pl.when(s == 0)
        def _():
            for k in (0, 1, 2, 3, 5):
                load_saved(k, layer).wait()
            for k in (0, 1):
                load_weight(k, layer).wait()

        line.finish(s, 0)
        gain = gains[0, layer, 0:1].astype(F32)

        def back(r):
            g = part[s, r] + dr[s, r]
            normed = n1[layer, s, r]
            out = norm_back(g, normed, i1[layer, s, r][:, 0:1], gain)
            dr[s, r] = out
            low[s, r] = out.astype(BF)
            g_vec[layer, 0] += fold(g * normed)
            g_vec[layer, 2] += fold(g)
            g_vec[layer, 5] += fold(out)

        tiles(rows, back)
        tick(i, 0)
        dmix = nt(low[s], wm[layer]).astype(BF)
        tick(i, 1)
        masks = head_masks(local, 1.0)
        for hd in range(heads):
            chance_b = probs[layer, s, hd]
            chance = chance_b.astype(F32)
            dm = dmix * masks[hd]
            dch = nt(dm, proj[layer, s, 2])
            ds = chance * (dch - jnp.sum(chance * dch, axis=-1, keepdims=True))
            draw = (ds * HEAD_DIM**-0.5).astype(BF)
            dq = nn(draw, proj[layer, s, 1] * masks[hd])
            dk = tn(draw, proj[layer, s, 0] * masks[hd])
            dv = tn(chance_b, dm)
            if hd == 0:
                dqkv[0] = dq
                dqkv[1] = dk
                dqkv[2] = dv
            else:
                dqkv[0] += dq
                dqkv[1] += dk
                dqkv[2] += dv
            tick(i, 2 + hd)
        g_abias[layer, 0] += fold(dqkv[0])
        g_abias[layer, 1] += fold(dqkv[2])
        for j in range(3):
            dsc[j] = dqkv[j].astype(BF)
        part[s] = nn(dsc[0], wqkv[layer, 0]) + nn(dsc[1], wqkv[layer, 1]) + nn(dsc[2], wqkv[layer, 2])
        line.begin(s)
        tick(i, *range(2 + heads, 6))
        plane("take", True, 0, s == 0, step)
        plane("send", True, 1, s == 0, step)
        plane("take", True, 1, s == streams - 1, step)
        plane("send", True, 2, s == streams - 1, step)
        plane("take", False, 2, (step > 0) & (s == 0), step - 1)
        for j in range(3):
            add_to(False, j // 2, j % 2, layer, s, tn(xin[layer, s], dsc[j]))
        tick(i, 6)
        add_to(False, 1, 1, layer, s, tn(low[s], mixed[layer, s]))
        tick(i, *range(7, CHUNKS + LAG))
        plane("send", False, 0, s == streams - 1, step)

    def layer_step(step, carry):
        def m_step(s, c):
            mlp_back(step, s)
            return c

        def a_step(s, c):
            attention_back(step, s)
            return c

        lax.fori_loop(0, streams, m_step, 0)
        lax.fori_loop(0, streams, a_step, 0)
        return carry

    lax.fori_loop(0, layers, layer_step, 0)

    for layer in range(layers):
        for k in range(7):
            vec[layer * 7 + k : layer * 7 + k + 1] = jnp.sum(g_vec[layer, k], axis=0, keepdims=True)
        for k in range(2):
            row = layers * 7 + layer * 2 + k
            vec[row : row + 1, 0:local] = jnp.sum(g_abias[layer, k], axis=0, keepdims=True)

    def vec_copy(stage):
        return pltpu.make_async_remote_copy(
            src_ref=vec, dst_ref=v_rcv.at[stage], send_sem=v_send.at[stage], recv_sem=v_recv.at[stage],
            device_id=big.partner["cxy"[stage]], device_id_type=MESH)

    def vec_take(stage):
        if inside:
            vec_copy(stage).wait()
            vec[...] += v_rcv[stage]

    def vec_send(stage):
        if inside:
            vec_copy(stage).start()

    end = layers - 1
    vec_send(0)
    tick(last, 0, 1)
    plane("take", False, 0, True, end)
    plane("send", False, 1, True, end)
    vec_take(0)
    vec_send(1)
    tick(last, 2, 3, 4)
    plane("take", True, 2, True, end)
    tick(last, 5, 6)
    plane("take", False, 1, True, end)
    plane("send", False, 2, True, end)
    vec_take(1)
    vec_send(2)
    tick(last, *range(7, CHUNKS + LAG))

    def tail(s, carry):
        line.finish(s, 1)

        def back(r):
            low[s, r] = (part[s, r] + dr[s, r]).astype(BF)

        tiles(rows, back)
        down = lax.broadcasted_iota(jnp.int32, (rows, rows), 0).astype(F32)
        pick = jnp.where(slots[s, 0:1] == down, 1.0, 0.0).astype(BF)
        low[s] = tn(pick, low[s]).astype(BF)
        share = rows // lax.axis_size("tensor")
        start = pl.multiple_of(lax.axis_index("tensor") * share, 16)
        g_in[s] = low[s, pl.ds(start, share)]
        return carry

    lax.fori_loop(0, streams, tail, 0)
    plane("take", False, 2, True, end)
    vec_take(2)


def run_backward(inside, seed, slots, negatives, saved, weights):
    wqkv, abias, wm, mbias, we, ebias, ws, sbias, gains, shifts = weights
    layers, micro, rows, width = saved[0].shape
    local, units = wm.shape[2], we.shape[3]
    tall = 8 * ((9 * layers + 2 + 7) // 8)
    kinds = ((units // 2, "big"), (local, "small"))
    high = width // 8 if inside else width
    shapes = [((micro, rows // lax.axis_size("tensor"), width), BF), ((tall, width), F32)]
    shapes += [((layers, 2, 2, high, w), F32) for w, _ in kinds]
    vm = pl.BlockSpec(memory_space=pltpu.VMEM)
    hb = pl.BlockSpec(memory_space=pl.ANY)
    dma = pltpu.SemaphoreType.DMA
    scratch = [pltpu.VMEM(v.shape, v.dtype) for v in saved]
    scratch += [pltpu.VMEM(w.shape[1:], BF) for w in (wqkv, wm, we, ws)]
    scratch += [
        pltpu.VMEM((layers, 7, 8, width), F32),
        pltpu.VMEM((layers, 2, 8, local), F32),
        pltpu.VMEM((micro, rows, width), F32),
        pltpu.VMEM((micro, rows, width), BF),
        pltpu.VMEM((rows, units), BF),
        pltpu.VMEM((rows, units), F32),
        pltpu.VMEM((3, rows, local), F32),
        pltpu.VMEM((3, rows, local), BF),
        pltpu.VMEM((micro, 8, width), F32),
        dma((15, layers)),
    ]
    scratch += line_scratch(micro, rows, width)
    if inside:
        scratch += [pltpu.VMEM((2, 2, width, w), F32) for w, _ in kinds]
        for w, _ in kinds:
            for _ in range(2):
                scratch += [pltpu.VMEM((2, 2, width // n, w), BF) for n in (2, 4, 8)]
        scratch += [dma((2, 3, 2))] * 4
        scratch += [pltpu.SemaphoreType.REGULAR((2, 3))] * 2
        scratch += [pltpu.VMEM((3, tall, width), F32), dma((3,)), dma((3,))]
        scratch += [
            pltpu.VMEM((16, width), BF),
            pltpu.VMEM((16, width), BF),
            pltpu.VMEM((2, 8, width), F32),
            pltpu.VMEM((8, 8, width), F32),
            dma((2,)),
            dma((8,)),
            dma((8,)),
        ]
    return pl.pallas_call(
        functools.partial(backward_kernel, inside),
        out_shape=[jax.ShapeDtypeStruct(*s) for s in shapes],
        in_specs=[vm] * 4 + [hb] * 15,
        out_specs=[vm] * len(shapes),
        scratch_shapes=scratch,
        compiler_params=pltpu.CompilerParams(
            collective_id=1, has_side_effects=True, vmem_limit_bytes=VMEM_LIMIT
        ),
        name="encoder_backward",
    )(seed, slots, negatives, gains, *saved, wqkv, wm, we, ws)


def contrast_inside(pooled, negs, pgrad, vec, ask, asked, reply, heard, ask_sem, reply_sem, heard_sem):
    z, rep = lax.axis_index("tensor"), lax.axis_index("rep")
    micro = pgrad.shape[0]
    width = negs.shape[1]
    scales, counts, dirs, key_dirs, positives = [], [], [], [], []
    ask[...] = jnp.zeros_like(ask)
    for m in range(micro):
        count = pooled[micro + m, 1:2]
        mean_q = pooled[micro + m, 0:1] / count
        mean_k = pooled[m, 0:1] / pooled[m, 1:2]
        scale = lax.rsqrt(jnp.sum(mean_q * mean_q, axis=-1, keepdims=True) + UNIT_EPS)
        key_dir = mean_k * lax.rsqrt(jnp.sum(mean_k * mean_k, axis=-1, keepdims=True) + UNIT_EPS)
        direction = mean_q * scale
        ask[m : m + 1] = direction.astype(BF)
        positives.append(jnp.sum(direction * key_dir, axis=-1, keepdims=True) / SOFTMAX_WARMTH)
        scales.append(scale)
        counts.append(count)
        dirs.append(direction)
        key_dirs.append(key_dir)
    question = pltpu.make_async_remote_copy(
        src_ref=ask, dst_ref=asked, send_sem=ask_sem.at[0], recv_sem=ask_sem.at[1],
        device_id={"rep": 1 - rep}, device_id_type=MESH)
    question.start()

    def answer(which, rows_now):
        logits = nt(rows_now, negs[...]) / SOFTMAX_WARMTH
        top = jnp.max(logits, axis=-1, keepdims=True)
        expo = jnp.exp(logits - top)
        total = jnp.sum(expo, axis=-1, keepdims=True)
        high = expo.astype(BF)
        rest = expo - high.astype(F32)
        mid = rest.astype(BF)
        tiny = (rest - mid.astype(F32)).astype(BF)
        keys = nn(high, negs[...]) + nn(mid, negs[...]) + nn(tiny, negs[...])
        reply[which, 0:micro] = keys[0:micro]
        reply[which, micro : 2 * micro] = jnp.broadcast_to(top[0:micro], (micro, width))
        reply[which, 2 * micro : 3 * micro] = jnp.broadcast_to(total[0:micro], (micro, width))

    def tell(which, d):
        other = {"tensor": (z + d) % 4} if which == 0 else {"rep": 1 - rep, "tensor": (z + d) % 4}
        k = which * 4 + d
        return pltpu.make_async_remote_copy(
            src_ref=reply.at[which], dst_ref=heard.at[k], send_sem=reply_sem.at[k], recv_sem=heard_sem.at[k],
            device_id=other, device_id_type=MESH)

    answer(0, ask[...])
    for d in (1, 2, 3):
        tell(0, d).start()
    question.wait()
    answer(1, asked[...])
    for d in (0, 1, 2, 3):
        tell(1, d).start()
    for k in range(1, 8):
        tell(k // 4, k % 4).wait()
    everyone = [reply[0]] + [heard[k] for k in range(1, 8)]
    loss = 0.0
    for m in range(micro):
        positive = positives[m]
        best = positive
        for one in everyone:
            best = jnp.maximum(best, one[micro + m : micro + m + 1, 0:1])
        own = jnp.exp(positive - best)
        total, keys = own, own * key_dirs[m]
        for one in everyone:
            weight = jnp.exp(one[micro + m : micro + m + 1, 0:1] - best)
            total = total + weight * one[2 * micro + m : 2 * micro + m + 1, 0:1]
            keys = keys + weight * one[m : m + 1]
        loss = loss + best + jnp.log(total) - positive
        dqn = (keys / total - key_dirs[m]) * (CROP_SLOTS / SOFTMAX_WARMTH)
        mean_grad = scales[m] * (dqn - dirs[m] * jnp.sum(dirs[m] * dqn, axis=-1, keepdims=True))
        pgrad[m, 0:1] = mean_grad / counts[m]
        pgrad[m, 1:2] = counts[m]
    vec[vec.shape[0] - 1 : vec.shape[0]] = jnp.broadcast_to(loss, (1, width))


def outputs_kernel(layers, size, acts, g_in, vec, big, small, o_acts, o_in, o_attend, o_abias, o_merge, o_mbias,
                   o_expand, o_ebias, o_shrink, o_sbias, o_gain, o_shift, o_loss):
    width = vec.shape[1]
    local = small.shape[4]
    half = big.shape[4]
    group = lax.axis_index("dp") * lax.axis_size("rep") + lax.axis_index("rep")
    blocks = width // size
    own = pltpu.roll(vec[...], ((blocks - group) % blocks) * size, axis=1)[:, :size]
    o_acts[:, 0] = acts[...]
    o_in[:, 0] = g_in[...]
    for l in range(layers):
        for h in (0, 1):
            cols = slice(h * half, (h + 1) * half)
            o_shrink[l, :, cols] = big[l, 0, h]
            o_expand[l, :, cols] = big[l, 1, h]
        for j in range(3):
            o_attend[l, j] = small[l, j // 2, j % 2]
        o_merge[l] = small[l, 1, 1].T
        row = 7 * l
        o_gain[l] = own[row : row + 2]
        o_shift[l] = own[row + 2 : row + 4]
        o_sbias[l : l + 1] = own[row + 4 : row + 5]
        o_mbias[l : l + 1] = own[row + 5 : row + 6]
        o_ebias[l : l + 1] = vec[row + 6 : row + 7]
        o_abias[l] = vec[7 * layers + 2 * l : 7 * layers + 2 * l + 2, :local]
    o_loss[...] = vec[vec.shape[0] - 1 :, 0:1]


def run_outputs(acts, g_in, vec, big, small):
    micro, share, width = acts.shape
    layers, _, _, size, half = big.shape
    local = small.shape[4]
    shapes = [
        ((micro, 1, share, width), BF),
        ((micro, 1, share, width), BF),
        ((layers, 3, size, local), F32),
        ((layers, 2, local), F32),
        ((layers, local, size), F32),
        ((layers, size), F32),
        ((layers, size, 2 * half), F32),
        ((layers, width), F32),
        ((layers, size, 2 * half), F32),
        ((layers, size), F32),
        ((layers, 2, size), F32),
        ((layers, 2, size), F32),
        ((1, 1), F32),
    ]
    vm = pl.BlockSpec(memory_space=pltpu.VMEM)
    return pl.pallas_call(
        functools.partial(outputs_kernel, layers, size),
        out_shape=[jax.ShapeDtypeStruct(*s) for s in shapes],
        in_specs=[vm] * 5,
        out_specs=[vm] * len(shapes),
        compiler_params=pltpu.CompilerParams(vmem_limit_bytes=VMEM_LIMIT),
        name="outputs",
    )(acts, g_in, vec, big, small)


def contrast(mean_q, mean_k, negatives):
    key_dir = mean_k * lax.rsqrt(jnp.sum(mean_k * mean_k, axis=-1, keepdims=True) + UNIT_EPS)
    scale = lax.rsqrt(jnp.sum(mean_q * mean_q, axis=-1, keepdims=True) + UNIT_EPS)
    direction = mean_q * scale
    positive = jnp.sum(direction * key_dir, axis=-1) / SOFTMAX_WARMTH
    micro, width = mean_q.shape
    asked = lax.all_gather(direction.astype(BF), "rep", axis=0, tiled=True)
    logits = nt(asked, negatives) / SOFTMAX_WARMTH
    top = jnp.max(logits, axis=-1, keepdims=True)
    expo = jnp.exp(logits - top)
    total = jnp.sum(expo, axis=-1, keepdims=True)
    keys = jnp.dot(expo, negatives.astype(F32), precision=TOP_PRECISION)
    packed = jnp.concatenate([keys, jnp.broadcast_to(top, (top.shape[0], 128)), jnp.broadcast_to(total, (top.shape[0], 128))], axis=1)
    pieces = lax.all_gather(packed, ("rep", "tensor"), axis=0, tiled=False)
    mine = lax.dynamic_slice_in_dim(pieces, lax.axis_index("rep") * micro, micro, 1)
    keys, top, total = mine[..., :width], mine[..., width], mine[..., width + 128]
    best = jnp.maximum(jnp.max(top, axis=0), positive)
    weight = jnp.exp(top - best)
    own = jnp.exp(positive - best)
    total = jnp.sum(total * weight, axis=0) + own
    keys = jnp.sum(keys * weight[..., None], axis=0) + own[:, None] * key_dir
    per_query = best + jnp.log(total) - positive
    dqn = (keys / total[:, None] - key_dir) * (CROP_SLOTS / SOFTMAX_WARMTH)
    mean_grad = scale * (dqn - direction * jnp.sum(direction * dqn, axis=-1, keepdims=True))
    return per_query, mean_grad


def per_device(
    query_tokens, query_drop, query_length, key_tokens, key_drop, key_length, negatives,
    attend_weight, attend_bias, merge_weight, merge_bias, expand_weight, expand_bias,
    shrink_weight, shrink_bias, norm_gain, norm_shift,
):
    micro, _, rows, width = query_tokens.shape
    weights = (
        jnp.transpose(attend_weight, (0, 1, 3, 4, 2)),
        attend_bias,
        merge_weight,
        merge_bias,
        expand_weight,
        expand_bias,
        shrink_weight,
        shrink_bias,
        norm_gain,
        norm_shift,
    )
    acts, pooled, slots, *saved = run_forward(
        query_tokens, query_drop, query_length.reshape(micro), key_tokens, key_drop, key_length.reshape(micro), weights
    )
    groups = ("dp", "rep")
    inside = lax.axis_size("dp") == 4 and lax.axis_size("rep") == 2
    if inside:
        g_in, vec, g_big, g_small = run_backward(inside, pooled, slots, negatives, saved, weights)
    else:
        counts = pooled[:, 1]
        means = pooled[:, 0] / counts
        per_query, mean_grad = contrast(means[micro:], means[:micro], negatives)
        pgrad = jnp.concatenate(
            [(mean_grad / counts[micro:])[:, None], counts[micro:, None], jnp.zeros((micro, 6, width), F32)], axis=1
        )
        g_in, vec, g_big, g_small = run_backward(inside, pgrad, slots, negatives, saved, weights)
        g_big = lax.psum_scatter(g_big, groups, scatter_dimension=3, tiled=True)
        g_small = lax.psum_scatter(g_small, groups, scatter_dimension=3, tiled=True)
        vec = lax.psum(vec.at[-1].add(jnp.sum(per_query)), groups)
    outs = run_outputs(acts, g_in, vec, g_big, g_small)
    loss = outs[12].reshape(()) / (micro * lax.axis_size("dp") * lax.axis_size("rep"))
    return (
        outs[0], outs[1], jnp.transpose(outs[2], (0, 2, 1, 3)), *outs[3:8],
        jnp.transpose(outs[8], (0, 2, 1)), *outs[9:12], loss,
    )


def solution(mesh):
    return jax.shard_map(
        per_device,
        mesh=mesh,
        in_specs=(
            P(None, ("dp", "rep"), None, None),
            P(None, ("dp", "rep"), None),
            P(None, ("dp", "rep")),
            P(None, ("dp", "rep"), None, None),
            P(None, ("dp", "rep"), None),
            P(None, ("dp", "rep")),
            P(("rep", "tensor"), None),
            P(None, None, None, None, "tensor"),
            P(None, None, None, "tensor"),
            P(None, None, "tensor", None),
            P(),
            P(None, None, None, "tensor"),
            P(None, None, "tensor"),
            P(None, None, "tensor", None),
            P(),
            P(),
            P(),
        ),
        out_specs=(
            P(None, ("dp", "rep"), "tensor", None),
            P(None, ("dp", "rep"), "tensor", None),
            P(None, ("dp", "rep"), None, "tensor"),
            P(None, None, "tensor"),
            P(None, "tensor", ("dp", "rep")),
            P(None, ("dp", "rep")),
            P(None, ("dp", "rep"), "tensor"),
            P(None, "tensor"),
            P(None, "tensor", ("dp", "rep")),
            P(None, ("dp", "rep")),
            P(None, None, ("dp", "rep")),
            P(None, None, ("dp", "rep")),
            P(),
        ),
        check_vma=False,
    )
```

```python
import functools

import jax
import jax.numpy as jnp
from jax import lax
from jax.experimental import pallas as pl
from jax.experimental.pallas import tpu as pltpu
from jax.sharding import PartitionSpec as P

HEAD_DIM = 64
CROP_SLOTS = 256
SOFTMAX_WARMTH = 0.05
NORM_EPS = 1e-12
UNIT_EPS = 1e-06
MASKED = -1e30
TOP_PRECISION = lax.Precision.HIGHEST
ROOT_HALF = 0.7071067811865476
INV_ROOT_TAU = 0.3989422804014327

MESH = pl.DeviceIdType.MESH
BF = jnp.bfloat16
F32 = jnp.float32
CHUNKS = 8
LAG = 3
EARLY = 2
TILE = 64
VMEM_LIMIT = 62 * 1024 * 1024


def nn(a, b):
    return jnp.dot(a, b, preferred_element_type=F32)


def nt(a, b):
    return lax.dot_general(a, b, (((1,), (1,)), ((), ())), preferred_element_type=F32)


def tn(a, b):
    return lax.dot_general(a, b, (((0,), (0,)), ((), ())), preferred_element_type=F32)


def greet_line():
    z = lax.axis_index("tensor")
    sem = pltpu.get_barrier_semaphore()
    for d in (1, 2, 3):
        pl.semaphore_signal(sem, inc=1, device_id={"tensor": (z + d) % 4}, device_id_type=MESH)
    pl.semaphore_wait(sem, 3)


class Line:
    def __init__(self, part, sbuf, tbuf, x1, x2, s_sem, t_sem, r1, r2):
        z = lax.axis_index("tensor")
        self.mid = (z + 1) // 2 == 1
        self.end = (z + 1) // 2 != 1
        self.inner = 1 + z // 2
        self.outer = 3 * (z // 2)
        self.cross = 3 - z
        self.part, self.sbuf, self.tbuf, self.x1, self.x2 = part, sbuf, tbuf, x1, x2
        self.s_sem, self.t_sem, self.r1, self.r2 = s_sem, t_sem, r1, r2
        self.size = part.shape[1] // CHUNKS

    def rows(self, c):
        return pl.ds(pl.multiple_of(c * self.size, self.size), self.size)

    def to_inner(self, s, c):
        return pltpu.make_async_remote_copy(
            src_ref=self.sbuf.at[s, self.rows(c)], dst_ref=self.x2.at[s, self.rows(c)],
            send_sem=self.s_sem.at[s, c], recv_sem=self.r2.at[s, c],
            device_id={"tensor": self.inner}, device_id_type=MESH)

    def to_cross(self, s, c, slot):
        return pltpu.make_async_remote_copy(
            src_ref=self.sbuf.at[s, self.rows(c)], dst_ref=self.x1.at[slot, s, self.rows(c)],
            send_sem=self.s_sem.at[s, c], recv_sem=self.r1.at[slot, s, c],
            device_id={"tensor": self.cross}, device_id_type=MESH)

    def to_outer(self, s, c, slot):
        return pltpu.make_async_remote_copy(
            src_ref=self.tbuf.at[s, self.rows(c)], dst_ref=self.x1.at[slot, s, self.rows(c)],
            send_sem=self.t_sem.at[s, c], recv_sem=self.r1.at[slot, s, c],
            device_id={"tensor": self.outer}, device_id_type=MESH)

    def begin(self, s):
        @pl.when(self.end)
        def _():
            for c in range(CHUNKS):
                rows = self.rows(c)
                self.sbuf[s, rows] = self.part[s, rows].astype(BF)
                self.to_inner(s, c).start()

    def inward(self, s, c, slot, live):
        @pl.when(self.mid & live)
        def _():
            rows = self.rows(c)
            self.to_inner(s, c).wait_recv()
            self.sbuf[s, rows] = (self.part[s, rows] + self.x2[s, rows].astype(F32)).astype(BF)
            self.to_cross(s, c, slot).start()

    def outward(self, s, c, slot, live):
        @pl.when(self.mid & live)
        def _():
            rows = self.rows(c)
            self.to_cross(s, c, slot).wait_recv()
            joint = self.part[s, rows] + self.x1[slot, s, rows].astype(F32)
            self.part[s, rows] = joint + self.x2[s, rows].astype(F32)
            self.tbuf[s, rows] = joint.astype(BF)
            self.to_outer(s, c, slot).start()

    def settle(self, s, slot, tile):
        per = TILE // self.size

        @pl.when(self.end)
        def _():
            for d in range(per):
                c = tile * per + d
                rows = self.rows(c)
                self.to_outer(s, c, slot).wait_recv()
                self.part[s, rows] = self.part[s, rows] + self.x1[slot, s, rows].astype(F32)

    def release(self, s, slot):
        @pl.when(self.end)
        def _():
            for c in range(CHUNKS):
                self.to_inner(s, c).wait_send()

        @pl.when(self.mid)
        def _():
            for c in range(CHUNKS):
                self.to_cross(s, c, slot).wait_send()
                self.to_outer(s, c, slot).wait_send()


def line_scratch(streams, rows, width):
    return [
        pltpu.VMEM((streams, rows, width), F32),
        pltpu.VMEM((streams, rows, width), BF),
        pltpu.VMEM((streams, rows, width), BF),
        pltpu.VMEM((2, streams, rows, width), BF),
        pltpu.VMEM((streams, rows, width), BF),
        pltpu.SemaphoreType.DMA((streams, CHUNKS)),
        pltpu.SemaphoreType.DMA((streams, CHUNKS)),
        pltpu.SemaphoreType.DMA((2, streams, CHUNKS)),
        pltpu.SemaphoreType.DMA((streams, CHUNKS)),
    ]


def tiles(rows, body, ready=None):
    def step(c, carry):
        if ready is not None:
            ready(c)
        body(pl.ds(pl.multiple_of(c * TILE, TILE), TILE))
        return carry

    lax.fori_loop(0, rows // TILE, step, 0)


def normalize(total, gain, shift):
    mean = jnp.mean(total, axis=-1, keepdims=True)
    centered = total - mean
    inverse = lax.rsqrt(jnp.mean(centered * centered, axis=-1, keepdims=True) + NORM_EPS)
    normed = centered * inverse
    return normed * gain + shift, normed, inverse


def head_masks(width, scale):
    lane = lax.broadcasted_iota(jnp.int32, (1, width), 1)
    return [
        jnp.where((lane >= h * HEAD_DIM) & (lane < (h + 1) * HEAD_DIM), scale, 0.0).astype(BF)
        for h in range(width // HEAD_DIM)
    ]


def forward_kernel(
    q_tok, q_drop, q_len, k_tok, k_drop, k_len,
    wqkv, abias, wm, mbias, we, ebias, ws, sbias, gains, shifts,
    acts, pooled, slots, *rest,
):
    kept, rest = rest[:11], rest[11:]
    saved, rest = rest[:11], rest[11:]
    loaded, rest = rest[:4], rest[4:]
    h, hb, qkv, pb, mx, inner, act, vbias, valid, vecs, save_sem, load_sem, *line_refs = rest
    xin, proj, probs, mixed, n1, i1, first, slope, active, n2, i2 = saved
    part = line_refs[0]
    stored = (wqkv, wm, we, ws)
    wqkv, wm, we, ws = loaded
    micro = q_tok.shape[0]
    rows, width = q_tok.shape[2:]
    layers = we.shape[1]
    local = wm.shape[2]
    heads = local // HEAD_DIM
    streams = 2 * micro
    last = 2 * layers * streams

    def load(k, e, layer):
        return pltpu.make_async_copy(stored[k].at[e, layer], loaded[k].at[e, layer], load_sem.at[k, e, layer])

    for layer in range(layers):
        for e in (1, 0):
            for k in range(4):
                load(k, e, layer).start()

    def save(k, layer, m):
        return pltpu.make_async_copy(saved[k].at[layer, m], kept[k].at[layer, m], save_sem.at[k, layer, m])

    for e in range(2):
        for layer in range(layers):
            for row, ref in enumerate((mbias, ebias, sbias)):
                vecs[e, layer, row : row + 1] = ref[e, layer : layer + 1].astype(F32)
            vecs[e, layer, 3:5] = gains[e, layer].astype(F32)
            vecs[e, layer, 5:7] = shifts[e, layer].astype(F32)
    greet_line()
    line = Line(*line_refs)

    def compact(tok, drop, length, slots_out, s, m):
        pos = lax.broadcasted_iota(jnp.int32, (1, rows), 1)
        kept = (pos < length) & ((drop[m] == 0) | (pos == 0))
        kept_f = jnp.broadcast_to(jnp.where(kept, 1.0, 0.0), (16, rows))
        down = lax.broadcasted_iota(jnp.int32, (rows, rows), 0)
        along = lax.broadcasted_iota(jnp.int32, (rows, rows), 1)
        tri = jnp.where(down <= along, 1.0, 0.0).astype(BF)
        order = nn(kept_f.astype(BF), tri)[0:1] - 1.0
        order = jnp.where(kept, order, -1.0)
        count = jnp.sum(kept_f[0:1], axis=-1, keepdims=True)
        pick = jnp.where(order == down.astype(F32), 1.0, 0.0).astype(BF)
        rows_now = nn(pick, tok[m, 0])
        h[s] = rows_now
        hb[...] = rows_now.astype(BF)
        fits = pos.astype(F32) < count
        vbias[s] = jnp.broadcast_to(jnp.where(fits, 0.0, MASKED), (8, rows))
        valid[s] = jnp.broadcast_to(jnp.where(fits, 1.0, 0.0), (8, rows))
        pooled[s, 1:2] = jnp.broadcast_to(count, (1, width))
        if slots_out:
            slots[m] = jnp.broadcast_to(order, (8, rows))

    def at(i):
        j = jnp.maximum(i, 0)
        return j % streams, (j // streams) % 2, (i >= 0) & (i < last)

    def tick(i, *which):
        for c in which:
            s, slot, live = at(i - 1)
            line.inward(s, c, slot, live)
            if c < LAG:
                s, slot, live = at(i - 2)
            line.outward(s, (c - LAG) % CHUNKS, slot, live)

    def attention_pass(layer, s):
        i = layer * 2 * streams + s
        e, m = 1 - s // micro, s % micro
        is_q = s >= micro
        tick(i, 0)

        @pl.when(layer == 0)
        def _():
            @pl.when(s < micro)
            def _():
                compact(k_tok, k_drop, k_len[m], False, s, m)

            @pl.when(is_q)
            def _():
                compact(q_tok, q_drop, q_len[m], True, s, m)

        @pl.when(layer > 0)
        def _():
            lp = layer - 1
            bias, gain, shift = vecs[e, lp, 2:3], vecs[e, lp, 4:5], vecs[e, lp, 6:7]

            def norm(r):
                out, normed, inverse = normalize(h[s, r] + part[s, r] + bias, gain, shift)
                h[s, r] = out
                hb[r] = out.astype(BF)

                @pl.when(is_q)
                def _():
                    n2[lp, m, r] = normed
                    i2[lp, m, r] = jnp.broadcast_to(inverse, (TILE, 128))

            tiles(rows, norm, lambda t: line.settle(s, 1, t))
            line.release(s, 1)

            @pl.when(is_q)
            def _():
                for k in (9, 10):
                    save(k, lp, m).start()

        tick(i, 1, 2)

        @pl.when((layer < layers) & (m == 0))
        def _():
            for k in (0, 1):
                load(k, e, layer).wait()

        @pl.when(layer < layers)
        def _():
            @pl.when(is_q)
            def _():
                xin[layer, m] = hb[...]
                save(0, layer, m).start()

            rows_now = hb[...]
            for j in range(3):
                bias = 0.0 if j == 1 else abias[e, layer, j // 2 : j // 2 + 1].astype(F32)
                qkv[j] = (nt(rows_now, wqkv[e, layer, j]) + bias).astype(BF)

            @pl.when(is_q)
            def _():
                for j in range(3):
                    proj[layer, m, j] = qkv[j]
                save(1, layer, m).start()

        tick(i, 3)
        q_masks = head_masks(local, HEAD_DIM**-0.5)
        v_masks = head_masks(local, 1.0)

        def one_head(hd):
            @pl.when(layer < layers)
            def _():
                scores = nt(qkv[0] * q_masks[hd], qkv[1]) + vbias[s, 0:1]
                expo = jnp.exp(scores - jnp.max(scores, axis=-1, keepdims=True))
                chance = (expo / jnp.sum(expo, axis=-1, keepdims=True)).astype(BF)
                pb[hd] = chance

                @pl.when(is_q)
                def _():
                    probs[layer, m, hd] = chance

                out = nn(chance, qkv[2] * v_masks[hd])
                if hd == 0:
                    mx[...] = out
                else:
                    mx[...] += out

        for hd in range(heads):
            one_head(hd)
            tick(i, 4 + hd)

        @pl.when(layer < layers)
        def _():
            mixed_now = mx[...].astype(BF)

            @pl.when(is_q)
            def _():
                mixed[layer, m] = mixed_now
                for k in (2, 3):
                    save(k, layer, m).start()

            part[s] = nn(mixed_now, wm[e, layer])
            line.begin(s)

        tick(i, *range(4 + heads, CHUNKS))

        @pl.when(layer == layers)
        def _():
            pooled[s, 0:1] = jnp.dot(valid[s], h[s], precision=TOP_PRECISION, preferred_element_type=F32)[0:1]

            @pl.when(is_q)
            def _():
                share = rows // lax.axis_size("tensor")
                start = pl.multiple_of(lax.axis_index("tensor") * share, 16)
                acts[m] = hb[pl.ds(start, share)]

    def forward_pass(layer, s):
        i = (layer * 2 + 1) * streams + s
        e, m = 1 - s // micro, s % micro
        is_q = s >= micro
        tick(i, 0, 1)
        bias, gain, shift = vecs[e, layer, 0:1], vecs[e, layer, 3:4], vecs[e, layer, 5:6]

        def norm(r):
            out, normed, inverse = normalize(h[s, r] + part[s, r] + bias, gain, shift)
            h[s, r] = out
            hb[r] = out.astype(BF)

            @pl.when(is_q)
            def _():
                n1[layer, m, r] = normed
                i1[layer, m, r] = jnp.broadcast_to(inverse, (TILE, 128))
                first[layer, m, r] = out.astype(BF)

        tiles(rows, norm, lambda t: line.settle(s, 0, t))
        line.release(s, 0)

        @pl.when(m == 0)
        def _():
            for k in (2, 3):
                load(k, e, layer).wait()

        @pl.when(is_q)
        def _():
            for k in (4, 5, 6):
                save(k, layer, m).start()

        tick(i, 2, 3)
        inner[...] = nn(hb[...], we[e, layer])
        tick(i, 4)
        bias_e = vecs[e, layer, 1:2]

        def gelu(r):
            u = inner[r] + bias_e
            phi = 0.5 * (1.0 + lax.erf(u * ROOT_HALF))
            out = (u * phi).astype(BF)
            act[r] = out

            @pl.when(is_q)
            def _():
                active[layer, m, r] = out
                slope[layer, m, r] = phi + u * jnp.exp(-0.5 * u * u) * INV_ROOT_TAU

        tiles(rows, gelu)

        @pl.when(is_q)
        def _():
            for k in (7, 8):
                save(k, layer, m).start()

        tick(i, 5, 6)
        part[s] = nn(act[...], ws[e, layer])
        line.begin(s)
        tick(i, 7)

    def layer_step(layer, carry):
        def a_step(s, c):
            attention_pass(layer, s)
            return c

        lax.fori_loop(0, streams, a_step, 0)

        @pl.when(layer < layers)
        def _():
            def f_step(s, c):
                forward_pass(layer, s)
                return c

            lax.fori_loop(0, streams, f_step, 0)

        return carry

    lax.fori_loop(0, layers + 1, layer_step, 0)

    def drain(j, carry):
        for k in range(len(saved)):
            save(k, j // micro, j % micro).wait()
        return carry

    lax.fori_loop(0, layers * micro, drain, 0)


def run_forward(q_tok, q_drop, q_len, k_tok, k_drop, k_len, weights):
    micro, _, rows, width = q_tok.shape
    wqkv, abias, wm, mbias, we, ebias, ws, sbias, gains, shifts = weights
    layers, local, units = we.shape[1], wm.shape[2], we.shape[3]
    heads = local // HEAD_DIM
    streams = 2 * micro
    lm = (layers, micro)
    shapes = [
        ((micro, rows // lax.axis_size("tensor"), width), BF),
        ((streams, 8, width), F32),
        ((micro, 8, rows), F32),
        (lm + (rows, width), BF),
        (lm + (3, rows, local), BF),
        (lm + (heads, rows, rows), BF),
        (lm + (rows, local), BF),
        (lm + (rows, width), F32),
        (lm + (rows, 128), F32),
        (lm + (rows, width), BF),
        (lm + (rows, units), F32),
        (lm + (rows, units), BF),
        (lm + (rows, width), F32),
        (lm + (rows, 128), F32),
    ]
    vm = pl.BlockSpec(memory_space=pltpu.VMEM)
    hb = pl.BlockSpec(memory_space=pl.ANY)
    sm = pl.BlockSpec(memory_space=pltpu.SMEM)
    return pl.pallas_call(
        forward_kernel,
        out_shape=[jax.ShapeDtypeStruct(*s) for s in shapes],
        in_specs=[vm, vm, sm, vm, vm, sm] + [hb, vm, hb, vm, hb, vm, hb, vm, vm, vm],
        out_specs=[vm] * 3 + [hb] * 11,
        scratch_shapes=[pltpu.VMEM(*s) for s in shapes[3:]]
        + [pltpu.VMEM(w.shape, BF) for w in (wqkv, wm, we, ws)]
        + [
            pltpu.VMEM((streams, rows, width), F32),
            pltpu.VMEM((rows, width), BF),
            pltpu.VMEM((3, rows, local), BF),
            pltpu.VMEM((heads, rows, rows), BF),
            pltpu.VMEM((rows, local), F32),
            pltpu.VMEM((rows, units), F32),
            pltpu.VMEM((rows, units), BF),
            pltpu.VMEM((streams, 8, rows), F32),
            pltpu.VMEM((streams, 8, rows), F32),
            pltpu.VMEM((2, layers, 8, width), F32),
            pltpu.SemaphoreType.DMA((11,) + lm),
            pltpu.SemaphoreType.DMA((4, 2, layers)),
        ]
        + line_scratch(streams, rows, width),
        compiler_params=pltpu.CompilerParams(
            collective_id=0, has_side_effects=True, vmem_limit_bytes=VMEM_LIMIT
        ),
        name="encoders_forward",
    )(q_tok, q_drop, q_len, k_tok, k_drop, k_len, *weights)


def norm_back(g, normed, inverse, gain):
    scaled = g * gain
    return inverse * (
        scaled
        - jnp.mean(scaled, axis=-1, keepdims=True)
        - normed * jnp.mean(scaled * normed, axis=-1, keepdims=True)
    )


def fold(x):
    return jnp.sum(x.reshape(x.shape[0] // 8, 8, x.shape[1]), axis=0)


class Plane:
    def __init__(self, grads, sends, recvs, out, send_sem, recv_sem, credit):
        dp, self.x = lax.axis_index("dp"), lax.axis_index("rep")
        self.y, self.c = dp // 2, dp % 2
        self.partner = {
            "c": {"dp": dp + 1 - 2 * self.c},
            "x": {"rep": 1 - self.x},
            "y": {"dp": (dp + 2) % 4},
        }
        self.grads, self.sends, self.recvs, self.out = grads, sends, recvs, out
        self.send_sem, self.recv_sem, self.credit = send_sem, recv_sem, credit
        self.block = grads.shape[2] // 8

    def copy(self, u, stage, half):
        way = ("c", "xy"[half], "yx"[half])[stage]
        return pltpu.make_async_remote_copy(
            src_ref=self.sends[stage].at[u, half], dst_ref=self.recvs[stage].at[u, half],
            send_sem=self.send_sem.at[u, stage, half], recv_sem=self.recv_sem.at[u, stage, half],
            device_id=self.partner[way], device_id_type=MESH)

    def spots(self, stage, half, own):
        pick = (lambda v: v) if own else (lambda v: 1 - v)
        if stage == 0:
            return [(4 * y + 2 * pick(self.c), 2 * y, 2) for y in (0, 1)]
        if stage == 1 and half == 0:
            return [(4 * y + 2 * self.c + pick(self.x), y, 1) for y in (0, 1)]
        if stage == 1:
            return [(4 * pick(self.y) + 2 * self.c, 0, 2)]
        if half == 0:
            return [(4 * pick(self.y) + 2 * self.c + self.x, 0, 1)]
        return [(4 * self.y + 2 * self.c + pick(self.x), 0, 1)]

    def parts(self, stage, half, own):
        for here, there, blocks in self.spots(stage, half, own):
            for b in range(blocks):
                start = (here + b) * self.block
                yield pl.ds(pl.multiple_of(start, 8), self.block), pl.ds((there + b) * self.block, self.block)

    def send(self, u, stage, live, spend):
        @pl.when(live)
        def _():
            for half in (0, 1):
                for here, there in self.parts(stage, half, False):
                    self.sends[stage][u, half, there] = self.grads[u, half, here].astype(BF)

            @pl.when(spend)
            def _():
                pl.semaphore_wait(self.credit.at[u, stage], 2)

            for half in (0, 1):
                self.copy(u, stage, half).start()

    def take(self, u, stage, live, give, layer):
        @pl.when(live)
        def _():
            for half in (0, 1):
                self.copy(u, stage, half).wait()
                for here, there in self.parts(stage, half, True):
                    total = self.grads[u, half, here] + self.recvs[stage][u, half, there].astype(F32)
                    if stage == 2:
                        self.out[layer, u, half] = total
                    else:
                        self.grads[u, half, here] = total

            @pl.when(give)
            def _():
                for half in (0, 1):
                    way = ("c", "xy"[half], "yx"[half])[stage]
                    pl.semaphore_signal(
                        self.credit.at[u, stage], inc=1, device_id=self.partner[way], device_id_type=MESH
                    )


def greet_all():
    z, dp, rep = lax.axis_index("tensor"), lax.axis_index("dp"), lax.axis_index("rep")
    sem = pltpu.get_barrier_semaphore()
    others = [{"tensor": (z + d) % 4} for d in (1, 2, 3)]
    others += [{"rep": 1 - rep, "tensor": (z + d) % 4} for d in (0, 1, 2, 3)]
    others += [{"dp": dp + 1 - 2 * (dp % 2)}, {"dp": (dp + 2) % 4}]
    for other in others:
        pl.semaphore_signal(sem, inc=1, device_id=other, device_id_type=MESH)
    pl.semaphore_wait(sem, len(others))


def backward_kernel(inside, *refs):
    seed, slots, negs, gains, *rest = refs
    kept, rest = rest[:11], rest[11:]
    stored, rest = rest[:4], rest[4:]
    g_in, vec, out_big, out_small, *rest = rest
    saved, rest = rest[:11], rest[11:]
    loaded, rest = rest[:4], rest[4:]
    g_vec, g_abias, dr, low, dinner, tmp, dqkv, dsc, pgrad, load_sem, *rest = rest
    line_refs, rest = rest[:9], rest[9:]
    xin, proj, probs, mixed, n1, i1, first, slope, active, n2, i2 = saved
    wqkv, wm, we, ws = loaded
    part = line_refs[0]
    layers, micro, rows, width = xin.shape
    local = wm.shape[1]
    half_units = we.shape[2] // 2
    heads = local // HEAD_DIM
    streams = micro
    last = 2 * layers * streams
    order = (9, 10, 7, 8, 6, 4, 5, 3, 2, 1, 0)

    def load_saved(k, layer):
        return pltpu.make_async_copy(kept[k].at[layer], saved[k].at[layer], load_sem.at[k, layer])

    def load_weight(k, layer):
        return pltpu.make_async_copy(stored[k].at[0, layer], loaded[k].at[layer], load_sem.at[11 + k, layer])

    for layer in reversed(range(layers)):
        for k in order[:2]:
            load_saved(k, layer).start()
        for k in (3, 2):
            load_weight(k, layer).start()
        for k in order[2:]:
            load_saved(k, layer).start()
        for k in (1, 0):
            load_weight(k, layer).start()
    g_vec[...] = jnp.zeros_like(g_vec)
    g_abias[...] = jnp.zeros_like(g_abias)
    vec[...] = jnp.zeros_like(vec)
    if inside:
        (g_big, g_small, b1, b2, b3, e1, e2, e3, s1, s2, s3, t1, t2, t3, big_s, big_r, small_s, small_r,
         big_c, small_c, v_rcv, v_send, v_recv, ask, asked, reply, heard, ask_sem, reply_sem, heard_sem) = rest
        greet_all()
        big = Plane(g_big, (b1, b2, b3), (e1, e2, e3), out_big, big_s, big_r, big_c)
        small = Plane(g_small, (s1, s2, s3), (t1, t2, t3), out_small, small_s, small_r, small_c)
        contrast_inside(seed, negs, pgrad, vec, ask, asked, reply, heard, ask_sem, reply_sem, heard_sem)
    else:
        greet_line()
        pgrad[...] = seed[...]
    line = Line(*line_refs)

    def at(j):
        return jnp.maximum(j, 0) % streams, (jnp.maximum(j, 0) // streams) % 2, (j >= 0) & (j < last)

    def tick(i, *which):
        for g in which:
            s, slot, live = at(i - 1)
            if g >= 1 and g - 1 < CHUNKS:
                line.outward(s, g - 1, slot, live)
            c = g + EARLY
            if c >= CHUNKS + 1:
                s, slot, live = at(i)
                c -= CHUNKS + 1
                if c < EARLY:
                    line.inward(s, c, slot, live)
            elif c < CHUNKS:
                line.inward(s, c, slot, live)

    def add_to(large, u, half, layer, s, value):
        if inside:
            ref = (g_big if large else g_small).at[u, half]
        else:
            ref = (out_big if large else out_small).at[layer, u, half]

        @pl.when(s == 0)
        def _():
            ref[...] = value

        @pl.when(s > 0)
        def _():
            ref[...] += value

    def plane(what, large, stage, live, step):
        if inside:
            group = big if large else small
            for u in (0, 1):
                if what == "send":
                    group.send(u, stage, live, step > 0)
                else:
                    group.take(u, stage, live, step < layers - 1, layers - 1 - step)

    def mlp_back(step, s):
        layer = layers - 1 - step
        i = step * 2 * streams + s

        @pl.when(s == 0)
        def _():
            for k in (4, 6, 7, 8, 9, 10):
                load_saved(k, layer).wait()
            for k in (2, 3):
                load_weight(k, layer).wait()

        @pl.when(step == 0)
        def _():
            def begin(c, carry):
                r = pl.ds(pl.multiple_of(c * TILE, TILE), TILE)
                pos = (lax.broadcasted_iota(jnp.int32, (TILE, 1), 0) + c * TILE).astype(F32)
                part[s, r] = jnp.where(pos < pgrad[s, 1:2, 0:1], pgrad[s, 0:1], 0.0)
                dr[s, r] = jnp.zeros((TILE, width), F32)
                return carry

            lax.fori_loop(0, rows // TILE, begin, 0)

        gain = gains[0, layer, 1:2].astype(F32)

        def back(r):
            g = part[s, r] + dr[s, r]
            normed = n2[layer, s, r]
            out = norm_back(g, normed, i2[layer, s, r][:, 0:1], gain)
            dr[s, r] = out
            low[s, r] = out.astype(BF)
            g_vec[layer, 1] += fold(g * normed)
            g_vec[layer, 3] += fold(g)
            g_vec[layer, 4] += fold(out)

        def ready(t):
            @pl.when(step > 0)
            def _():
                line.settle(s, 1, t)

        tiles(rows, back, ready)

        @pl.when(step > 0)
        def _():
            line.release(s, 1)

        tick(i, 0)
        tmp[...] = nt(low[s], ws[layer])
        tick(i, 1)

        def slopes(r):
            out = tmp[r] * slope[layer, s, r]
            dinner[r] = out.astype(BF)
            g_vec[layer, 6] += fold(out)

        tiles(rows, slopes)
        tick(i, 2)
        part[s] = nt(dinner[...], we[layer])
        line.begin(s)
        tick(i, 3)
        plane("take", True, 2, (step > 0) & (s == 0), step - 1)
        plane("take", False, 0, (step > 0) & (s == 0), step - 1)
        plane("send", False, 1, (step > 0) & (s == 0), step - 1)
        for half in (0, 1):
            cols = pl.ds(half * half_units, half_units)
            add_to(True, 0, half, layer, s, tn(low[s], active[layer, s, :, cols]))
            tick(i, 4 + half)
        for half in (0, 1):
            cols = pl.ds(half * half_units, half_units)
            add_to(True, 1, half, layer, s, tn(first[layer, s], dinner[:, cols]))
            tick(i, 6 + half)
        plane("send", True, 0, s == streams - 1, step)
        plane("take", False, 1, (step > 0) & (s == streams - 1), step - 1)
        plane("send", False, 2, (step > 0) & (s == streams - 1), step - 1)
        tick(i, CHUNKS)

    def attention_back(step, s):
        layer = layers - 1 - step
        i = (step * 2 + 1) * streams + s

        @pl.when(s == 0)
        def _():
            for k in (0, 1, 2, 3, 5):
                load_saved(k, layer).wait()
            for k in (0, 1):
                load_weight(k, layer).wait()

        gain = gains[0, layer, 0:1].astype(F32)

        def back(r):
            g = part[s, r] + dr[s, r]
            normed = n1[layer, s, r]
            out = norm_back(g, normed, i1[layer, s, r][:, 0:1], gain)
            dr[s, r] = out
            low[s, r] = out.astype(BF)
            g_vec[layer, 0] += fold(g * normed)
            g_vec[layer, 2] += fold(g)
            g_vec[layer, 5] += fold(out)

        tiles(rows, back, lambda t: line.settle(s, 0, t))
        line.release(s, 0)
        tick(i, 0)
        dmix = nt(low[s], wm[layer]).astype(BF)
        tick(i, 1)
        masks = head_masks(local, 1.0)
        for hd in range(heads):
            chance_b = probs[layer, s, hd]
            chance = chance_b.astype(F32)
            dm = dmix * masks[hd]
            dch = nt(dm, proj[layer, s, 2])
            ds = chance * (dch - jnp.sum(chance * dch, axis=-1, keepdims=True))
            draw = (ds * HEAD_DIM**-0.5).astype(BF)
            dq = nn(draw, proj[layer, s, 1] * masks[hd])
            dk = tn(draw, proj[layer, s, 0] * masks[hd])
            dv = tn(chance_b, dm)
            if hd == 0:
                dqkv[0] = dq
                dqkv[1] = dk
                dqkv[2] = dv
            else:
                dqkv[0] += dq
                dqkv[1] += dk
                dqkv[2] += dv
            tick(i, 2 + hd)
        g_abias[layer, 0] += fold(dqkv[0])
        g_abias[layer, 1] += fold(dqkv[2])
        for j in range(3):
            dsc[j] = dqkv[j].astype(BF)
        part[s] = nn(dsc[0], wqkv[layer, 0]) + nn(dsc[1], wqkv[layer, 1]) + nn(dsc[2], wqkv[layer, 2])
        line.begin(s)
        tick(i, *range(2 + heads, 6))
        plane("take", True, 0, s == 0, step)
        plane("send", True, 1, s == 0, step)
        plane("take", True, 1, s == streams - 1, step)
        plane("send", True, 2, s == streams - 1, step)
        plane("take", False, 2, (step > 0) & (s == 0), step - 1)
        for j in range(3):
            add_to(False, j // 2, j % 2, layer, s, tn(xin[layer, s], dsc[j]))
        tick(i, 6)
        add_to(False, 1, 1, layer, s, tn(low[s], mixed[layer, s]))
        tick(i, 7, CHUNKS)
        plane("send", False, 0, s == streams - 1, step)

    def layer_step(step, carry):
        def m_step(s, c):
            mlp_back(step, s)
            return c

        def a_step(s, c):
            attention_back(step, s)
            return c

        lax.fori_loop(0, streams, m_step, 0)
        lax.fori_loop(0, streams, a_step, 0)
        return carry

    lax.fori_loop(0, layers, layer_step, 0)

    for layer in range(layers):
        for k in range(7):
            vec[layer * 7 + k : layer * 7 + k + 1] = jnp.sum(g_vec[layer, k], axis=0, keepdims=True)
        for k in range(2):
            row = layers * 7 + layer * 2 + k
            vec[row : row + 1, 0:local] = jnp.sum(g_abias[layer, k], axis=0, keepdims=True)

    def vec_copy(stage):
        return pltpu.make_async_remote_copy(
            src_ref=vec, dst_ref=v_rcv.at[stage], send_sem=v_send.at[stage], recv_sem=v_recv.at[stage],
            device_id=big.partner["cxy"[stage]], device_id_type=MESH)

    def vec_take(stage):
        if inside:
            vec_copy(stage).wait()
            vec[...] += v_rcv[stage]

    def vec_send(stage):
        if inside:
            vec_copy(stage).start()

    end = layers - 1
    vec_send(0)
    tick(last, 0, 1)
    plane("take", False, 0, True, end)
    plane("send", False, 1, True, end)
    vec_take(0)
    vec_send(1)
    tick(last, 2, 3, 4)
    plane("take", True, 2, True, end)
    tick(last, 5, 6)
    plane("take", False, 1, True, end)
    plane("send", False, 2, True, end)
    vec_take(1)
    vec_send(2)
    tick(last, 7, CHUNKS)

    def tail(s, carry):
        def back(r):
            low[s, r] = (part[s, r] + dr[s, r]).astype(BF)

        tiles(rows, back, lambda t: line.settle(s, 1, t))
        line.release(s, 1)
        down = lax.broadcasted_iota(jnp.int32, (rows, rows), 0).astype(F32)
        pick = jnp.where(slots[s, 0:1] == down, 1.0, 0.0).astype(BF)
        low[s] = tn(pick, low[s]).astype(BF)
        share = rows // lax.axis_size("tensor")
        start = pl.multiple_of(lax.axis_index("tensor") * share, 16)
        g_in[s] = low[s, pl.ds(start, share)]
        return carry

    lax.fori_loop(0, streams, tail, 0)
    plane("take", False, 2, True, end)
    vec_take(2)


def run_backward(inside, seed, slots, negatives, saved, weights):
    wqkv, abias, wm, mbias, we, ebias, ws, sbias, gains, shifts = weights
    layers, micro, rows, width = saved[0].shape
    local, units = wm.shape[2], we.shape[3]
    tall = 8 * ((9 * layers + 2 + 7) // 8)
    kinds = ((units // 2, "big"), (local, "small"))
    high = width // 8 if inside else width
    shapes = [((micro, rows // lax.axis_size("tensor"), width), BF), ((tall, width), F32)]
    shapes += [((layers, 2, 2, high, w), F32) for w, _ in kinds]
    vm = pl.BlockSpec(memory_space=pltpu.VMEM)
    hb = pl.BlockSpec(memory_space=pl.ANY)
    dma = pltpu.SemaphoreType.DMA
    scratch = [pltpu.VMEM(v.shape, v.dtype) for v in saved]
    scratch += [pltpu.VMEM(w.shape[1:], BF) for w in (wqkv, wm, we, ws)]
    scratch += [
        pltpu.VMEM((layers, 7, 8, width), F32),
        pltpu.VMEM((layers, 2, 8, local), F32),
        pltpu.VMEM((micro, rows, width), F32),
        pltpu.VMEM((micro, rows, width), BF),
        pltpu.VMEM((rows, units), BF),
        pltpu.VMEM((rows, units), F32),
        pltpu.VMEM((3, rows, local), F32),
        pltpu.VMEM((3, rows, local), BF),
        pltpu.VMEM((micro, 8, width), F32),
        dma((15, layers)),
    ]
    scratch += line_scratch(micro, rows, width)
    if inside:
        scratch += [pltpu.VMEM((2, 2, width, w), F32) for w, _ in kinds]
        for w, _ in kinds:
            for _ in range(2):
                scratch += [pltpu.VMEM((2, 2, width // n, w), BF) for n in (2, 4, 8)]
        scratch += [dma((2, 3, 2))] * 4
        scratch += [pltpu.SemaphoreType.REGULAR((2, 3))] * 2
        scratch += [pltpu.VMEM((3, tall, width), F32), dma((3,)), dma((3,))]
        scratch += [
            pltpu.VMEM((16, width), BF),
            pltpu.VMEM((16, width), BF),
            pltpu.VMEM((2, 8, width), F32),
            pltpu.VMEM((8, 8, width), F32),
            dma((2,)),
            dma((8,)),
            dma((8,)),
        ]
    return pl.pallas_call(
        functools.partial(backward_kernel, inside),
        out_shape=[jax.ShapeDtypeStruct(*s) for s in shapes],
        in_specs=[vm] * 4 + [hb] * 15,
        out_specs=[vm] * len(shapes),
        scratch_shapes=scratch,
        compiler_params=pltpu.CompilerParams(
            collective_id=1, has_side_effects=True, vmem_limit_bytes=VMEM_LIMIT
        ),
        name="encoder_backward",
    )(seed, slots, negatives, gains, *saved, wqkv, wm, we, ws)


def contrast_inside(pooled, negs, pgrad, vec, ask, asked, reply, heard, ask_sem, reply_sem, heard_sem):
    z, rep = lax.axis_index("tensor"), lax.axis_index("rep")
    micro = pgrad.shape[0]
    width = negs.shape[1]
    scales, counts, dirs, key_dirs, positives = [], [], [], [], []
    ask[...] = jnp.zeros_like(ask)
    for m in range(micro):
        count = pooled[micro + m, 1:2]
        mean_q = pooled[micro + m, 0:1] / count
        mean_k = pooled[m, 0:1] / pooled[m, 1:2]
        scale = lax.rsqrt(jnp.sum(mean_q * mean_q, axis=-1, keepdims=True) + UNIT_EPS)
        key_dir = mean_k * lax.rsqrt(jnp.sum(mean_k * mean_k, axis=-1, keepdims=True) + UNIT_EPS)
        direction = mean_q * scale
        ask[m : m + 1] = direction.astype(BF)
        positives.append(jnp.sum(direction * key_dir, axis=-1, keepdims=True) / SOFTMAX_WARMTH)
        scales.append(scale)
        counts.append(count)
        dirs.append(direction)
        key_dirs.append(key_dir)
    question = pltpu.make_async_remote_copy(
        src_ref=ask, dst_ref=asked, send_sem=ask_sem.at[0], recv_sem=ask_sem.at[1],
        device_id={"rep": 1 - rep}, device_id_type=MESH)
    question.start()

    def answer(which, rows_now):
        logits = nt(rows_now, negs[...]) / SOFTMAX_WARMTH
        top = jnp.max(logits, axis=-1, keepdims=True)
        expo = jnp.exp(logits - top)
        total = jnp.sum(expo, axis=-1, keepdims=True)
        high = expo.astype(BF)
        rest = expo - high.astype(F32)
        mid = rest.astype(BF)
        tiny = (rest - mid.astype(F32)).astype(BF)
        keys = nn(high, negs[...]) + nn(mid, negs[...]) + nn(tiny, negs[...])
        reply[which, 0:micro] = keys[0:micro]
        reply[which, micro : 2 * micro] = jnp.broadcast_to(top[0:micro], (micro, width))
        reply[which, 2 * micro : 3 * micro] = jnp.broadcast_to(total[0:micro], (micro, width))

    def tell(which, d):
        other = {"tensor": (z + d) % 4} if which == 0 else {"rep": 1 - rep, "tensor": (z + d) % 4}
        k = which * 4 + d
        return pltpu.make_async_remote_copy(
            src_ref=reply.at[which], dst_ref=heard.at[k], send_sem=reply_sem.at[k], recv_sem=heard_sem.at[k],
            device_id=other, device_id_type=MESH)

    answer(0, ask[...])
    for d in (1, 2, 3):
        tell(0, d).start()
    question.wait()
    answer(1, asked[...])
    for d in (0, 1, 2, 3):
        tell(1, d).start()
    for k in range(1, 8):
        tell(k // 4, k % 4).wait()
    everyone = [reply[0]] + [heard[k] for k in range(1, 8)]
    loss = 0.0
    for m in range(micro):
        positive = positives[m]
        best = positive
        for one in everyone:
            best = jnp.maximum(best, one[micro + m : micro + m + 1, 0:1])
        own = jnp.exp(positive - best)
        total, keys = own, own * key_dirs[m]
        for one in everyone:
            weight = jnp.exp(one[micro + m : micro + m + 1, 0:1] - best)
            total = total + weight * one[2 * micro + m : 2 * micro + m + 1, 0:1]
            keys = keys + weight * one[m : m + 1]
        loss = loss + best + jnp.log(total) - positive
        dqn = (keys / total - key_dirs[m]) * (CROP_SLOTS / SOFTMAX_WARMTH)
        mean_grad = scales[m] * (dqn - dirs[m] * jnp.sum(dirs[m] * dqn, axis=-1, keepdims=True))
        pgrad[m, 0:1] = mean_grad / counts[m]
        pgrad[m, 1:2] = counts[m]
    vec[vec.shape[0] - 1 : vec.shape[0]] = jnp.broadcast_to(loss, (1, width))


def outputs_kernel(layers, size, acts, g_in, vec, big, small, o_acts, o_in, o_attend, o_abias, o_merge, o_mbias,
                   o_expand, o_ebias, o_shrink, o_sbias, o_gain, o_shift, o_loss):
    width = vec.shape[1]
    local = small.shape[4]
    half = big.shape[4]
    group = lax.axis_index("dp") * lax.axis_size("rep") + lax.axis_index("rep")
    blocks = width // size
    own = pltpu.roll(vec[...], ((blocks - group) % blocks) * size, axis=1)[:, :size]
    o_acts[:, 0] = acts[...]
    o_in[:, 0] = g_in[...]
    for l in range(layers):
        for h in (0, 1):
            cols = slice(h * half, (h + 1) * half)
            o_shrink[l, :, cols] = big[l, 0, h]
            o_expand[l, :, cols] = big[l, 1, h]
        for j in range(3):
            o_attend[l, j] = small[l, j // 2, j % 2]
        o_merge[l] = small[l, 1, 1].T
        row = 7 * l
        o_gain[l] = own[row : row + 2]
        o_shift[l] = own[row + 2 : row + 4]
        o_sbias[l : l + 1] = own[row + 4 : row + 5]
        o_mbias[l : l + 1] = own[row + 5 : row + 6]
        o_ebias[l : l + 1] = vec[row + 6 : row + 7]
        o_abias[l] = vec[7 * layers + 2 * l : 7 * layers + 2 * l + 2, :local]
    o_loss[...] = vec[vec.shape[0] - 1 :, 0:1]


def run_outputs(acts, g_in, vec, big, small):
    micro, share, width = acts.shape
    layers, _, _, size, half = big.shape
    local = small.shape[4]
    shapes = [
        ((micro, 1, share, width), BF),
        ((micro, 1, share, width), BF),
        ((layers, 3, size, local), F32),
        ((layers, 2, local), F32),
        ((layers, local, size), F32),
        ((layers, size), F32),
        ((layers, size, 2 * half), F32),
        ((layers, width), F32),
        ((layers, size, 2 * half), F32),
        ((layers, size), F32),
        ((layers, 2, size), F32),
        ((layers, 2, size), F32),
        ((1, 1), F32),
    ]
    vm = pl.BlockSpec(memory_space=pltpu.VMEM)
    return pl.pallas_call(
        functools.partial(outputs_kernel, layers, size),
        out_shape=[jax.ShapeDtypeStruct(*s) for s in shapes],
        in_specs=[vm] * 5,
        out_specs=[vm] * len(shapes),
        compiler_params=pltpu.CompilerParams(vmem_limit_bytes=VMEM_LIMIT),
        name="outputs",
    )(acts, g_in, vec, big, small)


def contrast(mean_q, mean_k, negatives):
    key_dir = mean_k * lax.rsqrt(jnp.sum(mean_k * mean_k, axis=-1, keepdims=True) + UNIT_EPS)
    scale = lax.rsqrt(jnp.sum(mean_q * mean_q, axis=-1, keepdims=True) + UNIT_EPS)
    direction = mean_q * scale
    positive = jnp.sum(direction * key_dir, axis=-1) / SOFTMAX_WARMTH
    micro, width = mean_q.shape
    asked = lax.all_gather(direction.astype(BF), "rep", axis=0, tiled=True)
    logits = nt(asked, negatives) / SOFTMAX_WARMTH
    top = jnp.max(logits, axis=-1, keepdims=True)
    expo = jnp.exp(logits - top)
    total = jnp.sum(expo, axis=-1, keepdims=True)
    keys = jnp.dot(expo, negatives.astype(F32), precision=TOP_PRECISION)
    packed = jnp.concatenate([keys, jnp.broadcast_to(top, (top.shape[0], 128)), jnp.broadcast_to(total, (top.shape[0], 128))], axis=1)
    pieces = lax.all_gather(packed, ("rep", "tensor"), axis=0, tiled=False)
    mine = lax.dynamic_slice_in_dim(pieces, lax.axis_index("rep") * micro, micro, 1)
    keys, top, total = mine[..., :width], mine[..., width], mine[..., width + 128]
    best = jnp.maximum(jnp.max(top, axis=0), positive)
    weight = jnp.exp(top - best)
    own = jnp.exp(positive - best)
    total = jnp.sum(total * weight, axis=0) + own
    keys = jnp.sum(keys * weight[..., None], axis=0) + own[:, None] * key_dir
    per_query = best + jnp.log(total) - positive
    dqn = (keys / total[:, None] - key_dir) * (CROP_SLOTS / SOFTMAX_WARMTH)
    mean_grad = scale * (dqn - direction * jnp.sum(direction * dqn, axis=-1, keepdims=True))
    return per_query, mean_grad


def per_device(
    query_tokens, query_drop, query_length, key_tokens, key_drop, key_length, negatives,
    attend_weight, attend_bias, merge_weight, merge_bias, expand_weight, expand_bias,
    shrink_weight, shrink_bias, norm_gain, norm_shift,
):
    micro, _, rows, width = query_tokens.shape
    weights = (
        jnp.transpose(attend_weight, (0, 1, 3, 4, 2)),
        attend_bias,
        merge_weight,
        merge_bias,
        expand_weight,
        expand_bias,
        shrink_weight,
        shrink_bias,
        norm_gain,
        norm_shift,
    )
    acts, pooled, slots, *saved = run_forward(
        query_tokens, query_drop, query_length.reshape(micro), key_tokens, key_drop, key_length.reshape(micro), weights
    )
    groups = ("dp", "rep")
    inside = lax.axis_size("dp") == 4 and lax.axis_size("rep") == 2
    if inside:
        g_in, vec, g_big, g_small = run_backward(inside, pooled, slots, negatives, saved, weights)
    else:
        counts = pooled[:, 1]
        means = pooled[:, 0] / counts
        per_query, mean_grad = contrast(means[micro:], means[:micro], negatives)
        pgrad = jnp.concatenate(
            [(mean_grad / counts[micro:])[:, None], counts[micro:, None], jnp.zeros((micro, 6, width), F32)], axis=1
        )
        g_in, vec, g_big, g_small = run_backward(inside, pgrad, slots, negatives, saved, weights)
        g_big = lax.psum_scatter(g_big, groups, scatter_dimension=3, tiled=True)
        g_small = lax.psum_scatter(g_small, groups, scatter_dimension=3, tiled=True)
        vec = lax.psum(vec.at[-1].add(jnp.sum(per_query)), groups)
    outs = run_outputs(acts, g_in, vec, g_big, g_small)
    loss = outs[12].reshape(()) / (micro * lax.axis_size("dp") * lax.axis_size("rep"))
    return (
        outs[0], outs[1], jnp.transpose(outs[2], (0, 2, 1, 3)), *outs[3:8],
        jnp.transpose(outs[8], (0, 2, 1)), *outs[9:12], loss,
    )


def solution(mesh):
    return jax.shard_map(
        per_device,
        mesh=mesh,
        in_specs=(
            P(None, ("dp", "rep"), None, None),
            P(None, ("dp", "rep"), None),
            P(None, ("dp", "rep")),
            P(None, ("dp", "rep"), None, None),
            P(None, ("dp", "rep"), None),
            P(None, ("dp", "rep")),
            P(("rep", "tensor"), None),
            P(None, None, None, None, "tensor"),
            P(None, None, None, "tensor"),
            P(None, None, "tensor", None),
            P(),
            P(None, None, None, "tensor"),
            P(None, None, "tensor"),
            P(None, None, "tensor", None),
            P(),
            P(),
            P(),
        ),
        out_specs=(
            P(None, ("dp", "rep"), "tensor", None),
            P(None, ("dp", "rep"), "tensor", None),
            P(None, ("dp", "rep"), None, "tensor"),
            P(None, None, "tensor"),
            P(None, "tensor", ("dp", "rep")),
            P(None, ("dp", "rep")),
            P(None, ("dp", "rep"), "tensor"),
            P(None, "tensor"),
            P(None, "tensor", ("dp", "rep")),
            P(None, ("dp", "rep")),
            P(None, None, ("dp", "rep")),
            P(None, None, ("dp", "rep")),
            P(),
        ),
        check_vma=False,
    )
```

```python
import functools

import jax
import jax.numpy as jnp
from jax import lax
from jax.experimental import pallas as pl
from jax.experimental.pallas import tpu as pltpu
from jax.sharding import PartitionSpec as P

HEAD_DIM = 64
CROP_SLOTS = 256
SOFTMAX_WARMTH = 0.05
NORM_EPS = 1e-12
UNIT_EPS = 1e-06
MASKED = -1e30
TOP_PRECISION = lax.Precision.HIGHEST
ROOT_HALF = 0.7071067811865476
INV_ROOT_TAU = 0.3989422804014327

MESH = pl.DeviceIdType.MESH
BF = jnp.bfloat16
F32 = jnp.float32
CHUNKS = 8
LAG = 5
EARLY = 3
TILE = 64
VMEM_LIMIT = 62 * 1024 * 1024


def nn(a, b):
    return jnp.dot(a, b, preferred_element_type=F32)


def nt(a, b):
    return lax.dot_general(a, b, (((1,), (1,)), ((), ())), preferred_element_type=F32)


def tn(a, b):
    return lax.dot_general(a, b, (((0,), (0,)), ((), ())), preferred_element_type=F32)


class Line:
    def __init__(self, part, sbuf, tbuf, x1, x2, s_sem, t_sem, r1, r2):
        z = lax.axis_index("tensor")
        self.mid = (z + 1) // 2 == 1
        self.end = (z + 1) // 2 != 1
        self.lower = z // 2 == 0
        self.inner = 1 + z // 2
        self.outer = 3 * (z // 2)
        self.cross = 3 - z
        self.part, self.sbuf, self.tbuf, self.x1, self.x2 = part, sbuf, tbuf, x1, x2
        self.s_sem, self.t_sem, self.r1, self.r2 = s_sem, t_sem, r1, r2
        self.size = part.shape[1] // CHUNKS

    def rows(self, c):
        return pl.ds(pl.multiple_of(c * self.size, self.size), self.size)

    def near(self, c):
        return (c < CHUNKS // 2) == self.lower

    def outbound(self, c, narrow):
        return (c >= 0) if narrow is False else jnp.logical_not(narrow & self.near(c))

    def homebound(self, c, narrow):
        return (c >= 0) if narrow is False else jnp.logical_not(narrow) | self.near(c)

    def to_inner(self, s, c):
        return pltpu.make_async_remote_copy(
            src_ref=self.sbuf.at[s, self.rows(c)], dst_ref=self.x2.at[s, self.rows(c)],
            send_sem=self.s_sem.at[s, c], recv_sem=self.r2.at[s, c],
            device_id={"tensor": self.inner}, device_id_type=MESH)

    def to_cross(self, s, c, slot):
        return pltpu.make_async_remote_copy(
            src_ref=self.sbuf.at[s, self.rows(c)], dst_ref=self.x1.at[slot, s, self.rows(c)],
            send_sem=self.s_sem.at[s, c], recv_sem=self.r1.at[slot, s, c],
            device_id={"tensor": self.cross}, device_id_type=MESH)

    def to_outer(self, s, c, slot):
        return pltpu.make_async_remote_copy(
            src_ref=self.tbuf.at[s, self.rows(c)], dst_ref=self.x1.at[slot, s, self.rows(c)],
            send_sem=self.t_sem.at[s, c], recv_sem=self.r1.at[slot, s, c],
            device_id={"tensor": self.outer}, device_id_type=MESH)

    def begin(self, s, narrow=False):
        for c in range(CHUNKS):
            @pl.when(self.end & self.outbound(c, narrow))
            def _():
                rows = self.rows(c)
                self.sbuf[s, rows] = self.part[s, rows].astype(BF)
                self.to_inner(s, c).start()

    def inward(self, s, c, slot, live, narrow=False):
        @pl.when(self.mid & live & self.outbound(c, narrow))
        def _():
            rows = self.rows(c)
            self.to_inner(s, c).wait_recv()
            self.sbuf[s, rows] = (self.part[s, rows] + self.x2[s, rows].astype(F32)).astype(BF)
            self.to_cross(s, c, slot).start()

    def outward(self, s, c, slot, live, narrow=False):
        @pl.when(self.mid & live & self.homebound(c, narrow))
        def _():
            rows = self.rows(c)
            self.to_cross(s, c, slot).wait_recv()
            joint = self.part[s, rows] + self.x1[slot, s, rows].astype(F32)
            self.part[s, rows] = joint + self.x2[s, rows].astype(F32)
            self.tbuf[s, rows] = joint.astype(BF)
            self.to_outer(s, c, slot).start()

    def settle(self, s, slot, tile, narrow=False):
        per = TILE // self.size
        for d in range(per):
            c = tile * per + d

            @pl.when(self.end & self.homebound(c, narrow))
            def _():
                rows = self.rows(c)
                self.to_outer(s, c, slot).wait_recv()
                self.part[s, rows] = self.part[s, rows] + self.x1[slot, s, rows].astype(F32)

    def release(self, s, slot, narrow=False):
        for c in range(CHUNKS):
            @pl.when(self.end & self.outbound(c, narrow))
            def _():
                self.to_inner(s, c).wait_send()

            @pl.when(self.mid & self.outbound(c, narrow))
            def _():
                self.to_cross(s, c, slot).wait_send()

            @pl.when(self.mid & self.homebound(c, narrow))
            def _():
                self.to_outer(s, c, slot).wait_send()


def line_scratch(streams, rows, width):
    return [
        pltpu.VMEM((streams, rows, width), F32),
        pltpu.VMEM((streams, rows, width), BF),
        pltpu.VMEM((streams, rows, width), BF),
        pltpu.VMEM((2, streams, rows, width), BF),
        pltpu.VMEM((streams, rows, width), BF),
        pltpu.SemaphoreType.DMA((streams, CHUNKS)),
        pltpu.SemaphoreType.DMA((streams, CHUNKS)),
        pltpu.SemaphoreType.DMA((2, streams, CHUNKS)),
        pltpu.SemaphoreType.DMA((streams, CHUNKS)),
    ]


def tiles(rows, body, ready=None):
    def step(c, carry):
        if ready is not None:
            ready(c)
        body(pl.ds(pl.multiple_of(c * TILE, TILE), TILE))
        return carry

    lax.fori_loop(0, rows // TILE, step, 0)


def normalize(total, gain, shift):
    mean = jnp.mean(total, axis=-1, keepdims=True)
    centered = total - mean
    inverse = lax.rsqrt(jnp.mean(centered * centered, axis=-1, keepdims=True) + NORM_EPS)
    normed = centered * inverse
    return normed * gain + shift, normed, inverse


def head_masks(width, scale):
    lane = lax.broadcasted_iota(jnp.int32, (1, width), 1)
    return [
        jnp.where((lane >= h * HEAD_DIM) & (lane < (h + 1) * HEAD_DIM), scale, 0.0).astype(BF)
        for h in range(width // HEAD_DIM)
    ]


def norm_back(g, normed, inverse, gain):
    scaled = g * gain
    return inverse * (
        scaled
        - jnp.mean(scaled, axis=-1, keepdims=True)
        - normed * jnp.mean(scaled * normed, axis=-1, keepdims=True)
    )


def fold(x):
    return jnp.sum(x.reshape(x.shape[0] // 8, 8, x.shape[1]), axis=0)


class Plane:
    def __init__(self, grads, sends, spots, recvs, out, send_sem, recv_sem, credit):
        dp, self.x = lax.axis_index("dp"), lax.axis_index("rep")
        self.y, self.c = dp // 2, dp % 2
        self.partner = {
            "c": {"dp": dp + 1 - 2 * self.c},
            "x": {"rep": 1 - self.x},
            "y": {"dp": (dp + 2) % 4},
        }
        self.grads, self.sends, self.places, self.recvs, self.out = grads, sends, spots, recvs, out
        self.send_sem, self.recv_sem, self.credit = send_sem, recv_sem, credit
        self.block = grads.shape[2] // 8

    def message(self, u, stage, half, rows):
        if self.places is None:
            return self.sends[stage].at[u, half, rows]
        row, lane = self.places[stage]
        start = half * (self.grads.shape[2] // 2) + row
        return self.sends.at[u, pl.ds(start + rows.start, rows.size), pl.ds(lane, self.grads.shape[3])]

    def copy(self, u, stage, half):
        way = ("c", "xy"[half], "yx"[half])[stage]
        return pltpu.make_async_remote_copy(
            src_ref=self.message(u, stage, half, pl.ds(0, self.recvs[stage].shape[2])), dst_ref=self.recvs[stage].at[u, half],
            send_sem=self.send_sem.at[u, stage, half], recv_sem=self.recv_sem.at[u, stage, half],
            device_id=self.partner[way], device_id_type=MESH)

    def spots(self, stage, half, own):
        pick = (lambda v: v) if own else (lambda v: 1 - v)
        if stage == 0:
            return [(4 * y + 2 * pick(self.c), 2 * y, 2) for y in (0, 1)]
        if stage == 1 and half == 0:
            return [(4 * y + 2 * self.c + pick(self.x), y, 1) for y in (0, 1)]
        if stage == 1:
            return [(4 * pick(self.y) + 2 * self.c, 0, 2)]
        if half == 0:
            return [(4 * pick(self.y) + 2 * self.c + self.x, 0, 1)]
        return [(4 * self.y + 2 * self.c + pick(self.x), 0, 1)]

    def parts(self, stage, half, own):
        for here, there, blocks in self.spots(stage, half, own):
            for b in range(blocks):
                start = (here + b) * self.block
                yield pl.ds(pl.multiple_of(start, 8), self.block), pl.ds((there + b) * self.block, self.block)

    def send(self, u, stage, live, spend):
        @pl.when(live)
        def _():
            for half in (0, 1):
                for here, there in self.parts(stage, half, False):
                    self.message(u, stage, half, there)[...] = self.grads[u, half, here].astype(BF)

            @pl.when(spend)
            def _():
                pl.semaphore_wait(self.credit.at[u, stage], 2)

            for half in (0, 1):
                self.copy(u, stage, half).start()

    def take(self, u, stage, live, give, layer):
        @pl.when(live)
        def _():
            for half in (0, 1):
                self.copy(u, stage, half).wait()
                for here, there in self.parts(stage, half, True):
                    total = self.grads[u, half, here] + self.recvs[stage][u, half, there].astype(F32)
                    if stage == 2:
                        self.out[layer, u, half] = total
                    else:
                        self.grads[u, half, here] = total

            @pl.when(give)
            def _():
                for half in (0, 1):
                    way = ("c", "xy"[half], "yx"[half])[stage]
                    pl.semaphore_signal(
                        self.credit.at[u, stage], inc=1, device_id=self.partner[way], device_id_type=MESH
                    )


def greet(inside):
    z, dp, rep = lax.axis_index("tensor"), lax.axis_index("dp"), lax.axis_index("rep")
    sem = pltpu.get_barrier_semaphore()
    others = [{"tensor": (z + d) % 4} for d in (1, 2, 3)]
    if inside:
        others += [{"rep": 1 - rep, "tensor": (z + d) % 4} for d in (0, 1, 2, 3)]
        others += [{"dp": dp + 1 - 2 * (dp % 2)}, {"dp": (dp + 2) % 4}]
    for other in others:
        pl.semaphore_signal(sem, inc=1, device_id=other, device_id_type=MESH)
    pl.semaphore_wait(sem, len(others))


class Contrast:
    def __init__(self, inside, micro, pooled, keys, pgrad, vec, state, bufs):
        self.inside, self.micro, self.pooled, self.keys = inside, micro, pooled, keys
        self.pgrad, self.vec, self.state = pgrad, vec, state
        self.z, self.rep = lax.axis_index("tensor"), lax.axis_index("rep")
        if inside:
            (self.asks, self.asked, self.reply, self.heard, self.ask_sem, self.reply_sem, self.heard_sem) = bufs
        else:
            (self.source, self.key_sem) = bufs

    def question(self, m):
        return pltpu.make_async_remote_copy(
            src_ref=self.asks.at[m], dst_ref=self.asked.at[m], send_sem=self.ask_sem.at[m, 0],
            recv_sem=self.ask_sem.at[m, 1], device_id={"rep": 1 - self.rep}, device_id_type=MESH)

    def tell(self, m, which, d):
        other = {"tensor": (self.z + d) % 4}
        if which == 1:
            other["rep"] = 1 - self.rep
        k = which * 4 + d
        return pltpu.make_async_remote_copy(
            src_ref=self.reply.at[m, which], dst_ref=self.heard.at[m, k], send_sem=self.reply_sem.at[m, k],
            recv_sem=self.heard_sem.at[m, k], device_id=other, device_id_type=MESH)

    def score(self, rows_now):
        keys = self.keys[...]
        logits = nt(rows_now, keys) / SOFTMAX_WARMTH
        top = jnp.max(logits, axis=-1, keepdims=True)
        expo = jnp.exp(logits - top)
        total = jnp.sum(expo, axis=-1, keepdims=True)
        high = expo.astype(BF)
        rest = expo - high.astype(F32)
        mid = rest.astype(BF)
        tiny = (rest - mid.astype(F32)).astype(BF)
        weighted = nn(high, keys) + nn(mid, keys) + nn(tiny, keys)
        return weighted[0:1], top[0:1], total[0:1]

    def answer(self, m, which, rows_now):
        weighted, top, total = self.score(rows_now)
        width = weighted.shape[1]
        self.reply[m, which, 0:1] = weighted
        self.reply[m, which, 1:2] = jnp.broadcast_to(top, (1, width))
        self.reply[m, which, 2:3] = jnp.broadcast_to(total, (1, width))

    def ask(self, m):
        count = self.pooled[self.micro + m, 1:2]
        mean = self.pooled[self.micro + m, 0:1] / count
        scale = lax.rsqrt(jnp.sum(mean * mean, axis=-1, keepdims=True) + UNIT_EPS)
        direction = mean * scale
        self.state[m, 0:1] = direction
        self.state[m, 1:2] = jnp.broadcast_to(scale, count.shape)
        self.state[m, 2:3] = count
        if self.inside:
            self.asks[m] = jnp.broadcast_to(direction, self.asks.shape[1:]).astype(BF)
            self.question(m).start()
            self.answer(m, 0, self.asks[m])
            for d in (1, 2, 3):
                self.tell(m, 0, d).start()

    def respond(self, m):
        if self.inside:
            self.question(m).wait()
            self.answer(m, 1, self.asked[m])
            for d in (0, 1, 2, 3):
                self.tell(m, 1, d).start()

    def close(self, m, pooled_key):
        direction, scale, count = self.state[m, 0:1], self.state[m, 1:2, 0:1], self.state[m, 2:3]
        mean = pooled_key / self.pooled[m, 1:2]
        key_dir = mean * lax.rsqrt(jnp.sum(mean * mean, axis=-1, keepdims=True) + UNIT_EPS)
        positive = jnp.sum(direction * key_dir, axis=-1, keepdims=True) / SOFTMAX_WARMTH
        if self.inside:
            for k in range(1, 8):
                self.tell(m, k // 4, k % 4).wait()
            everyone = [self.reply[m, 0]] + [self.heard[m, k] for k in range(1, 8)]
            best = positive
            for one in everyone:
                best = jnp.maximum(best, one[1:2, 0:1])
            own = jnp.exp(positive - best)
            total, keys = own, own * key_dir
            for one in everyone:
                weight = jnp.exp(one[1:2, 0:1] - best)
                total = total + weight * one[2:3, 0:1]
                keys = keys + weight * one[0:1]
        else:
            rows_now = jnp.broadcast_to(direction, (16, direction.shape[1])).astype(BF)

            def piece(c, carry):
                best, total, keys = carry
                size = self.keys.shape[0]
                copy = pltpu.make_async_copy(
                    self.source.at[pl.ds(pl.multiple_of(c * size, size), size)], self.keys, self.key_sem)
                copy.start()
                copy.wait()
                weighted, top, part = self.score(rows_now)
                now = jnp.maximum(best, top)
                old, new = jnp.exp(best - now), jnp.exp(top - now)
                return now, total * old + part * new, keys * old + weighted * new

            start = (positive, jnp.ones_like(positive), key_dir)
            best, total, keys = lax.fori_loop(0, self.source.shape[0] // self.keys.shape[0], piece, start)
        loss = best + jnp.log(total) - positive
        last = self.vec.shape[0] - 1
        self.vec[last : last + 1] += jnp.broadcast_to(loss, direction.shape)
        dqn = (keys / total - key_dir) * (CROP_SLOTS / SOFTMAX_WARMTH)
        mean_grad = scale * (dqn - direction * jnp.sum(direction * dqn, axis=-1, keepdims=True))
        self.pgrad[m, 0:1] = mean_grad / count
        self.pgrad[m, 1:2] = count


def step_kernel(inside, *refs):
    q_tok, q_drop, q_len, k_tok, k_drop, k_len, negs, *refs = refs
    wqkv_in, abias, wm_in, mbias, we_in, ebias, ws_in, sbias, gains, shifts, *refs = refs
    acts, g_in, vec, out_big, out_small, *refs = refs
    xin, proj, probs, mixed, n1, first, slope, active, n2, inv, *refs = refs
    wqkv, wm, we, ws, tok, h, hb, qkv, mx, inner, *refs = refs
    vbias, valid, vecs, slots, pooled, state, pgrad, g_vec, g_abias, g_big, g_small, *refs = refs
    load_sem, tok_sem, kpart, kheard, kp_sem, kh_sem, *refs = refs
    line = Line(*refs[:9])
    part, sbuf, tbuf = refs[:3]
    refs = refs[9:]
    stored, loaded = (wqkv_in, wm_in, we_in, ws_in), (wqkv, wm, we, ws)
    micro = q_tok.shape[0]
    rows, width = q_tok.shape[2:]
    layers = we.shape[1]
    local = wm.shape[2]
    half_units = we.shape[3] // 2
    heads = local // HEAD_DIM
    streams = 2 * micro
    third = width // 3
    z = lax.axis_index("tensor")
    share = rows // lax.axis_size("tensor")
    own_rows = pl.ds(pl.multiple_of(z * share, 16), share)

    def load(k, e, layer):
        return pltpu.make_async_copy(stored[k].at[e, layer], loaded[k].at[e, layer], load_sem.at[k, e, layer])

    def load_tokens(s):
        source = k_tok if s < micro else q_tok
        return pltpu.make_async_copy(source.at[s % micro, 0], tok.at[pl.ds(s * rows, rows)], tok_sem.at[s])

    def load_keys():
        return pltpu.make_async_copy(negs, tok, tok_sem.at[streams])

    for layer in range(layers):
        for e in (1, 0):
            for k in (0, 1):
                load(k, e, layer).start()
            if layer == 0:
                for s in range((1 - e) * micro, (2 - e) * micro):
                    load_tokens(s).start()
            for k in (2, 3):
                load(k, e, layer).start()
    vec[...] = jnp.zeros_like(vec)
    g_vec[...] = jnp.zeros_like(g_vec)
    g_abias[...] = jnp.zeros_like(g_abias)
    for e in range(2):
        for layer in range(layers):
            for row, ref in enumerate((mbias, ebias, sbias)):
                vecs[e, layer, row : row + 1] = ref[e, layer : layer + 1].astype(F32)
            vecs[e, layer, 3:5] = gains[e, layer].astype(F32)
            vecs[e, layer, 5:7] = shifts[e, layer].astype(F32)
    greet(inside)

    last_f = 2 * layers * streams

    def at_f(i):
        j = jnp.maximum(i, 0)
        s, stage = j % streams, j // streams
        return s, stage % 2, (i >= 0) & (i < last_f), (stage == 2 * layers - 1) & (s < micro)

    def tick_f(i, *which):
        for c in which:
            s, slot, live, narrow = at_f(i - 1)
            line.inward(s, c, slot, live, narrow)
            if c < LAG:
                s, slot, live, narrow = at_f(i - 2)
            line.outward(s, (c - LAG) % CHUNKS, slot, live, narrow)

    def compact(drop, length, is_q, s, m):
        pos = lax.broadcasted_iota(jnp.int32, (1, rows), 1)
        kept = (pos < length) & ((drop[m] == 0) | (pos == 0))
        kept_f = jnp.broadcast_to(jnp.where(kept, 1.0, 0.0), (16, rows))
        down = lax.broadcasted_iota(jnp.int32, (rows, rows), 0)
        along = lax.broadcasted_iota(jnp.int32, (rows, rows), 1)
        tri = jnp.where(down <= along, 1.0, 0.0).astype(BF)
        order = nn(kept_f.astype(BF), tri)[0:1] - 1.0
        order = jnp.where(kept, order, -1.0)
        count = jnp.sum(kept_f[0:1], axis=-1, keepdims=True)
        pick = jnp.where(order == down.astype(F32), 1.0, 0.0).astype(BF)
        rows_now = nn(pick, tok[pl.ds(pl.multiple_of(s * rows, rows), rows)])
        h[s] = rows_now
        hb[...] = rows_now.astype(BF)
        fits = pos.astype(F32) < count
        vbias[s] = jnp.broadcast_to(jnp.where(fits, 0.0, MASKED), (8, rows))
        if not is_q:
            fits = fits & line.end & ((pos < rows // 2) == line.lower)
        valid[s] = jnp.broadcast_to(jnp.where(fits, 1.0, 0.0), (8, rows))
        pooled[s, 1:2] = jnp.broadcast_to(count, (1, width))
        if is_q:
            slots[m] = jnp.broadcast_to(order, (8, rows))

    def second_norm(lp, e, s, narrow):
        m, is_q = s % micro, s >= micro
        bias, gain, shift = vecs[e, lp, 2:3], vecs[e, lp, 4:5], vecs[e, lp, 6:7]

        def norm(r):
            out, normed, inverse = normalize(h[s, r] + part[s, r] + bias, gain, shift)
            h[s, r] = out
            hb[r] = out.astype(BF)

            @pl.when(is_q)
            def _():
                n2[lp, m, r] = normed.astype(BF)
                inv[lp, m, r, 64:128] = jnp.broadcast_to(inverse, (TILE, 64))

        tiles(rows, norm, lambda t: line.settle(s, 1, t, narrow))
        line.release(s, 1, narrow)

    def attention_pass(layer, s):
        i = layer * 2 * streams + s
        e, m = 1 - s // micro, s % micro
        is_q = s >= micro
        tick_f(i, 0)

        @pl.when(layer == 0)
        def _():
            @pl.when(s < micro)
            def _():
                pltpu.make_async_copy(k_tok.at[m, 0], tok.at[pl.ds(0, rows)], tok_sem.at[s]).wait()
                compact(k_drop, k_len[m], False, s, m)

            @pl.when(is_q)
            def _():
                pltpu.make_async_copy(q_tok.at[m, 0], tok.at[pl.ds(0, rows)], tok_sem.at[s]).wait()
                compact(q_drop, q_len[m], True, s, m)

        @pl.when(layer > 0)
        def _():
            second_norm(layer - 1, e, s, False)

        tick_f(i, 1, 2)

        @pl.when(m == 0)
        def _():
            for k in (0, 1):
                load(k, e, layer).wait()

        @pl.when(is_q)
        def _():
            xin[layer, m] = hb[...]

        rows_now = hb[...]
        for j in range(3):
            bias = 0.0 if j == 1 else abias[e, layer, j // 2 : j // 2 + 1].astype(F32)
            qkv[j] = (nt(rows_now, wqkv[e, layer, j]) + bias).astype(BF)

        @pl.when(is_q)
        def _():
            for j in range(3):
                proj[layer, m, j] = qkv[j]

        tick_f(i, 3)
        q_masks = head_masks(local, HEAD_DIM**-0.5)
        v_masks = head_masks(local, 1.0)
        for hd in range(heads):
            scores = nt(qkv[0] * q_masks[hd], qkv[1]) + vbias[s, 0:1]
            expo = jnp.exp(scores - jnp.max(scores, axis=-1, keepdims=True))
            chance = (expo / jnp.sum(expo, axis=-1, keepdims=True)).astype(BF)

            @pl.when(is_q)
            def _():
                probs[layer, m, hd] = chance

            out = nn(chance, qkv[2] * v_masks[hd])
            if hd == 0:
                mx[...] = out
            else:
                mx[...] += out
            tick_f(i, 4 + hd)
        mixed_now = mx[...].astype(BF)

        @pl.when(is_q)
        def _():
            mixed[layer, m] = mixed_now

        part[s] = nn(mixed_now, wm[e, layer])
        line.begin(s)
        tick_f(i, *range(4 + heads, CHUNKS))

    def forward_pass(layer, s):
        i = (layer * 2 + 1) * streams + s
        e, m = 1 - s // micro, s % micro
        is_q = s >= micro
        tick_f(i, 0, 1)
        bias, gain, shift = vecs[e, layer, 0:1], vecs[e, layer, 3:4], vecs[e, layer, 5:6]

        def norm(r):
            out, normed, inverse = normalize(h[s, r] + part[s, r] + bias, gain, shift)
            h[s, r] = out
            hb[r] = out.astype(BF)

            @pl.when(is_q)
            def _():
                n1[layer, m, r] = normed.astype(BF)
                inv[layer, m, r, 0:64] = jnp.broadcast_to(inverse, (TILE, 64))
                first[layer, m, r] = out.astype(BF)

        tiles(rows, norm, lambda t: line.settle(s, 0, t))
        line.release(s, 0)

        @pl.when(m == 0)
        def _():
            for k in (2, 3):
                load(k, e, layer).wait()

        tick_f(i, 2, 3)
        inner[...] = nn(hb[...], we[e, layer])
        tick_f(i, 4)
        bias_e = vecs[e, layer, 1:2]

        def gelu(r):
            u = inner[r] + bias_e
            phi = 0.5 * (1.0 + lax.erf(u * ROOT_HALF))
            out = (u * phi).astype(BF)
            tbuf[s, r] = out

            @pl.when(is_q)
            def _():
                active[layer, m, r] = out
                slope[layer, m, r] = (phi + u * jnp.exp(-0.5 * u * u) * INV_ROOT_TAU).astype(BF)

        tiles(rows, gelu)
        tick_f(i, 5, 6)
        part[s] = nn(tbuf[s], ws[e, layer])
        line.begin(s, (layer == layers - 1) & (s < micro))
        tick_f(i, 7)

    def layer_step(layer, carry):
        def a_step(s, c):
            attention_pass(layer, s)
            return c

        def f_step(s, c):
            forward_pass(layer, s)
            return c

        lax.fori_loop(0, streams, a_step, 0)
        if inside:
            @pl.when(layer == 0)
            def _():
                load_keys().start()

        lax.fori_loop(0, streams, f_step, 0)
        return carry

    lax.fori_loop(0, layers, layer_step, 0)

    def pool(s):
        return jnp.dot(valid[s], h[s], precision=TOP_PRECISION, preferred_element_type=F32)

    def kshare(m, d):
        return pltpu.make_async_remote_copy(
            src_ref=kpart.at[m], dst_ref=kheard.at[z // 3, m], send_sem=kp_sem.at[m, d - 1],
            recv_sem=kh_sem.at[z // 3, m], device_id={"tensor": (z + d) % 4}, device_id_type=MESH)

    def last_key(m):
        second_norm(layers - 1, 1, m, line.part.shape[0] > 0)
        kpart[m] = pool(m)

        @pl.when(line.end)
        def _():
            for d in (1, 2, 3):
                kshare(m, d).start()

    def last_query(m):
        second_norm(layers - 1, 0, micro + m, False)
        pooled[micro + m, 0:1] = pool(micro + m)[0:1]
        acts[m] = hb[own_rows]

    def pooled_key(m):
        @pl.when(line.end)
        def _():
            for d in (1, 2, 3):
                kshare(m, d).wait_send()

        total = kpart[m, 0:1]
        for e in (0, 1):
            @pl.when(z != 3 * e)
            def _():
                pltpu.make_async_remote_copy(
                    src_ref=kpart.at[m], dst_ref=kheard.at[e, m], send_sem=kp_sem.at[m, 0],
                    recv_sem=kh_sem.at[e, m], device_id={"tensor": 3 - z}, device_id_type=MESH).wait_recv()

            total = total + jnp.where(z != 3 * e, kheard[e, m, 0:1], 0.0)
        return total

    if inside:
        e1, e2, e3, t1, t2, t3, d1, d2, d3, big_s, big_r, small_s, small_r, big_c, small_c, v_rcv, v_send, v_recv, *bufs = refs
        w_big, quarter = half_units, width // 4
        big = Plane(g_big, we.at[1], ((0, 0), (0, w_big), (quarter, w_big)), (e1, e2, e3), out_big, big_s, big_r, big_c)
        small = Plane(g_small, (d1, d2, d3), None, (t1, t2, t3), out_small, small_s, small_r, small_c)
    else:
        g_sem, key_sem = refs
        bufs = (negs, key_sem)
    queue = Contrast(inside, micro, pooled, tok, pgrad, vec, state, bufs)
    tick_f(last_f, 0, 1, 2)
    for m in range(micro):
        last_key(m)
        tick_f(last_f, 3 + m)
    if inside:
        load_keys().wait()
    for m in range(micro):
        if m == micro - 1:
            tick_f(last_f, *range(3 + micro, CHUNKS))
            tick_f(last_f + 1, *range(LAG))
        if m > 0:
            queue.respond(m - 1)
        last_query(m)
        queue.ask(m)

    last_b = 2 * layers * micro
    dinner = tbuf.at[1]
    heads_f = [h.at[0, :, pl.ds(j * third, local)] for j in range(3)]
    heads_b = [tbuf.at[0, :, pl.ds(j * third, local)] for j in range(3)]

    def at_b(i):
        j = jnp.maximum(i, 0)
        return micro + j % micro, (j // micro) % 2, (i >= 0) & (i < last_b)

    def tick(i, *which):
        for g in which:
            s, slot, live = at_b(i - 1)
            if g >= 1 and g - 1 < CHUNKS:
                line.outward(s, g - 1, slot, live)
            c = g + EARLY
            if c >= CHUNKS + 1:
                s, slot, live = at_b(i)
                c -= CHUNKS + 1
                if c < EARLY:
                    line.inward(s, c, slot, live)
            elif c < CHUNKS:
                line.inward(s, c, slot, live)

    def drained(large, layer, u, half):
        source, target = (g_big, out_big) if large else (g_small, out_small)
        return pltpu.make_async_copy(source.at[u, half], target.at[layer, u, half], g_sem.at[0 if large else 1, u, half])

    def add_to(large, u, half, s, value):
        ref = (g_big if large else g_small).at[u, half]

        @pl.when(s == 0)
        def _():
            ref[...] = value

        @pl.when(s > 0)
        def _():
            ref[...] += value

    def plane(what, large, stage, live, step):
        for u in (0, 1):
            if inside:
                group = big if large else small
                if what == "send":
                    group.send(u, stage, live, step > 0)
                else:
                    group.take(u, stage, live, step < layers - 1, layers - 1 - step)
            elif (what, stage) in (("send", 0), ("take", 2)):
                @pl.when(live)
                def _():
                    for half in (0, 1):
                        copy = drained(large, layers - 1 - step, u, half)
                        copy.start() if what == "send" else copy.wait()

    def mlp_back(step, m):
        layer = layers - 1 - step
        i = step * 2 * micro + m
        s = micro + m
        low = sbuf.at[m]

        @pl.when(step == 0)
        def _():
            queue.close(m, pooled_key(m))

            def begin(c, carry):
                r = pl.ds(pl.multiple_of(c * TILE, TILE), TILE)
                pos = (lax.broadcasted_iota(jnp.int32, (TILE, 1), 0) + c * TILE).astype(F32)
                part[s, r] = jnp.where(pos < pgrad[m, 1:2, 0:1], pgrad[m, 0:1], 0.0)
                h[s, r] = jnp.zeros((TILE, width), F32)
                return carry

            lax.fori_loop(0, rows // TILE, begin, 0)

        gain = vecs[0, layer, 4:5]

        def back(r):
            g = part[s, r] + h[s, r]
            normed = n2[layer, m, r].astype(F32)
            out = norm_back(g, normed, inv[layer, m, r][:, 64:65], gain)
            h[s, r] = out
            low[r] = out.astype(BF)
            g_vec[layer, 1] += fold(g * normed)
            g_vec[layer, 3] += fold(g)
            g_vec[layer, 4] += fold(out)

        def ready(t):
            @pl.when(step > 0)
            def _():
                line.settle(s, 1, t)

        tiles(rows, back, ready)

        @pl.when(step > 0)
        def _():
            line.release(s, 1)

        tick(i, 0)
        inner[...] = nt(low[...], ws[0, layer])
        tick(i, 1)

        def slopes(r):
            out = inner[r] * slope[layer, m, r].astype(F32)
            dinner[r] = out.astype(BF)
            g_vec[layer, 6] += fold(out)

        tiles(rows, slopes)
        tick(i, 2)
        part[s] = nt(dinner[...], we[0, layer])
        line.begin(s)
        tick(i, 3)

        @pl.when((step == 0) & (m == 0))
        def _():
            queue.respond(micro - 1)

        plane("take", True, 2, (step > 0) & (m == 0), step - 1)
        plane("take", False, 0, (step > 0) & (m == 0), step - 1)
        plane("send", False, 1, (step > 0) & (m == 0), step - 1)
        for half in (0, 1):
            cols = pl.ds(half * half_units, half_units)
            add_to(True, 0, half, m, tn(low[...], active[layer, m, :, cols]))
            tick(i, 4 + half)
        for half in (0, 1):
            cols = pl.ds(half * half_units, half_units)
            add_to(True, 1, half, m, tn(first[layer, m], dinner[:, cols]))
            tick(i, 6 + half)
        plane("send", True, 0, m == micro - 1, step)
        plane("take", False, 1, (step > 0) & (m == micro - 1), step - 1)
        plane("send", False, 2, (step > 0) & (m == micro - 1), step - 1)
        tick(i, CHUNKS)

    def attention_back(step, m):
        layer = layers - 1 - step
        i = (step * 2 + 1) * micro + m
        s = micro + m
        low = sbuf.at[m]
        gain = vecs[0, layer, 3:4]

        def back(r):
            g = part[s, r] + h[s, r]
            normed = n1[layer, m, r].astype(F32)
            out = norm_back(g, normed, inv[layer, m, r][:, 0:1], gain)
            h[s, r] = out
            low[r] = out.astype(BF)
            g_vec[layer, 0] += fold(g * normed)
            g_vec[layer, 2] += fold(g)
            g_vec[layer, 5] += fold(out)

        tiles(rows, back, lambda t: line.settle(s, 0, t))
        line.release(s, 0)
        tick(i, 0)
        dmix = nt(low[...], wm[0, layer]).astype(BF)
        tick(i, 1)
        masks = head_masks(local, 1.0)
        for hd in range(heads):
            chance_b = probs[layer, m, hd]
            chance = chance_b.astype(F32)
            dm = dmix * masks[hd]
            dch = nt(dm, proj[layer, m, 2])
            ds = chance * (dch - jnp.sum(chance * dch, axis=-1, keepdims=True))
            draw = (ds * HEAD_DIM**-0.5).astype(BF)
            dq = nn(draw, proj[layer, m, 1] * masks[hd])
            dk = tn(draw, proj[layer, m, 0] * masks[hd])
            dv = tn(chance_b, dm)
            for ref, value in zip(heads_f, (dq, dk, dv)):
                if hd == 0:
                    ref[...] = value
                else:
                    ref[...] += value
            tick(i, 2 + hd)
        g_abias[layer, 0] += fold(heads_f[0][...])
        g_abias[layer, 1] += fold(heads_f[2][...])
        for j in range(3):
            heads_b[j][...] = heads_f[j][...].astype(BF)
        part[s] = sum(nn(heads_b[j][...], wqkv[0, layer, j]) for j in range(3))
        line.begin(s)
        tick(i, *range(2 + heads, 6))
        plane("take", True, 0, m == 0, step)
        plane("send", True, 1, m == 0, step)
        plane("take", True, 1, m == micro - 1, step)
        plane("send", True, 2, m == micro - 1, step)
        plane("take", False, 2, (step > 0) & (m == 0), step - 1)
        for j in range(3):
            add_to(False, j // 2, j % 2, m, tn(xin[layer, m], heads_b[j][...]))
        tick(i, 6)
        add_to(False, 1, 1, m, tn(low[...], mixed[layer, m]))
        tick(i, 7, CHUNKS)
        plane("send", False, 0, m == micro - 1, step)

    def back_step(step, carry):
        def m_step(m, c):
            mlp_back(step, m)
            return c

        def a_step(m, c):
            attention_back(step, m)
            return c

        lax.fori_loop(0, micro, m_step, 0)
        lax.fori_loop(0, micro, a_step, 0)
        return carry

    lax.fori_loop(0, layers, back_step, 0)

    for layer in range(layers):
        for k in range(7):
            vec[layer * 7 + k : layer * 7 + k + 1] = jnp.sum(g_vec[layer, k], axis=0, keepdims=True)
        for k in range(2):
            row = layers * 7 + layer * 2 + k
            vec[row : row + 1, 0:local] = jnp.sum(g_abias[layer, k], axis=0, keepdims=True)

    def vec_copy(stage):
        return pltpu.make_async_remote_copy(
            src_ref=vec, dst_ref=v_rcv.at[stage], send_sem=v_send.at[stage], recv_sem=v_recv.at[stage],
            device_id=big.partner["cxy"[stage]], device_id_type=MESH)

    def vec_take(stage):
        if inside:
            vec_copy(stage).wait()
            vec[...] += v_rcv[stage]

    def vec_send(stage):
        if inside:
            vec_copy(stage).start()

    final = layers - 1
    vec_send(0)
    tick(last_b, 0, 1)
    plane("take", False, 0, True, final)
    plane("send", False, 1, True, final)
    vec_take(0)
    vec_send(1)
    tick(last_b, 2, 3, 4)
    plane("take", True, 2, True, final)
    tick(last_b, 5, 6)
    plane("take", False, 1, True, final)
    plane("send", False, 2, True, final)
    vec_take(1)
    vec_send(2)
    tick(last_b, 7, CHUNKS)

    def finish(m, carry):
        s = micro + m
        low = sbuf.at[m]

        def back(r):
            low[r] = (part[s, r] + h[s, r]).astype(BF)

        tiles(rows, back, lambda t: line.settle(s, 1, t))
        line.release(s, 1)
        down = lax.broadcasted_iota(jnp.int32, (rows, rows), 0).astype(F32)
        pick = jnp.where(slots[m, 0:1] == down, 1.0, 0.0).astype(BF)
        low[...] = tn(pick, low[...]).astype(BF)
        g_in[m] = low[own_rows]
        return carry

    lax.fori_loop(0, micro, finish, 0)
    plane("take", False, 2, True, final)
    vec_take(2)


def run_step(inside, tokens, negatives, weights):
    q_tok = tokens[0]
    micro, _, rows, width = q_tok.shape
    wqkv, abias, wm, mbias, we, ebias, ws, sbias, gains, shifts = weights
    layers, local, units = we.shape[1], wm.shape[2], we.shape[3]
    heads = local // HEAD_DIM
    streams = 2 * micro
    share = rows // lax.axis_size("tensor")
    lm = (layers, micro)
    tall = 8 * ((9 * layers + 2 + 7) // 8)
    kinds = (units // 2, local)
    high = width // 8 if inside else width
    shapes = [((micro, share, width), BF), ((micro, share, width), BF), ((tall, width), F32)]
    shapes += [((layers, 2, 2, high, w), F32) for w in kinds]
    vm = pl.BlockSpec(memory_space=pltpu.VMEM)
    hb = pl.BlockSpec(memory_space=pl.ANY)
    sm = pl.BlockSpec(memory_space=pltpu.SMEM)
    dma = pltpu.SemaphoreType.DMA
    v = pltpu.VMEM
    scratch = [
        v(lm + (rows, width), BF),
        v(lm + (3, rows, local), BF),
        v(lm + (heads, rows, rows), BF),
        v(lm + (rows, local), BF),
        v(lm + (rows, width), BF),
        v(lm + (rows, width), BF),
        v(lm + (rows, units), BF),
        v(lm + (rows, units), BF),
        v(lm + (rows, width), BF),
        v(lm + (rows, 128), F32),
    ]
    scratch += [v(w.shape, BF) for w in (wqkv, wm, we, ws)]
    scratch += [
        v((streams * rows, width), BF),
        v((streams, rows, width), F32),
        v((rows, width), BF),
        v((3, rows, local), BF),
        v((rows, local), F32),
        v((rows, units), F32),
        v((streams, 8, rows), F32),
        v((streams, 8, rows), F32),
        v((2, layers, 8, width), F32),
        v((micro, 8, rows), F32),
        v((streams, 8, width), F32),
        v((micro, 8, width), F32),
        v((micro, 8, width), F32),
        v((layers, 7, 8, width), F32),
        v((layers, 2, 8, local), F32),
    ]
    scratch += [v((2, 2, width, w), F32) for w in kinds]
    scratch += [
        dma((4, 2, layers)),
        dma((streams + 1,)),
        v((micro, 8, width), F32),
        v((2, micro, 8, width), F32),
        dma((micro, 3)),
        dma((2, micro)),
    ]
    scratch += line_scratch(streams, rows, width)
    if inside:
        for w in kinds + kinds[1:]:
            scratch += [v((2, 2, width // n, w), BF) for n in (2, 4, 8)]
        scratch += [dma((2, 3, 2))] * 4
        scratch += [pltpu.SemaphoreType.REGULAR((2, 3))] * 2
        scratch += [v((3, tall, width), F32), dma((3,)), dma((3,))]
        scratch += [
            v((micro, 16, width), BF),
            v((micro, 16, width), BF),
            v((micro, 2, 8, width), F32),
            v((micro, 8, 8, width), F32),
            dma((micro, 2)),
            dma((micro, 8)),
            dma((micro, 8)),
        ]
    else:
        scratch += [dma((2, 2, 2)), dma(())]
    return pl.pallas_call(
        functools.partial(step_kernel, inside),
        out_shape=[jax.ShapeDtypeStruct(*s) for s in shapes],
        in_specs=[hb, vm, sm, hb, vm, sm, hb] + [hb, vm, hb, vm, hb, vm, hb, vm, vm, vm],
        out_specs=[vm] * 3 + [vm if inside else hb] * 2,
        scratch_shapes=scratch,
        compiler_params=pltpu.CompilerParams(
            collective_id=0, has_side_effects=True, vmem_limit_bytes=VMEM_LIMIT
        ),
        name="training_step",
    )(*tokens, negatives, *weights)


def outputs_kernel(layers, size, acts, g_in, vec, big, small, o_acts, o_in, o_attend, o_abias, o_merge, o_mbias,
                   o_expand, o_ebias, o_shrink, o_sbias, o_gain, o_shift, o_loss):
    width = vec.shape[1]
    local = small.shape[4]
    half = big.shape[4]
    group = lax.axis_index("dp") * lax.axis_size("rep") + lax.axis_index("rep")
    blocks = width // size
    own = pltpu.roll(vec[...], ((blocks - group) % blocks) * size, axis=1)[:, :size]
    o_acts[:, 0] = acts[...]
    o_in[:, 0] = g_in[...]
    for l in range(layers):
        for h in (0, 1):
            cols = slice(h * half, (h + 1) * half)
            o_shrink[l, :, cols] = big[l, 0, h]
            o_expand[l, :, cols] = big[l, 1, h]
        for j in range(3):
            o_attend[l, j] = small[l, j // 2, j % 2]
        o_merge[l] = small[l, 1, 1].T
        row = 7 * l
        o_gain[l] = own[row : row + 2]
        o_shift[l] = own[row + 2 : row + 4]
        o_sbias[l : l + 1] = own[row + 4 : row + 5]
        o_mbias[l : l + 1] = own[row + 5 : row + 6]
        o_ebias[l : l + 1] = vec[row + 6 : row + 7]
        o_abias[l] = vec[7 * layers + 2 * l : 7 * layers + 2 * l + 2, :local]
    o_loss[...] = vec[vec.shape[0] - 1 :, 0:1]


def run_outputs(acts, g_in, vec, big, small):
    micro, share, width = acts.shape
    layers, _, _, size, half = big.shape
    local = small.shape[4]
    shapes = [
        ((micro, 1, share, width), BF),
        ((micro, 1, share, width), BF),
        ((layers, 3, size, local), F32),
        ((layers, 2, local), F32),
        ((layers, local, size), F32),
        ((layers, size), F32),
        ((layers, size, 2 * half), F32),
        ((layers, width), F32),
        ((layers, size, 2 * half), F32),
        ((layers, size), F32),
        ((layers, 2, size), F32),
        ((layers, 2, size), F32),
        ((1, 1), F32),
    ]
    vm = pl.BlockSpec(memory_space=pltpu.VMEM)
    return pl.pallas_call(
        functools.partial(outputs_kernel, layers, size),
        out_shape=[jax.ShapeDtypeStruct(*s) for s in shapes],
        in_specs=[vm] * 5,
        out_specs=[vm] * len(shapes),
        compiler_params=pltpu.CompilerParams(vmem_limit_bytes=VMEM_LIMIT),
        name="outputs",
    )(acts, g_in, vec, big, small)


def per_device(
    query_tokens, query_drop, query_length, key_tokens, key_drop, key_length, negatives,
    attend_weight, attend_bias, merge_weight, merge_bias, expand_weight, expand_bias,
    shrink_weight, shrink_bias, norm_gain, norm_shift,
):
    micro = query_tokens.shape[0]
    weights = (
        jnp.transpose(attend_weight, (0, 1, 3, 4, 2)),
        attend_bias,
        merge_weight,
        merge_bias,
        expand_weight,
        expand_bias,
        shrink_weight,
        shrink_bias,
        norm_gain,
        norm_shift,
    )
    tokens = (query_tokens, query_drop, query_length.reshape(micro), key_tokens, key_drop, key_length.reshape(micro))
    groups = ("dp", "rep")
    inside = lax.axis_size("dp") == 4 and lax.axis_size("rep") == 2
    if not inside:
        negatives = lax.all_gather(negatives, ("rep", "tensor"), axis=0, tiled=True)
    acts, g_in, vec, g_big, g_small = run_step(inside, tokens, negatives, weights)
    if not inside:
        g_big = lax.psum_scatter(g_big, groups, scatter_dimension=3, tiled=True)
        g_small = lax.psum_scatter(g_small, groups, scatter_dimension=3, tiled=True)
        vec = lax.psum(vec, groups)
    outs = run_outputs(acts, g_in, vec, g_big, g_small)
    loss = outs[12].reshape(()) / (micro * lax.axis_size("dp") * lax.axis_size("rep"))
    return (
        outs[0], outs[1], jnp.transpose(outs[2], (0, 2, 1, 3)), *outs[3:8],
        jnp.transpose(outs[8], (0, 2, 1)), *outs[9:12], loss,
    )


def solution(mesh):
    return jax.shard_map(
        per_device,
        mesh=mesh,
        in_specs=(
            P(None, ("dp", "rep"), None, None),
            P(None, ("dp", "rep"), None),
            P(None, ("dp", "rep")),
            P(None, ("dp", "rep"), None, None),
            P(None, ("dp", "rep"), None),
            P(None, ("dp", "rep")),
            P(("rep", "tensor"), None),
            P(None, None, None, None, "tensor"),
            P(None, None, None, "tensor"),
            P(None, None, "tensor", None),
            P(),
            P(None, None, None, "tensor"),
            P(None, None, "tensor"),
            P(None, None, "tensor", None),
            P(),
            P(),
            P(),
        ),
        out_specs=(
            P(None, ("dp", "rep"), "tensor", None),
            P(None, ("dp", "rep"), "tensor", None),
            P(None, ("dp", "rep"), None, "tensor"),
            P(None, None, "tensor"),
            P(None, "tensor", ("dp", "rep")),
            P(None, ("dp", "rep")),
            P(None, ("dp", "rep"), "tensor"),
            P(None, "tensor"),
            P(None, "tensor", ("dp", "rep")),
            P(None, ("dp", "rep")),
            P(None, None, ("dp", "rep")),
            P(None, None, ("dp", "rep")),
            P(),
        ),
        check_vma=False,
    )
```

```python
import functools

import jax
import jax.numpy as jnp
from jax import lax
from jax.experimental import pallas as pl
from jax.experimental.pallas import tpu as pltpu
from jax.sharding import PartitionSpec as P

HEAD_DIM = 64
CROP_SLOTS = 256
SOFTMAX_WARMTH = 0.05
NORM_EPS = 1e-12
UNIT_EPS = 1e-06
MASKED = -1e30
TOP_PRECISION = lax.Precision.HIGHEST
ROOT_HALF = 0.7071067811865476
INV_ROOT_TAU = 0.3989422804014327

MESH = pl.DeviceIdType.MESH
BF = jnp.bfloat16
F32 = jnp.float32
CHUNKS = 8
LAG = 5
EARLY = 3
TILE = 64
VMEM_LIMIT = 62 * 1024 * 1024


def nn(a, b):
    return jnp.dot(a, b, preferred_element_type=F32)


def nt(a, b):
    return lax.dot_general(a, b, (((1,), (1,)), ((), ())), preferred_element_type=F32)


def tn(a, b):
    return lax.dot_general(a, b, (((0,), (0,)), ((), ())), preferred_element_type=F32)


class Line:
    def __init__(self, part, sbuf, tbuf, x1, x2, s_sem, t_sem, r1, r2):
        z = lax.axis_index("tensor")
        self.mid = (z + 1) // 2 == 1
        self.end = (z + 1) // 2 != 1
        self.lower = z // 2 == 0
        self.inner = 1 + z // 2
        self.outer = 3 * (z // 2)
        self.cross = 3 - z
        self.part, self.sbuf, self.tbuf, self.x1, self.x2 = part, sbuf, tbuf, x1, x2
        self.s_sem, self.t_sem, self.r1, self.r2 = s_sem, t_sem, r1, r2
        self.size = part.shape[1] // CHUNKS

    def rows(self, c):
        return pl.ds(pl.multiple_of(c * self.size, self.size), self.size)

    def near(self, c):
        return (c < CHUNKS // 2) == self.lower

    def outbound(self, c, narrow):
        return (c >= 0) if narrow is False else jnp.logical_not(narrow & self.near(c))

    def homebound(self, c, narrow):
        return (c >= 0) if narrow is False else jnp.logical_not(narrow) | self.near(c)

    def to_inner(self, s, c):
        return pltpu.make_async_remote_copy(
            src_ref=self.sbuf.at[s, self.rows(c)], dst_ref=self.x2.at[s, self.rows(c)],
            send_sem=self.s_sem.at[s, c], recv_sem=self.r2.at[s, c],
            device_id={"tensor": self.inner}, device_id_type=MESH)

    def to_cross(self, s, c, slot):
        return pltpu.make_async_remote_copy(
            src_ref=self.sbuf.at[s, self.rows(c)], dst_ref=self.x1.at[slot, s, self.rows(c)],
            send_sem=self.s_sem.at[s, c], recv_sem=self.r1.at[slot, s, c],
            device_id={"tensor": self.cross}, device_id_type=MESH)

    def to_outer(self, s, c, slot):
        return pltpu.make_async_remote_copy(
            src_ref=self.tbuf.at[s, self.rows(c)], dst_ref=self.x1.at[slot, s, self.rows(c)],
            send_sem=self.t_sem.at[s, c], recv_sem=self.r1.at[slot, s, c],
            device_id={"tensor": self.outer}, device_id_type=MESH)

    def begin(self, s, narrow=False):
        for c in range(CHUNKS):
            @pl.when(self.end & self.outbound(c, narrow))
            def _():
                rows = self.rows(c)
                self.sbuf[s, rows] = self.part[s, rows].astype(BF)
                self.to_inner(s, c).start()

    def inward(self, s, c, slot, live, narrow=False):
        @pl.when(self.mid & live & self.outbound(c, narrow))
        def _():
            rows = self.rows(c)
            self.to_inner(s, c).wait_recv()
            self.sbuf[s, rows] = (self.part[s, rows] + self.x2[s, rows].astype(F32)).astype(BF)
            self.to_cross(s, c, slot).start()

    def outward(self, s, c, slot, live, narrow=False):
        @pl.when(self.mid & live & self.homebound(c, narrow))
        def _():
            rows = self.rows(c)
            self.to_cross(s, c, slot).wait_recv()
            joint = self.part[s, rows] + self.x1[slot, s, rows].astype(F32)
            self.part[s, rows] = joint + self.x2[s, rows].astype(F32)
            self.tbuf[s, rows] = joint.astype(BF)
            self.to_outer(s, c, slot).start()

    def settle(self, s, slot, tile, narrow=False):
        per = TILE // self.size
        for d in range(per):
            c = tile * per + d

            @pl.when(self.end & self.homebound(c, narrow))
            def _():
                rows = self.rows(c)
                self.to_outer(s, c, slot).wait_recv()
                self.part[s, rows] = self.part[s, rows] + self.x1[slot, s, rows].astype(F32)

    def release(self, s, slot, narrow=False):
        for c in range(CHUNKS):
            @pl.when(self.end & self.outbound(c, narrow))
            def _():
                self.to_inner(s, c).wait_send()

            @pl.when(self.mid & self.outbound(c, narrow))
            def _():
                self.to_cross(s, c, slot).wait_send()

            @pl.when(self.mid & self.homebound(c, narrow))
            def _():
                self.to_outer(s, c, slot).wait_send()


def line_scratch(streams, rows, width):
    return [
        pltpu.VMEM((streams, rows, width), F32),
        pltpu.VMEM((streams, rows, width), BF),
        pltpu.VMEM((streams, rows, width), BF),
        pltpu.VMEM((2, streams, rows, width), BF),
        pltpu.VMEM((streams, rows, width), BF),
        pltpu.SemaphoreType.DMA((streams, CHUNKS)),
        pltpu.SemaphoreType.DMA((streams, CHUNKS)),
        pltpu.SemaphoreType.DMA((2, streams, CHUNKS)),
        pltpu.SemaphoreType.DMA((streams, CHUNKS)),
    ]


def tiles(rows, body, ready=None):
    def step(c, carry):
        if ready is not None:
            ready(c)
        body(pl.ds(pl.multiple_of(c * TILE, TILE), TILE))
        return carry

    lax.fori_loop(0, rows // TILE, step, 0)


def normalize(total, gain, shift):
    mean = jnp.mean(total, axis=-1, keepdims=True)
    centered = total - mean
    inverse = lax.rsqrt(jnp.mean(centered * centered, axis=-1, keepdims=True) + NORM_EPS)
    normed = centered * inverse
    return normed * gain + shift, normed, inverse


def head_masks(width, scale):
    lane = lax.broadcasted_iota(jnp.int32, (1, width), 1)
    return [
        jnp.where((lane >= h * HEAD_DIM) & (lane < (h + 1) * HEAD_DIM), scale, 0.0).astype(BF)
        for h in range(width // HEAD_DIM)
    ]


def norm_back(g, normed, inverse, gain):
    scaled = g * gain
    return inverse * (
        scaled
        - jnp.mean(scaled, axis=-1, keepdims=True)
        - normed * jnp.mean(scaled * normed, axis=-1, keepdims=True)
    )


def fold(x):
    return jnp.sum(x.reshape(x.shape[0] // 8, 8, x.shape[1]), axis=0)


class Plane:
    def __init__(self, grads, sends, spots, recvs, out, send_sem, recv_sem, credit):
        dp, self.x = lax.axis_index("dp"), lax.axis_index("rep")
        self.y, self.c = dp // 2, dp % 2
        self.partner = {
            "c": {"dp": dp + 1 - 2 * self.c},
            "x": {"rep": 1 - self.x},
            "y": {"dp": (dp + 2) % 4},
        }
        self.grads, self.sends, self.places, self.recvs, self.out = grads, sends, spots, recvs, out
        self.send_sem, self.recv_sem, self.credit = send_sem, recv_sem, credit
        self.block = grads.shape[2] // 8

    def message(self, u, stage, half, rows):
        if self.places is None:
            return self.sends[stage].at[u, half, rows]
        row, lane = self.places[stage]
        start = half * (self.grads.shape[2] // 2) + row
        return self.sends.at[u, pl.ds(start + rows.start, rows.size), pl.ds(lane, self.grads.shape[3])]

    def copy(self, u, stage, half):
        way = ("c", "xy"[half], "yx"[half])[stage]
        return pltpu.make_async_remote_copy(
            src_ref=self.message(u, stage, half, pl.ds(0, self.recvs[stage].shape[2])), dst_ref=self.recvs[stage].at[u, half],
            send_sem=self.send_sem.at[u, stage, half], recv_sem=self.recv_sem.at[u, stage, half],
            device_id=self.partner[way], device_id_type=MESH)

    def spots(self, stage, half, own):
        pick = (lambda v: v) if own else (lambda v: 1 - v)
        if stage == 0:
            return [(4 * y + 2 * pick(self.c), 2 * y, 2) for y in (0, 1)]
        if stage == 1 and half == 0:
            return [(4 * y + 2 * self.c + pick(self.x), y, 1) for y in (0, 1)]
        if stage == 1:
            return [(4 * pick(self.y) + 2 * self.c, 0, 2)]
        if half == 0:
            return [(4 * pick(self.y) + 2 * self.c + self.x, 0, 1)]
        return [(4 * self.y + 2 * self.c + pick(self.x), 0, 1)]

    def parts(self, stage, half, own):
        for here, there, blocks in self.spots(stage, half, own):
            for b in range(blocks):
                start = (here + b) * self.block
                yield pl.ds(pl.multiple_of(start, 8), self.block), pl.ds((there + b) * self.block, self.block)

    def send(self, u, stage, live, spend):
        @pl.when(live)
        def _():
            for half in (0, 1):
                for here, there in self.parts(stage, half, False):
                    self.message(u, stage, half, there)[...] = self.grads[u, half, here].astype(BF)

            @pl.when(spend)
            def _():
                pl.semaphore_wait(self.credit.at[u, stage], 2)

            for half in (0, 1):
                self.copy(u, stage, half).start()

    def take(self, u, stage, live, give, layer):
        @pl.when(live)
        def _():
            for half in (0, 1):
                self.copy(u, stage, half).wait()
                for here, there in self.parts(stage, half, True):
                    total = self.grads[u, half, here] + self.recvs[stage][u, half, there].astype(F32)
                    if stage == 2:
                        self.out[layer, u, half] = total
                    else:
                        self.grads[u, half, here] = total

            @pl.when(give)
            def _():
                for half in (0, 1):
                    way = ("c", "xy"[half], "yx"[half])[stage]
                    pl.semaphore_signal(
                        self.credit.at[u, stage], inc=1, device_id=self.partner[way], device_id_type=MESH
                    )


def greet(inside):
    z, dp, rep = lax.axis_index("tensor"), lax.axis_index("dp"), lax.axis_index("rep")
    sem = pltpu.get_barrier_semaphore()
    others = [{"tensor": (z + d) % 4} for d in (1, 2, 3)]
    if inside:
        others += [{"rep": 1 - rep, "tensor": (z + d) % 4} for d in (0, 1, 2, 3)]
        others += [{"dp": dp + 1 - 2 * (dp % 2)}, {"dp": (dp + 2) % 4}]
    for other in others:
        pl.semaphore_signal(sem, inc=1, device_id=other, device_id_type=MESH)
    pl.semaphore_wait(sem, len(others))


class Contrast:
    def __init__(self, inside, micro, pooled, keys, pgrad, vec, state, bufs):
        self.inside, self.micro, self.pooled, self.keys = inside, micro, pooled, keys
        self.pgrad, self.vec, self.state = pgrad, vec, state
        self.z, self.rep = lax.axis_index("tensor"), lax.axis_index("rep")
        if inside:
            (self.asks, self.asked, self.reply, self.heard, self.ask_sem, self.reply_sem, self.heard_sem) = bufs
        else:
            (self.source, self.key_sem) = bufs

    def question(self, m):
        return pltpu.make_async_remote_copy(
            src_ref=self.asks.at[m], dst_ref=self.asked.at[m], send_sem=self.ask_sem.at[m, 0],
            recv_sem=self.ask_sem.at[m, 1], device_id={"rep": 1 - self.rep}, device_id_type=MESH)

    def tell(self, m, which, d):
        other = {"tensor": (self.z + d) % 4}
        if which == 1:
            other["rep"] = 1 - self.rep
        k = which * 4 + d
        return pltpu.make_async_remote_copy(
            src_ref=self.reply.at[m, which], dst_ref=self.heard.at[m, k], send_sem=self.reply_sem.at[m, k],
            recv_sem=self.heard_sem.at[m, k], device_id=other, device_id_type=MESH)

    def score(self, rows_now):
        keys = self.keys[...]
        logits = nt(rows_now, keys) / SOFTMAX_WARMTH
        top = jnp.max(logits, axis=-1, keepdims=True)
        expo = jnp.exp(logits - top)
        total = jnp.sum(expo, axis=-1, keepdims=True)
        high = expo.astype(BF)
        rest = expo - high.astype(F32)
        mid = rest.astype(BF)
        tiny = (rest - mid.astype(F32)).astype(BF)
        weighted = nn(jnp.concatenate([high, mid, tiny], axis=0), keys)
        n = rows_now.shape[0]
        return weighted[:n] + weighted[n : 2 * n] + weighted[2 * n :], top, total

    def ask(self, m):
        count = self.pooled[self.micro + m, 1:2]
        mean = self.pooled[self.micro + m, 0:1] / count
        scale = lax.rsqrt(jnp.sum(mean * mean, axis=-1, keepdims=True) + UNIT_EPS)
        direction = mean * scale
        self.state[m, 0:1] = direction
        self.state[m, 1:2] = jnp.broadcast_to(scale, count.shape)
        self.state[m, 2:3] = count
        if self.inside:
            self.asks[m] = jnp.broadcast_to(direction, self.asks.shape[1:]).astype(BF)
            self.question(m).start()

    def respond(self, m):
        if self.inside:
            self.question(m).wait()
            half = lax.broadcasted_iota(jnp.int32, self.asks.shape[1:], 0) < 8
            weighted, top, total = self.score(jnp.where(half, self.asks[m], self.asked[m]))
            wide = (1, weighted.shape[1])
            for which in (0, 1):
                row = slice(8 * which, 8 * which + 1)
                self.reply[m, which, 0:1] = weighted[row]
                self.reply[m, which, 1:2] = jnp.broadcast_to(top[row], wide)
                self.reply[m, which, 2:3] = jnp.broadcast_to(total[row], wide)
            for d in (0, 1, 2, 3):
                self.tell(m, 1, d).start()
            for d in (1, 2, 3):
                self.tell(m, 0, d).start()

    def close(self, m, pooled_key):
        direction, scale, count = self.state[m, 0:1], self.state[m, 1:2, 0:1], self.state[m, 2:3]
        mean = pooled_key / self.pooled[m, 1:2]
        key_dir = mean * lax.rsqrt(jnp.sum(mean * mean, axis=-1, keepdims=True) + UNIT_EPS)
        positive = jnp.sum(direction * key_dir, axis=-1, keepdims=True) / SOFTMAX_WARMTH
        if self.inside:
            for k in range(1, 8):
                self.tell(m, k // 4, k % 4).wait()
            everyone = [self.reply[m, 0]] + [self.heard[m, k] for k in range(1, 8)]
            best = positive
            for one in everyone:
                best = jnp.maximum(best, one[1:2, 0:1])
            own = jnp.exp(positive - best)
            total, keys = own, own * key_dir
            for one in everyone:
                weight = jnp.exp(one[1:2, 0:1] - best)
                total = total + weight * one[2:3, 0:1]
                keys = keys + weight * one[0:1]
        else:
            rows_now = jnp.broadcast_to(direction, (16, direction.shape[1])).astype(BF)

            def piece(c, carry):
                best, total, keys = carry
                size = self.keys.shape[0]
                copy = pltpu.make_async_copy(
                    self.source.at[pl.ds(pl.multiple_of(c * size, size), size)], self.keys, self.key_sem)
                copy.start()
                copy.wait()
                weighted, top, part = (v[0:1] for v in self.score(rows_now))
                now = jnp.maximum(best, top)
                old, new = jnp.exp(best - now), jnp.exp(top - now)
                return now, total * old + part * new, keys * old + weighted * new

            start = (positive, jnp.ones_like(positive), key_dir)
            best, total, keys = lax.fori_loop(0, self.source.shape[0] // self.keys.shape[0], piece, start)
        loss = best + jnp.log(total) - positive
        last = self.vec.shape[0] - 1
        self.vec[last : last + 1] += jnp.broadcast_to(loss, direction.shape)
        dqn = (keys / total - key_dir) * (CROP_SLOTS / SOFTMAX_WARMTH)
        mean_grad = scale * (dqn - direction * jnp.sum(direction * dqn, axis=-1, keepdims=True))
        self.pgrad[m, 0:1] = mean_grad / count
        self.pgrad[m, 1:2] = count


def step_kernel(inside, *refs):
    q_tok, q_drop, q_len, k_tok, k_drop, k_len, negs, *refs = refs
    wqkv_in, abias, wm_in, mbias, we_in, ebias, ws_in, sbias, gains, shifts, *refs = refs
    acts, g_in, vec, out_big, out_small, *refs = refs
    xin, proj, probs, mixed, n1, first, slope, active, n2, inv, *refs = refs
    wqkv, wm, we, ws, tok, h, hb, qkv, mx, inner, *refs = refs
    vbias, valid, vecs, slots, pooled, state, pgrad, g_vec, g_abias, g_big, g_small, *refs = refs
    load_sem, tok_sem, kpart, kheard, kp_sem, kh_sem, *refs = refs
    line = Line(*refs[:9])
    part, sbuf, tbuf = refs[:3]
    refs = refs[9:]
    stored, loaded = (wqkv_in, wm_in, we_in, ws_in), (wqkv, wm, we, ws)
    micro = q_tok.shape[0]
    rows, width = q_tok.shape[2:]
    layers = we.shape[1]
    local = wm.shape[2]
    half_units = we.shape[3] // 2
    heads = local // HEAD_DIM
    streams = 2 * micro
    third = width // 3
    z = lax.axis_index("tensor")
    share = rows // lax.axis_size("tensor")
    own_rows = pl.ds(pl.multiple_of(z * share, 16), share)

    def load(k, e, layer):
        return pltpu.make_async_copy(stored[k].at[e, layer], loaded[k].at[e, layer], load_sem.at[k, e, layer])

    def load_tokens(s):
        source = k_tok if s < micro else q_tok
        return pltpu.make_async_copy(source.at[s % micro, 0], tok.at[pl.ds(s * rows, rows)], tok_sem.at[s])

    def load_keys():
        return pltpu.make_async_copy(negs, tok, tok_sem.at[streams])

    for layer in range(layers):
        for e in (1, 0):
            for k in (0, 1):
                load(k, e, layer).start()
            if layer == 0:
                for s in range((1 - e) * micro, (2 - e) * micro):
                    load_tokens(s).start()
            for k in (2, 3):
                load(k, e, layer).start()
    vec[...] = jnp.zeros_like(vec)
    g_vec[...] = jnp.zeros_like(g_vec)
    g_abias[...] = jnp.zeros_like(g_abias)
    for e in range(2):
        for layer in range(layers):
            for row, ref in enumerate((mbias, ebias, sbias)):
                vecs[e, layer, row : row + 1] = ref[e, layer : layer + 1].astype(F32)
            vecs[e, layer, 3:5] = gains[e, layer].astype(F32)
            vecs[e, layer, 5:7] = shifts[e, layer].astype(F32)
    greet(inside)

    if inside:
        turn, e1, e2, e3, t1, t2, t3, d1, d2, d3, big_s, big_r, small_s, small_r, big_c, small_c, v_rcv, v_send, v_recv, *bufs = refs
        w_big, quarter = half_units, width // 4
        big = Plane(g_big, we.at[1], ((0, 0), (0, w_big), (quarter, w_big)), (e1, e2, e3), out_big, big_s, big_r, big_c)
        small = Plane(g_small, (d1, d2, d3), None, (t1, t2, t3), out_small, small_s, small_r, small_c)
    else:
        g_sem, key_sem = refs
        bufs = (negs, key_sem)
    last_f = 2 * layers * streams

    def at_f(i):
        j = jnp.maximum(i, 0)
        s, stage = j % streams, j // streams
        return s, stage % 2, (i >= 0) & (i < last_f), (stage == 2 * layers - 1) & (s < micro)

    def tick_f(i, *which):
        for c in which:
            s, slot, live, narrow = at_f(i - 1)
            line.inward(s, c, slot, live, narrow)
            if c < LAG:
                s, slot, live, narrow = at_f(i - 2)
            line.outward(s, (c - LAG) % CHUNKS, slot, live, narrow)

    def compact(drop, length, is_q, s, m):
        pos = lax.broadcasted_iota(jnp.int32, (1, rows), 1)
        kept = (pos < length) & ((drop[m] == 0) | (pos == 0))
        kept_f = jnp.broadcast_to(jnp.where(kept, 1.0, 0.0), (16, rows))
        down = lax.broadcasted_iota(jnp.int32, (rows, rows), 0)
        along = lax.broadcasted_iota(jnp.int32, (rows, rows), 1)
        tri = jnp.where(down <= along, 1.0, 0.0).astype(BF)
        order = nn(kept_f.astype(BF), tri)[0:1] - 1.0
        order = jnp.where(kept, order, -1.0)
        count = jnp.sum(kept_f[0:1], axis=-1, keepdims=True)
        pick = jnp.where(order == down.astype(F32), 1.0, 0.0).astype(BF)
        rows_now = nn(pick, tok[pl.ds(pl.multiple_of(s * rows, rows), rows)])
        h[s] = rows_now
        hb[...] = rows_now.astype(BF)
        fits = pos.astype(F32) < count
        vbias[s] = jnp.broadcast_to(jnp.where(fits, 0.0, MASKED), (8, rows))
        if not is_q:
            fits = fits & line.end & ((pos < rows // 2) == line.lower)
        valid[s] = jnp.broadcast_to(jnp.where(fits, 1.0, 0.0), (8, rows))
        pooled[s, 1:2] = jnp.broadcast_to(count, (1, width))
        if is_q:
            slots[m] = jnp.broadcast_to(order, (8, rows))

    def second_norm(lp, e, s, narrow):
        m, is_q = s % micro, s >= micro
        bias, gain, shift = vecs[e, lp, 2:3], vecs[e, lp, 4:5], vecs[e, lp, 6:7]

        def norm(r):
            out, normed, inverse = normalize(h[s, r] + part[s, r] + bias, gain, shift)
            h[s, r] = out
            hb[r] = out.astype(BF)

            @pl.when(is_q)
            def _():
                n2[lp, m, r] = normed.astype(BF)
                inv[lp, m, r, 64:128] = jnp.broadcast_to(inverse, (TILE, 64))

        tiles(rows, norm, lambda t: line.settle(s, 1, t, narrow))
        line.release(s, 1, narrow)

    def attention_pass(layer, s):
        i = layer * 2 * streams + s
        e, m = 1 - s // micro, s % micro
        is_q = s >= micro
        tick_f(i, 0)

        @pl.when(layer == 0)
        def _():
            @pl.when(s < micro)
            def _():
                pltpu.make_async_copy(k_tok.at[m, 0], tok.at[pl.ds(0, rows)], tok_sem.at[s]).wait()
                compact(k_drop, k_len[m], False, s, m)

            @pl.when(is_q)
            def _():
                pltpu.make_async_copy(q_tok.at[m, 0], tok.at[pl.ds(0, rows)], tok_sem.at[s]).wait()
                compact(q_drop, q_len[m], True, s, m)

        @pl.when(layer > 0)
        def _():
            second_norm(layer - 1, e, s, False)

        tick_f(i, 1, 2)

        @pl.when(m == 0)
        def _():
            for k in (0, 1):
                load(k, e, layer).wait()

        @pl.when(is_q)
        def _():
            xin[layer, m] = hb[...]

        rows_now = hb[...]
        for j in range(3):
            bias = 0.0 if j == 1 else abias[e, layer, j // 2 : j // 2 + 1].astype(F32)
            qkv[j] = (nt(rows_now, wqkv[e, layer, j]) + bias).astype(BF)

        @pl.when(is_q)
        def _():
            for j in range(3):
                proj[layer, m, j] = qkv[j]

        tick_f(i, 3)
        q_masks = head_masks(local, HEAD_DIM**-0.5)
        v_masks = head_masks(local, 1.0)
        for hd in range(heads):
            scores = nt(qkv[0] * q_masks[hd], qkv[1]) + vbias[s, 0:1]
            expo = jnp.exp(scores - jnp.max(scores, axis=-1, keepdims=True))
            chance = (expo / jnp.sum(expo, axis=-1, keepdims=True)).astype(BF)

            @pl.when(is_q)
            def _():
                probs[layer, m, hd] = chance

            out = nn(chance, qkv[2] * v_masks[hd])
            if hd == 0:
                mx[...] = out
            else:
                mx[...] += out
            tick_f(i, 4 + hd)
        if inside:
            @pl.when((i == 1) & (big.c == 0) & line.end)
            def _():
                pl.semaphore_signal(turn, inc=1, device_id=big.partner["c"], device_id_type=MESH)

        mixed_now = mx[...].astype(BF)

        @pl.when(is_q)
        def _():
            mixed[layer, m] = mixed_now

        part[s] = nn(mixed_now, wm[e, layer])
        if inside:
            @pl.when((i == 0) & (big.c == 1) & line.end)
            def _():
                pl.semaphore_wait(turn, 1)

        line.begin(s)
        tick_f(i, *range(4 + heads, CHUNKS))

    def forward_pass(layer, s):
        i = (layer * 2 + 1) * streams + s
        e, m = 1 - s // micro, s % micro
        is_q = s >= micro
        tick_f(i, 0, 1)
        bias, gain, shift = vecs[e, layer, 0:1], vecs[e, layer, 3:4], vecs[e, layer, 5:6]

        def norm(r):
            out, normed, inverse = normalize(h[s, r] + part[s, r] + bias, gain, shift)
            h[s, r] = out
            hb[r] = out.astype(BF)

            @pl.when(is_q)
            def _():
                n1[layer, m, r] = normed.astype(BF)
                inv[layer, m, r, 0:64] = jnp.broadcast_to(inverse, (TILE, 64))
                first[layer, m, r] = out.astype(BF)

        tiles(rows, norm, lambda t: line.settle(s, 0, t))
        line.release(s, 0)

        @pl.when(m == 0)
        def _():
            for k in (2, 3):
                load(k, e, layer).wait()

        tick_f(i, 2, 3)
        inner[...] = nn(hb[...], we[e, layer])
        tick_f(i, 4)
        bias_e = vecs[e, layer, 1:2]

        def gelu(r):
            u = inner[r] + bias_e
            phi = 0.5 * (1.0 + lax.erf(u * ROOT_HALF))
            out = (u * phi).astype(BF)
            tbuf[s, r] = out

            @pl.when(is_q)
            def _():
                active[layer, m, r] = out
                slope[layer, m, r] = (phi + u * jnp.exp(-0.5 * u * u) * INV_ROOT_TAU).astype(BF)

        tiles(rows, gelu)
        tick_f(i, 5, 6)
        part[s] = nn(tbuf[s], ws[e, layer])
        line.begin(s, (layer == layers - 1) & (s < micro))
        tick_f(i, 7)

    def layer_step(layer, carry):
        def a_step(s, c):
            attention_pass(layer, s)
            return c

        def f_step(s, c):
            forward_pass(layer, s)
            return c

        lax.fori_loop(0, streams, a_step, 0)
        if inside:
            @pl.when(layer == 0)
            def _():
                load_keys().start()

        lax.fori_loop(0, streams, f_step, 0)
        return carry

    lax.fori_loop(0, layers, layer_step, 0)

    def pool(s):
        return jnp.dot(valid[s], h[s], precision=TOP_PRECISION, preferred_element_type=F32)

    def kshare(m, d):
        return pltpu.make_async_remote_copy(
            src_ref=kpart.at[m], dst_ref=kheard.at[z // 3, m], send_sem=kp_sem.at[m, d - 1],
            recv_sem=kh_sem.at[z // 3, m], device_id={"tensor": (z + d) % 4}, device_id_type=MESH)

    def last_key(m):
        second_norm(layers - 1, 1, m, line.part.shape[0] > 0)
        kpart[m] = pool(m)

        @pl.when(line.end)
        def _():
            for d in (1, 2, 3):
                kshare(m, d).start()

    def last_query(m):
        second_norm(layers - 1, 0, micro + m, False)
        pooled[micro + m, 0:1] = pool(micro + m)[0:1]
        acts[m] = hb[own_rows]

    def pooled_key(m):
        @pl.when(line.end)
        def _():
            for d in (1, 2, 3):
                kshare(m, d).wait_send()

        total = kpart[m, 0:1]
        for e in (0, 1):
            @pl.when(z != 3 * e)
            def _():
                pltpu.make_async_remote_copy(
                    src_ref=kpart.at[m], dst_ref=kheard.at[e, m], send_sem=kp_sem.at[m, 0],
                    recv_sem=kh_sem.at[e, m], device_id={"tensor": 3 - z}, device_id_type=MESH).wait_recv()

            total = total + jnp.where(z != 3 * e, kheard[e, m, 0:1], 0.0)
        return total

    queue = Contrast(inside, micro, pooled, tok, pgrad, vec, state, bufs)
    tick_f(last_f, 0, 1, 2)
    for m in range(micro):
        last_key(m)
        tick_f(last_f, 3 + m)
    if inside:
        load_keys().wait()
    for m in range(micro):
        if m == micro - 1:
            tick_f(last_f, *range(3 + micro, CHUNKS))
            tick_f(last_f + 1, *range(LAG))
        if m > 0:
            queue.respond(m - 1)
        last_query(m)
        queue.ask(m)

    last_b = 2 * layers * micro
    dinner = tbuf.at[1]
    heads_f = [h.at[0, :, pl.ds(j * third, local)] for j in range(3)]
    heads_b = [tbuf.at[0, :, pl.ds(j * third, local)] for j in range(3)]

    def at_b(i):
        j = jnp.maximum(i, 0)
        return micro + j % micro, (j // micro) % 2, (i >= 0) & (i < last_b)

    def tick(i, *which):
        for g in which:
            s, slot, live = at_b(i - 1)
            if g >= 1 and g - 1 < CHUNKS:
                line.outward(s, g - 1, slot, live)
            c = g + EARLY
            if c >= CHUNKS + 1:
                s, slot, live = at_b(i)
                c -= CHUNKS + 1
                if c < EARLY:
                    line.inward(s, c, slot, live)
            elif c < CHUNKS:
                line.inward(s, c, slot, live)

    def drained(large, layer, u, half):
        source, target = (g_big, out_big) if large else (g_small, out_small)
        return pltpu.make_async_copy(source.at[u, half], target.at[layer, u, half], g_sem.at[0 if large else 1, u, half])

    def add_to(large, u, half, s, value):
        ref = (g_big if large else g_small).at[u, half]

        @pl.when(s == 0)
        def _():
            ref[...] = value

        @pl.when(s > 0)
        def _():
            ref[...] += value

    def plane(what, large, stage, live, step):
        for u in (0, 1):
            if inside:
                group = big if large else small
                if what == "send":
                    group.send(u, stage, live, step > 0)
                else:
                    group.take(u, stage, live, step < layers - 1, layers - 1 - step)
            elif (what, stage) in (("send", 0), ("take", 2)):
                @pl.when(live)
                def _():
                    for half in (0, 1):
                        copy = drained(large, layers - 1 - step, u, half)
                        copy.start() if what == "send" else copy.wait()

    def mlp_back(step, m):
        layer = layers - 1 - step
        i = step * 2 * micro + m
        s = micro + m
        low = sbuf.at[m]

        @pl.when(step == 0)
        def _():
            queue.close(m, pooled_key(m))

            def begin(c, carry):
                r = pl.ds(pl.multiple_of(c * TILE, TILE), TILE)
                pos = (lax.broadcasted_iota(jnp.int32, (TILE, 1), 0) + c * TILE).astype(F32)
                part[s, r] = jnp.where(pos < pgrad[m, 1:2, 0:1], pgrad[m, 0:1], 0.0)
                h[s, r] = jnp.zeros((TILE, width), F32)
                return carry

            lax.fori_loop(0, rows // TILE, begin, 0)

        gain = vecs[0, layer, 4:5]

        def back(r):
            g = part[s, r] + h[s, r]
            normed = n2[layer, m, r].astype(F32)
            out = norm_back(g, normed, inv[layer, m, r][:, 64:65], gain)
            h[s, r] = out
            low[r] = out.astype(BF)
            g_vec[layer, 1] += fold(g * normed)
            g_vec[layer, 3] += fold(g)
            g_vec[layer, 4] += fold(out)

        def ready(t):
            @pl.when(step > 0)
            def _():
                line.settle(s, 1, t)

        tiles(rows, back, ready)

        @pl.when(step > 0)
        def _():
            line.release(s, 1)

        tick(i, 0)
        inner[...] = nt(low[...], ws[0, layer])

        @pl.when((step == 0) & (m == 0))
        def _():
            queue.respond(micro - 1)

        tick(i, 1)

        def slopes(r):
            out = inner[r] * slope[layer, m, r].astype(F32)
            dinner[r] = out.astype(BF)
            g_vec[layer, 6] += fold(out)

        tiles(rows, slopes)
        tick(i, 2)
        part[s] = nt(dinner[...], we[0, layer])
        line.begin(s)
        tick(i, 3)

        plane("take", True, 2, (step > 0) & (m == 0), step - 1)
        plane("take", False, 0, (step > 0) & (m == 0), step - 1)
        plane("send", False, 1, (step > 0) & (m == 0), step - 1)
        for half in (0, 1):
            cols = pl.ds(half * half_units, half_units)
            add_to(True, 0, half, m, tn(low[...], active[layer, m, :, cols]))
            tick(i, 4 + half)
        for half in (0, 1):
            cols = pl.ds(half * half_units, half_units)
            add_to(True, 1, half, m, tn(first[layer, m], dinner[:, cols]))
            tick(i, 6 + half)
        plane("send", True, 0, m == micro - 1, step)
        plane("take", False, 1, (step > 0) & (m == micro - 1), step - 1)
        plane("send", False, 2, (step > 0) & (m == micro - 1), step - 1)
        tick(i, CHUNKS)

    def attention_back(step, m):
        layer = layers - 1 - step
        i = (step * 2 + 1) * micro + m
        s = micro + m
        low = sbuf.at[m]
        gain = vecs[0, layer, 3:4]

        def back(r):
            g = part[s, r] + h[s, r]
            normed = n1[layer, m, r].astype(F32)
            out = norm_back(g, normed, inv[layer, m, r][:, 0:1], gain)
            h[s, r] = out
            low[r] = out.astype(BF)
            g_vec[layer, 0] += fold(g * normed)
            g_vec[layer, 2] += fold(g)
            g_vec[layer, 5] += fold(out)

        tiles(rows, back, lambda t: line.settle(s, 0, t))
        line.release(s, 0)
        tick(i, 0)
        dmix = nt(low[...], wm[0, layer]).astype(BF)
        tick(i, 1)
        masks = head_masks(local, 1.0)
        for hd in range(heads):
            chance_b = probs[layer, m, hd]
            chance = chance_b.astype(F32)
            dm = dmix * masks[hd]
            dch = nt(dm, proj[layer, m, 2])
            ds = chance * (dch - jnp.sum(chance * dch, axis=-1, keepdims=True))
            draw = (ds * HEAD_DIM**-0.5).astype(BF)
            dq = nn(draw, proj[layer, m, 1] * masks[hd])
            dk = tn(draw, proj[layer, m, 0] * masks[hd])
            dv = tn(chance_b, dm)
            for ref, value in zip(heads_f, (dq, dk, dv)):
                if hd == 0:
                    ref[...] = value
                else:
                    ref[...] += value
            tick(i, 2 + hd)
        g_abias[layer, 0] += fold(heads_f[0][...])
        g_abias[layer, 1] += fold(heads_f[2][...])
        for j in range(3):
            heads_b[j][...] = heads_f[j][...].astype(BF)
        part[s] = sum(nn(heads_b[j][...], wqkv[0, layer, j]) for j in range(3))
        line.begin(s)
        tick(i, *range(2 + heads, 6))
        plane("take", True, 0, m == 0, step)
        plane("send", True, 1, m == 0, step)
        plane("take", True, 1, m == micro - 1, step)
        plane("send", True, 2, m == micro - 1, step)
        plane("take", False, 2, (step > 0) & (m == 0), step - 1)
        for j in range(3):
            add_to(False, j // 2, j % 2, m, tn(xin[layer, m], heads_b[j][...]))
        tick(i, 6)
        add_to(False, 1, 1, m, tn(low[...], mixed[layer, m]))
        tick(i, 7, CHUNKS)
        plane("send", False, 0, m == micro - 1, step)

    def back_step(step, carry):
        def m_step(m, c):
            mlp_back(step, m)
            return c

        def a_step(m, c):
            attention_back(step, m)
            return c

        lax.fori_loop(0, micro, m_step, 0)
        lax.fori_loop(0, micro, a_step, 0)
        return carry

    lax.fori_loop(0, layers, back_step, 0)

    for layer in range(layers):
        for k in range(7):
            vec[layer * 7 + k : layer * 7 + k + 1] = jnp.sum(g_vec[layer, k], axis=0, keepdims=True)
        for k in range(2):
            row = layers * 7 + layer * 2 + k
            vec[row : row + 1, 0:local] = jnp.sum(g_abias[layer, k], axis=0, keepdims=True)

    def vec_copy(stage):
        return pltpu.make_async_remote_copy(
            src_ref=vec, dst_ref=v_rcv.at[stage], send_sem=v_send.at[stage], recv_sem=v_recv.at[stage],
            device_id=big.partner["cxy"[stage]], device_id_type=MESH)

    def vec_take(stage):
        if inside:
            vec_copy(stage).wait()
            vec[...] += v_rcv[stage]

    def vec_send(stage):
        if inside:
            vec_copy(stage).start()

    final = layers - 1
    vec_send(0)
    tick(last_b, 0, 1)
    plane("take", False, 0, True, final)
    plane("send", False, 1, True, final)
    vec_take(0)
    vec_send(1)
    tick(last_b, 2, 3, 4)
    plane("take", True, 2, True, final)
    tick(last_b, 5, 6)
    plane("take", False, 1, True, final)
    plane("send", False, 2, True, final)
    vec_take(1)
    vec_send(2)
    tick(last_b, 7, CHUNKS)

    def finish(m, carry):
        s = micro + m
        low = sbuf.at[m]

        def back(r):
            low[r] = (part[s, r] + h[s, r]).astype(BF)

        tiles(rows, back, lambda t: line.settle(s, 1, t))
        line.release(s, 1)
        down = lax.broadcasted_iota(jnp.int32, (rows, rows), 0).astype(F32)
        pick = jnp.where(slots[m, 0:1] == down, 1.0, 0.0).astype(BF)
        low[...] = tn(pick, low[...]).astype(BF)
        g_in[m] = low[own_rows]
        return carry

    lax.fori_loop(0, micro, finish, 0)
    plane("take", False, 2, True, final)
    vec_take(2)


def run_step(inside, tokens, negatives, weights):
    q_tok = tokens[0]
    micro, _, rows, width = q_tok.shape
    wqkv, abias, wm, mbias, we, ebias, ws, sbias, gains, shifts = weights
    layers, local, units = we.shape[1], wm.shape[2], we.shape[3]
    heads = local // HEAD_DIM
    streams = 2 * micro
    share = rows // lax.axis_size("tensor")
    lm = (layers, micro)
    tall = 8 * ((9 * layers + 2 + 7) // 8)
    kinds = (units // 2, local)
    high = width // 8 if inside else width
    shapes = [((micro, share, width), BF), ((micro, share, width), BF), ((tall, width), F32)]
    shapes += [((layers, 2, 2, high, w), F32) for w in kinds]
    vm = pl.BlockSpec(memory_space=pltpu.VMEM)
    hb = pl.BlockSpec(memory_space=pl.ANY)
    sm = pl.BlockSpec(memory_space=pltpu.SMEM)
    dma = pltpu.SemaphoreType.DMA
    v = pltpu.VMEM
    scratch = [
        v(lm + (rows, width), BF),
        v(lm + (3, rows, local), BF),
        v(lm + (heads, rows, rows), BF),
        v(lm + (rows, local), BF),
        v(lm + (rows, width), BF),
        v(lm + (rows, width), BF),
        v(lm + (rows, units), BF),
        v(lm + (rows, units), BF),
        v(lm + (rows, width), BF),
        v(lm + (rows, 128), F32),
    ]
    scratch += [v(w.shape, BF) for w in (wqkv, wm, we, ws)]
    scratch += [
        v((streams * rows, width), BF),
        v((streams, rows, width), F32),
        v((rows, width), BF),
        v((3, rows, local), BF),
        v((rows, local), F32),
        v((rows, units), F32),
        v((streams, 8, rows), F32),
        v((streams, 8, rows), F32),
        v((2, layers, 8, width), F32),
        v((micro, 8, rows), F32),
        v((streams, 8, width), F32),
        v((micro, 8, width), F32),
        v((micro, 8, width), F32),
        v((layers, 7, 8, width), F32),
        v((layers, 2, 8, local), F32),
    ]
    scratch += [v((2, 2, width, w), F32) for w in kinds]
    scratch += [
        dma((4, 2, layers)),
        dma((streams + 1,)),
        v((micro, 8, width), F32),
        v((2, micro, 8, width), F32),
        dma((micro, 3)),
        dma((2, micro)),
    ]
    scratch += line_scratch(streams, rows, width)
    if inside:
        scratch += [pltpu.SemaphoreType.REGULAR(())]
        for w in kinds + kinds[1:]:
            scratch += [v((2, 2, width // n, w), BF) for n in (2, 4, 8)]
        scratch += [dma((2, 3, 2))] * 4
        scratch += [pltpu.SemaphoreType.REGULAR((2, 3))] * 2
        scratch += [v((3, tall, width), F32), dma((3,)), dma((3,))]
        scratch += [
            v((micro, 16, width), BF),
            v((micro, 16, width), BF),
            v((micro, 2, 8, width), F32),
            v((micro, 8, 8, width), F32),
            dma((micro, 2)),
            dma((micro, 8)),
            dma((micro, 8)),
        ]
    else:
        scratch += [dma((2, 2, 2)), dma(())]
    return pl.pallas_call(
        functools.partial(step_kernel, inside),
        out_shape=[jax.ShapeDtypeStruct(*s) for s in shapes],
        in_specs=[hb, vm, sm, hb, vm, sm, hb] + [hb, vm, hb, vm, hb, vm, hb, vm, vm, vm],
        out_specs=[vm] * 3 + [vm if inside else hb] * 2,
        scratch_shapes=scratch,
        compiler_params=pltpu.CompilerParams(
            collective_id=0, has_side_effects=True, vmem_limit_bytes=VMEM_LIMIT
        ),
        name="training_step",
    )(*tokens, negatives, *weights)


def outputs_kernel(layers, size, acts, g_in, vec, big, small, o_acts, o_in, o_attend, o_abias, o_merge, o_mbias,
                   o_expand, o_ebias, o_shrink, o_sbias, o_gain, o_shift, o_loss):
    width = vec.shape[1]
    local = small.shape[4]
    half = big.shape[4]
    group = lax.axis_index("dp") * lax.axis_size("rep") + lax.axis_index("rep")
    blocks = width // size
    own = pltpu.roll(vec[...], ((blocks - group) % blocks) * size, axis=1)[:, :size]
    o_acts[:, 0] = acts[...]
    o_in[:, 0] = g_in[...]
    for l in range(layers):
        for h in (0, 1):
            cols = slice(h * half, (h + 1) * half)
            o_shrink[l, :, cols] = big[l, 0, h]
            o_expand[l, :, cols] = big[l, 1, h]
        for j in range(3):
            o_attend[l, j] = small[l, j // 2, j % 2]
        o_merge[l] = small[l, 1, 1].T
        row = 7 * l
        o_gain[l] = own[row : row + 2]
        o_shift[l] = own[row + 2 : row + 4]
        o_sbias[l : l + 1] = own[row + 4 : row + 5]
        o_mbias[l : l + 1] = own[row + 5 : row + 6]
        o_ebias[l : l + 1] = vec[row + 6 : row + 7]
        o_abias[l] = vec[7 * layers + 2 * l : 7 * layers + 2 * l + 2, :local]
    o_loss[...] = vec[vec.shape[0] - 1 :, 0:1]


def run_outputs(acts, g_in, vec, big, small):
    micro, share, width = acts.shape
    layers, _, _, size, half = big.shape
    local = small.shape[4]
    shapes = [
        ((micro, 1, share, width), BF),
        ((micro, 1, share, width), BF),
        ((layers, 3, size, local), F32),
        ((layers, 2, local), F32),
        ((layers, local, size), F32),
        ((layers, size), F32),
        ((layers, size, 2 * half), F32),
        ((layers, width), F32),
        ((layers, size, 2 * half), F32),
        ((layers, size), F32),
        ((layers, 2, size), F32),
        ((layers, 2, size), F32),
        ((1, 1), F32),
    ]
    vm = pl.BlockSpec(memory_space=pltpu.VMEM)
    return pl.pallas_call(
        functools.partial(outputs_kernel, layers, size),
        out_shape=[jax.ShapeDtypeStruct(*s) for s in shapes],
        in_specs=[vm] * 5,
        out_specs=[vm] * len(shapes),
        compiler_params=pltpu.CompilerParams(vmem_limit_bytes=VMEM_LIMIT),
        name="outputs",
    )(acts, g_in, vec, big, small)


def per_device(
    query_tokens, query_drop, query_length, key_tokens, key_drop, key_length, negatives,
    attend_weight, attend_bias, merge_weight, merge_bias, expand_weight, expand_bias,
    shrink_weight, shrink_bias, norm_gain, norm_shift,
):
    micro = query_tokens.shape[0]
    weights = (
        jnp.transpose(attend_weight, (0, 1, 3, 4, 2)),
        attend_bias,
        merge_weight,
        merge_bias,
        expand_weight,
        expand_bias,
        shrink_weight,
        shrink_bias,
        norm_gain,
        norm_shift,
    )
    tokens = (query_tokens, query_drop, query_length.reshape(micro), key_tokens, key_drop, key_length.reshape(micro))
    groups = ("dp", "rep")
    inside = lax.axis_size("dp") == 4 and lax.axis_size("rep") == 2
    if not inside:
        negatives = lax.all_gather(negatives, ("rep", "tensor"), axis=0, tiled=True)
    acts, g_in, vec, g_big, g_small = run_step(inside, tokens, negatives, weights)
    if not inside:
        g_big = lax.psum_scatter(g_big, groups, scatter_dimension=3, tiled=True)
        g_small = lax.psum_scatter(g_small, groups, scatter_dimension=3, tiled=True)
        vec = lax.psum(vec, groups)
    outs = run_outputs(acts, g_in, vec, g_big, g_small)
    loss = outs[12].reshape(()) / (micro * lax.axis_size("dp") * lax.axis_size("rep"))
    return (
        outs[0], outs[1], jnp.transpose(outs[2], (0, 2, 1, 3)), *outs[3:8],
        jnp.transpose(outs[8], (0, 2, 1)), *outs[9:12], loss,
    )


def solution(mesh):
    return jax.shard_map(
        per_device,
        mesh=mesh,
        in_specs=(
            P(None, ("dp", "rep"), None, None),
            P(None, ("dp", "rep"), None),
            P(None, ("dp", "rep")),
            P(None, ("dp", "rep"), None, None),
            P(None, ("dp", "rep"), None),
            P(None, ("dp", "rep")),
            P(("rep", "tensor"), None),
            P(None, None, None, None, "tensor"),
            P(None, None, None, "tensor"),
            P(None, None, "tensor", None),
            P(),
            P(None, None, None, "tensor"),
            P(None, None, "tensor"),
            P(None, None, "tensor", None),
            P(),
            P(),
            P(),
        ),
        out_specs=(
            P(None, ("dp", "rep"), "tensor", None),
            P(None, ("dp", "rep"), "tensor", None),
            P(None, ("dp", "rep"), None, "tensor"),
            P(None, None, "tensor"),
            P(None, "tensor", ("dp", "rep")),
            P(None, ("dp", "rep")),
            P(None, ("dp", "rep"), "tensor"),
            P(None, "tensor"),
            P(None, "tensor", ("dp", "rep")),
            P(None, ("dp", "rep")),
            P(None, None, ("dp", "rep")),
            P(None, None, ("dp", "rep")),
            P(),
        ),
        check_vma=False,
    )
```

```python
import functools

import jax
import jax.numpy as jnp
from jax import lax
from jax.experimental import pallas as pl
from jax.experimental.pallas import tpu as pltpu
from jax.sharding import PartitionSpec as P

HEAD_DIM = 64
CROP_SLOTS = 256
SOFTMAX_WARMTH = 0.05
NORM_EPS = 1e-12
UNIT_EPS = 1e-06
MASKED = -1e30
TOP_PRECISION = lax.Precision.HIGHEST
ROOT_HALF = 0.7071067811865476
INV_ROOT_TAU = 0.3989422804014327

MESH = pl.DeviceIdType.MESH
BF = jnp.bfloat16
F32 = jnp.float32
CHUNKS = 8
LAG = 5
EARLY = 3
TILE = 64
VMEM_LIMIT = 62 * 1024 * 1024


def nn(a, b):
    return jnp.dot(a, b, preferred_element_type=F32)


def nt(a, b):
    return lax.dot_general(a, b, (((1,), (1,)), ((), ())), preferred_element_type=F32)


def tn(a, b):
    return lax.dot_general(a, b, (((0,), (0,)), ((), ())), preferred_element_type=F32)


class Line:
    def __init__(self, part, sbuf, tbuf, x1, x2, s_sem, t_sem, r1, r2):
        z = lax.axis_index("tensor")
        self.mid = (z + 1) // 2 == 1
        self.end = (z + 1) // 2 != 1
        self.lower = z // 2 == 0
        self.inner = 1 + z // 2
        self.outer = 3 * (z // 2)
        self.cross = 3 - z
        self.part, self.sbuf, self.tbuf, self.x1, self.x2 = part, sbuf, tbuf, x1, x2
        self.s_sem, self.t_sem, self.r1, self.r2 = s_sem, t_sem, r1, r2
        self.size = part.shape[1] // CHUNKS

    def rows(self, c):
        return pl.ds(pl.multiple_of(c * self.size, self.size), self.size)

    def near(self, c):
        return (c < CHUNKS // 2) == self.lower

    def outbound(self, c, narrow):
        return (c >= 0) if narrow is False else jnp.logical_not(narrow & self.near(c))

    def homebound(self, c, narrow):
        return (c >= 0) if narrow is False else jnp.logical_not(narrow) | self.near(c)

    def to_inner(self, s, c):
        return pltpu.make_async_remote_copy(
            src_ref=self.sbuf.at[s, self.rows(c)], dst_ref=self.x2.at[s, self.rows(c)],
            send_sem=self.s_sem.at[s, c], recv_sem=self.r2.at[s, c],
            device_id={"tensor": self.inner}, device_id_type=MESH)

    def to_cross(self, s, c, slot):
        return pltpu.make_async_remote_copy(
            src_ref=self.sbuf.at[s, self.rows(c)], dst_ref=self.x1.at[slot, s, self.rows(c)],
            send_sem=self.s_sem.at[s, c], recv_sem=self.r1.at[slot, s, c],
            device_id={"tensor": self.cross}, device_id_type=MESH)

    def to_outer(self, s, c, slot):
        return pltpu.make_async_remote_copy(
            src_ref=self.tbuf.at[s, self.rows(c)], dst_ref=self.x1.at[slot, s, self.rows(c)],
            send_sem=self.t_sem.at[s, c], recv_sem=self.r1.at[slot, s, c],
            device_id={"tensor": self.outer}, device_id_type=MESH)

    def begin(self, s, narrow=False, chunks=range(CHUNKS)):
        for c in chunks:
            @pl.when(self.end & self.outbound(c, narrow))
            def _():
                rows = self.rows(c)
                self.sbuf[s, rows] = self.part[s, rows].astype(BF)
                self.to_inner(s, c).start()

    def inward(self, s, c, slot, live, narrow=False):
        @pl.when(self.mid & live & self.outbound(c, narrow))
        def _():
            rows = self.rows(c)
            self.to_inner(s, c).wait_recv()
            self.sbuf[s, rows] = (self.part[s, rows] + self.x2[s, rows].astype(F32)).astype(BF)
            self.to_cross(s, c, slot).start()

    def outward(self, s, c, slot, live, narrow=False):
        @pl.when(self.mid & live & self.homebound(c, narrow))
        def _():
            rows = self.rows(c)
            self.to_cross(s, c, slot).wait_recv()
            joint = self.part[s, rows] + self.x1[slot, s, rows].astype(F32)
            self.part[s, rows] = joint + self.x2[s, rows].astype(F32)
            self.tbuf[s, rows] = joint.astype(BF)
            self.to_outer(s, c, slot).start()

    def settle(self, s, slot, tile, narrow=False):
        per = TILE // self.size
        for d in range(per):
            c = tile * per + d

            @pl.when(self.end & self.homebound(c, narrow))
            def _():
                rows = self.rows(c)
                self.to_outer(s, c, slot).wait_recv()
                self.part[s, rows] = self.part[s, rows] + self.x1[slot, s, rows].astype(F32)

    def release(self, s, slot, narrow=False):
        self.release_end(s, narrow)
        self.release_mid(s, slot, narrow)

    def release_end(self, s, narrow=False):
        for c in range(CHUNKS):
            @pl.when(self.end & self.outbound(c, narrow))
            def _():
                self.to_inner(s, c).wait_send()

    def release_mid(self, s, slot, narrow=False):
        for c in range(CHUNKS):
            @pl.when(self.mid & self.outbound(c, narrow))
            def _():
                self.to_cross(s, c, slot).wait_send()

            @pl.when(self.mid & self.homebound(c, narrow))
            def _():
                self.to_outer(s, c, slot).wait_send()


def line_scratch(streams, rows, width):
    return [
        pltpu.VMEM((streams, rows, width), F32),
        pltpu.VMEM((streams, rows, width), BF),
        pltpu.VMEM((streams, rows, width), BF),
        pltpu.VMEM((2, streams, rows, width), BF),
        pltpu.VMEM((streams, rows, width), BF),
        pltpu.SemaphoreType.DMA((streams, CHUNKS)),
        pltpu.SemaphoreType.DMA((streams, CHUNKS)),
        pltpu.SemaphoreType.DMA((2, streams, CHUNKS)),
        pltpu.SemaphoreType.DMA((streams, CHUNKS)),
    ]


def tiles(rows, body, ready=None, first=0):
    def step(c, carry):
        if ready is not None:
            ready(c)
        body(pl.ds(pl.multiple_of(c * TILE, TILE), TILE))
        return carry

    lax.fori_loop(first // TILE, rows // TILE, step, 0)


def normalize(total, gain, shift):
    mean = jnp.mean(total, axis=-1, keepdims=True)
    centered = total - mean
    inverse = lax.rsqrt(jnp.mean(centered * centered, axis=-1, keepdims=True) + NORM_EPS)
    normed = centered * inverse
    return normed * gain + shift, normed, inverse


def head_masks(width, scale):
    lane = lax.broadcasted_iota(jnp.int32, (1, width), 1)
    return [
        jnp.where((lane >= h * HEAD_DIM) & (lane < (h + 1) * HEAD_DIM), scale, 0.0).astype(BF)
        for h in range(width // HEAD_DIM)
    ]


def norm_back(g, normed, inverse, gain):
    scaled = g * gain
    return inverse * (
        scaled
        - jnp.mean(scaled, axis=-1, keepdims=True)
        - normed * jnp.mean(scaled * normed, axis=-1, keepdims=True)
    )


def fold(x):
    return jnp.sum(x.reshape(x.shape[0] // 8, 8, x.shape[1]), axis=0)


class Plane:
    def __init__(self, grads, sends, spots, recvs, out, send_sem, recv_sem, credit):
        dp, self.x = lax.axis_index("dp"), lax.axis_index("rep")
        self.y, self.c = dp // 2, dp % 2
        self.partner = {
            "c": {"dp": dp + 1 - 2 * self.c},
            "x": {"rep": 1 - self.x},
            "y": {"dp": (dp + 2) % 4},
        }
        self.grads, self.sends, self.places, self.recvs, self.out = grads, sends, spots, recvs, out
        self.send_sem, self.recv_sem, self.credit = send_sem, recv_sem, credit
        self.block = grads.shape[2] // 8
        self.wide = len(out.shape) == 4

    def message(self, u, stage, half, rows):
        if self.places is None:
            return self.sends[stage].at[u, half, rows]
        row, lane = self.places[stage]
        start = half * (self.grads.shape[2] // 2) + row
        return self.sends.at[u, pl.ds(start + rows.start, rows.size), pl.ds(lane, self.grads.shape[3])]

    def copy(self, u, stage, half):
        way = ("c", "xy"[half], "yx"[half])[stage]
        return pltpu.make_async_remote_copy(
            src_ref=self.message(u, stage, half, pl.ds(0, self.recvs[stage].shape[2])), dst_ref=self.recvs[stage].at[u, half],
            send_sem=self.send_sem.at[u, stage, half], recv_sem=self.recv_sem.at[u, stage, half],
            device_id=self.partner[way], device_id_type=MESH)

    def spots(self, stage, half, own):
        pick = (lambda v: v) if own else (lambda v: 1 - v)
        if stage == 0:
            return [(4 * y + 2 * pick(self.c), 2 * y, 2) for y in (0, 1)]
        if stage == 1 and half == 0:
            return [(4 * y + 2 * self.c + pick(self.x), y, 1) for y in (0, 1)]
        if stage == 1:
            return [(4 * pick(self.y) + 2 * self.c, 0, 2)]
        if half == 0:
            return [(4 * pick(self.y) + 2 * self.c + self.x, 0, 1)]
        return [(4 * self.y + 2 * self.c + pick(self.x), 0, 1)]

    def parts(self, stage, half, own):
        for here, there, blocks in self.spots(stage, half, own):
            for b in range(blocks):
                start = (here + b) * self.block
                yield pl.ds(pl.multiple_of(start, 8), self.block), pl.ds((there + b) * self.block, self.block)

    def send(self, u, stage, live, spend):
        @pl.when(live)
        def _():
            for half in (0, 1):
                for here, there in self.parts(stage, half, False):
                    self.message(u, stage, half, there)[...] = self.grads[u, half, here].astype(BF)

            @pl.when(spend)
            def _():
                pl.semaphore_wait(self.credit.at[u, stage], 2)

            for half in (0, 1):
                self.copy(u, stage, half).start()

    def take(self, u, stage, live, give, layer):
        @pl.when(live)
        def _():
            for half in (0, 1):
                self.copy(u, stage, half).wait()
                for here, there in self.parts(stage, half, True):
                    total = self.grads[u, half, here] + self.recvs[stage][u, half, there].astype(F32)
                    if stage == 2 and self.wide:
                        cols = self.grads.shape[3]
                        self.out[layer, u, :, half * cols : (half + 1) * cols] = total
                    elif stage == 2:
                        self.out[layer, u, half] = total
                    else:
                        self.grads[u, half, here] = total

            @pl.when(give)
            def _():
                for half in (0, 1):
                    way = ("c", "xy"[half], "yx"[half])[stage]
                    pl.semaphore_signal(
                        self.credit.at[u, stage], inc=1, device_id=self.partner[way], device_id_type=MESH
                    )


def greet(inside, ahead):
    z, dp, rep = lax.axis_index("tensor"), lax.axis_index("dp"), lax.axis_index("rep")
    sem = pltpu.get_barrier_semaphore()
    others = [{"tensor": (z + d) % 4} for d in (1, 2, 3)]
    if inside:
        others += [{"rep": 1 - rep, "tensor": (z + d) % 4} for d in (0, 1, 2, 3)]
        others += [{"dp": dp + 1 - 2 * (dp % 2)}, {"dp": (dp + 2) % 4}]
    for other in others:
        pl.semaphore_signal(sem, inc=1, device_id=other, device_id_type=MESH)
    ahead()
    pl.semaphore_wait(sem, len(others))


class Contrast:
    def __init__(self, inside, micro, pooled, keys, pgrad, vec, state, bufs):
        self.inside, self.micro, self.pooled, self.keys = inside, micro, pooled, keys
        self.pgrad, self.vec, self.state = pgrad, vec, state
        self.z, self.rep = lax.axis_index("tensor"), lax.axis_index("rep")
        if inside:
            (self.asks, self.asked, self.reply, self.heard, self.ask_sem, self.reply_sem, self.heard_sem) = bufs
        else:
            (self.source, self.key_sem) = bufs

    def question(self, m):
        return pltpu.make_async_remote_copy(
            src_ref=self.asks.at[m], dst_ref=self.asked.at[m], send_sem=self.ask_sem.at[m, 0],
            recv_sem=self.ask_sem.at[m, 1], device_id={"rep": 1 - self.rep}, device_id_type=MESH)

    def tell(self, m, which, d):
        other = {"tensor": (self.z + d) % 4}
        if which == 1:
            other["rep"] = 1 - self.rep
        k = which * 4 + d
        return pltpu.make_async_remote_copy(
            src_ref=self.reply.at[m, which], dst_ref=self.heard.at[m, k], send_sem=self.reply_sem.at[m, k],
            recv_sem=self.heard_sem.at[m, k], device_id=other, device_id_type=MESH)

    def score(self, rows_now):
        keys = self.keys[...]
        logits = nt(rows_now, keys) / SOFTMAX_WARMTH
        top = jnp.max(logits, axis=-1, keepdims=True)
        expo = jnp.exp(logits - top)
        total = jnp.sum(expo, axis=-1, keepdims=True)
        high = expo.astype(BF)
        rest = expo - high.astype(F32)
        mid = rest.astype(BF)
        tiny = (rest - mid.astype(F32)).astype(BF)
        weighted = nn(jnp.concatenate([high, mid, tiny], axis=0), keys)
        n = rows_now.shape[0]
        return weighted[:n] + weighted[n : 2 * n] + weighted[2 * n :], top, total

    def ask(self, m):
        count = self.pooled[self.micro + m, 1:2]
        mean = self.pooled[self.micro + m, 0:1] / count
        scale = lax.rsqrt(jnp.sum(mean * mean, axis=-1, keepdims=True) + UNIT_EPS)
        direction = mean * scale
        self.state[m, 0:1] = direction
        self.state[m, 1:2] = jnp.broadcast_to(scale, count.shape)
        self.state[m, 2:3] = count
        if self.inside:
            self.asks[m] = jnp.broadcast_to(direction, self.asks.shape[1:]).astype(BF)
            self.question(m).start()

    def respond(self, m):
        if self.inside:
            self.question(m).wait()
            half = lax.broadcasted_iota(jnp.int32, self.asks.shape[1:], 0) < 8
            weighted, top, total = self.score(jnp.where(half, self.asks[m], self.asked[m]))
            wide = (1, weighted.shape[1])
            for which in (0, 1):
                row = slice(8 * which, 8 * which + 1)
                self.reply[m, which, 0:1] = weighted[row]
                self.reply[m, which, 1:2] = jnp.broadcast_to(top[row], wide)
                self.reply[m, which, 2:3] = jnp.broadcast_to(total[row], wide)
            for d in (0, 1, 2, 3):
                self.tell(m, 1, d).start()
            for d in (1, 2, 3):
                self.tell(m, 0, d).start()

    def close(self, m, pooled_key):
        direction, scale, count = self.state[m, 0:1], self.state[m, 1:2, 0:1], self.state[m, 2:3]
        mean = pooled_key / self.pooled[m, 1:2]
        key_dir = mean * lax.rsqrt(jnp.sum(mean * mean, axis=-1, keepdims=True) + UNIT_EPS)
        positive = jnp.sum(direction * key_dir, axis=-1, keepdims=True) / SOFTMAX_WARMTH
        if self.inside:
            for k in range(1, 8):
                self.tell(m, k // 4, k % 4).wait()
            everyone = [self.reply[m, 0]] + [self.heard[m, k] for k in range(1, 8)]
            best = positive
            for one in everyone:
                best = jnp.maximum(best, one[1:2, 0:1])
            own = jnp.exp(positive - best)
            total, keys = own, own * key_dir
            for one in everyone:
                weight = jnp.exp(one[1:2, 0:1] - best)
                total = total + weight * one[2:3, 0:1]
                keys = keys + weight * one[0:1]
        else:
            rows_now = jnp.broadcast_to(direction, (16, direction.shape[1])).astype(BF)

            def piece(c, carry):
                best, total, keys = carry
                size = self.keys.shape[0]
                copy = pltpu.make_async_copy(
                    self.source.at[pl.ds(pl.multiple_of(c * size, size), size)], self.keys, self.key_sem)
                copy.start()
                copy.wait()
                weighted, top, part = (v[0:1] for v in self.score(rows_now))
                now = jnp.maximum(best, top)
                old, new = jnp.exp(best - now), jnp.exp(top - now)
                return now, total * old + part * new, keys * old + weighted * new

            start = (positive, jnp.ones_like(positive), key_dir)
            best, total, keys = lax.fori_loop(0, self.source.shape[0] // self.keys.shape[0], piece, start)
        loss = best + jnp.log(total) - positive
        last = self.vec.shape[0] - 1
        self.vec[last : last + 1] += jnp.broadcast_to(loss, direction.shape)
        dqn = (keys / total - key_dir) * (CROP_SLOTS / SOFTMAX_WARMTH)
        mean_grad = scale * (dqn - direction * jnp.sum(direction * dqn, axis=-1, keepdims=True))
        self.pgrad[m, 0:1] = mean_grad / count
        self.pgrad[m, 1:2] = count


def step_kernel(inside, *refs):
    q_tok, q_drop, q_len, k_tok, k_drop, k_len, negs, *refs = refs
    wqkv_in, abias, wm_in, mbias, we_in, ebias, ws_in, sbias, gains, shifts, *refs = refs
    acts, g_in, vec, out_big, out_small, *refs = refs
    xin, proj, probs, mixed, n1, first, slope, active, n2, inv, *refs = refs
    wqkv, wm, we, ws, tok, h, hb, qkv, mx, inner, *refs = refs
    vbias, valid, vecs, slots, pooled, state, pgrad, g_vec, g_abias, g_big, g_small, *refs = refs
    load_sem, tok_sem, kpart, kheard, kp_sem, kh_sem, *refs = refs
    line = Line(*refs[:9])
    part, sbuf, tbuf = refs[:3]
    refs = refs[9:]
    stored, loaded = (wqkv_in, wm_in, we_in, ws_in), (wqkv, wm, we, ws)
    micro = q_tok.shape[0]
    rows, width = q_tok.shape[2:]
    layers = we.shape[1]
    local = wm.shape[2]
    half_units = we.shape[3] // 2
    heads = local // HEAD_DIM
    streams = 2 * micro
    third = width // 3
    z = lax.axis_index("tensor")
    share = rows // lax.axis_size("tensor")
    own_rows = pl.ds(pl.multiple_of(z * share, 16), share)

    def load(k, e, layer):
        return pltpu.make_async_copy(stored[k].at[e, layer], loaded[k].at[e, layer], load_sem.at[k, e, layer])

    def load_tokens(s):
        source = k_tok if s < micro else q_tok
        return pltpu.make_async_copy(source.at[s % micro, 0], tok.at[pl.ds(s * rows, rows)], tok_sem.at[s])

    def load_keys():
        return pltpu.make_async_copy(negs, tok, tok_sem.at[streams])

    def compact(drop, length, is_q, s, m):
        pos = lax.broadcasted_iota(jnp.int32, (1, rows), 1)
        kept = (pos < length) & ((drop[m] == 0) | (pos == 0))
        kept_f = jnp.broadcast_to(jnp.where(kept, 1.0, 0.0), (16, rows))
        down = lax.broadcasted_iota(jnp.int32, (rows, rows), 0)
        along = lax.broadcasted_iota(jnp.int32, (rows, rows), 1)
        tri = jnp.where(down <= along, 1.0, 0.0).astype(BF)
        order = nn(kept_f.astype(BF), tri)[0:1] - 1.0
        order = jnp.where(kept, order, -1.0)
        count = jnp.sum(kept_f[0:1], axis=-1, keepdims=True)
        pick = jnp.where(order == down.astype(F32), 1.0, 0.0).astype(BF)
        rows_now = nn(pick, tok[pl.ds(s * rows if isinstance(s, int) else pl.multiple_of(s * rows, rows), rows)])
        h[s] = rows_now
        hb[...] = rows_now.astype(BF)
        fits = pos.astype(F32) < count
        vbias[s] = jnp.broadcast_to(jnp.where(fits, 0.0, MASKED), (8, rows))
        if not is_q:
            fits = fits & line.end & ((pos < rows // 2) == line.lower)
        valid[s] = jnp.broadcast_to(jnp.where(fits, 1.0, 0.0), (8, rows))
        pooled[s, 1:2] = jnp.broadcast_to(count, (1, width))
        if is_q:
            slots[m] = jnp.broadcast_to(order, (8, rows))

    def prepare():
        for layer in range(layers):
            for e in (1, 0):
                for k in (0, 1):
                    load(k, e, layer).start()
                if layer == 0:
                    for s in range((1 - e) * micro, (2 - e) * micro):
                        load_tokens(s).start()
                for k in (2, 3):
                    load(k, e, layer).start()
        vec[...] = jnp.zeros_like(vec)
        g_vec[...] = jnp.zeros_like(g_vec)
        g_abias[...] = jnp.zeros_like(g_abias)
        for e in range(2):
            for layer in range(layers):
                for row, ref in enumerate((mbias, ebias, sbias)):
                    vecs[e, layer, row : row + 1] = ref[e, layer : layer + 1].astype(F32)
                vecs[e, layer, 3:5] = gains[e, layer].astype(F32)
                vecs[e, layer, 5:7] = shifts[e, layer].astype(F32)
        load_tokens(0).wait()
        compact(k_drop, k_len[0], False, 0, 0)

    greet(inside, prepare)

    if inside:
        turn, red_big, red_small, red_sem, e1, e2, e3, t1, t2, t3, d1, d2, d3, big_s, big_r, small_s, small_r, big_c, small_c, v_rcv, v_send, v_recv, *bufs = refs
        w_big, quarter = half_units, width // 4
        big = Plane(g_big, we.at[1], ((0, 0), (0, w_big), (quarter, w_big)), (e1, e2, e3), red_big, big_s, big_r, big_c)
        small = Plane(g_small, (d1, d2, d3), None, (t1, t2, t3), red_small, small_s, small_r, small_c)
    else:
        g_sem, key_sem = refs
        bufs = (negs, key_sem)
    last_f = 2 * layers * streams

    def at_f(i):
        j = jnp.maximum(i, 0)
        s, stage = j % streams, j // streams
        return s, stage % 2, (i >= 0) & (i < last_f), (stage == 2 * layers - 1) & (s < micro)

    def tick_f(i, *which):
        for c in which:
            s, slot, live, narrow = at_f(i - 1)
            line.inward(s, c, slot, live, narrow)
            if c < LAG:
                s, slot, live, narrow = at_f(i - 2)
            line.outward(s, (c - LAG) % CHUNKS, slot, live, narrow)

    def second_norm(lp, e, s, narrow):
        m, is_q = s % micro, s >= micro
        bias, gain, shift = vecs[e, lp, 2:3], vecs[e, lp, 4:5], vecs[e, lp, 6:7]

        def norm(r):
            out, normed, inverse = normalize(h[s, r] + part[s, r] + bias, gain, shift)
            h[s, r] = out
            hb[r] = out.astype(BF)

            @pl.when(is_q)
            def _():
                n2[lp, m, r] = normed.astype(BF)
                inv[lp, m, r, 64:128] = jnp.broadcast_to(inverse, (TILE, 64))

        tiles(rows, norm, lambda t: line.settle(s, 1, t, narrow))
        line.release(s, 1, narrow)

    def attention_pass(layer, s):
        i = layer * 2 * streams + s
        e, m = 1 - s // micro, s % micro
        is_q = s >= micro
        tick_f(i, 0)

        @pl.when(layer == 0)
        def _():
            @pl.when((s > 0) & (s < micro))
            def _():
                pltpu.make_async_copy(k_tok.at[m, 0], tok.at[pl.ds(0, rows)], tok_sem.at[s]).wait()
                compact(k_drop, k_len[m], False, s, m)

            @pl.when(is_q)
            def _():
                pltpu.make_async_copy(q_tok.at[m, 0], tok.at[pl.ds(0, rows)], tok_sem.at[s]).wait()
                compact(q_drop, q_len[m], True, s, m)

        @pl.when(layer > 0)
        def _():
            second_norm(layer - 1, e, s, False)

        tick_f(i, 1, 2)

        @pl.when(m == 0)
        def _():
            for k in (0, 1):
                load(k, e, layer).wait()

        @pl.when(is_q)
        def _():
            xin[layer, m] = hb[...]

        rows_now = hb[...]
        for j in range(3):
            bias = 0.0 if j == 1 else abias[e, layer, j // 2 : j // 2 + 1].astype(F32)
            qkv[j] = (nt(rows_now, wqkv[e, layer, j]) + bias).astype(BF)

        @pl.when(is_q)
        def _():
            for j in range(3):
                proj[layer, m, j] = qkv[j]

        tick_f(i, 3)
        q_masks = head_masks(local, HEAD_DIM**-0.5)
        v_masks = head_masks(local, 1.0)
        for hd in range(heads):
            scores = nt(qkv[0] * q_masks[hd], qkv[1]) + vbias[s, 0:1]
            expo = jnp.exp(scores - jnp.max(scores, axis=-1, keepdims=True))
            chance = (expo / jnp.sum(expo, axis=-1, keepdims=True)).astype(BF)

            @pl.when(is_q)
            def _():
                probs[layer, m, hd] = chance

            out = nn(chance, qkv[2] * v_masks[hd])
            if hd == 0:
                mx[...] = out
            else:
                mx[...] += out
            tick_f(i, 4 + hd)
        if inside:
            @pl.when((i == 1) & (big.c == 0) & line.end)
            def _():
                pl.semaphore_signal(turn, inc=1, device_id=big.partner["c"], device_id_type=MESH)

        mixed_now = mx[...].astype(BF)

        @pl.when(is_q)
        def _():
            mixed[layer, m] = mixed_now

        part[s] = nn(mixed_now, wm[e, layer])
        if inside:
            @pl.when((i == 0) & (big.c == 1) & line.end)
            def _():
                pl.semaphore_wait(turn, 1)

        line.begin(s)
        tick_f(i, *range(4 + heads, CHUNKS))

    def forward_pass(layer, s):
        i = (layer * 2 + 1) * streams + s
        e, m = 1 - s // micro, s % micro
        is_q = s >= micro
        tick_f(i, 0, 1)
        bias, gain, shift = vecs[e, layer, 0:1], vecs[e, layer, 3:4], vecs[e, layer, 5:6]

        def norm(r):
            out, normed, inverse = normalize(h[s, r] + part[s, r] + bias, gain, shift)
            h[s, r] = out
            hb[r] = out.astype(BF)

            @pl.when(is_q)
            def _():
                n1[layer, m, r] = normed.astype(BF)
                inv[layer, m, r, 0:64] = jnp.broadcast_to(inverse, (TILE, 64))
                first[layer, m, r] = out.astype(BF)

        tiles(rows, norm, lambda t: line.settle(s, 0, t))
        line.release(s, 0)

        @pl.when(m == 0)
        def _():
            for k in (2, 3):
                load(k, e, layer).wait()

        tick_f(i, 2, 3)
        inner[...] = nn(hb[...], we[e, layer])
        tick_f(i, 4)
        bias_e = vecs[e, layer, 1:2]

        def gelu(r):
            u = inner[r] + bias_e
            phi = 0.5 * (1.0 + lax.erf(u * ROOT_HALF))
            out = (u * phi).astype(BF)
            tbuf[s, r] = out

            @pl.when(is_q)
            def _():
                active[layer, m, r] = out
                slope[layer, m, r] = (phi + u * jnp.exp(-0.5 * u * u) * INV_ROOT_TAU).astype(BF)

        tiles(rows, gelu)
        tick_f(i, 5, 6)
        part[s] = nn(tbuf[s], ws[e, layer])
        line.begin(s, (layer == layers - 1) & (s < micro))
        tick_f(i, 7)

    def layer_step(layer, carry):
        def a_step(s, c):
            attention_pass(layer, s)
            return c

        def f_step(s, c):
            forward_pass(layer, s)
            return c

        lax.fori_loop(0, streams, a_step, 0)
        if inside:
            @pl.when(layer == 0)
            def _():
                load_keys().start()

        lax.fori_loop(0, streams, f_step, 0)
        return carry

    lax.fori_loop(0, layers, layer_step, 0)

    def pool(s):
        return jnp.dot(valid[s], h[s], precision=TOP_PRECISION, preferred_element_type=F32)

    def kshare(m, d):
        return pltpu.make_async_remote_copy(
            src_ref=kpart.at[m], dst_ref=kheard.at[z // 3, m], send_sem=kp_sem.at[m, d - 1],
            recv_sem=kh_sem.at[z // 3, m], device_id={"tensor": (z + d) % 4}, device_id_type=MESH)

    def last_key(m):
        second_norm(layers - 1, 1, m, line.part.shape[0] > 0)
        kpart[m] = pool(m)

        @pl.when(line.end)
        def _():
            for d in (1, 2, 3):
                kshare(m, d).start()

    def last_query(m):
        second_norm(layers - 1, 0, micro + m, False)
        pooled[micro + m, 0:1] = pool(micro + m)[0:1]
        acts[m] = hb[own_rows]

    def pooled_key(m):
        @pl.when(line.end)
        def _():
            for d in (1, 2, 3):
                kshare(m, d).wait_send()

        total = kpart[m, 0:1]
        for e in (0, 1):
            @pl.when(z != 3 * e)
            def _():
                pltpu.make_async_remote_copy(
                    src_ref=kpart.at[m], dst_ref=kheard.at[e, m], send_sem=kp_sem.at[m, 0],
                    recv_sem=kh_sem.at[e, m], device_id={"tensor": 3 - z}, device_id_type=MESH).wait_recv()

            total = total + jnp.where(z != 3 * e, kheard[e, m, 0:1], 0.0)
        return total

    queue = Contrast(inside, micro, pooled, tok, pgrad, vec, state, bufs)
    tick_f(last_f, 0, 1, 2)
    for m in range(micro):
        last_key(m)
        tick_f(last_f, 3 + m)
    if inside:
        load_keys().wait()
    for m in range(micro):
        if m == micro - 1:
            tick_f(last_f, *range(3 + micro, CHUNKS))
            tick_f(last_f + 1, *range(LAG))
        if m > 0:
            queue.respond(m - 1)
        last_query(m)
        queue.ask(m)

    last_b = 2 * layers * micro
    dinner = tbuf.at[1]
    heads_f = [h.at[0, :, pl.ds(j * third, local)] for j in range(3)]
    heads_b = [tbuf.at[0, :, pl.ds(j * third, local)] for j in range(3)]

    def at_b(i):
        j = jnp.maximum(i, 0)
        return micro + j % micro, (j // micro) % 2, (i >= 0) & (i < last_b)

    def tick(i, *which):
        for g in which:
            s, slot, live = at_b(i - 1)
            if g >= 1 and g - 1 < CHUNKS:
                line.outward(s, g - 1, slot, live)
            c = g + EARLY
            if c >= CHUNKS + 1:
                s, slot, live = at_b(i)
                c -= CHUNKS + 1
                if c < EARLY:
                    line.inward(s, c, slot, live)
            elif c < CHUNKS:
                line.inward(s, c, slot, live)

    def drained(large, layer, u, half):
        source, target = (g_big, out_big) if large else (g_small, out_small)
        return pltpu.make_async_copy(source.at[u, half], target.at[layer, u, half], g_sem.at[0 if large else 1, u, half])

    def add_to(large, u, half, s, value):
        ref = (g_big if large else g_small).at[u, half]

        @pl.when(s == 0)
        def _():
            ref[...] = value

        @pl.when(s > 0)
        def _():
            ref[...] += value

    def leave(large, layer):
        source, target = (red_big, out_big) if large else (red_small, out_small)
        return pltpu.make_async_copy(source.at[layer], target.at[layer], red_sem.at[0 if large else 1, layer])

    def plane(what, large, stage, live, step):
        for u in (0, 1):
            if inside:
                group = big if large else small
                if what == "send":
                    group.send(u, stage, live, step > 0)
                else:
                    group.take(u, stage, live, step < layers - 1, layers - 1 - step)
            elif (what, stage) in (("send", 0), ("take", 2)):
                @pl.when(live)
                def _():
                    for half in (0, 1):
                        copy = drained(large, layers - 1 - step, u, half)
                        copy.start() if what == "send" else copy.wait()
        if inside and (what, stage) == ("take", 2):
            @pl.when(live)
            def _():
                leave(large, layers - 1 - step).start()

    def mlp_back(step, m):
        layer = layers - 1 - step
        i = step * 2 * micro + m
        s = micro + m
        low = sbuf.at[m]

        @pl.when(step == 0)
        def _():
            queue.close(m, pooled_key(m))

            def begin(c, carry):
                r = pl.ds(pl.multiple_of(c * TILE, TILE), TILE)
                pos = (lax.broadcasted_iota(jnp.int32, (TILE, 1), 0) + c * TILE).astype(F32)
                part[s, r] = jnp.where(pos < pgrad[m, 1:2, 0:1], pgrad[m, 0:1], 0.0)
                h[s, r] = jnp.zeros((TILE, width), F32)
                return carry

            lax.fori_loop(0, rows // TILE, begin, 0)

        gain = vecs[0, layer, 4:5]

        def back(r):
            g = part[s, r] + h[s, r]
            normed = n2[layer, m, r].astype(F32)
            out = norm_back(g, normed, inv[layer, m, r][:, 64:65], gain)
            h[s, r] = out
            low[r] = out.astype(BF)
            g_vec[layer, 1] += fold(g * normed)
            g_vec[layer, 3] += fold(g)
            g_vec[layer, 4] += fold(out)

        def ready(t):
            @pl.when(step > 0)
            def _():
                line.settle(s, 1, t)

        def slopes(r):
            out = inner[r] * slope[layer, m, r].astype(F32)
            dinner[r] = out.astype(BF)
            g_vec[layer, 6] += fold(out)

        for half in (0, 1):
            first_row, last_row = half * rows // 2, (half + 1) * rows // 2
            span = pl.ds(first_row, rows // 2)
            tiles(last_row, back, ready, first_row)
            if half == 0:
                @pl.when(step > 0)
                def _():
                    line.release_end(s)

            tick(i, 2 * half)
            inner[span] = nt(low[span], ws[0, layer])

            if half == 1:
                @pl.when((step == 0) & (m == 0))
                def _():
                    queue.respond(micro - 1)

            tick(i, 2 * half + 1)
            tiles(last_row, slopes, None, first_row)
            part[s, span] = nt(dinner[span], we[0, layer])
            line.begin(s, False, range(half * CHUNKS // 2, (half + 1) * CHUNKS // 2))

        @pl.when(step > 0)
        def _():
            line.release_mid(s, 1)

        plane("take", True, 2, (step > 0) & (m == 0), step - 1)
        for half in (0, 1):
            cols = pl.ds(half * half_units, half_units)
            add_to(True, 0, half, m, tn(low[...], active[layer, m, :, cols]))
            tick(i, 4 + half)
        for half in (0, 1):
            cols = pl.ds(half * half_units, half_units)
            add_to(True, 1, half, m, tn(first[layer, m], dinner[:, cols]))
            tick(i, 6 + half)
        plane("take", False, 0, (step > 0) & (m == 0), step - 1)
        plane("send", False, 1, (step > 0) & (m == 0), step - 1)
        plane("send", True, 0, m == micro - 1, step)
        plane("take", False, 1, (step > 0) & (m == micro - 1), step - 1)
        plane("send", False, 2, (step > 0) & (m == micro - 1), step - 1)
        tick(i, CHUNKS)

    def attention_back(step, m):
        layer = layers - 1 - step
        i = (step * 2 + 1) * micro + m
        s = micro + m
        low = sbuf.at[m]
        gain = vecs[0, layer, 3:4]

        def back(r):
            g = part[s, r] + h[s, r]
            normed = n1[layer, m, r].astype(F32)
            out = norm_back(g, normed, inv[layer, m, r][:, 0:1], gain)
            h[s, r] = out
            low[r] = out.astype(BF)
            g_vec[layer, 0] += fold(g * normed)
            g_vec[layer, 2] += fold(g)
            g_vec[layer, 5] += fold(out)

        tiles(rows, back, lambda t: line.settle(s, 0, t))
        line.release(s, 0)
        tick(i, 0)
        dmix = nt(low[...], wm[0, layer]).astype(BF)
        tick(i, 1)
        masks = head_masks(local, 1.0)
        for hd in range(heads):
            chance_b = probs[layer, m, hd]
            chance = chance_b.astype(F32)
            dm = dmix * masks[hd]
            dch = nt(dm, proj[layer, m, 2])
            ds = chance * (dch - jnp.sum(chance * dch, axis=-1, keepdims=True))
            draw = (ds * HEAD_DIM**-0.5).astype(BF)
            dq = nn(draw, proj[layer, m, 1] * masks[hd])
            dk = tn(draw, proj[layer, m, 0] * masks[hd])
            dv = tn(chance_b, dm)
            for ref, value in zip(heads_f, (dq, dk, dv)):
                if hd == 0:
                    ref[...] = value
                else:
                    ref[...] += value
            tick(i, 2 + hd)
        g_abias[layer, 0] += fold(heads_f[0][...])
        g_abias[layer, 1] += fold(heads_f[2][...])
        for j in range(3):
            heads_b[j][...] = heads_f[j][...].astype(BF)
        for half in (0, 1):
            span = pl.ds(half * rows // 2, rows // 2)
            part[s, span] = sum(nn(tbuf[0, span, j * third : j * third + local], wqkv[0, layer, j]) for j in range(3))
            line.begin(s, False, range(half * CHUNKS // 2, (half + 1) * CHUNKS // 2))
        tick(i, *range(2 + heads, 6))
        plane("take", True, 0, m == 0, step)
        plane("send", True, 1, m == 0, step)
        plane("take", True, 1, m == micro - 1, step)
        plane("send", True, 2, m == micro - 1, step)
        plane("take", False, 2, (step > 0) & (m == 0), step - 1)
        for j in range(3):
            add_to(False, j // 2, j % 2, m, tn(xin[layer, m], heads_b[j][...]))
        tick(i, 6)
        add_to(False, 1, 1, m, tn(low[...], mixed[layer, m]))
        tick(i, 7, CHUNKS)
        plane("send", False, 0, m == micro - 1, step)

    def back_step(step, carry):
        def m_step(m, c):
            mlp_back(step, m)
            return c

        def a_step(m, c):
            attention_back(step, m)
            return c

        lax.fori_loop(0, micro, m_step, 0)
        lax.fori_loop(0, micro, a_step, 0)
        return carry

    lax.fori_loop(0, layers, back_step, 0)

    for layer in range(layers):
        for k in range(7):
            vec[layer * 7 + k : layer * 7 + k + 1] = jnp.sum(g_vec[layer, k], axis=0, keepdims=True)
        for k in range(2):
            row = layers * 7 + layer * 2 + k
            vec[row : row + 1, 0:local] = jnp.sum(g_abias[layer, k], axis=0, keepdims=True)

    def vec_copy(stage):
        return pltpu.make_async_remote_copy(
            src_ref=vec, dst_ref=v_rcv.at[stage], send_sem=v_send.at[stage], recv_sem=v_recv.at[stage],
            device_id=big.partner["cxy"[stage]], device_id_type=MESH)

    def vec_take(stage):
        if inside:
            vec_copy(stage).wait()
            vec[...] += v_rcv[stage]

    def vec_send(stage):
        if inside:
            vec_copy(stage).start()

    final = layers - 1
    vec_send(0)
    tick(last_b, 0, 1)
    plane("take", False, 0, True, final)
    plane("send", False, 1, True, final)
    vec_take(0)
    vec_send(1)
    tick(last_b, 2, 3, 4)
    plane("take", True, 2, True, final)
    tick(last_b, 5, 6)
    plane("take", False, 1, True, final)
    plane("send", False, 2, True, final)
    vec_take(1)
    vec_send(2)
    tick(last_b, 7, CHUNKS)

    def finish(m, carry):
        s = micro + m
        low = sbuf.at[m]

        def back(r):
            low[r] = (part[s, r] + h[s, r]).astype(BF)

        tiles(rows, back, lambda t: line.settle(s, 1, t))
        line.release(s, 1)
        down = lax.broadcasted_iota(jnp.int32, (rows, rows), 0).astype(F32)
        pick = jnp.where(slots[m, 0:1] == down, 1.0, 0.0).astype(BF)
        low[...] = tn(pick, low[...]).astype(BF)
        g_in[m] = low[own_rows]
        return carry

    plane("take", False, 2, True, final)
    vec_take(2)
    lax.fori_loop(0, micro, finish, 0)
    if inside:
        for layer in range(layers):
            leave(True, layer).wait()
            leave(False, layer).wait()


def run_step(inside, tokens, negatives, weights):
    q_tok = tokens[0]
    micro, _, rows, width = q_tok.shape
    wqkv, abias, wm, mbias, we, ebias, ws, sbias, gains, shifts = weights
    layers, local, units = we.shape[1], wm.shape[2], we.shape[3]
    heads = local // HEAD_DIM
    streams = 2 * micro
    share = rows // lax.axis_size("tensor")
    lm = (layers, micro)
    tall = 8 * ((9 * layers + 2 + 7) // 8)
    kinds = (units // 2, local)
    high = width // 8 if inside else width
    shapes = [((micro, share, width), BF), ((micro, share, width), BF), ((tall, width), F32)]
    if inside:
        shapes += [((layers, 2, high, units), F32), ((layers, 2, 2, high, local), F32)]
    else:
        shapes += [((layers, 2, 2, high, w), F32) for w in kinds]
    vm = pl.BlockSpec(memory_space=pltpu.VMEM)
    hb = pl.BlockSpec(memory_space=pl.ANY)
    sm = pl.BlockSpec(memory_space=pltpu.SMEM)
    dma = pltpu.SemaphoreType.DMA
    v = pltpu.VMEM
    scratch = [
        v(lm + (rows, width), BF),
        v(lm + (3, rows, local), BF),
        v(lm + (heads, rows, rows), BF),
        v(lm + (rows, local), BF),
        v(lm + (rows, width), BF),
        v(lm + (rows, width), BF),
        v(lm + (rows, units), BF),
        v(lm + (rows, units), BF),
        v(lm + (rows, width), BF),
        v(lm + (rows, 128), F32),
    ]
    scratch += [v(w.shape, BF) for w in (wqkv, wm, we, ws)]
    scratch += [
        v((streams * rows, width), BF),
        v((streams, rows, width), F32),
        v((rows, width), BF),
        v((3, rows, local), BF),
        v((rows, local), F32),
        v((rows, units), F32),
        v((streams, 8, rows), F32),
        v((streams, 8, rows), F32),
        v((2, layers, 8, width), F32),
        v((micro, 8, rows), F32),
        v((streams, 8, width), F32),
        v((micro, 8, width), F32),
        v((micro, 8, width), F32),
        v((layers, 7, 8, width), F32),
        v((layers, 2, 8, local), F32),
    ]
    scratch += [v((2, 2, width, w), F32) for w in kinds]
    scratch += [
        dma((4, 2, layers)),
        dma((streams + 1,)),
        v((micro, 8, width), F32),
        v((2, micro, 8, width), F32),
        dma((micro, 3)),
        dma((2, micro)),
    ]
    scratch += line_scratch(streams, rows, width)
    if inside:
        scratch += [pltpu.SemaphoreType.REGULAR(()), v(*shapes[3]), v(*shapes[4]), dma((2, layers))]
        for w in kinds + kinds[1:]:
            scratch += [v((2, 2, width // n, w), BF) for n in (2, 4, 8)]
        scratch += [dma((2, 3, 2))] * 4
        scratch += [pltpu.SemaphoreType.REGULAR((2, 3))] * 2
        scratch += [v((3, tall, width), F32), dma((3,)), dma((3,))]
        scratch += [
            v((micro, 16, width), BF),
            v((micro, 16, width), BF),
            v((micro, 2, 8, width), F32),
            v((micro, 8, 8, width), F32),
            dma((micro, 2)),
            dma((micro, 8)),
            dma((micro, 8)),
        ]
    else:
        scratch += [dma((2, 2, 2)), dma(())]
    return pl.pallas_call(
        functools.partial(step_kernel, inside),
        out_shape=[jax.ShapeDtypeStruct(*s) for s in shapes],
        in_specs=[hb, vm, sm, hb, vm, sm, hb] + [hb, vm, hb, vm, hb, vm, hb, vm, vm, vm],
        out_specs=[vm] * 3 + [hb] * 2,
        scratch_shapes=scratch,
        compiler_params=pltpu.CompilerParams(
            collective_id=0, has_side_effects=True, vmem_limit_bytes=VMEM_LIMIT
        ),
        name="training_step",
    )(*tokens, negatives, *weights)


def outputs_kernel(layers, size, acts, g_in, vec, big, small, o_acts, o_in, o_attend, o_abias, o_merge, o_mbias,
                   o_expand, o_ebias, o_shrink, o_sbias, o_gain, o_shift, o_loss):
    width = vec.shape[1]
    local = small.shape[4]
    o_acts[:, 0] = acts[...]
    o_in[:, 0] = g_in[...]
    for l in range(layers):
        o_shrink[l] = big[l, 0]
        o_expand[l] = big[l, 1]
        for j in range(3):
            o_attend[l, j] = small[l, j // 2, j % 2]
        o_merge[l] = small[l, 1, 1].T
    group = lax.axis_index("dp") * lax.axis_size("rep") + lax.axis_index("rep")
    blocks = width // size
    own = pltpu.roll(vec[...], ((blocks - group) % blocks) * size, axis=1)[:, :size]
    for l in range(layers):
        row = 7 * l
        o_gain[l] = own[row : row + 2]
        o_shift[l] = own[row + 2 : row + 4]
        o_sbias[l : l + 1] = own[row + 4 : row + 5]
        o_mbias[l : l + 1] = own[row + 5 : row + 6]
        o_ebias[l : l + 1] = vec[row + 6 : row + 7]
        o_abias[l] = vec[7 * layers + 2 * l : 7 * layers + 2 * l + 2, :local]
    o_loss[...] = vec[vec.shape[0] - 1 :, 0:1]


def run_outputs(acts, g_in, vec, big, small):
    micro, share, width = acts.shape
    layers, _, size, units = big.shape
    local = small.shape[4]
    shapes = [
        ((micro, 1, share, width), BF),
        ((micro, 1, share, width), BF),
        ((layers, 3, size, local), F32),
        ((layers, 2, local), F32),
        ((layers, local, size), F32),
        ((layers, size), F32),
        ((layers, size, units), F32),
        ((layers, width), F32),
        ((layers, size, units), F32),
        ((layers, size), F32),
        ((layers, 2, size), F32),
        ((layers, 2, size), F32),
        ((1, 1), F32),
    ]
    vm = pl.BlockSpec(memory_space=pltpu.VMEM)
    return pl.pallas_call(
        functools.partial(outputs_kernel, layers, size),
        out_shape=[jax.ShapeDtypeStruct(*s) for s in shapes],
        in_specs=[vm] * 5,
        out_specs=[vm] * len(shapes),
        compiler_params=pltpu.CompilerParams(vmem_limit_bytes=VMEM_LIMIT),
        name="outputs",
    )(acts, g_in, vec, big, small)


def per_device(
    query_tokens, query_drop, query_length, key_tokens, key_drop, key_length, negatives,
    attend_weight, attend_bias, merge_weight, merge_bias, expand_weight, expand_bias,
    shrink_weight, shrink_bias, norm_gain, norm_shift,
):
    micro = query_tokens.shape[0]
    weights = (
        jnp.transpose(attend_weight, (0, 1, 3, 4, 2)),
        attend_bias,
        merge_weight,
        merge_bias,
        expand_weight,
        expand_bias,
        shrink_weight,
        shrink_bias,
        norm_gain,
        norm_shift,
    )
    tokens = (query_tokens, query_drop, query_length.reshape(micro), key_tokens, key_drop, key_length.reshape(micro))
    groups = ("dp", "rep")
    inside = lax.axis_size("dp") == 4 and lax.axis_size("rep") == 2
    if not inside:
        negatives = lax.all_gather(negatives, ("rep", "tensor"), axis=0, tiled=True)
    acts, g_in, vec, g_big, g_small = run_step(inside, tokens, negatives, weights)
    if not inside:
        g_big = lax.psum_scatter(g_big, groups, scatter_dimension=3, tiled=True)
        g_small = lax.psum_scatter(g_small, groups, scatter_dimension=3, tiled=True)
        vec = lax.psum(vec, groups)
        g_big = g_big.transpose(0, 1, 3, 2, 4).reshape(g_big.shape[:2] + (g_big.shape[3], -1))
    outs = run_outputs(acts, g_in, vec, g_big, g_small)
    loss = outs[12].reshape(()) / (micro * lax.axis_size("dp") * lax.axis_size("rep"))
    return (
        outs[0], outs[1], jnp.transpose(outs[2], (0, 2, 1, 3)), *outs[3:8],
        jnp.transpose(outs[8], (0, 2, 1)), *outs[9:12], loss,
    )


def solution(mesh):
    return jax.shard_map(
        per_device,
        mesh=mesh,
        in_specs=(
            P(None, ("dp", "rep"), None, None),
            P(None, ("dp", "rep"), None),
            P(None, ("dp", "rep")),
            P(None, ("dp", "rep"), None, None),
            P(None, ("dp", "rep"), None),
            P(None, ("dp", "rep")),
            P(("rep", "tensor"), None),
            P(None, None, None, None, "tensor"),
            P(None, None, None, "tensor"),
            P(None, None, "tensor", None),
            P(),
            P(None, None, None, "tensor"),
            P(None, None, "tensor"),
            P(None, None, "tensor", None),
            P(),
            P(),
            P(),
        ),
        out_specs=(
            P(None, ("dp", "rep"), "tensor", None),
            P(None, ("dp", "rep"), "tensor", None),
            P(None, ("dp", "rep"), None, "tensor"),
            P(None, None, "tensor"),
            P(None, "tensor", ("dp", "rep")),
            P(None, ("dp", "rep")),
            P(None, ("dp", "rep"), "tensor"),
            P(None, "tensor"),
            P(None, "tensor", ("dp", "rep")),
            P(None, ("dp", "rep")),
            P(None, None, ("dp", "rep")),
            P(None, None, ("dp", "rep")),
            P(),
        ),
        check_vma=False,
    )
```

```python
import functools

import jax
import jax.numpy as jnp
from jax import lax
from jax.experimental import pallas as pl
from jax.experimental.pallas import tpu as pltpu
from jax.sharding import PartitionSpec as P

HEAD_DIM = 64
CROP_SLOTS = 256
SOFTMAX_WARMTH = 0.05
NORM_EPS = 1e-12
UNIT_EPS = 1e-06
MASKED = -1e30
TOP_PRECISION = lax.Precision.HIGHEST
ROOT_HALF = 0.7071067811865476
INV_ROOT_TAU = 0.3989422804014327

MESH = pl.DeviceIdType.MESH
BF = jnp.bfloat16
F32 = jnp.float32
CHUNKS = 8
LAG = 5
EARLY = 3
TILE = 64
VMEM_LIMIT = 62 * 1024 * 1024


def nn(a, b):
    return jnp.dot(a, b, preferred_element_type=F32)


def nt(a, b):
    return lax.dot_general(a, b, (((1,), (1,)), ((), ())), preferred_element_type=F32)


def tn(a, b):
    return lax.dot_general(a, b, (((0,), (0,)), ((), ())), preferred_element_type=F32)


class Line:
    def __init__(self, part, sbuf, tbuf, x1, x2, s_sem, t_sem, r1, r2):
        z = lax.axis_index("tensor")
        self.mid = (z + 1) // 2 == 1
        self.end = (z + 1) // 2 != 1
        self.lower = z // 2 == 0
        self.inner = 1 + z // 2
        self.outer = 3 * (z // 2)
        self.cross = 3 - z
        self.part, self.sbuf, self.tbuf, self.x1, self.x2 = part, sbuf, tbuf, x1, x2
        self.s_sem, self.t_sem, self.r1, self.r2 = s_sem, t_sem, r1, r2
        self.size = part.shape[1] // CHUNKS

    def rows(self, c):
        return pl.ds(pl.multiple_of(c * self.size, self.size), self.size)

    def near(self, c):
        return (c < CHUNKS // 2) == self.lower

    def outbound(self, c, narrow):
        return (c >= 0) if narrow is False else jnp.logical_not(narrow & self.near(c))

    def homebound(self, c, narrow):
        return (c >= 0) if narrow is False else jnp.logical_not(narrow) | self.near(c)

    def to_inner(self, s, c):
        return pltpu.make_async_remote_copy(
            src_ref=self.sbuf.at[s, self.rows(c)], dst_ref=self.x2.at[s, self.rows(c)],
            send_sem=self.s_sem.at[s, c], recv_sem=self.r2.at[s, c],
            device_id={"tensor": self.inner}, device_id_type=MESH)

    def to_cross(self, s, c, slot):
        return pltpu.make_async_remote_copy(
            src_ref=self.sbuf.at[s, self.rows(c)], dst_ref=self.x1.at[slot, s, self.rows(c)],
            send_sem=self.s_sem.at[s, c], recv_sem=self.r1.at[slot, s, c],
            device_id={"tensor": self.cross}, device_id_type=MESH)

    def to_outer(self, s, c, slot):
        return pltpu.make_async_remote_copy(
            src_ref=self.tbuf.at[s, self.rows(c)], dst_ref=self.x1.at[slot, s, self.rows(c)],
            send_sem=self.t_sem.at[s, c], recv_sem=self.r1.at[slot, s, c],
            device_id={"tensor": self.outer}, device_id_type=MESH)

    def begin(self, s, narrow=False, chunks=range(CHUNKS)):
        for c in chunks:
            @pl.when(self.end & self.outbound(c, narrow))
            def _():
                rows = self.rows(c)
                self.sbuf[s, rows] = self.part[s, rows].astype(BF)
                self.to_inner(s, c).start()

    def inward(self, s, c, slot, live, narrow=False):
        @pl.when(self.mid & live & self.outbound(c, narrow))
        def _():
            rows = self.rows(c)
            self.to_inner(s, c).wait_recv()
            self.sbuf[s, rows] = (self.part[s, rows] + self.x2[s, rows].astype(F32)).astype(BF)
            self.to_cross(s, c, slot).start()

    def outward(self, s, c, slot, live, narrow=False):
        @pl.when(self.mid & live & self.homebound(c, narrow))
        def _():
            rows = self.rows(c)
            self.to_cross(s, c, slot).wait_recv()
            joint = self.part[s, rows] + self.x1[slot, s, rows].astype(F32)
            self.part[s, rows] = joint + self.x2[s, rows].astype(F32)
            self.tbuf[s, rows] = joint.astype(BF)
            self.to_outer(s, c, slot).start()

    def settle(self, s, slot, tile, narrow=False):
        per = TILE // self.size
        for d in range(per):
            c = tile * per + d

            @pl.when(self.end & self.homebound(c, narrow))
            def _():
                rows = self.rows(c)
                self.to_outer(s, c, slot).wait_recv()
                self.part[s, rows] = self.part[s, rows] + self.x1[slot, s, rows].astype(F32)

    def release(self, s, slot, narrow=False):
        self.release_end(s, narrow)
        self.release_mid(s, slot, narrow)

    def release_end(self, s, narrow=False):
        for c in range(CHUNKS):
            @pl.when(self.end & self.outbound(c, narrow))
            def _():
                self.to_inner(s, c).wait_send()

    def release_mid(self, s, slot, narrow=False):
        for c in range(CHUNKS):
            @pl.when(self.mid & self.outbound(c, narrow))
            def _():
                self.to_cross(s, c, slot).wait_send()

            @pl.when(self.mid & self.homebound(c, narrow))
            def _():
                self.to_outer(s, c, slot).wait_send()


def line_scratch(streams, rows, width):
    return [
        pltpu.VMEM((streams, rows, width), F32),
        pltpu.VMEM((streams, rows, width), BF),
        pltpu.VMEM((streams, rows, width), BF),
        pltpu.VMEM((2, streams, rows, width), BF),
        pltpu.VMEM((streams, rows, width), BF),
        pltpu.SemaphoreType.DMA((streams, CHUNKS)),
        pltpu.SemaphoreType.DMA((streams, CHUNKS)),
        pltpu.SemaphoreType.DMA((2, streams, CHUNKS)),
        pltpu.SemaphoreType.DMA((streams, CHUNKS)),
    ]


def tiles(rows, body, ready=None, first=0):
    def step(c, carry):
        if ready is not None:
            ready(c)
        body(pl.ds(pl.multiple_of(c * TILE, TILE), TILE))
        return carry

    lax.fori_loop(first // TILE, rows // TILE, step, 0)


def normalize(total, gain, shift):
    mean = jnp.mean(total, axis=-1, keepdims=True)
    centered = total - mean
    inverse = lax.rsqrt(jnp.mean(centered * centered, axis=-1, keepdims=True) + NORM_EPS)
    normed = centered * inverse
    return normed * gain + shift, normed, inverse


def head_masks(width, scale):
    lane = lax.broadcasted_iota(jnp.int32, (1, width), 1)
    return [
        jnp.where((lane >= h * HEAD_DIM) & (lane < (h + 1) * HEAD_DIM), scale, 0.0).astype(BF)
        for h in range(width // HEAD_DIM)
    ]


def norm_back(g, normed, inverse, gain):
    scaled = g * gain
    return inverse * (
        scaled
        - jnp.mean(scaled, axis=-1, keepdims=True)
        - normed * jnp.mean(scaled * normed, axis=-1, keepdims=True)
    )


def fold(x):
    return jnp.sum(x.reshape(x.shape[0] // 8, 8, x.shape[1]), axis=0)


class Plane:
    def __init__(self, grads, sends, spots, recvs, out, send_sem, recv_sem, credit):
        dp, self.x = lax.axis_index("dp"), lax.axis_index("rep")
        self.y, self.c = dp // 2, dp % 2
        self.partner = {
            "c": {"dp": dp + 1 - 2 * self.c},
            "x": {"rep": 1 - self.x},
            "y": {"dp": (dp + 2) % 4},
        }
        self.grads, self.sends, self.places, self.recvs, self.out = grads, sends, spots, recvs, out
        self.send_sem, self.recv_sem, self.credit = send_sem, recv_sem, credit
        self.block = grads.shape[2] // 8
        self.wide = len(out.shape) == 4

    def message(self, u, stage, half, rows):
        if self.places is None:
            return self.sends[stage].at[u, half, rows]
        row, lane = self.places[stage]
        start = half * (self.grads.shape[2] // 2) + row
        return self.sends.at[u, pl.ds(start + rows.start, rows.size), pl.ds(lane, self.grads.shape[3])]

    def copy(self, u, stage, half):
        way = ("c", "xy"[half], "yx"[half])[stage]
        return pltpu.make_async_remote_copy(
            src_ref=self.message(u, stage, half, pl.ds(0, self.recvs[stage].shape[2])), dst_ref=self.recvs[stage].at[u, half],
            send_sem=self.send_sem.at[u, stage, half], recv_sem=self.recv_sem.at[u, stage, half],
            device_id=self.partner[way], device_id_type=MESH)

    def spots(self, stage, half, own):
        pick = (lambda v: v) if own else (lambda v: 1 - v)
        if stage == 0:
            return [(4 * y + 2 * pick(self.c), 2 * y, 2) for y in (0, 1)]
        if stage == 1 and half == 0:
            return [(4 * y + 2 * self.c + pick(self.x), y, 1) for y in (0, 1)]
        if stage == 1:
            return [(4 * pick(self.y) + 2 * self.c, 0, 2)]
        if half == 0:
            return [(4 * pick(self.y) + 2 * self.c + self.x, 0, 1)]
        return [(4 * self.y + 2 * self.c + pick(self.x), 0, 1)]

    def parts(self, stage, half, own):
        for here, there, blocks in self.spots(stage, half, own):
            for b in range(blocks):
                start = (here + b) * self.block
                yield pl.ds(pl.multiple_of(start, 8), self.block), pl.ds((there + b) * self.block, self.block)

    def send(self, u, stage, live, spend):
        @pl.when(live)
        def _():
            for half in (0, 1):
                for here, there in self.parts(stage, half, False):
                    self.message(u, stage, half, there)[...] = self.grads[u, half, here].astype(BF)

            @pl.when(spend)
            def _():
                pl.semaphore_wait(self.credit.at[u, stage], 2)

            for half in (0, 1):
                self.copy(u, stage, half).start()

    def take(self, u, stage, live, give, layer):
        @pl.when(live)
        def _():
            for half in (0, 1):
                self.copy(u, stage, half).wait()
                for here, there in self.parts(stage, half, True):
                    total = self.grads[u, half, here] + self.recvs[stage][u, half, there].astype(F32)
                    if stage == 2 and self.wide:
                        cols = self.grads.shape[3]
                        self.out[layer, u, :, half * cols : (half + 1) * cols] = total
                    elif stage == 2:
                        self.out[layer, u, half] = total
                    else:
                        self.grads[u, half, here] = total

            @pl.when(give)
            def _():
                for half in (0, 1):
                    way = ("c", "xy"[half], "yx"[half])[stage]
                    pl.semaphore_signal(
                        self.credit.at[u, stage], inc=1, device_id=self.partner[way], device_id_type=MESH
                    )


def greet(inside, ahead):
    z, dp, rep = lax.axis_index("tensor"), lax.axis_index("dp"), lax.axis_index("rep")
    sem = pltpu.get_barrier_semaphore()
    others = [{"tensor": (z + d) % 4} for d in (1, 2, 3)]
    if inside:
        others += [{"rep": 1 - rep, "tensor": (z + d) % 4} for d in (0, 1, 2, 3)]
        others += [{"dp": dp + 1 - 2 * (dp % 2)}, {"dp": (dp + 2) % 4}]
    for other in others:
        pl.semaphore_signal(sem, inc=1, device_id=other, device_id_type=MESH)
    ahead()
    pl.semaphore_wait(sem, len(others))


class Contrast:
    def __init__(self, inside, micro, pooled, keys, pgrad, vec, state, bufs):
        self.inside, self.micro, self.pooled, self.keys = inside, micro, pooled, keys
        self.pgrad, self.vec, self.state = pgrad, vec, state
        self.z, self.rep = lax.axis_index("tensor"), lax.axis_index("rep")
        if inside:
            (self.asks, self.asked, self.reply, self.heard, self.ask_sem, self.reply_sem, self.heard_sem) = bufs
        else:
            (self.source, self.key_sem) = bufs

    def question(self, m):
        return pltpu.make_async_remote_copy(
            src_ref=self.asks.at[m], dst_ref=self.asked.at[m], send_sem=self.ask_sem.at[m, 0],
            recv_sem=self.ask_sem.at[m, 1], device_id={"rep": 1 - self.rep}, device_id_type=MESH)

    def tell(self, m, which, d):
        other = {"tensor": (self.z + d) % 4}
        if which == 1:
            other["rep"] = 1 - self.rep
        k = which * 4 + d
        return pltpu.make_async_remote_copy(
            src_ref=self.reply.at[m, which], dst_ref=self.heard.at[m, k], send_sem=self.reply_sem.at[m, k],
            recv_sem=self.heard_sem.at[m, k], device_id=other, device_id_type=MESH)

    def score(self, rows_now):
        keys = self.keys[...]
        logits = nt(rows_now, keys) / SOFTMAX_WARMTH
        top = jnp.max(logits, axis=-1, keepdims=True)
        expo = jnp.exp(logits - top)
        total = jnp.sum(expo, axis=-1, keepdims=True)
        high = expo.astype(BF)
        rest = expo - high.astype(F32)
        mid = rest.astype(BF)
        tiny = (rest - mid.astype(F32)).astype(BF)
        weighted = nn(jnp.concatenate([high, mid, tiny], axis=0), keys)
        n = rows_now.shape[0]
        return weighted[:n] + weighted[n : 2 * n] + weighted[2 * n :], top, total

    def ask(self, m):
        count = self.pooled[self.micro + m, 1:2]
        mean = self.pooled[self.micro + m, 0:1] / count
        scale = lax.rsqrt(jnp.sum(mean * mean, axis=-1, keepdims=True) + UNIT_EPS)
        direction = mean * scale
        self.state[m, 0:1] = direction
        self.state[m, 1:2] = jnp.broadcast_to(scale, count.shape)
        self.state[m, 2:3] = count
        if self.inside:
            self.asks[m] = jnp.broadcast_to(direction, self.asks.shape[1:]).astype(BF)
            self.question(m).start()

    def respond(self, m):
        if self.inside:
            self.question(m).wait()
            half = lax.broadcasted_iota(jnp.int32, self.asks.shape[1:], 0) < 8
            weighted, top, total = self.score(jnp.where(half, self.asks[m], self.asked[m]))
            wide = (1, weighted.shape[1])
            for which in (0, 1):
                row = slice(8 * which, 8 * which + 1)
                self.reply[m, which, 0:1] = weighted[row]
                self.reply[m, which, 1:2] = jnp.broadcast_to(top[row], wide)
                self.reply[m, which, 2:3] = jnp.broadcast_to(total[row], wide)
            for d in (0, 1, 2, 3):
                self.tell(m, 1, d).start()
            for d in (1, 2, 3):
                self.tell(m, 0, d).start()

    def close(self, m, pooled_key):
        direction, scale, count = self.state[m, 0:1], self.state[m, 1:2, 0:1], self.state[m, 2:3]
        mean = pooled_key / self.pooled[m, 1:2]
        key_dir = mean * lax.rsqrt(jnp.sum(mean * mean, axis=-1, keepdims=True) + UNIT_EPS)
        positive = jnp.sum(direction * key_dir, axis=-1, keepdims=True) / SOFTMAX_WARMTH
        if self.inside:
            for k in range(1, 8):
                self.tell(m, k // 4, k % 4).wait()
            everyone = [self.reply[m, 0]] + [self.heard[m, k] for k in range(1, 8)]
            best = positive
            for one in everyone:
                best = jnp.maximum(best, one[1:2, 0:1])
            own = jnp.exp(positive - best)
            total, keys = own, own * key_dir
            for one in everyone:
                weight = jnp.exp(one[1:2, 0:1] - best)
                total = total + weight * one[2:3, 0:1]
                keys = keys + weight * one[0:1]
        else:
            rows_now = jnp.broadcast_to(direction, (16, direction.shape[1])).astype(BF)

            def piece(c, carry):
                best, total, keys = carry
                size = self.keys.shape[0]
                copy = pltpu.make_async_copy(
                    self.source.at[pl.ds(pl.multiple_of(c * size, size), size)], self.keys, self.key_sem)
                copy.start()
                copy.wait()
                weighted, top, part = (v[0:1] for v in self.score(rows_now))
                now = jnp.maximum(best, top)
                old, new = jnp.exp(best - now), jnp.exp(top - now)
                return now, total * old + part * new, keys * old + weighted * new

            start = (positive, jnp.ones_like(positive), key_dir)
            best, total, keys = lax.fori_loop(0, self.source.shape[0] // self.keys.shape[0], piece, start)
        loss = best + jnp.log(total) - positive
        last = self.vec.shape[0] - 1
        self.vec[last : last + 1] += jnp.broadcast_to(loss, direction.shape)
        dqn = (keys / total - key_dir) * (CROP_SLOTS / SOFTMAX_WARMTH)
        mean_grad = scale * (dqn - direction * jnp.sum(direction * dqn, axis=-1, keepdims=True))
        self.pgrad[m, 0:1] = mean_grad / count
        self.pgrad[m, 1:2] = count


def step_kernel(inside, *refs):
    q_tok, q_drop, q_len, k_tok, k_drop, k_len, negs, *refs = refs
    wqkv_in, abias, wm_in, mbias, we_in, ebias, ws_in, sbias, gains, shifts, *refs = refs
    acts, g_in, vec, out_big, out_small, *refs = refs
    xin, proj, probs, mixed, n1, first, slope, active, n2, inv, *refs = refs
    wqkv, wm, we, ws, tok, h, hb, qkv, mx, inner, *refs = refs
    vbias, valid, vecs, slots, pooled, state, pgrad, g_vec, g_abias, g_big, g_small, *refs = refs
    load_sem, tok_sem, kpart, kheard, kp_sem, kh_sem, *refs = refs
    line = Line(*refs[:9])
    part, sbuf, tbuf = refs[:3]
    refs = refs[9:]
    stored, loaded = (wqkv_in, wm_in, we_in, ws_in), (wqkv, wm, we, ws)
    micro = q_tok.shape[0]
    rows, width = q_tok.shape[2:]
    layers = we.shape[1]
    local = wm.shape[2]
    half_units = we.shape[3] // 2
    heads = local // HEAD_DIM
    streams = 2 * micro
    third = width // 3
    z = lax.axis_index("tensor")
    share = rows // lax.axis_size("tensor")
    own_rows = pl.ds(pl.multiple_of(z * share, 16), share)

    def load(k, e, layer):
        return pltpu.make_async_copy(stored[k].at[e, layer], loaded[k].at[e, layer], load_sem.at[k, e, layer])

    def load_tokens(s):
        source = k_tok if s < micro else q_tok
        return pltpu.make_async_copy(source.at[s % micro, 0], tok.at[pl.ds(s * rows, rows)], tok_sem.at[s])

    def load_keys():
        return pltpu.make_async_copy(negs, tok, tok_sem.at[streams])

    def compact(drop, length, is_q, s, m):
        pos = lax.broadcasted_iota(jnp.int32, (1, rows), 1)
        kept = (pos < length) & ((drop[m] == 0) | (pos == 0))
        kept_f = jnp.broadcast_to(jnp.where(kept, 1.0, 0.0), (16, rows))
        down = lax.broadcasted_iota(jnp.int32, (rows, rows), 0)
        along = lax.broadcasted_iota(jnp.int32, (rows, rows), 1)
        tri = jnp.where(down <= along, 1.0, 0.0).astype(BF)
        order = nn(kept_f.astype(BF), tri)[0:1] - 1.0
        order = jnp.where(kept, order, -1.0)
        count = jnp.sum(kept_f[0:1], axis=-1, keepdims=True)
        pick = jnp.where(order == down.astype(F32), 1.0, 0.0).astype(BF)
        rows_now = nn(pick, tok[pl.ds(s * rows if isinstance(s, int) else pl.multiple_of(s * rows, rows), rows)])
        h[s] = rows_now
        hb[...] = rows_now.astype(BF)
        fits = pos.astype(F32) < count
        vbias[s] = jnp.broadcast_to(jnp.where(fits, 0.0, MASKED), (8, rows))
        if not is_q:
            fits = fits & line.end & ((pos < rows // 2) == line.lower)
        valid[s] = jnp.broadcast_to(jnp.where(fits, 1.0, 0.0), (8, rows))
        pooled[s, 1:2] = jnp.broadcast_to(count, (1, width))
        if is_q:
            slots[m] = jnp.broadcast_to(order, (8, rows))

    def prepare():
        for layer in range(layers):
            for e in (1, 0):
                for k in (0, 1):
                    load(k, e, layer).start()
                if layer == 0:
                    for s in range((1 - e) * micro, (2 - e) * micro):
                        load_tokens(s).start()
                for k in (2, 3):
                    load(k, e, layer).start()
        vec[...] = jnp.zeros_like(vec)
        g_vec[...] = jnp.zeros_like(g_vec)
        g_abias[...] = jnp.zeros_like(g_abias)
        for e in range(2):
            for layer in range(layers):
                for row, ref in enumerate((mbias, ebias, sbias)):
                    vecs[e, layer, row : row + 1] = ref[e, layer : layer + 1].astype(F32)
                vecs[e, layer, 3:5] = gains[e, layer].astype(F32)
                vecs[e, layer, 5:7] = shifts[e, layer].astype(F32)
        load_tokens(0).wait()
        compact(k_drop, k_len[0], False, 0, 0)

    greet(inside, prepare)

    if inside:
        turn, red_big, red_small, red_sem, e1, e2, e3, t1, t2, t3, d1, d2, d3, big_s, big_r, small_s, small_r, big_c, small_c, v_rcv, v_send, v_recv, *bufs = refs
        w_big, quarter = half_units, width // 4
        big = Plane(g_big, we.at[1], ((0, 0), (0, w_big), (quarter, w_big)), (e1, e2, e3), red_big, big_s, big_r, big_c)
        small = Plane(g_small, (d1, d2, d3), None, (t1, t2, t3), red_small, small_s, small_r, small_c)
    else:
        g_sem, key_sem = refs
        bufs = (negs, key_sem)
    last_f = 2 * layers * streams

    def at_f(i):
        j = jnp.maximum(i, 0)
        s, stage = j % streams, j // streams
        return s, stage % 2, (i >= 0) & (i < last_f), (stage == 2 * layers - 1) & (s < micro)

    def tick_f(i, *which):
        for c in which:
            s, slot, live, narrow = at_f(i - 1)
            line.inward(s, c, slot, live, narrow)
            if c < LAG:
                s, slot, live, narrow = at_f(i - 2)
            line.outward(s, (c - LAG) % CHUNKS, slot, live, narrow)

    def second_norm(lp, e, s, narrow):
        m, is_q = s % micro, s >= micro
        bias, gain, shift = vecs[e, lp, 2:3], vecs[e, lp, 4:5], vecs[e, lp, 6:7]

        def norm(r):
            out, normed, inverse = normalize(h[s, r] + part[s, r] + bias, gain, shift)
            h[s, r] = out
            hb[r] = out.astype(BF)

            @pl.when(is_q)
            def _():
                n2[lp, m, r] = normed.astype(BF)
                inv[lp, m, r, 64:128] = jnp.broadcast_to(inverse, (TILE, 64))

        tiles(rows, norm, lambda t: line.settle(s, 1, t, narrow))
        line.release(s, 1, narrow)

    def attention_pass(layer, s):
        i = layer * 2 * streams + s
        e, m = 1 - s // micro, s % micro
        is_q = s >= micro
        tick_f(i, 0)

        @pl.when(layer == 0)
        def _():
            @pl.when((s > 0) & (s < micro))
            def _():
                pltpu.make_async_copy(k_tok.at[m, 0], tok.at[pl.ds(0, rows)], tok_sem.at[s]).wait()
                compact(k_drop, k_len[m], False, s, m)

            @pl.when(is_q)
            def _():
                pltpu.make_async_copy(q_tok.at[m, 0], tok.at[pl.ds(0, rows)], tok_sem.at[s]).wait()
                compact(q_drop, q_len[m], True, s, m)

        @pl.when(layer > 0)
        def _():
            second_norm(layer - 1, e, s, False)

        tick_f(i, 1, 2)

        @pl.when(m == 0)
        def _():
            for k in (0, 1):
                load(k, e, layer).wait()

        @pl.when(is_q)
        def _():
            xin[layer, m] = hb[...]

        rows_now = hb[...]
        for j in range(3):
            bias = 0.0 if j == 1 else abias[e, layer, j // 2 : j // 2 + 1].astype(F32)
            qkv[j] = (nt(rows_now, wqkv[e, layer, j]) + bias).astype(BF)

        @pl.when(is_q)
        def _():
            for j in range(3):
                proj[layer, m, j] = qkv[j]

        tick_f(i, 3)
        q_masks = head_masks(local, HEAD_DIM**-0.5)
        v_masks = head_masks(local, 1.0)
        for hd in range(heads):
            scores = nt(qkv[0] * q_masks[hd], qkv[1]) + vbias[s, 0:1]
            expo = jnp.exp(scores - jnp.max(scores, axis=-1, keepdims=True))
            chance = (expo / jnp.sum(expo, axis=-1, keepdims=True)).astype(BF)

            @pl.when(is_q)
            def _():
                probs[layer, m, hd] = chance

            out = nn(chance, qkv[2] * v_masks[hd])
            if hd == 0:
                mx[...] = out
            else:
                mx[...] += out
            tick_f(i, 4 + hd)
        if inside:
            @pl.when((i == 1) & (big.c == 0) & line.end)
            def _():
                pl.semaphore_signal(turn, inc=1, device_id=big.partner["c"], device_id_type=MESH)

        mixed_now = mx[...].astype(BF)

        @pl.when(is_q)
        def _():
            mixed[layer, m] = mixed_now

        part[s] = nn(mixed_now, wm[e, layer])
        if inside:
            @pl.when((i == 0) & (big.c == 1) & line.end)
            def _():
                pl.semaphore_wait(turn, 1)

        line.begin(s)
        tick_f(i, *range(4 + heads, CHUNKS))

    def forward_pass(layer, s):
        i = (layer * 2 + 1) * streams + s
        e, m = 1 - s // micro, s % micro
        is_q = s >= micro
        tick_f(i, 0, 1)
        bias, gain, shift = vecs[e, layer, 0:1], vecs[e, layer, 3:4], vecs[e, layer, 5:6]

        def norm(r):
            out, normed, inverse = normalize(h[s, r] + part[s, r] + bias, gain, shift)
            h[s, r] = out
            hb[r] = out.astype(BF)

            @pl.when(is_q)
            def _():
                n1[layer, m, r] = normed.astype(BF)
                inv[layer, m, r, 0:64] = jnp.broadcast_to(inverse, (TILE, 64))
                first[layer, m, r] = out.astype(BF)

        tiles(rows, norm, lambda t: line.settle(s, 0, t))
        line.release(s, 0)

        @pl.when(m == 0)
        def _():
            for k in (2, 3):
                load(k, e, layer).wait()

        tick_f(i, 2, 3)
        inner[...] = nn(hb[...], we[e, layer])
        tick_f(i, 4)
        bias_e = vecs[e, layer, 1:2]

        def gelu(r):
            u = inner[r] + bias_e
            phi = 0.5 * (1.0 + lax.erf(u * ROOT_HALF))
            out = (u * phi).astype(BF)
            tbuf[s, r] = out

            @pl.when(is_q)
            def _():
                active[layer, m, r] = out
                slope[layer, m, r] = (phi + u * jnp.exp(-0.5 * u * u) * INV_ROOT_TAU).astype(BF)

        tiles(rows, gelu)
        tick_f(i, 5, 6)
        part[s] = nn(tbuf[s], ws[e, layer])
        line.begin(s, (layer == layers - 1) & (s < micro))
        tick_f(i, 7)

    def layer_step(layer, carry):
        def a_step(s, c):
            attention_pass(layer, s)
            return c

        def f_step(s, c):
            forward_pass(layer, s)
            return c

        lax.fori_loop(0, streams, a_step, 0)
        if inside:
            @pl.when(layer == 0)
            def _():
                load_keys().start()

        lax.fori_loop(0, streams, f_step, 0)
        return carry

    lax.fori_loop(0, layers, layer_step, 0)

    def pool(s):
        return jnp.dot(valid[s], h[s], precision=TOP_PRECISION, preferred_element_type=F32)

    def kshare(m, d):
        return pltpu.make_async_remote_copy(
            src_ref=kpart.at[m], dst_ref=kheard.at[z // 3, m], send_sem=kp_sem.at[m, d - 1],
            recv_sem=kh_sem.at[z // 3, m], device_id={"tensor": (z + d) % 4}, device_id_type=MESH)

    def last_key(m):
        second_norm(layers - 1, 1, m, line.part.shape[0] > 0)
        kpart[m] = pool(m)

        @pl.when(line.end)
        def _():
            for d in (1, 2, 3):
                kshare(m, d).start()

    def last_query(m):
        second_norm(layers - 1, 0, micro + m, False)
        pooled[micro + m, 0:1] = pool(micro + m)[0:1]
        acts[m] = hb[own_rows]

    def pooled_key(m):
        @pl.when(line.end)
        def _():
            for d in (1, 2, 3):
                kshare(m, d).wait_send()

        total = kpart[m, 0:1]
        for e in (0, 1):
            @pl.when(z != 3 * e)
            def _():
                pltpu.make_async_remote_copy(
                    src_ref=kpart.at[m], dst_ref=kheard.at[e, m], send_sem=kp_sem.at[m, 0],
                    recv_sem=kh_sem.at[e, m], device_id={"tensor": 3 - z}, device_id_type=MESH).wait_recv()

            total = total + jnp.where(z != 3 * e, kheard[e, m, 0:1], 0.0)
        return total

    queue = Contrast(inside, micro, pooled, tok, pgrad, vec, state, bufs)
    tick_f(last_f, 0, 1, 2)
    for m in range(micro):
        last_key(m)
        tick_f(last_f, 3 + m)
    if inside:
        load_keys().wait()
    for m in range(micro):
        if m == micro - 1:
            tick_f(last_f, *range(3 + micro, CHUNKS))
            tick_f(last_f + 1, *range(LAG))
        if m > 0:
            queue.respond(m - 1)
        last_query(m)
        queue.ask(m)

    last_b = 2 * layers * micro
    dinner = tbuf.at[1]
    heads_f = [h.at[0, :, pl.ds(j * third, local)] for j in range(3)]
    heads_b = [tbuf.at[0, :, pl.ds(j * third, local)] for j in range(3)]

    def at_b(i):
        j = jnp.maximum(i, 0)
        return micro + j % micro, (j // micro) % 2, (i >= 0) & (i < last_b)

    def tick(i, *which):
        for g in which:
            s, slot, live = at_b(i - 1)
            if g >= 1 and g - 1 < CHUNKS:
                line.outward(s, g - 1, slot, live)
            c = g + EARLY
            if c >= CHUNKS + 1:
                s, slot, live = at_b(i)
                c -= CHUNKS + 1
                if c < EARLY:
                    line.inward(s, c, slot, live)
            elif c < CHUNKS:
                line.inward(s, c, slot, live)

    def drained(large, layer, u, half):
        source, target = (g_big, out_big) if large else (g_small, out_small)
        return pltpu.make_async_copy(source.at[u, half], target.at[layer, u, half], g_sem.at[0 if large else 1, u, half])

    def add_to(large, u, half, s, value):
        ref = (g_big if large else g_small).at[u, half]

        @pl.when(s == 0)
        def _():
            ref[...] = value

        @pl.when(s > 0)
        def _():
            ref[...] += value

    def leave(large, layer):
        source, target = (red_big, out_big) if large else (red_small, out_small)
        return pltpu.make_async_copy(source.at[layer], target.at[layer], red_sem.at[0 if large else 1, layer])

    def plane(what, large, stage, live, step):
        for u in (0, 1):
            if inside:
                group = big if large else small
                if what == "send":
                    group.send(u, stage, live, step > 0)
                else:
                    group.take(u, stage, live, step < layers - 1, layers - 1 - step)
            elif (what, stage) in (("send", 0), ("take", 2)):
                @pl.when(live)
                def _():
                    for half in (0, 1):
                        copy = drained(large, layers - 1 - step, u, half)
                        copy.start() if what == "send" else copy.wait()
        if inside and (what, stage) == ("take", 2):
            @pl.when(live)
            def _():
                leave(large, layers - 1 - step).start()

    def mlp_back(step, m):
        layer = layers - 1 - step
        i = step * 2 * micro + m
        s = micro + m
        low = sbuf.at[m]

        @pl.when(step == 0)
        def _():
            queue.close(m, pooled_key(m))

            def begin(c, carry):
                r = pl.ds(pl.multiple_of(c * TILE, TILE), TILE)
                pos = (lax.broadcasted_iota(jnp.int32, (TILE, 1), 0) + c * TILE).astype(F32)
                part[s, r] = jnp.where(pos < pgrad[m, 1:2, 0:1], pgrad[m, 0:1], 0.0)
                h[s, r] = jnp.zeros((TILE, width), F32)
                return carry

            lax.fori_loop(0, rows // TILE, begin, 0)

        gain = vecs[0, layer, 4:5]

        def back(r):
            g = part[s, r] + h[s, r]
            normed = n2[layer, m, r].astype(F32)
            out = norm_back(g, normed, inv[layer, m, r][:, 64:65], gain)
            h[s, r] = out
            low[r] = out.astype(BF)
            g_vec[layer, 1] += fold(g * normed)
            g_vec[layer, 3] += fold(g)
            g_vec[layer, 4] += fold(out)

        def ready(t):
            @pl.when(step > 0)
            def _():
                line.settle(s, 1, t)

        def slopes(r):
            out = inner[r] * slope[layer, m, r].astype(F32)
            dinner[r] = out.astype(BF)
            g_vec[layer, 6] += fold(out)

        for half in (0, 1):
            first_row, last_row = half * rows // 2, (half + 1) * rows // 2
            span = pl.ds(first_row, rows // 2)
            tiles(last_row, back, ready, first_row)
            if half == 0:
                @pl.when(step > 0)
                def _():
                    line.release_end(s)

            tick(i, 2 * half)
            inner[span] = nt(low[span], ws[0, layer])

            tick(i, 2 * half + 1)
            tiles(last_row, slopes, None, first_row)
            part[s, span] = nt(dinner[span], we[0, layer])
            line.begin(s, False, range(half * CHUNKS // 2, (half + 1) * CHUNKS // 2))
            if half == 0:
                @pl.when((step == 0) & (m == 0))
                def _():
                    queue.respond(micro - 1)

        @pl.when(step > 0)
        def _():
            line.release_mid(s, 1)

        plane("take", True, 2, (step > 0) & (m == 0), step - 1)
        for half in (0, 1):
            cols = pl.ds(half * half_units, half_units)
            add_to(True, 0, half, m, tn(low[...], active[layer, m, :, cols]))
            tick(i, 4 + half)
        for half in (0, 1):
            cols = pl.ds(half * half_units, half_units)
            add_to(True, 1, half, m, tn(first[layer, m], dinner[:, cols]))
            tick(i, 6 + half)
        plane("take", False, 0, (step > 0) & (m == 0), step - 1)
        plane("send", False, 1, (step > 0) & (m == 0), step - 1)
        plane("send", True, 0, m == micro - 1, step)
        plane("take", False, 1, (step > 0) & (m == micro - 1), step - 1)
        plane("send", False, 2, (step > 0) & (m == micro - 1), step - 1)
        tick(i, CHUNKS)

    def attention_back(step, m):
        layer = layers - 1 - step
        i = (step * 2 + 1) * micro + m
        s = micro + m
        low = sbuf.at[m]
        gain = vecs[0, layer, 3:4]

        def back(r):
            g = part[s, r] + h[s, r]
            normed = n1[layer, m, r].astype(F32)
            out = norm_back(g, normed, inv[layer, m, r][:, 0:1], gain)
            h[s, r] = out
            low[r] = out.astype(BF)
            g_vec[layer, 0] += fold(g * normed)
            g_vec[layer, 2] += fold(g)
            g_vec[layer, 5] += fold(out)

        tiles(rows, back, lambda t: line.settle(s, 0, t))
        line.release(s, 0)
        tick(i, 0)
        dmix = nt(low[...], wm[0, layer]).astype(BF)
        tick(i, 1)
        masks = head_masks(local, 1.0)
        for hd in range(heads):
            chance_b = probs[layer, m, hd]
            chance = chance_b.astype(F32)
            dm = dmix * masks[hd]
            dch = nt(dm, proj[layer, m, 2])
            ds = chance * (dch - jnp.sum(chance * dch, axis=-1, keepdims=True))
            draw = (ds * HEAD_DIM**-0.5).astype(BF)
            dq = nn(draw, proj[layer, m, 1] * masks[hd])
            dk = tn(draw, proj[layer, m, 0] * masks[hd])
            dv = tn(chance_b, dm)
            for ref, value in zip(heads_f, (dq, dk, dv)):
                if hd == 0:
                    ref[...] = value
                else:
                    ref[...] += value
            tick(i, 2 + hd)
        g_abias[layer, 0] += fold(heads_f[0][...])
        g_abias[layer, 1] += fold(heads_f[2][...])
        for j in range(3):
            heads_b[j][...] = heads_f[j][...].astype(BF)
        for half in (0, 1):
            span = pl.ds(half * rows // 2, rows // 2)
            part[s, span] = sum(nn(tbuf[0, span, j * third : j * third + local], wqkv[0, layer, j]) for j in range(3))
            line.begin(s, False, range(half * CHUNKS // 2, (half + 1) * CHUNKS // 2))
        tick(i, *range(2 + heads, 6))
        plane("take", True, 0, m == 0, step)
        plane("send", True, 1, m == 0, step)
        plane("take", True, 1, m == micro - 1, step)
        plane("send", True, 2, m == micro - 1, step)
        plane("take", False, 2, (step > 0) & (m == 0), step - 1)
        for j in range(3):
            add_to(False, j // 2, j % 2, m, tn(xin[layer, m], heads_b[j][...]))
        tick(i, 6)
        add_to(False, 1, 1, m, tn(low[...], mixed[layer, m]))
        tick(i, 7, CHUNKS)
        plane("send", False, 0, m == micro - 1, step)

    def back_step(step, carry):
        def m_step(m, c):
            mlp_back(step, m)
            return c

        def a_step(m, c):
            attention_back(step, m)
            return c

        lax.fori_loop(0, micro, m_step, 0)
        lax.fori_loop(0, micro, a_step, 0)
        return carry

    lax.fori_loop(0, layers, back_step, 0)

    for layer in range(layers):
        for k in range(7):
            vec[layer * 7 + k : layer * 7 + k + 1] = jnp.sum(g_vec[layer, k], axis=0, keepdims=True)
        for k in range(2):
            row = layers * 7 + layer * 2 + k
            vec[row : row + 1, 0:local] = jnp.sum(g_abias[layer, k], axis=0, keepdims=True)

    def vec_copy(stage):
        return pltpu.make_async_remote_copy(
            src_ref=vec, dst_ref=v_rcv.at[stage], send_sem=v_send.at[stage], recv_sem=v_recv.at[stage],
            device_id=big.partner["cxy"[stage]], device_id_type=MESH)

    def vec_take(stage):
        if inside:
            vec_copy(stage).wait()
            vec[...] += v_rcv[stage]

    def vec_send(stage):
        if inside:
            vec_copy(stage).start()

    final = layers - 1
    vec_send(0)
    tick(last_b, 0, 1)
    plane("take", False, 0, True, final)
    plane("send", False, 1, True, final)
    vec_take(0)
    vec_send(1)
    tick(last_b, 2, 3, 4)
    plane("take", True, 2, True, final)
    tick(last_b, 5, 6)
    plane("take", False, 1, True, final)
    plane("send", False, 2, True, final)
    vec_take(1)
    vec_send(2)
    tick(last_b, 7, CHUNKS)

    def finish(m, carry):
        s = micro + m
        low = sbuf.at[m]

        def back(r):
            low[r] = (part[s, r] + h[s, r]).astype(BF)

        tiles(rows, back, lambda t: line.settle(s, 1, t))
        line.release(s, 1)
        down = lax.broadcasted_iota(jnp.int32, (rows, rows), 0).astype(F32)
        pick = jnp.where(slots[m, 0:1] == down, 1.0, 0.0).astype(BF)
        low[...] = tn(pick, low[...]).astype(BF)
        g_in[m] = low[own_rows]
        return carry

    plane("take", False, 2, True, final)
    vec_take(2)
    lax.fori_loop(0, micro, finish, 0)
    if inside:
        for layer in range(layers):
            leave(True, layer).wait()
            leave(False, layer).wait()


def run_step(inside, tokens, negatives, weights):
    q_tok = tokens[0]
    micro, _, rows, width = q_tok.shape
    wqkv, abias, wm, mbias, we, ebias, ws, sbias, gains, shifts = weights
    layers, local, units = we.shape[1], wm.shape[2], we.shape[3]
    heads = local // HEAD_DIM
    streams = 2 * micro
    share = rows // lax.axis_size("tensor")
    lm = (layers, micro)
    tall = 8 * ((9 * layers + 2 + 7) // 8)
    kinds = (units // 2, local)
    high = width // 8 if inside else width
    shapes = [((micro, share, width), BF), ((micro, share, width), BF), ((tall, width), F32)]
    if inside:
        shapes += [((layers, 2, high, units), F32), ((layers, 2, 2, high, local), F32)]
    else:
        shapes += [((layers, 2, 2, high, w), F32) for w in kinds]
    vm = pl.BlockSpec(memory_space=pltpu.VMEM)
    hb = pl.BlockSpec(memory_space=pl.ANY)
    sm = pl.BlockSpec(memory_space=pltpu.SMEM)
    dma = pltpu.SemaphoreType.DMA
    v = pltpu.VMEM
    scratch = [
        v(lm + (rows, width), BF),
        v(lm + (3, rows, local), BF),
        v(lm + (heads, rows, rows), BF),
        v(lm + (rows, local), BF),
        v(lm + (rows, width), BF),
        v(lm + (rows, width), BF),
        v(lm + (rows, units), BF),
        v(lm + (rows, units), BF),
        v(lm + (rows, width), BF),
        v(lm + (rows, 128), F32),
    ]
    scratch += [v(w.shape, BF) for w in (wqkv, wm, we, ws)]
    scratch += [
        v((streams * rows, width), BF),
        v((streams, rows, width), F32),
        v((rows, width), BF),
        v((3, rows, local), BF),
        v((rows, local), F32),
        v((rows, units), F32),
        v((streams, 8, rows), F32),
        v((streams, 8, rows), F32),
        v((2, layers, 8, width), F32),
        v((micro, 8, rows), F32),
        v((streams, 8, width), F32),
        v((micro, 8, width), F32),
        v((micro, 8, width), F32),
        v((layers, 7, 8, width), F32),
        v((layers, 2, 8, local), F32),
    ]
    scratch += [v((2, 2, width, w), F32) for w in kinds]
    scratch += [
        dma((4, 2, layers)),
        dma((streams + 1,)),
        v((micro, 8, width), F32),
        v((2, micro, 8, width), F32),
        dma((micro, 3)),
        dma((2, micro)),
    ]
    scratch += line_scratch(streams, rows, width)
    if inside:
        scratch += [pltpu.SemaphoreType.REGULAR(()), v(*shapes[3]), v(*shapes[4]), dma((2, layers))]
        for w in kinds + kinds[1:]:
            scratch += [v((2, 2, width // n, w), BF) for n in (2, 4, 8)]
        scratch += [dma((2, 3, 2))] * 4
        scratch += [pltpu.SemaphoreType.REGULAR((2, 3))] * 2
        scratch += [v((3, tall, width), F32), dma((3,)), dma((3,))]
        scratch += [
            v((micro, 16, width), BF),
            v((micro, 16, width), BF),
            v((micro, 2, 8, width), F32),
            v((micro, 8, 8, width), F32),
            dma((micro, 2)),
            dma((micro, 8)),
            dma((micro, 8)),
        ]
    else:
        scratch += [dma((2, 2, 2)), dma(())]
    return pl.pallas_call(
        functools.partial(step_kernel, inside),
        out_shape=[jax.ShapeDtypeStruct(*s) for s in shapes],
        in_specs=[hb, vm, sm, hb, vm, sm, hb] + [hb, vm, hb, vm, hb, vm, hb, vm, vm, vm],
        out_specs=[vm] * 3 + [hb] * 2,
        scratch_shapes=scratch,
        compiler_params=pltpu.CompilerParams(
            collective_id=0, has_side_effects=True, vmem_limit_bytes=VMEM_LIMIT
        ),
        name="training_step",
    )(*tokens, negatives, *weights)


def outputs_kernel(layers, size, acts, g_in, vec, big, small, o_acts, o_in, o_attend, o_abias, o_merge, o_mbias,
                   o_expand, o_ebias, o_shrink, o_sbias, o_gain, o_shift, o_loss):
    width = vec.shape[1]
    local = small.shape[4]
    o_acts[:, 0] = acts[...]
    o_in[:, 0] = g_in[...]
    for l in range(layers):
        o_shrink[l] = big[l, 0]
        o_expand[l] = big[l, 1]
        for j in range(3):
            o_attend[l, j] = small[l, j // 2, j % 2]
        o_merge[l] = small[l, 1, 1].T
    group = lax.axis_index("dp") * lax.axis_size("rep") + lax.axis_index("rep")
    blocks = width // size
    own = pltpu.roll(vec[...], ((blocks - group) % blocks) * size, axis=1)[:, :size]
    for l in range(layers):
        row = 7 * l
        o_gain[l] = own[row : row + 2]
        o_shift[l] = own[row + 2 : row + 4]
        o_sbias[l : l + 1] = own[row + 4 : row + 5]
        o_mbias[l : l + 1] = own[row + 5 : row + 6]
        o_ebias[l : l + 1] = vec[row + 6 : row + 7]
        o_abias[l] = vec[7 * layers + 2 * l : 7 * layers + 2 * l + 2, :local]
    o_loss[...] = vec[vec.shape[0] - 1 :, 0:1]


def run_outputs(acts, g_in, vec, big, small):
    micro, share, width = acts.shape
    layers, _, size, units = big.shape
    local = small.shape[4]
    shapes = [
        ((micro, 1, share, width), BF),
        ((micro, 1, share, width), BF),
        ((layers, 3, size, local), F32),
        ((layers, 2, local), F32),
        ((layers, local, size), F32),
        ((layers, size), F32),
        ((layers, size, units), F32),
        ((layers, width), F32),
        ((layers, size, units), F32),
        ((layers, size), F32),
        ((layers, 2, size), F32),
        ((layers, 2, size), F32),
        ((1, 1), F32),
    ]
    vm = pl.BlockSpec(memory_space=pltpu.VMEM)
    return pl.pallas_call(
        functools.partial(outputs_kernel, layers, size),
        out_shape=[jax.ShapeDtypeStruct(*s) for s in shapes],
        in_specs=[vm] * 5,
        out_specs=[vm] * len(shapes),
        compiler_params=pltpu.CompilerParams(vmem_limit_bytes=VMEM_LIMIT),
        name="outputs",
    )(acts, g_in, vec, big, small)


def per_device(
    query_tokens, query_drop, query_length, key_tokens, key_drop, key_length, negatives,
    attend_weight, attend_bias, merge_weight, merge_bias, expand_weight, expand_bias,
    shrink_weight, shrink_bias, norm_gain, norm_shift,
):
    micro = query_tokens.shape[0]
    weights = (
        jnp.transpose(attend_weight, (0, 1, 3, 4, 2)),
        attend_bias,
        merge_weight,
        merge_bias,
        expand_weight,
        expand_bias,
        shrink_weight,
        shrink_bias,
        norm_gain,
        norm_shift,
    )
    tokens = (query_tokens, query_drop, query_length.reshape(micro), key_tokens, key_drop, key_length.reshape(micro))
    groups = ("dp", "rep")
    inside = lax.axis_size("dp") == 4 and lax.axis_size("rep") == 2
    if not inside:
        negatives = lax.all_gather(negatives, ("rep", "tensor"), axis=0, tiled=True)
    acts, g_in, vec, g_big, g_small = run_step(inside, tokens, negatives, weights)
    if not inside:
        g_big = lax.psum_scatter(g_big, groups, scatter_dimension=3, tiled=True)
        g_small = lax.psum_scatter(g_small, groups, scatter_dimension=3, tiled=True)
        vec = lax.psum(vec, groups)
        g_big = g_big.transpose(0, 1, 3, 2, 4).reshape(g_big.shape[:2] + (g_big.shape[3], -1))
    outs = run_outputs(acts, g_in, vec, g_big, g_small)
    loss = outs[12].reshape(()) / (micro * lax.axis_size("dp") * lax.axis_size("rep"))
    return (
        outs[0], outs[1], jnp.transpose(outs[2], (0, 2, 1, 3)), *outs[3:8],
        jnp.transpose(outs[8], (0, 2, 1)), *outs[9:12], loss,
    )


def solution(mesh):
    return jax.shard_map(
        per_device,
        mesh=mesh,
        in_specs=(
            P(None, ("dp", "rep"), None, None),
            P(None, ("dp", "rep"), None),
            P(None, ("dp", "rep")),
            P(None, ("dp", "rep"), None, None),
            P(None, ("dp", "rep"), None),
            P(None, ("dp", "rep")),
            P(("rep", "tensor"), None),
            P(None, None, None, None, "tensor"),
            P(None, None, None, "tensor"),
            P(None, None, "tensor", None),
            P(),
            P(None, None, None, "tensor"),
            P(None, None, "tensor"),
            P(None, None, "tensor", None),
            P(),
            P(),
            P(),
        ),
        out_specs=(
            P(None, ("dp", "rep"), "tensor", None),
            P(None, ("dp", "rep"), "tensor", None),
            P(None, ("dp", "rep"), None, "tensor"),
            P(None, None, "tensor"),
            P(None, "tensor", ("dp", "rep")),
            P(None, ("dp", "rep")),
            P(None, ("dp", "rep"), "tensor"),
            P(None, "tensor"),
            P(None, "tensor", ("dp", "rep")),
            P(None, ("dp", "rep")),
            P(None, None, ("dp", "rep")),
            P(None, None, ("dp", "rep")),
            P(),
        ),
        check_vma=False,
    )
```

```python
import functools

import jax
import jax.numpy as jnp
from jax import lax
from jax.experimental import pallas as pl
from jax.experimental.pallas import tpu as pltpu
from jax.sharding import PartitionSpec as P

HEAD_DIM = 64
CROP_SLOTS = 256
SOFTMAX_WARMTH = 0.05
NORM_EPS = 1e-12
UNIT_EPS = 1e-06
MASKED = -1e30
TOP_PRECISION = lax.Precision.HIGHEST
ROOT_HALF = 0.7071067811865476
INV_ROOT_TAU = 0.3989422804014327

MESH = pl.DeviceIdType.MESH
BF = jnp.bfloat16
F32 = jnp.float32
CHUNKS = 8
LAG = 5
EARLY = 3
TILE = 64
VMEM_LIMIT = 62 * 1024 * 1024


def nn(a, b):
    return jnp.dot(a, b, preferred_element_type=F32)


def nt(a, b):
    return lax.dot_general(a, b, (((1,), (1,)), ((), ())), preferred_element_type=F32)


def tn(a, b):
    return lax.dot_general(a, b, (((0,), (0,)), ((), ())), preferred_element_type=F32)


class Line:
    def __init__(self, part, sbuf, tbuf, x1, x2, s_sem, t_sem, r1, r2):
        z = lax.axis_index("tensor")
        self.mid = (z + 1) // 2 == 1
        self.end = (z + 1) // 2 != 1
        self.lower = z // 2 == 0
        self.inner = 1 + z // 2
        self.outer = 3 * (z // 2)
        self.cross = 3 - z
        self.part, self.sbuf, self.tbuf, self.x1, self.x2 = part, sbuf, tbuf, x1, x2
        self.s_sem, self.t_sem, self.r1, self.r2 = s_sem, t_sem, r1, r2
        self.size = part.shape[1] // CHUNKS

    def rows(self, c):
        return pl.ds(pl.multiple_of(c * self.size, self.size), self.size)

    def near(self, c):
        return (c < CHUNKS // 2) == self.lower

    def outbound(self, c, narrow):
        return (c >= 0) if narrow is False else jnp.logical_not(narrow & self.near(c))

    def homebound(self, c, narrow):
        return (c >= 0) if narrow is False else jnp.logical_not(narrow) | self.near(c)

    def to_inner(self, s, c):
        return pltpu.make_async_remote_copy(
            src_ref=self.sbuf.at[s, self.rows(c)], dst_ref=self.x2.at[s, self.rows(c)],
            send_sem=self.s_sem.at[s, c], recv_sem=self.r2.at[s, c],
            device_id={"tensor": self.inner}, device_id_type=MESH)

    def to_cross(self, s, c, slot):
        return pltpu.make_async_remote_copy(
            src_ref=self.sbuf.at[s, self.rows(c)], dst_ref=self.x1.at[slot, s, self.rows(c)],
            send_sem=self.s_sem.at[s, c], recv_sem=self.r1.at[slot, s, c],
            device_id={"tensor": self.cross}, device_id_type=MESH)

    def to_outer(self, s, c, slot):
        return pltpu.make_async_remote_copy(
            src_ref=self.tbuf.at[s, self.rows(c)], dst_ref=self.x1.at[slot, s, self.rows(c)],
            send_sem=self.t_sem.at[s, c], recv_sem=self.r1.at[slot, s, c],
            device_id={"tensor": self.outer}, device_id_type=MESH)

    def begin(self, s, narrow=False, chunks=range(CHUNKS)):
        for c in chunks:
            @pl.when(self.end & self.outbound(c, narrow))
            def _():
                rows = self.rows(c)
                self.sbuf[s, rows] = self.part[s, rows].astype(BF)
                self.to_inner(s, c).start()

    def inward(self, s, c, slot, live, narrow=False):
        @pl.when(self.mid & live & self.outbound(c, narrow))
        def _():
            rows = self.rows(c)
            self.to_inner(s, c).wait_recv()
            self.sbuf[s, rows] = (self.part[s, rows] + self.x2[s, rows].astype(F32)).astype(BF)
            self.to_cross(s, c, slot).start()

    def outward(self, s, c, slot, live, narrow=False):
        @pl.when(self.mid & live & self.homebound(c, narrow))
        def _():
            rows = self.rows(c)
            self.to_cross(s, c, slot).wait_recv()
            joint = self.part[s, rows] + self.x1[slot, s, rows].astype(F32)
            self.part[s, rows] = joint + self.x2[s, rows].astype(F32)
            self.tbuf[s, rows] = joint.astype(BF)
            self.to_outer(s, c, slot).start()

    def settle(self, s, slot, tile, narrow=False):
        per = TILE // self.size
        for d in range(per):
            c = tile * per + d

            @pl.when(self.end & self.homebound(c, narrow))
            def _():
                rows = self.rows(c)
                self.to_outer(s, c, slot).wait_recv()
                self.part[s, rows] = self.part[s, rows] + self.x1[slot, s, rows].astype(F32)

    def release(self, s, slot, narrow=False):
        self.release_end(s, narrow)
        self.release_mid(s, slot, narrow)

    def release_end(self, s, narrow=False):
        for c in range(CHUNKS):
            @pl.when(self.end & self.outbound(c, narrow))
            def _():
                self.to_inner(s, c).wait_send()

    def release_mid(self, s, slot, narrow=False):
        for c in range(CHUNKS):
            @pl.when(self.mid & self.outbound(c, narrow))
            def _():
                self.to_cross(s, c, slot).wait_send()

            @pl.when(self.mid & self.homebound(c, narrow))
            def _():
                self.to_outer(s, c, slot).wait_send()


def line_scratch(streams, rows, width):
    return [
        pltpu.VMEM((streams, rows, width), F32),
        pltpu.VMEM((streams, rows, width), BF),
        pltpu.VMEM((streams, rows, width), BF),
        pltpu.VMEM((2, streams, rows, width), BF),
        pltpu.VMEM((streams, rows, width), BF),
        pltpu.SemaphoreType.DMA((streams, CHUNKS)),
        pltpu.SemaphoreType.DMA((streams, CHUNKS)),
        pltpu.SemaphoreType.DMA((2, streams, CHUNKS)),
        pltpu.SemaphoreType.DMA((streams, CHUNKS)),
    ]


def tiles(rows, body, ready=None, first=0):
    def step(c, carry):
        if ready is not None:
            ready(c)
        body(pl.ds(pl.multiple_of(c * TILE, TILE), TILE))
        return carry

    lax.fori_loop(first // TILE, rows // TILE, step, 0)


def normalize(total, gain, shift):
    mean = jnp.mean(total, axis=-1, keepdims=True)
    centered = total - mean
    inverse = lax.rsqrt(jnp.mean(centered * centered, axis=-1, keepdims=True) + NORM_EPS)
    normed = centered * inverse
    return normed * gain + shift, normed, inverse


def head_masks(width, scale):
    lane = lax.broadcasted_iota(jnp.int32, (1, width), 1)
    return [
        jnp.where((lane >= h * HEAD_DIM) & (lane < (h + 1) * HEAD_DIM), scale, 0.0).astype(BF)
        for h in range(width // HEAD_DIM)
    ]


def norm_back(g, normed, inverse, gain):
    scaled = g * gain
    return inverse * (
        scaled
        - jnp.mean(scaled, axis=-1, keepdims=True)
        - normed * jnp.mean(scaled * normed, axis=-1, keepdims=True)
    )


def fold(x):
    return jnp.sum(x.reshape(x.shape[0] // 8, 8, x.shape[1]), axis=0)


class Plane:
    def __init__(self, grads, sends, spots, recvs, out, send_sem, recv_sem, credit):
        dp, self.x = lax.axis_index("dp"), lax.axis_index("rep")
        self.y, self.c = dp // 2, dp % 2
        self.partner = {
            "c": {"dp": dp + 1 - 2 * self.c},
            "x": {"rep": 1 - self.x},
            "y": {"dp": (dp + 2) % 4},
        }
        self.grads, self.sends, self.places, self.recvs, self.out = grads, sends, spots, recvs, out
        self.send_sem, self.recv_sem, self.credit = send_sem, recv_sem, credit
        self.block = grads.shape[2] // 8
        self.wide = len(out.shape) == 4

    def message(self, u, stage, half, rows):
        if self.places is None:
            return self.sends[stage].at[u, half, rows]
        row, lane = self.places[stage]
        start = half * (self.grads.shape[2] // 2) + row
        return self.sends.at[u, pl.ds(start + rows.start, rows.size), pl.ds(lane, self.grads.shape[3])]

    def copy(self, u, stage, half):
        way = ("c", "xy"[half], "yx"[half])[stage]
        return pltpu.make_async_remote_copy(
            src_ref=self.message(u, stage, half, pl.ds(0, self.recvs[stage].shape[2])), dst_ref=self.recvs[stage].at[u, half],
            send_sem=self.send_sem.at[u, stage, half], recv_sem=self.recv_sem.at[u, stage, half],
            device_id=self.partner[way], device_id_type=MESH)

    def spots(self, stage, half, own):
        pick = (lambda v: v) if own else (lambda v: 1 - v)
        if stage == 0:
            return [(4 * y + 2 * pick(self.c), 2 * y, 2) for y in (0, 1)]
        if stage == 1 and half == 0:
            return [(4 * y + 2 * self.c + pick(self.x), y, 1) for y in (0, 1)]
        if stage == 1:
            return [(4 * pick(self.y) + 2 * self.c, 0, 2)]
        if half == 0:
            return [(4 * pick(self.y) + 2 * self.c + self.x, 0, 1)]
        return [(4 * self.y + 2 * self.c + pick(self.x), 0, 1)]

    def parts(self, stage, half, own):
        for here, there, blocks in self.spots(stage, half, own):
            for b in range(blocks):
                start = (here + b) * self.block
                yield pl.ds(pl.multiple_of(start, 8), self.block), pl.ds((there + b) * self.block, self.block)

    def send(self, u, stage, live, spend):
        @pl.when(live)
        def _():
            for half in (0, 1):
                for here, there in self.parts(stage, half, False):
                    self.message(u, stage, half, there)[...] = self.grads[u, half, here].astype(BF)

            @pl.when(spend)
            def _():
                pl.semaphore_wait(self.credit.at[u, stage], 2)

            for half in (0, 1):
                self.copy(u, stage, half).start()

    def take(self, u, stage, live, give, layer):
        @pl.when(live)
        def _():
            for half in (0, 1):
                self.copy(u, stage, half).wait()
                for here, there in self.parts(stage, half, True):
                    total = self.grads[u, half, here] + self.recvs[stage][u, half, there].astype(F32)
                    if stage == 2 and self.wide:
                        cols = self.grads.shape[3]
                        self.out[layer, u, :, half * cols : (half + 1) * cols] = total
                    elif stage == 2:
                        self.out[layer, u, half] = total
                    else:
                        self.grads[u, half, here] = total

            @pl.when(give)
            def _():
                for half in (0, 1):
                    way = ("c", "xy"[half], "yx"[half])[stage]
                    pl.semaphore_signal(
                        self.credit.at[u, stage], inc=1, device_id=self.partner[way], device_id_type=MESH
                    )


def greet(inside, ahead):
    z, dp, rep = lax.axis_index("tensor"), lax.axis_index("dp"), lax.axis_index("rep")
    sem = pltpu.get_barrier_semaphore()
    others = [{"tensor": (z + d) % 4} for d in (1, 2, 3)]
    if inside:
        others += [{"rep": 1 - rep, "tensor": (z + d) % 4} for d in (0, 1, 2, 3)]
        others += [{"dp": dp + 1 - 2 * (dp % 2)}, {"dp": (dp + 2) % 4}]
    for other in others:
        pl.semaphore_signal(sem, inc=1, device_id=other, device_id_type=MESH)
    ahead()
    pl.semaphore_wait(sem, len(others))


class Contrast:
    def __init__(self, inside, micro, pooled, keys, pgrad, vec, state, bufs):
        self.inside, self.micro, self.pooled, self.keys = inside, micro, pooled, keys
        self.pgrad, self.vec, self.state = pgrad, vec, state
        self.z, self.rep = lax.axis_index("tensor"), lax.axis_index("rep")
        if inside:
            (self.asks, self.asked, self.reply, self.heard, self.ask_sem, self.reply_sem, self.heard_sem) = bufs
        else:
            (self.source, self.key_sem) = bufs

    def question(self, m):
        return pltpu.make_async_remote_copy(
            src_ref=self.asks.at[m], dst_ref=self.asked.at[m], send_sem=self.ask_sem.at[m, 0],
            recv_sem=self.ask_sem.at[m, 1], device_id={"rep": 1 - self.rep}, device_id_type=MESH)

    def tell(self, m, which, d):
        other = {"tensor": (self.z + d) % 4}
        if which == 1:
            other["rep"] = 1 - self.rep
        k = which * 4 + d
        return pltpu.make_async_remote_copy(
            src_ref=self.reply.at[m, which], dst_ref=self.heard.at[m, k], send_sem=self.reply_sem.at[m, k],
            recv_sem=self.heard_sem.at[m, k], device_id=other, device_id_type=MESH)

    def score(self, rows_now):
        keys = self.keys[...]
        logits = nt(rows_now, keys) / SOFTMAX_WARMTH
        top = jnp.max(logits, axis=-1, keepdims=True)
        expo = jnp.exp(logits - top)
        total = jnp.sum(expo, axis=-1, keepdims=True)
        high = expo.astype(BF)
        rest = expo - high.astype(F32)
        mid = rest.astype(BF)
        tiny = (rest - mid.astype(F32)).astype(BF)
        weighted = nn(jnp.concatenate([high, mid, tiny], axis=0), keys)
        n = rows_now.shape[0]
        return weighted[:n] + weighted[n : 2 * n] + weighted[2 * n :], top, total

    def ask(self, m):
        count = self.pooled[self.micro + m, 1:2]
        mean = self.pooled[self.micro + m, 0:1] / count
        scale = lax.rsqrt(jnp.sum(mean * mean, axis=-1, keepdims=True) + UNIT_EPS)
        direction = mean * scale
        self.state[m, 0:1] = direction
        self.state[m, 1:2] = jnp.broadcast_to(scale, count.shape)
        self.state[m, 2:3] = count
        if self.inside:
            self.asks[m] = jnp.broadcast_to(direction, self.asks.shape[1:]).astype(BF)
            self.question(m).start()

    def respond(self, m):
        if self.inside:
            self.question(m).wait()
            half = lax.broadcasted_iota(jnp.int32, self.asks.shape[1:], 0) < 8
            weighted, top, total = self.score(jnp.where(half, self.asks[m], self.asked[m]))
            wide = (1, weighted.shape[1])
            for which in (0, 1):
                row = slice(8 * which, 8 * which + 1)
                self.reply[m, which, 0:1] = weighted[row]
                self.reply[m, which, 1:2] = jnp.broadcast_to(top[row], wide)
                self.reply[m, which, 2:3] = jnp.broadcast_to(total[row], wide)
            for d in (0, 1, 2, 3):
                self.tell(m, 1, d).start()
            for d in (1, 2, 3):
                self.tell(m, 0, d).start()

    def close(self, m, pooled_key):
        direction, scale, count = self.state[m, 0:1], self.state[m, 1:2, 0:1], self.state[m, 2:3]
        mean = pooled_key / self.pooled[m, 1:2]
        key_dir = mean * lax.rsqrt(jnp.sum(mean * mean, axis=-1, keepdims=True) + UNIT_EPS)
        positive = jnp.sum(direction * key_dir, axis=-1, keepdims=True) / SOFTMAX_WARMTH
        if self.inside:
            for k in range(1, 8):
                self.tell(m, k // 4, k % 4).wait()
            everyone = [self.reply[m, 0]] + [self.heard[m, k] for k in range(1, 8)]
            best = positive
            for one in everyone:
                best = jnp.maximum(best, one[1:2, 0:1])
            own = jnp.exp(positive - best)
            total, keys = own, own * key_dir
            for one in everyone:
                weight = jnp.exp(one[1:2, 0:1] - best)
                total = total + weight * one[2:3, 0:1]
                keys = keys + weight * one[0:1]
        else:
            rows_now = jnp.broadcast_to(direction, (16, direction.shape[1])).astype(BF)

            def piece(c, carry):
                best, total, keys = carry
                size = self.keys.shape[0]
                copy = pltpu.make_async_copy(
                    self.source.at[pl.ds(pl.multiple_of(c * size, size), size)], self.keys, self.key_sem)
                copy.start()
                copy.wait()
                weighted, top, part = (v[0:1] for v in self.score(rows_now))
                now = jnp.maximum(best, top)
                old, new = jnp.exp(best - now), jnp.exp(top - now)
                return now, total * old + part * new, keys * old + weighted * new

            start = (positive, jnp.ones_like(positive), key_dir)
            best, total, keys = lax.fori_loop(0, self.source.shape[0] // self.keys.shape[0], piece, start)
        loss = best + jnp.log(total) - positive
        last = self.vec.shape[0] - 1
        self.vec[last : last + 1] += jnp.broadcast_to(loss, direction.shape)
        dqn = (keys / total - key_dir) * (CROP_SLOTS / SOFTMAX_WARMTH)
        mean_grad = scale * (dqn - direction * jnp.sum(direction * dqn, axis=-1, keepdims=True))
        self.pgrad[m, 0:1] = mean_grad / count
        self.pgrad[m, 1:2] = count


def step_kernel(inside, *refs):
    q_tok, q_drop, q_len, k_tok, k_drop, k_len, negs, *refs = refs
    wqkv_in, abias, wm_in, mbias, we_in, ebias, ws_in, sbias, gains, shifts, *refs = refs
    acts, g_in, vec, out_big, out_small, *refs = refs
    xin, proj, probs, mixed, n1, first, slope, active, n2, inv, *refs = refs
    wqkv, wm, we, ws, tok, h, hb, qkv, mx, inner, *refs = refs
    vbias, valid, vecs, slots, pooled, state, pgrad, g_vec, g_abias, g_big, g_small, *refs = refs
    load_sem, tok_sem, kpart, kheard, kp_sem, kh_sem, *refs = refs
    line = Line(*refs[:9])
    part, sbuf, tbuf = refs[:3]
    refs = refs[9:]
    stored, loaded = (wqkv_in, wm_in, we_in, ws_in), (wqkv, wm, we, ws)
    micro = q_tok.shape[0]
    rows, width = q_tok.shape[2:]
    layers = we.shape[1]
    local = wm.shape[2]
    half_units = we.shape[3] // 2
    heads = local // HEAD_DIM
    streams = 2 * micro
    third = width // 3
    z = lax.axis_index("tensor")
    share = rows // lax.axis_size("tensor")
    own_rows = pl.ds(pl.multiple_of(z * share, 16), share)

    def load(k, e, layer):
        return pltpu.make_async_copy(stored[k].at[e, layer], loaded[k].at[e, layer], load_sem.at[k, e, layer])

    def load_tokens(s):
        source = k_tok if s < micro else q_tok
        return pltpu.make_async_copy(source.at[s % micro, 0], tok.at[pl.ds(s * rows, rows)], tok_sem.at[s])

    def load_keys():
        return pltpu.make_async_copy(negs, tok, tok_sem.at[streams])

    def compact(drop, length, is_q, s, m):
        pos = lax.broadcasted_iota(jnp.int32, (1, rows), 1)
        kept = (pos < length) & ((drop[m] == 0) | (pos == 0))
        kept_f = jnp.broadcast_to(jnp.where(kept, 1.0, 0.0), (16, rows))
        down = lax.broadcasted_iota(jnp.int32, (rows, rows), 0)
        along = lax.broadcasted_iota(jnp.int32, (rows, rows), 1)
        tri = jnp.where(down <= along, 1.0, 0.0).astype(BF)
        order = nn(kept_f.astype(BF), tri)[0:1] - 1.0
        order = jnp.where(kept, order, -1.0)
        count = jnp.sum(kept_f[0:1], axis=-1, keepdims=True)
        pick = jnp.where(order == down.astype(F32), 1.0, 0.0).astype(BF)
        rows_now = nn(pick, tok[pl.ds(s * rows if isinstance(s, int) else pl.multiple_of(s * rows, rows), rows)])
        h[s] = rows_now
        hb[...] = rows_now.astype(BF)
        fits = pos.astype(F32) < count
        vbias[s] = jnp.broadcast_to(jnp.where(fits, 0.0, MASKED), (8, rows))
        if not is_q:
            fits = fits & line.end & ((pos < rows // 2) == line.lower)
        valid[s] = jnp.broadcast_to(jnp.where(fits, 1.0, 0.0), (8, rows))
        pooled[s, 1:2] = jnp.broadcast_to(count, (1, width))
        if is_q:
            slots[m] = jnp.broadcast_to(order, (8, rows))

    def prepare():
        for layer in range(layers):
            for e in (1, 0):
                for k in (0, 1):
                    load(k, e, layer).start()
                if layer == 0:
                    for s in range((1 - e) * micro, (2 - e) * micro):
                        load_tokens(s).start()
                for k in (2, 3):
                    load(k, e, layer).start()
        vec[...] = jnp.zeros_like(vec)
        g_vec[...] = jnp.zeros_like(g_vec)
        g_abias[...] = jnp.zeros_like(g_abias)
        for e in range(2):
            for layer in range(layers):
                for row, ref in enumerate((mbias, ebias, sbias)):
                    vecs[e, layer, row : row + 1] = ref[e, layer : layer + 1].astype(F32)
                vecs[e, layer, 3:5] = gains[e, layer].astype(F32)
                vecs[e, layer, 5:7] = shifts[e, layer].astype(F32)
        load_tokens(0).wait()
        compact(k_drop, k_len[0], False, 0, 0)

    greet(inside, prepare)

    if inside:
        turn, red_big, red_small, red_sem, e1, e2, e3, t1, t2, t3, d1, d2, d3, big_s, big_r, small_s, small_r, big_c, small_c, v_rcv, v_send, v_recv, *bufs = refs
        w_big, quarter = half_units, width // 4
        big = Plane(g_big, we.at[1], ((0, 0), (0, w_big), (quarter, w_big)), (e1, e2, e3), red_big, big_s, big_r, big_c)
        small = Plane(g_small, (d1, d2, d3), None, (t1, t2, t3), red_small, small_s, small_r, small_c)
    else:
        g_sem, key_sem = refs
        bufs = (negs, key_sem)
    last_f = 2 * layers * streams

    def at_f(i):
        j = jnp.maximum(i, 0)
        s, stage = j % streams, j // streams
        return s, stage % 2, (i >= 0) & (i < last_f), (stage == 2 * layers - 1) & (s < micro)

    def tick_f(i, *which):
        for c in which:
            s, slot, live, narrow = at_f(i - 1)
            line.inward(s, c, slot, live, narrow)
            if c < LAG:
                s, slot, live, narrow = at_f(i - 2)
            line.outward(s, (c - LAG) % CHUNKS, slot, live, narrow)

    def second_norm(lp, e, s, narrow):
        m, is_q = s % micro, s >= micro
        bias, gain, shift = vecs[e, lp, 2:3], vecs[e, lp, 4:5], vecs[e, lp, 6:7]

        def norm(r):
            out, normed, inverse = normalize(h[s, r] + part[s, r] + bias, gain, shift)
            h[s, r] = out
            hb[r] = out.astype(BF)

            @pl.when(is_q)
            def _():
                n2[lp, m, r] = normed.astype(BF)
                inv[lp, m, r, 64:128] = jnp.broadcast_to(inverse, (TILE, 64))

        def own_half(r):
            @pl.when(line.end & ((r.start < rows // 2) == line.lower))
            def _():
                norm(r)

        tiles(rows, norm if narrow is False else own_half, lambda t: line.settle(s, 1, t, narrow))
        line.release(s, 1, narrow)

    def attention_pass(layer, s):
        i = layer * 2 * streams + s
        e, m = 1 - s // micro, s % micro
        is_q = s >= micro
        tick_f(i, 0)

        @pl.when(layer == 0)
        def _():
            @pl.when((s > 0) & (s < micro))
            def _():
                pltpu.make_async_copy(k_tok.at[m, 0], tok.at[pl.ds(0, rows)], tok_sem.at[s]).wait()
                compact(k_drop, k_len[m], False, s, m)

            @pl.when(is_q)
            def _():
                pltpu.make_async_copy(q_tok.at[m, 0], tok.at[pl.ds(0, rows)], tok_sem.at[s]).wait()
                compact(q_drop, q_len[m], True, s, m)

        @pl.when(layer > 0)
        def _():
            second_norm(layer - 1, e, s, False)

        tick_f(i, 1, 2)

        @pl.when(m == 0)
        def _():
            for k in (0, 1):
                load(k, e, layer).wait()

        @pl.when(is_q)
        def _():
            xin[layer, m] = hb[...]

        rows_now = hb[...]
        for j in range(3):
            bias = 0.0 if j == 1 else abias[e, layer, j // 2 : j // 2 + 1].astype(F32)
            qkv[j] = (nt(rows_now, wqkv[e, layer, j]) + bias).astype(BF)

        @pl.when(is_q)
        def _():
            for j in range(3):
                proj[layer, m, j] = qkv[j]

        tick_f(i, 3)
        q_masks = head_masks(local, HEAD_DIM**-0.5)
        v_masks = head_masks(local, 1.0)
        for hd in range(heads):
            scores = nt(qkv[0] * q_masks[hd], qkv[1]) + vbias[s, 0:1]
            expo = jnp.exp(scores - jnp.max(scores, axis=-1, keepdims=True))
            chance = (expo / jnp.sum(expo, axis=-1, keepdims=True)).astype(BF)

            @pl.when(is_q)
            def _():
                probs[layer, m, hd] = chance

            out = nn(chance, qkv[2] * v_masks[hd])
            if hd == 0:
                mx[...] = out
            else:
                mx[...] += out
            tick_f(i, 4 + hd)
        if inside:
            @pl.when((i == 1) & (big.c == 0) & line.end)
            def _():
                pl.semaphore_signal(turn, inc=1, device_id=big.partner["c"], device_id_type=MESH)

        mixed_now = mx[...].astype(BF)

        @pl.when(is_q)
        def _():
            mixed[layer, m] = mixed_now

        part[s] = nn(mixed_now, wm[e, layer])
        if inside:
            @pl.when((i == 0) & (big.c == 1) & line.end)
            def _():
                pl.semaphore_wait(turn, 1)

        line.begin(s)
        tick_f(i, *range(4 + heads, CHUNKS))

    def forward_pass(layer, s):
        i = (layer * 2 + 1) * streams + s
        e, m = 1 - s // micro, s % micro
        is_q = s >= micro
        tick_f(i, 0, 1)
        bias, gain, shift = vecs[e, layer, 0:1], vecs[e, layer, 3:4], vecs[e, layer, 5:6]

        def norm(r):
            out, normed, inverse = normalize(h[s, r] + part[s, r] + bias, gain, shift)
            h[s, r] = out
            hb[r] = out.astype(BF)

            @pl.when(is_q)
            def _():
                n1[layer, m, r] = normed.astype(BF)
                inv[layer, m, r, 0:64] = jnp.broadcast_to(inverse, (TILE, 64))
                first[layer, m, r] = out.astype(BF)

        tiles(rows, norm, lambda t: line.settle(s, 0, t))
        line.release(s, 0)

        @pl.when(m == 0)
        def _():
            for k in (2, 3):
                load(k, e, layer).wait()

        tick_f(i, 2, 3)
        inner[...] = nn(hb[...], we[e, layer])
        tick_f(i, 4)
        bias_e = vecs[e, layer, 1:2]

        def gelu(r):
            u = inner[r] + bias_e
            phi = 0.5 * (1.0 + lax.erf(u * ROOT_HALF))
            out = (u * phi).astype(BF)
            tbuf[s, r] = out

            @pl.when(is_q)
            def _():
                active[layer, m, r] = out
                slope[layer, m, r] = (phi + u * jnp.exp(-0.5 * u * u) * INV_ROOT_TAU).astype(BF)

        tiles(rows, gelu)
        tick_f(i, 5, 6)
        part[s] = nn(tbuf[s], ws[e, layer])
        line.begin(s, (layer == layers - 1) & (s < micro))
        tick_f(i, 7)

    def layer_step(layer, carry):
        def a_step(s, c):
            attention_pass(layer, s)
            return c

        def f_step(s, c):
            forward_pass(layer, s)
            return c

        lax.fori_loop(0, streams, a_step, 0)
        if inside:
            @pl.when(layer == 0)
            def _():
                load_keys().start()

        lax.fori_loop(0, streams, f_step, 0)
        return carry

    lax.fori_loop(0, layers, layer_step, 0)

    def pool(s):
        return jnp.dot(valid[s], h[s], precision=TOP_PRECISION, preferred_element_type=F32)

    def kshare(m, d):
        return pltpu.make_async_remote_copy(
            src_ref=kpart.at[m], dst_ref=kheard.at[z // 3, m], send_sem=kp_sem.at[m, d - 1],
            recv_sem=kh_sem.at[z // 3, m], device_id={"tensor": (z + d) % 4}, device_id_type=MESH)

    def last_key(m):
        second_norm(layers - 1, 1, m, line.part.shape[0] > 0)

        @pl.when(line.mid)
        def _():
            kpart[m] = jnp.zeros_like(kpart[m])

        @pl.when(line.end)
        def _():
            kpart[m] = pool(m)
            for d in (1, 2, 3):
                kshare(m, d).start()

    def last_query(m):
        second_norm(layers - 1, 0, micro + m, False)
        pooled[micro + m, 0:1] = pool(micro + m)[0:1]
        acts[m] = hb[own_rows]

    def pooled_key(m):
        @pl.when(line.end)
        def _():
            for d in (1, 2, 3):
                kshare(m, d).wait_send()

        total = kpart[m, 0:1]
        for e in (0, 1):
            @pl.when(z != 3 * e)
            def _():
                pltpu.make_async_remote_copy(
                    src_ref=kpart.at[m], dst_ref=kheard.at[e, m], send_sem=kp_sem.at[m, 0],
                    recv_sem=kh_sem.at[e, m], device_id={"tensor": 3 - z}, device_id_type=MESH).wait_recv()

            total = total + jnp.where(z != 3 * e, kheard[e, m, 0:1], 0.0)
        return total

    queue = Contrast(inside, micro, pooled, tok, pgrad, vec, state, bufs)
    tick_f(last_f, 0, 1, 2)
    for m in range(micro):
        last_key(m)
        tick_f(last_f, 3 + m)
    if inside:
        load_keys().wait()
    for m in range(micro):
        if m == micro - 1:
            tick_f(last_f, *range(3 + micro, CHUNKS))
            tick_f(last_f + 1, *range(LAG))
        if m > 0:
            queue.respond(m - 1)
        last_query(m)
        queue.ask(m)

    last_b = 2 * layers * micro
    dinner = tbuf.at[1]
    heads_f = [h.at[0, :, pl.ds(j * third, local)] for j in range(3)]
    heads_b = [tbuf.at[0, :, pl.ds(j * third, local)] for j in range(3)]

    def at_b(i):
        j = jnp.maximum(i, 0)
        return micro + j % micro, (j // micro) % 2, (i >= 0) & (i < last_b)

    def tick(i, *which):
        for g in which:
            s, slot, live = at_b(i - 1)
            if g >= 1 and g - 1 < CHUNKS:
                line.outward(s, g - 1, slot, live)
            c = g + EARLY
            if c >= CHUNKS + 1:
                s, slot, live = at_b(i)
                c -= CHUNKS + 1
                if c < EARLY:
                    line.inward(s, c, slot, live)
            elif c < CHUNKS:
                line.inward(s, c, slot, live)

    def drained(large, layer, u, half):
        source, target = (g_big, out_big) if large else (g_small, out_small)
        return pltpu.make_async_copy(source.at[u, half], target.at[layer, u, half], g_sem.at[0 if large else 1, u, half])

    def add_to(large, u, half, s, value):
        ref = (g_big if large else g_small).at[u, half]

        @pl.when(s == 0)
        def _():
            ref[...] = value

        @pl.when(s > 0)
        def _():
            ref[...] += value

    def leave(large, layer):
        source, target = (red_big, out_big) if large else (red_small, out_small)
        return pltpu.make_async_copy(source.at[layer], target.at[layer], red_sem.at[0 if large else 1, layer])

    def plane(what, large, stage, live, step):
        for u in (0, 1):
            if inside:
                group = big if large else small
                if what == "send":
                    group.send(u, stage, live, step > 0)
                else:
                    group.take(u, stage, live, step < layers - 1, layers - 1 - step)
            elif (what, stage) in (("send", 0), ("take", 2)):
                @pl.when(live)
                def _():
                    for half in (0, 1):
                        copy = drained(large, layers - 1 - step, u, half)
                        copy.start() if what == "send" else copy.wait()
        if inside and (what, stage) == ("take", 2):
            @pl.when(live)
            def _():
                leave(large, layers - 1 - step).start()

    def mlp_back(step, m):
        layer = layers - 1 - step
        i = step * 2 * micro + m
        s = micro + m
        low = sbuf.at[m]

        @pl.when(step == 0)
        def _():
            queue.close(m, pooled_key(m))

            def begin(c, carry):
                r = pl.ds(pl.multiple_of(c * TILE, TILE), TILE)
                pos = (lax.broadcasted_iota(jnp.int32, (TILE, 1), 0) + c * TILE).astype(F32)
                part[s, r] = jnp.where(pos < pgrad[m, 1:2, 0:1], pgrad[m, 0:1], 0.0)
                h[s, r] = jnp.zeros((TILE, width), F32)
                return carry

            lax.fori_loop(0, rows // TILE, begin, 0)

        gain = vecs[0, layer, 4:5]

        def back(r):
            g = part[s, r] + h[s, r]
            normed = n2[layer, m, r].astype(F32)
            out = norm_back(g, normed, inv[layer, m, r][:, 64:65], gain)
            h[s, r] = out
            low[r] = out.astype(BF)
            g_vec[layer, 1] += fold(g * normed)
            g_vec[layer, 3] += fold(g)
            g_vec[layer, 4] += fold(out)

        def ready(t):
            @pl.when(step > 0)
            def _():
                line.settle(s, 1, t)

        def slopes(r):
            out = inner[r] * slope[layer, m, r].astype(F32)
            dinner[r] = out.astype(BF)
            g_vec[layer, 6] += fold(out)

        for half in (0, 1):
            first_row, last_row = half * rows // 2, (half + 1) * rows // 2
            span = pl.ds(first_row, rows // 2)
            tiles(last_row, back, ready, first_row)
            if half == 0:
                @pl.when(step > 0)
                def _():
                    line.release_end(s)

            tick(i, 2 * half)
            inner[span] = nt(low[span], ws[0, layer])

            tick(i, 2 * half + 1)
            tiles(last_row, slopes, None, first_row)
            part[s, span] = nt(dinner[span], we[0, layer])
            line.begin(s, False, range(half * CHUNKS // 2, (half + 1) * CHUNKS // 2))
            if half == 0:
                @pl.when((step == 0) & (m == 0))
                def _():
                    queue.respond(micro - 1)

        @pl.when(step > 0)
        def _():
            line.release_mid(s, 1)

        plane("take", True, 2, (step > 0) & (m == 0), step - 1)
        for half in (0, 1):
            cols = pl.ds(half * half_units, half_units)
            add_to(True, 0, half, m, tn(low[...], active[layer, m, :, cols]))
            tick(i, 4 + half)
        for half in (0, 1):
            cols = pl.ds(half * half_units, half_units)
            add_to(True, 1, half, m, tn(first[layer, m], dinner[:, cols]))
            tick(i, 6 + half)
        plane("take", False, 0, (step > 0) & (m == 0), step - 1)
        plane("send", False, 1, (step > 0) & (m == 0), step - 1)
        plane("send", True, 0, m == micro - 1, step)
        plane("take", False, 1, (step > 0) & (m == micro - 1), step - 1)
        plane("send", False, 2, (step > 0) & (m == micro - 1), step - 1)
        tick(i, CHUNKS)

    def attention_back(step, m):
        layer = layers - 1 - step
        i = (step * 2 + 1) * micro + m
        s = micro + m
        low = sbuf.at[m]
        gain = vecs[0, layer, 3:4]

        def back(r):
            g = part[s, r] + h[s, r]
            normed = n1[layer, m, r].astype(F32)
            out = norm_back(g, normed, inv[layer, m, r][:, 0:1], gain)
            h[s, r] = out
            low[r] = out.astype(BF)
            g_vec[layer, 0] += fold(g * normed)
            g_vec[layer, 2] += fold(g)
            g_vec[layer, 5] += fold(out)

        tiles(rows, back, lambda t: line.settle(s, 0, t))
        line.release(s, 0)
        tick(i, 0)
        dmix = nt(low[...], wm[0, layer]).astype(BF)
        tick(i, 1)
        masks = head_masks(local, 1.0)
        for hd in range(heads):
            chance_b = probs[layer, m, hd]
            chance = chance_b.astype(F32)
            dm = dmix * masks[hd]
            dch = nt(dm, proj[layer, m, 2])
            ds = chance * (dch - jnp.sum(chance * dch, axis=-1, keepdims=True))
            draw = (ds * HEAD_DIM**-0.5).astype(BF)
            dq = nn(draw, proj[layer, m, 1] * masks[hd])
            dk = tn(draw, proj[layer, m, 0] * masks[hd])
            dv = tn(chance_b, dm)
            for ref, value in zip(heads_f, (dq, dk, dv)):
                if hd == 0:
                    ref[...] = value
                else:
                    ref[...] += value
            tick(i, 2 + hd)
        g_abias[layer, 0] += fold(heads_f[0][...])
        g_abias[layer, 1] += fold(heads_f[2][...])
        for j in range(3):
            heads_b[j][...] = heads_f[j][...].astype(BF)
        for half in (0, 1):
            span = pl.ds(half * rows // 2, rows // 2)
            part[s, span] = sum(nn(tbuf[0, span, j * third : j * third + local], wqkv[0, layer, j]) for j in range(3))
            line.begin(s, False, range(half * CHUNKS // 2, (half + 1) * CHUNKS // 2))
        tick(i, *range(2 + heads, 6))
        plane("take", True, 0, m == 0, step)
        plane("send", True, 1, m == 0, step)
        plane("take", True, 1, m == micro - 1, step)
        plane("send", True, 2, m == micro - 1, step)
        plane("take", False, 2, (step > 0) & (m == 0), step - 1)
        for j in range(3):
            add_to(False, j // 2, j % 2, m, tn(xin[layer, m], heads_b[j][...]))
        tick(i, 6)
        add_to(False, 1, 1, m, tn(low[...], mixed[layer, m]))
        tick(i, 7, CHUNKS)
        plane("send", False, 0, m == micro - 1, step)

    def back_step(step, carry):
        def m_step(m, c):
            mlp_back(step, m)
            return c

        def a_step(m, c):
            attention_back(step, m)
            return c

        lax.fori_loop(0, micro, m_step, 0)
        lax.fori_loop(0, micro, a_step, 0)
        return carry

    lax.fori_loop(0, layers, back_step, 0)

    for layer in range(layers):
        for k in range(7):
            vec[layer * 7 + k : layer * 7 + k + 1] = jnp.sum(g_vec[layer, k], axis=0, keepdims=True)
        for k in range(2):
            row = layers * 7 + layer * 2 + k
            vec[row : row + 1, 0:local] = jnp.sum(g_abias[layer, k], axis=0, keepdims=True)

    def vec_copy(stage):
        return pltpu.make_async_remote_copy(
            src_ref=vec, dst_ref=v_rcv.at[stage], send_sem=v_send.at[stage], recv_sem=v_recv.at[stage],
            device_id=big.partner["cxy"[stage]], device_id_type=MESH)

    def vec_take(stage):
        if inside:
            vec_copy(stage).wait()
            vec[...] += v_rcv[stage]

    def vec_send(stage):
        if inside:
            vec_copy(stage).start()

    final = layers - 1
    vec_send(0)
    tick(last_b, 0, 1)
    plane("take", False, 0, True, final)
    plane("send", False, 1, True, final)
    vec_take(0)
    vec_send(1)
    tick(last_b, 2, 3, 4)
    plane("take", True, 2, True, final)
    tick(last_b, 5, 6)
    plane("take", False, 1, True, final)
    plane("send", False, 2, True, final)
    vec_take(1)
    vec_send(2)
    tick(last_b, 7, CHUNKS)

    def finish(m, carry):
        s = micro + m
        low = sbuf.at[m]

        def back(r):
            low[r] = (part[s, r] + h[s, r]).astype(BF)

        tiles(rows, back, lambda t: line.settle(s, 1, t))
        line.release(s, 1)
        down = lax.broadcasted_iota(jnp.int32, (rows, rows), 0).astype(F32)
        pick = jnp.where(slots[m, 0:1] == down, 1.0, 0.0).astype(BF)
        low[...] = tn(pick, low[...]).astype(BF)
        g_in[m] = low[own_rows]
        return carry

    plane("take", False, 2, True, final)
    vec_take(2)
    lax.fori_loop(0, micro, finish, 0)
    if inside:
        for layer in range(layers):
            leave(True, layer).wait()
            leave(False, layer).wait()


def run_step(inside, tokens, negatives, weights):
    q_tok = tokens[0]
    micro, _, rows, width = q_tok.shape
    wqkv, abias, wm, mbias, we, ebias, ws, sbias, gains, shifts = weights
    layers, local, units = we.shape[1], wm.shape[2], we.shape[3]
    heads = local // HEAD_DIM
    streams = 2 * micro
    share = rows // lax.axis_size("tensor")
    lm = (layers, micro)
    tall = 8 * ((9 * layers + 2 + 7) // 8)
    kinds = (units // 2, local)
    high = width // 8 if inside else width
    shapes = [((micro, share, width), BF), ((micro, share, width), BF), ((tall, width), F32)]
    if inside:
        shapes += [((layers, 2, high, units), F32), ((layers, 2, 2, high, local), F32)]
    else:
        shapes += [((layers, 2, 2, high, w), F32) for w in kinds]
    vm = pl.BlockSpec(memory_space=pltpu.VMEM)
    hb = pl.BlockSpec(memory_space=pl.ANY)
    sm = pl.BlockSpec(memory_space=pltpu.SMEM)
    dma = pltpu.SemaphoreType.DMA
    v = pltpu.VMEM
    scratch = [
        v(lm + (rows, width), BF),
        v(lm + (3, rows, local), BF),
        v(lm + (heads, rows, rows), BF),
        v(lm + (rows, local), BF),
        v(lm + (rows, width), BF),
        v(lm + (rows, width), BF),
        v(lm + (rows, units), BF),
        v(lm + (rows, units), BF),
        v(lm + (rows, width), BF),
        v(lm + (rows, 128), F32),
    ]
    scratch += [v(w.shape, BF) for w in (wqkv, wm, we, ws)]
    scratch += [
        v((streams * rows, width), BF),
        v((streams, rows, width), F32),
        v((rows, width), BF),
        v((3, rows, local), BF),
        v((rows, local), F32),
        v((rows, units), F32),
        v((streams, 8, rows), F32),
        v((streams, 8, rows), F32),
        v((2, layers, 8, width), F32),
        v((micro, 8, rows), F32),
        v((streams, 8, width), F32),
        v((micro, 8, width), F32),
        v((micro, 8, width), F32),
        v((layers, 7, 8, width), F32),
        v((layers, 2, 8, local), F32),
    ]
    scratch += [v((2, 2, width, w), F32) for w in kinds]
    scratch += [
        dma((4, 2, layers)),
        dma((streams + 1,)),
        v((micro, 8, width), F32),
        v((2, micro, 8, width), F32),
        dma((micro, 3)),
        dma((2, micro)),
    ]
    scratch += line_scratch(streams, rows, width)
    if inside:
        scratch += [pltpu.SemaphoreType.REGULAR(()), v(*shapes[3]), v(*shapes[4]), dma((2, layers))]
        for w in kinds + kinds[1:]:
            scratch += [v((2, 2, width // n, w), BF) for n in (2, 4, 8)]
        scratch += [dma((2, 3, 2))] * 4
        scratch += [pltpu.SemaphoreType.REGULAR((2, 3))] * 2
        scratch += [v((3, tall, width), F32), dma((3,)), dma((3,))]
        scratch += [
            v((micro, 16, width), BF),
            v((micro, 16, width), BF),
            v((micro, 2, 8, width), F32),
            v((micro, 8, 8, width), F32),
            dma((micro, 2)),
            dma((micro, 8)),
            dma((micro, 8)),
        ]
    else:
        scratch += [dma((2, 2, 2)), dma(())]
    return pl.pallas_call(
        functools.partial(step_kernel, inside),
        out_shape=[jax.ShapeDtypeStruct(*s) for s in shapes],
        in_specs=[hb, vm, sm, hb, vm, sm, hb] + [hb, vm, hb, vm, hb, vm, hb, vm, vm, vm],
        out_specs=[vm] * 3 + [hb] * 2,
        scratch_shapes=scratch,
        compiler_params=pltpu.CompilerParams(
            collective_id=0, has_side_effects=True, vmem_limit_bytes=VMEM_LIMIT
        ),
        name="training_step",
    )(*tokens, negatives, *weights)


def outputs_kernel(layers, size, acts, g_in, vec, big, small, o_acts, o_in, o_attend, o_abias, o_merge, o_mbias,
                   o_expand, o_ebias, o_shrink, o_sbias, o_gain, o_shift, o_loss):
    width = vec.shape[1]
    local = small.shape[4]
    o_acts[:, 0] = acts[...]
    o_in[:, 0] = g_in[...]
    for l in range(layers):
        o_shrink[l] = big[l, 0]
        o_expand[l] = big[l, 1]
        for j in range(3):
            o_attend[l, j] = small[l, j // 2, j % 2]
        o_merge[l] = small[l, 1, 1].T
    group = lax.axis_index("dp") * lax.axis_size("rep") + lax.axis_index("rep")
    blocks = width // size
    own = pltpu.roll(vec[...], ((blocks - group) % blocks) * size, axis=1)[:, :size]
    for l in range(layers):
        row = 7 * l
        o_gain[l] = own[row : row + 2]
        o_shift[l] = own[row + 2 : row + 4]
        o_sbias[l : l + 1] = own[row + 4 : row + 5]
        o_mbias[l : l + 1] = own[row + 5 : row + 6]
        o_ebias[l : l + 1] = vec[row + 6 : row + 7]
        o_abias[l] = vec[7 * layers + 2 * l : 7 * layers + 2 * l + 2, :local]
    o_loss[...] = vec[vec.shape[0] - 1 :, 0:1]


def run_outputs(acts, g_in, vec, big, small):
    micro, share, width = acts.shape
    layers, _, size, units = big.shape
    local = small.shape[4]
    shapes = [
        ((micro, 1, share, width), BF),
        ((micro, 1, share, width), BF),
        ((layers, 3, size, local), F32),
        ((layers, 2, local), F32),
        ((layers, local, size), F32),
        ((layers, size), F32),
        ((layers, size, units), F32),
        ((layers, width), F32),
        ((layers, size, units), F32),
        ((layers, size), F32),
        ((layers, 2, size), F32),
        ((layers, 2, size), F32),
        ((1, 1), F32),
    ]
    vm = pl.BlockSpec(memory_space=pltpu.VMEM)
    return pl.pallas_call(
        functools.partial(outputs_kernel, layers, size),
        out_shape=[jax.ShapeDtypeStruct(*s) for s in shapes],
        in_specs=[vm] * 5,
        out_specs=[vm] * len(shapes),
        compiler_params=pltpu.CompilerParams(vmem_limit_bytes=VMEM_LIMIT),
        name="outputs",
    )(acts, g_in, vec, big, small)


def per_device(
    query_tokens, query_drop, query_length, key_tokens, key_drop, key_length, negatives,
    attend_weight, attend_bias, merge_weight, merge_bias, expand_weight, expand_bias,
    shrink_weight, shrink_bias, norm_gain, norm_shift,
):
    micro = query_tokens.shape[0]
    weights = (
        jnp.transpose(attend_weight, (0, 1, 3, 4, 2)),
        attend_bias,
        merge_weight,
        merge_bias,
        expand_weight,
        expand_bias,
        shrink_weight,
        shrink_bias,
        norm_gain,
        norm_shift,
    )
    tokens = (query_tokens, query_drop, query_length.reshape(micro), key_tokens, key_drop, key_length.reshape(micro))
    groups = ("dp", "rep")
    inside = lax.axis_size("dp") == 4 and lax.axis_size("rep") == 2
    if not inside:
        negatives = lax.all_gather(negatives, ("rep", "tensor"), axis=0, tiled=True)
    acts, g_in, vec, g_big, g_small = run_step(inside, tokens, negatives, weights)
    if not inside:
        g_big = lax.psum_scatter(g_big, groups, scatter_dimension=3, tiled=True)
        g_small = lax.psum_scatter(g_small, groups, scatter_dimension=3, tiled=True)
        vec = lax.psum(vec, groups)
        g_big = g_big.transpose(0, 1, 3, 2, 4).reshape(g_big.shape[:2] + (g_big.shape[3], -1))
    outs = run_outputs(acts, g_in, vec, g_big, g_small)
    loss = outs[12].reshape(()) / (micro * lax.axis_size("dp") * lax.axis_size("rep"))
    return (
        outs[0], outs[1], jnp.transpose(outs[2], (0, 2, 1, 3)), *outs[3:8],
        jnp.transpose(outs[8], (0, 2, 1)), *outs[9:12], loss,
    )


def solution(mesh):
    return jax.shard_map(
        per_device,
        mesh=mesh,
        in_specs=(
            P(None, ("dp", "rep"), None, None),
            P(None, ("dp", "rep"), None),
            P(None, ("dp", "rep")),
            P(None, ("dp", "rep"), None, None),
            P(None, ("dp", "rep"), None),
            P(None, ("dp", "rep")),
            P(("rep", "tensor"), None),
            P(None, None, None, None, "tensor"),
            P(None, None, None, "tensor"),
            P(None, None, "tensor", None),
            P(),
            P(None, None, None, "tensor"),
            P(None, None, "tensor"),
            P(None, None, "tensor", None),
            P(),
            P(),
            P(),
        ),
        out_specs=(
            P(None, ("dp", "rep"), "tensor", None),
            P(None, ("dp", "rep"), "tensor", None),
            P(None, ("dp", "rep"), None, "tensor"),
            P(None, None, "tensor"),
            P(None, "tensor", ("dp", "rep")),
            P(None, ("dp", "rep")),
            P(None, ("dp", "rep"), "tensor"),
            P(None, "tensor"),
            P(None, "tensor", ("dp", "rep")),
            P(None, ("dp", "rep")),
            P(None, None, ("dp", "rep")),
            P(None, None, ("dp", "rep")),
            P(),
        ),
        check_vma=False,
    )
```
